32 devices in a mesh: dp: 8 (over y, x, core), tensor: 4 (over z).
Axes of the slice: x: 2, y: 2, z: 4, core: 2. Of those that a mesh axis runs over, the one named last changes fastest.
Arguments:
- tokens: bfloat16 [32768, 768], P(('dp', 'tensor')), may hold values from -6 to 6
- cotangent: bfloat16 [32768, 768], P(('dp', 'tensor')), may hold values from -6 to 6
- source: int32 [32768], P(('dp', 'tensor')), may hold values from 0 to 32767, as said below
- target: int32 [32768], P(('dp', 'tensor')), may hold values from 0 to 32767, as said below
- lengths: int32 [8, 3], P('dp'), may hold values from 1 to 2048, as said below
- ln_gain: float32 [768], P(('dp', 'tensor')), may hold values from 0.5 to 1.5
- ln_bias: float32 [768], P(('dp', 'tensor')), may hold values from -1.75 to 1.75
- w_fwd: bfloat16 [768, 1536], P('dp', 'tensor'), may hold values from -0.21875 to 0.21875
- b_fwd: float32 [1536], P(('dp', 'tensor')), may hold values from -3 to 3
- w_bwd: bfloat16 [768, 1536], P('dp', 'tensor'), may hold values from -0.21875 to 0.21875
- b_bwd: float32 [1536], P(('dp', 'tensor')), may hold values from -3 to 3
- w_gate: bfloat16 [768, 2, 1536], P('dp', None, 'tensor'), may hold values from -0.21875 to 0.21875
- b_gate: float32 [2, 1536], P(None, ('dp', 'tensor')), may hold values from -3 to 3
- w_out: bfloat16 [2, 1536, 768], P(None, 'tensor', 'dp'), may hold values from -0.109375 to 0.109375
- b_out: float32 [768], P(('dp', 'tensor')), may hold values from -1.75 to 1.75
- log_dt: float32 [2, 1536], P(None, ('dp', 'tensor')), may hold values from -6.9 to -2.3
- log_rate: float32 [2, 1536, 64], P(None, ('dp', 'tensor')), may hold values from -0.7 to 4.2
- ssm_b: float32 [2, 1536, 64], P(None, ('dp', 'tensor')), may hold values from -6 to 6
- ssm_c: float32 [2, 1536, 64], P(None, ('dp', 'tensor')), may hold values from -6 to 6
- ssm_d: float32 [2, 1536], P(None, ('dp', 'tensor')), may hold values from -6 to 6
Outputs:
- layer_out: bfloat16 [32768, 768], P(('dp', 'tensor'))
- input_grad: bfloat16 [32768, 768], P(('dp', 'tensor'))
- ln_gain_grad: float32 [768], P(('dp', 'tensor'))
- ln_bias_grad: float32 [768], P(('dp', 'tensor'))
- w_fwd_grad: float32 [768, 1536], P('dp', 'tensor')
- b_fwd_grad: float32 [1536], P(('dp', 'tensor'))
- w_bwd_grad: float32 [768, 1536], P('dp', 'tensor')
- b_bwd_grad: float32 [1536], P(('dp', 'tensor'))
- w_gate_grad: float32 [768, 2, 1536], P('dp', None, 'tensor')
- b_gate_grad: float32 [2, 1536], P(None, ('dp', 'tensor'))
- w_out_grad: float32 [2, 1536, 768], P(None, 'tensor', 'dp')
- b_out_grad: float32 [768], P(('dp', 'tensor'))
- log_dt_grad: float32 [2, 1536], P(None, ('dp', 'tensor'))
- log_rate_grad: float32 [2, 1536, 64], P(None, ('dp', 'tensor'))
- ssm_b_grad: float32 [2, 1536, 64], P(None, ('dp', 'tensor'))
- ssm_c_grad: float32 [2, 1536, 64], P(None, ('dp', 'tensor'))
- ssm_d_grad: float32 [2, 1536], P(None, ('dp', 'tensor'))
The draws below stay inside these ranges and needn't reach their ends.
Inputs may be any that keep to these rules, and one draw needn't show every extreme that they name: Row q of the dealt order takes row source[q] of the given order. Both orders are cut into blocks of 1024 rows, one a device in the order of the dp+tensor placement; a row moves only between devices with the same tensor index, and exactly 1024 / (devices of dp) rows move from each such device to each such device. The inverse of source: source[target[r]] = r. `lengths`: the slots of a group's sequences, each rounded up to a multiple of 128 rows, fit in its 4096 rows; every group has a sequence of exactly 2048 rows.
All inputs are finite; a program needn't handle non-finite values.
Results may differ from the reference program's by a relative error of at most 0.012.
Values may be sent and summed in bfloat16 or wider, within the bound.
A program may use at most 448 MiB of HBM per device.

```python
import jax
import jax.numpy as jnp
from jax import lax

D = 768
U = 3072
V = 1536
N = 64
TOK_DEV = 1024
BLK = 128
GROUP_TOK = 4096
TOKENS = 32768
MOST = 2048
SEQ_GRP = 3
N_DP = 8
N_TENSOR = 4


def dealing(key):
    per_pair = TOK_DEV // N_DP
    first_key, second_key = jax.random.split(jax.random.fold_in(key, 11))
    key_count = N_DP * N_TENSOR
    permuter = jax.vmap(lambda sub_key: jax.random.permutation(sub_key, TOK_DEV))
    arrival = permuter(jax.random.split(first_key, key_count)).reshape(N_DP, N_TENSOR, TOK_DEV).astype(jnp.int32)
    shuffle = permuter(jax.random.split(second_key, key_count)).reshape(N_DP, N_TENSOR, TOK_DEV).astype(jnp.int32)
    sender = arrival // per_pair
    within = arrival % per_pair
    dest_dp = jnp.arange(N_DP, dtype=jnp.int32)[:, None, None]
    tensor_pos = jnp.arange(N_TENSOR, dtype=jnp.int32)[None, :, None]
    slot_rank = dest_dp * per_pair + within
    old_local = shuffle[sender, tensor_pos, slot_rank]
    source = ((sender * N_TENSOR + tensor_pos) * TOK_DEV + old_local).reshape(-1).astype(jnp.int32)
    target = jnp.zeros((TOKENS,), jnp.int32).at[source].set(jnp.arange(TOKENS, dtype=jnp.int32))
    return (source, target)


def draw_source(key, part):
    return dealing(key)[0]


def draw_target(key, part):
    return dealing(key)[1]


def draw_lengths(key, part):
    block_key, rem_key, top_key = jax.random.split(jax.random.fold_in(key, 5), 3)
    spare_blocks = (GROUP_TOK // BLK - MOST // BLK) // (SEQ_GRP - 1)
    blocks = jax.random.randint(block_key, (N_DP, SEQ_GRP), 1, spare_blocks + 1)
    trimmed = jax.random.randint(rem_key, (N_DP, SEQ_GRP), 0, BLK)
    chosen = jax.random.randint(top_key, (N_DP, 1), 0, SEQ_GRP)
    longest = jnp.arange(SEQ_GRP, dtype=jnp.int32)[None, :] == chosen
    return jnp.where(longest, MOST, blocks * BLK - trimmed).astype(jnp.int32)


def shard_levels(own_key, shape, shards, least, high):
    level = 1.0
    for axis_at, shards_of in shards:
        draws = jax.random.uniform(jax.random.fold_in(jax.random.fold_in(own_key, 6), axis_at), (shards_of,), jnp.float32, least / len(shards), high / len(shards))
        level = level * jnp.repeat(jnp.exp(draws), shape[axis_at] // shards_of).reshape((-1,) + (1,) * (len(shape) - 1 - axis_at))
    return level


def bell_draw(rng, extent, deviation, bound, pieces=(), held_as=jnp.bfloat16):
    drawn = jax.random.normal(rng, extent, jnp.float32) * deviation
    if len(pieces) > 0:
        drawn = shard_levels(rng, extent, pieces, -0.22, 0.18) * drawn
    return jnp.clip(drawn, min=-bound, max=bound).astype(held_as)


def setup_inputs(seed: int = 0) -> dict:
    keys = jax.random.split(jax.random.key(seed), 21)
    return {
        "tokens": bell_draw(keys[0], (TOKENS, D), 1.0, 6.0, ((0, 32),)),
        "cotangent": bell_draw(keys[1], (TOKENS, D), 1.0, 6.0, ((0, 32),)),
        "source": draw_source(jax.random.fold_in(keys[20], 71), 0),
        "target": draw_target(jax.random.fold_in(keys[20], 71), 0),
        "lengths": draw_lengths(jax.random.fold_in(keys[20], 71), 0),
        "ln_gain": jnp.clip(1.0 + 0.1 * jax.random.normal(keys[5], (D,), jnp.float32), 0.5, 1.5),
        "ln_bias": bell_draw(keys[6], (D,), 0.3, 1.75, ((0, 32),), jnp.float32),
        "w_fwd": bell_draw(keys[7], (D, V), D ** -0.5, 0.21875, ((0, 8), (1, 4))),
        "b_fwd": bell_draw(keys[8], (V,), 0.5, 3.0, ((0, 32),), jnp.float32),
        "w_bwd": bell_draw(keys[9], (D, V), D ** -0.5, 0.21875, ((0, 8), (1, 4))),
        "b_bwd": bell_draw(keys[10], (V,), 0.5, 3.0, ((0, 32),), jnp.float32),
        "w_gate": bell_draw(keys[11], (D, 2, V), D ** -0.5, 0.21875, ((0, 8), (2, 4))),
        "b_gate": bell_draw(keys[12], (2, V), 0.5, 3.0, ((1, 32),), jnp.float32),
        "w_out": bell_draw(keys[13], (2, V, D), U ** -0.5, 0.109375, ((1, 4), (2, 8))),
        "b_out": bell_draw(keys[14], (D,), 0.3, 1.75, ((0, 32),), jnp.float32),
        "log_dt": jnp.clip(-6.9 + 4.6000001430511475 * jax.random.uniform(keys[15], (2, V), jnp.float32) ** shard_levels(keys[15], (2, V), ((1, 32),), -0.2, 0.2), -6.9, -2.3),
        "log_rate": jnp.clip(-0.7 + 4.8999998 * jax.random.uniform(keys[16], (2, V, N), jnp.float32) ** shard_levels(keys[16], (2, V, N), ((1, 32),), -0.2, 0.2), -0.7, 4.2),
        "ssm_b": bell_draw(keys[17], (2, V, N), 1.0, 6.0, ((1, 32),), jnp.float32),
        "ssm_c": bell_draw(keys[18], (2, V, N), 1.0, 6.0, ((1, 32),), jnp.float32),
        "ssm_d": bell_draw(keys[19], (2, V), 1.0, 6.0, ((1, 32),), jnp.float32),
    }


epsilon = 1e-05
highest = lax.Precision.HIGHEST
lane_block = 128

@jax.custom_vjp
def low(v):
    return lax.optimization_barrier(v.astype(jnp.bfloat16)).astype(jnp.float32)

@jax.custom_vjp
def low_back(v):
    return v

def low_keep(v):
    return (low(v), None)

def low_pass(kept, grad):
    return (grad,)

def back_keep(v):
    return (v, None)

def back_low(kept, grad):
    return (low(grad),)
low.defvjp(low_keep, low_pass)
low_back.defvjp(back_keep, back_low)

def layout(seq_lens):
    slot_len = (seq_lens + BLK - 1) // BLK * BLK
    slot_end = jnp.cumsum(slot_len).astype(jnp.int32)
    slot_begin = (slot_end - slot_len).astype(jnp.int32)
    positions = jnp.arange(GROUP_TOK, dtype=jnp.int32)
    inside = (positions[:, None] >= slot_begin[None, :]) & (positions[:, None] < (slot_begin + seq_lens)[None, :])
    live_mask = lax.optimization_barrier(jnp.sum(inside.astype(jnp.float32), axis=1))
    seq_ids = jnp.clip(lax.optimization_barrier(jnp.sum((positions[:, None] >= slot_end[None, :]).astype(jnp.int32), axis=1)), 0, SEQ_GRP - 1)
    offsets = jnp.clip(positions - slot_begin[seq_ids], 0, MOST - 1)
    return (live_mask, slot_begin, seq_ids, offsets)

def kernel_block(entry):
    step_log, rate_log, in_coef, out_coef = entry
    rate_val = jnp.exp(rate_log)
    log_decay = -jnp.exp(step_log)[:, None] * rate_val
    drive = (1.0 - jnp.exp(log_decay)) / rate_val * in_coef
    steps = jnp.arange(MOST, dtype=jnp.float32)
    powers = jnp.exp(steps[None, :, None] * log_decay[:, None, :])
    return lax.optimization_barrier(jnp.sum((out_coef * drive)[:, None, :] * powers, axis=2))

def seq_scan(inputs, seq_lens, slot_begin, seq_ids, offsets, live_mask, step_log, rate_log, in_coef, out_coef, skip_coef, reverse):
    kernel = lax.map(kernel_block, (step_log.reshape(-1, lane_block), rate_log.reshape(-1, lane_block, N), in_coef.reshape(-1, lane_block, N), out_coef.reshape(-1, lane_block, N))).reshape(V, MOST)
    spans = jnp.arange(MOST, dtype=jnp.int32)
    index_map = jnp.clip(slot_begin[:, None] + spans[None, :], 0, GROUP_TOK - 1)
    valid = (spans[None, :] < seq_lens[:, None]).astype(jnp.float32)
    seqs = inputs[index_map] * valid[:, :, None]
    if reverse:
        seqs = jnp.flip(seqs, axis=1)
    length_fft = 2 * MOST
    spectrum = jnp.fft.rfft(seqs, n=length_fft, axis=1) * jnp.fft.rfft(kernel.T, n=length_fft, axis=0)[None]
    conv = jnp.fft.irfft(spectrum, n=length_fft, axis=1)[:, :MOST] + skip_coef * seqs
    if reverse:
        conv = jnp.flip(conv, axis=1)
    return conv[seq_ids, offsets] * live_mask[:, None]

def group_fn(weights, x_group, seq_lens):
    ln_gain, ln_bias, w_fwd, b_fwd, w_bwd, b_bwd, w_gate, b_gate, w_out, b_out, log_dt, log_rate, ssm_b, ssm_c, ssm_d = weights
    live_mask, slot_begin, seq_ids, offsets = layout(seq_lens)
    mean_val = lax.optimization_barrier(jnp.mean(x_group, axis=1, keepdims=True))
    centred = x_group - mean_val
    inv_std = lax.rsqrt(lax.optimization_barrier(jnp.mean(centred * centred, axis=1, keepdims=True)) + epsilon)
    normed = low(centred * inv_std * ln_gain + ln_bias)
    pre_fwd = low_back(jnp.dot(normed, w_fwd, precision=highest) + b_fwd)
    pre_bwd = low_back(jnp.dot(normed, w_bwd, precision=highest) + b_bwd)
    pre_gate = low_back(jnp.einsum('td,dkv->tkv', normed, w_gate, precision=highest) + b_gate)
    fwd_input = live_mask[:, None] * jax.nn.gelu(pre_fwd)
    bwd_input = live_mask[:, None] * jax.nn.gelu(pre_bwd)
    scan_fwd = seq_scan(fwd_input, seq_lens, slot_begin, seq_ids, offsets, live_mask, log_dt[0], log_rate[0], ssm_b[0], ssm_c[0], ssm_d[0], False)
    scan_bwd = seq_scan(bwd_input, seq_lens, slot_begin, seq_ids, offsets, live_mask, log_dt[1], log_rate[1], ssm_b[1], ssm_c[1], ssm_d[1], True)
    mixed = low(jnp.stack([scan_fwd, scan_bwd], axis=1) * jax.nn.gelu(pre_gate))
    branch = low_back(jnp.einsum('tkv,kvd->td', mixed, w_out, precision=highest))
    return x_group + live_mask[:, None] * (branch + b_out)

def reference(tokens, cotangent, source, target, lengths, ln_gain, ln_bias, w_fwd, b_fwd, w_bwd, b_bwd, w_gate, b_gate, w_out, b_out, log_dt, log_rate, ssm_b, ssm_c, ssm_d):
    params = (ln_gain.astype(jnp.float32), ln_bias.astype(jnp.float32), w_fwd.astype(jnp.float32), b_fwd.astype(jnp.float32), w_bwd.astype(jnp.float32), b_bwd.astype(jnp.float32), w_gate.astype(jnp.float32), b_gate.astype(jnp.float32), w_out.astype(jnp.float32), b_out.astype(jnp.float32), log_dt.astype(jnp.float32), log_rate.astype(jnp.float32), ssm_b.astype(jnp.float32), ssm_c.astype(jnp.float32), ssm_d.astype(jnp.float32))

    def forward(x_given, weights):
        x_dealt = x_given[source].reshape(N_DP, GROUP_TOK, D)

        def one_group(entry):
            return group_fn(weights, entry[0], entry[1])
        outputs = lax.map(jax.checkpoint(one_group), (x_dealt, lengths))
        return outputs.reshape(TOKENS, D)[target]
    result, pullback = jax.vjp(forward, tokens.astype(jnp.float32), params)
    grad_x, grad_w = pullback(cotangent.astype(jnp.float32))
    return (result.astype(jnp.bfloat16), grad_x.astype(jnp.bfloat16), grad_w[0], grad_w[1], grad_w[2], grad_w[3], grad_w[4], grad_w[5], grad_w[6], grad_w[7], grad_w[8], grad_w[9], grad_w[10], grad_w[11], grad_w[12], grad_w[13], grad_w[14])
```

```python
from functools import partial

import jax
import jax.numpy as jnp
import numpy as np
from jax import lax
from jax.experimental import pallas as pl
from jax.experimental.pallas import tpu as pltpu
from jax.sharding import PartitionSpec as P

BLK = 128
BIG = 256
MOST = 2048
LAGS = MOST // BIG
STATE = 64
epsilon = 1e-05
log2e = 1.4426950408889634
f32 = jnp.float32
bf16 = jnp.bfloat16
MIB = 2**20


def nn(a, b):
    return lax.dot_general(a, b, (((1,), (0,)), ((), ())), preferred_element_type=f32)


def nt(a, b):
    return lax.dot_general(a, b, (((1,), (1,)), ((), ())), preferred_element_type=f32)


def params(limit):
    return pltpu.CompilerParams(vmem_limit_bytes=limit * MIB)


def cost(flops, moved, trans=0):
    return pl.CostEstimate(flops=int(flops), bytes_accessed=int(moved), transcendentals=int(trans))


def halves(x):
    high = x.astype(bf16)
    return high, (x - high.astype(f32)).astype(bf16)


def wave_table():
    pos = np.arange(BIG)[:, None]
    freq = np.arange(BIG)[None, :]
    angle = 2 * np.pi * ((2 * freq + 1) * pos % (4 * BIG)) / (4 * BIG)
    return np.concatenate([np.cos(angle), np.sin(angle)], 1).astype(np.float32)


def chunk_of(channels, most):
    best = 16
    for size in range(16, most + 1, 16):
        if channels % size == 0:
            best = size
    return best


def permute_row_body(count, rank_ref, *refs):
    rows = rank_ref.shape[1]
    spot = lax.broadcasted_iota(jnp.int32, (rows, rows), 0)
    pick = jnp.where(spot == rank_ref[...], 1.0, 0.0).astype(bf16)
    for at in range(count):
        refs[count + at][...] = nn(pick, refs[at][...]).astype(bf16)


def permute_to(rank, arrays):
    rows, width = arrays[0].shape
    count = len(arrays)
    return pl.pallas_call(
        partial(permute_row_body, count),
        out_shape=[jax.ShapeDtypeStruct((rows, width), bf16)] * count,
        compiler_params=params(48),
        cost_estimate=cost(2 * count * rows * rows * width, 4 * count * rows * width),
    )(rank.reshape(1, rows), *arrays)


def permute_col_body(rank_ref, x_ref, o_ref):
    rows = x_ref.shape[0]
    spot = lax.broadcasted_iota(jnp.int32, (rows, rows), 1)
    pick = jnp.where(spot == rank_ref[...], 1.0, 0.0).astype(bf16)
    o_ref[...] = nn(pick, x_ref[...]).astype(bf16)


def permute_from(rank, x):
    rows, width = x.shape
    return pl.pallas_call(
        permute_col_body,
        out_shape=jax.ShapeDtypeStruct((rows, width), bf16),
        compiler_params=params(48),
        cost_estimate=cost(2 * rows * rows * width, 4 * rows * width),
    )(rank.reshape(rows, 1), x)


def deal_body(place_ref, x_ref, g_ref, live_ref, gain_ref, shift_ref, xt_ref, gt_ref, xd_ref, gd_ref, bo_ref):
    step = pl.program_id(0)
    rows = x_ref.shape[0]
    spot = lax.broadcasted_iota(jnp.int32, (BLK, rows), 1)
    pick = jnp.where(spot == place_ref[...], 1.0, 0.0).astype(bf16)
    live = live_ref[0]
    x = nn(pick, x_ref[...]).T
    xd_ref[0] = x.astype(bf16)
    centred = x - jnp.mean(x, axis=0, keepdims=True)
    inv_std = lax.rsqrt(jnp.mean(centred * centred, axis=0, keepdims=True) + epsilon)
    xt_ref[0] = (centred * inv_std * gain_ref[...] + shift_ref[...]).astype(bf16)
    g = nn(pick, g_ref[...]).T
    gd_ref[0] = g.astype(bf16)
    g = g * live
    gt_ref[0] = g.astype(bf16)

    @pl.when(step == 0)
    def _():
        bo_ref[...] = jnp.zeros_like(bo_ref)

    bo_ref[...] += g


def deal_rows(place, x, g, live, gain, shift):
    rows, width = x.shape
    blocks = rows // BLK
    whole = pl.BlockSpec((rows, width), lambda i: (0, 0))
    wide = pl.BlockSpec((width, BLK), lambda i: (0, 0))
    out = pl.BlockSpec((1, width, BLK), lambda i: (i, 0, 0))
    return pl.pallas_call(
        deal_body,
        grid=(blocks,),
        in_specs=[
            pl.BlockSpec((BLK, 1), lambda i: (i, 0)),
            whole,
            whole,
            pl.BlockSpec((1, 1, BLK), lambda i: (i, 0, 0)),
            wide,
            wide,
        ],
        out_specs=[out, out, out, out, wide],
        out_shape=[jax.ShapeDtypeStruct((blocks, width, BLK), bf16)] * 4
        + [jax.ShapeDtypeStruct((width, BLK), f32)],
        compiler_params=params(40),
        cost_estimate=cost(4 * rows * rows * width, 12 * rows * width),
    )(place.reshape(rows, 1), x, g, live, gain, shift)


def send_back(place_ref, out_s, o_ref):
    rows = out_s.shape[0]
    spot = lax.broadcasted_iota(jnp.int32, (rows, rows), 0)
    pick = jnp.where(spot == place_ref[...], 1.0, 0.0).astype(bf16)
    o_ref[...] = nn(pick, out_s[...]).astype(bf16)


def layer_body(place_ref, br_ref, xd_ref, live_ref, bias_ref, o_ref, out_s):
    for at in range(br_ref.shape[0]):
        y = xd_ref[at].astype(f32) + live_ref[at] * (br_ref[at].astype(f32) + bias_ref[...])
        out_s[at * BLK : (at + 1) * BLK, :] = y.T.astype(bf16)
    send_back(place_ref, out_s, o_ref)


def layer_rows(place, branch, xd, live, bias):
    blocks, width, _ = xd.shape
    rows = blocks * BLK
    return pl.pallas_call(
        layer_body,
        out_shape=jax.ShapeDtypeStruct((rows, width), bf16),
        scratch_shapes=[pltpu.VMEM((rows, width), bf16)],
        compiler_params=params(48),
        cost_estimate=cost(2 * rows * rows * width, 6 * rows * width),
    )(place.reshape(1, rows), branch, xd, live, bias)


def input_body(place_ref, gn_ref, xd_ref, gd_ref, gain_ref, o_ref, sums_ref, out_s):
    g_gain = jnp.zeros(gain_ref.shape, f32)
    g_shift = jnp.zeros(gain_ref.shape, f32)
    for at in range(gn_ref.shape[0]):
        x = xd_ref[at].astype(f32)
        centred = x - jnp.mean(x, axis=0, keepdims=True)
        inv_std = lax.rsqrt(jnp.mean(centred * centred, axis=0, keepdims=True) + epsilon)
        x_hat = centred * inv_std
        g = gn_ref[at].astype(f32)
        g_gain = g_gain + g * x_hat
        g_shift = g_shift + g
        hat = g * gain_ref[...]
        back = inv_std * (
            hat
            - jnp.mean(hat, axis=0, keepdims=True)
            - x_hat * jnp.mean(hat * x_hat, axis=0, keepdims=True)
        )
        out_s[at * BLK : (at + 1) * BLK, :] = (gd_ref[at].astype(f32) + back).T.astype(bf16)
    sums_ref[0] = g_gain
    sums_ref[1] = g_shift
    send_back(place_ref, out_s, o_ref)


def input_rows(place, gn, xd, gd, gain):
    blocks, width, _ = xd.shape
    rows = blocks * BLK
    return pl.pallas_call(
        input_body,
        out_shape=[
            jax.ShapeDtypeStruct((rows, width), bf16),
            jax.ShapeDtypeStruct((2, width, BLK), f32),
        ],
        scratch_shapes=[pltpu.VMEM((rows, width), bf16)],
        compiler_params=params(48),
        cost_estimate=cost(2 * rows * rows * width, 8 * rows * width),
    )(place.reshape(1, rows), gn, xd, gd, gain)


def project_body(ch, x_ref, g_ref, live_ref, wt_ref, bias_ref, u_ref, v_ref, gg_ref, gq_ref, da_ref, pre_s, gm_s):
    x = jnp.concatenate([x_ref[0], x_ref[1]], axis=1)
    g = jnp.concatenate([g_ref[0], g_ref[1]], axis=1)
    pre_s[...] = nn(wt_ref[0 : 4 * ch, :], x)
    gm_s[...] = nn(wt_ref[4 * ch : 6 * ch, :], g)
    live = live_ref[0]
    step = 32
    root = 0.7978845608028654

    def act(pre):
        square = pre * pre
        bent = jnp.tanh(root * pre * (1.0 + 0.044715 * square))
        rise = 0.5 + 0.5 * bent
        slope = rise + (0.5 * root) * pre * (1.0 - bent * bent) * (1.0 + 0.134145 * square)
        return pre * rise, slope

    def put(ref, k, at, value):
        value = value.astype(bf16)
        ref[k, 0, at, :] = value[:, :BLK]
        ref[k, 1, at, :] = value[:, BLK:]

    def chunk(i, carry):
        at = pl.ds(pl.multiple_of(i * step, step), step)
        for k in range(2):
            row = pl.ds(pl.multiple_of(k * ch + i * step, step), step)
            gate = pl.ds(pl.multiple_of((2 + k) * ch + i * step, step), step)
            bias = bias_ref[row, :]
            value, slope = act(pre_s[row, :] + jnp.concatenate([bias, bias], axis=1))
            put(u_ref if k == 0 else v_ref, k, at, live * value)
            put(da_ref, k, at, live * slope)
            bias = bias_ref[gate, :]
            value, slope = act(pre_s[gate, :] + jnp.concatenate([bias, bias], axis=1))
            gm = gm_s[row, :]
            put(gg_ref, k, at, value)
            put(v_ref if k == 0 else u_ref, k, at, gm * value)
            put(gq_ref, k, at, gm * slope)
        return carry

    lax.fori_loop(0, ch // step, chunk, 0)


def project(xt, gt, live, wt, bias):
    nb, width, _ = xt.shape
    ch = wt.shape[0] // 6
    rows = pl.BlockSpec((2, width, BLK), lambda i: (i, 0, 0))
    out = pl.BlockSpec((2, 2, ch, BLK), lambda i: (0, i, 0, 0))
    tok = nb * BLK
    return pl.pallas_call(
        partial(project_body, ch),
        grid=(nb // 2,),
        in_specs=[
            rows,
            rows,
            pl.BlockSpec((1, 1, BIG), lambda i: (i, 0, 0)),
            pl.BlockSpec((6 * ch, width), lambda i: (0, 0)),
            pl.BlockSpec((4 * ch, BLK), lambda i: (0, 0)),
        ],
        out_specs=[out] * 5,
        out_shape=[jax.ShapeDtypeStruct((2, nb, ch, BLK), bf16)] * 5,
        scratch_shapes=[pltpu.VMEM((4 * ch, BIG), f32), pltpu.VMEM((2 * ch, BIG), f32)],
        compiler_params=params(56),
        cost_estimate=cost(12 * tok * width * ch, 4 * tok * width + 20 * tok * ch, 4 * tok * ch),
    )(xt, gt, live, wt, bias)


def spectra_body(cc, ld_ref, w_ref, d_ref, wave_ref, kh_ref, k_s):
    t = lax.broadcasted_iota(jnp.int32, (BLK, BLK), 0).astype(f32)
    block = lax.broadcasted_iota(jnp.int32, (2 * LAGS, BLK), 0).astype(f32) * float(BLK)
    low = lax.broadcasted_iota(jnp.int32, (2 * LAGS, BLK), 1) < STATE
    count = 2 * LAGS

    def one(p, carry):
        ld = ld_ref[0, pl.ds(p, 1), :]
        decay = jnp.exp2(t * ld)
        scale = w_ref[0, pl.ds(p, 1), :] * jnp.exp2(block * ld)
        lhs = jnp.concatenate([jnp.where(low, scale, 0.0), jnp.where(low, 0.0, scale)], axis=0)
        lhs_high, lhs_low = halves(lhs)
        high, rest = halves(decay)
        k = nt(jnp.concatenate([lhs_high, lhs_low], axis=0), high)
        k = k[0 : 2 * count] + k[2 * count : 4 * count] + nt(lhs_high, rest)
        k_s[pl.ds(2 * p, count, stride=cc), :] = k[0:count]
        k_s[pl.ds(2 * p + 1, count, stride=cc), :] = k[count : 2 * count]
        return carry

    lax.fori_loop(0, cc // 2, one, 0, unroll=4)
    sign = jnp.where(lax.broadcasted_iota(jnp.int32, (cc, BIG), 1) % 2 == 0, 1.0, -1.0)
    before = None
    for big in range(LAGS):
        rows = jnp.concatenate(
            [k_s[pl.ds(2 * big * cc, cc), :], k_s[pl.ds((2 * big + 1) * cc, cc), :]], axis=1
        )
        high, rest = halves(rows)
        x = nn(high, wave_ref[...]) + nn(rest, wave_ref[...])
        xc, xs = x[:, :BIG], x[:, BIG:]
        if big == 0:
            kh_ref[0, 0, :, :BIG] = xc + d_ref[0][:, 0:1]
            kh_ref[0, 0, :, BIG:] = xs
        else:
            kh_ref[0, big, :, :BIG] = xc + sign * before[1]
            kh_ref[0, big, :, BIG:] = xs - sign * before[0]
        before = (xc, xs)


def spectra(ld, w, d, wave):
    ch = 2 * ld.shape[1]
    cc = chunk_of(ch, 128)
    return pl.pallas_call(
        partial(spectra_body, cc),
        grid=(2, ch // cc),
        in_specs=[pl.BlockSpec((1, cc // 2, BLK), lambda k, i: (k, i, 0))] * 2
        + [
            pl.BlockSpec((1, cc, BLK), lambda k, i: (k, i, 0)),
            pl.BlockSpec((BIG, 2 * BIG), lambda k, i: (0, 0)),
        ],
        out_specs=pl.BlockSpec((1, LAGS, cc, 2 * BIG), lambda k, i: (k, 0, i, 0)),
        out_shape=jax.ShapeDtypeStruct((2, LAGS, ch, 2 * BIG), f32),
        scratch_shapes=[pltpu.VMEM((2 * LAGS * cc, BLK), f32)],
        compiler_params=params(40),
        cost_estimate=cost(2 * ch * 40e6, 2 * ch * LAGS * 2 * BIG * 4),
    )(ld, w, d, wave)


def moments_body(cc, ld_ref, gh_ref, back_ref, s0_ref, s1_ref, g0_ref, g_s):
    sign = jnp.where(lax.broadcasted_iota(jnp.int32, (cc, BIG), 1) % 2 == 0, 1.0, -1.0)
    count = 2 * LAGS
    for big in range(LAGS):
        c = gh_ref[0, big, :, :BIG]
        s = gh_ref[0, big, :, BIG:]
        if big < LAGS - 1:
            c, s = c - sign * gh_ref[0, big + 1, :, BIG:], s + sign * gh_ref[0, big + 1, :, :BIG]
        high, rest = halves(jnp.concatenate([c, s], axis=1))
        g = nn(high, back_ref[...]) + nn(rest, back_ref[...])
        g_s[pl.ds(2 * big * cc, cc), :] = g[:, :BLK]
        g_s[pl.ds((2 * big + 1) * cc, cc), :] = g[:, BLK:]
        if big == 0:
            g0_ref[0] = g[:, :BLK]
    t = lax.broadcasted_iota(jnp.int32, (BLK, BLK), 0).astype(f32)
    lane = lax.broadcasted_iota(jnp.int32, (count, BLK), 1)
    lag = lane.astype(f32)
    block = lax.broadcasted_iota(jnp.int32, (count, BLK), 0).astype(f32) * float(BLK)
    low = lane < STATE

    def one(p, carry):
        ld = ld_ref[0, pl.ds(p, 1), :]
        decay = jnp.exp2(t * ld).astype(bf16)
        far = jnp.exp2(block * ld)
        ga = g_s[pl.ds(2 * p, count, stride=cc), :]
        gb = g_s[pl.ds(2 * p + 1, count, stride=cc), :]
        high, rest = halves(jnp.concatenate([ga, gb, ga * lag, gb * lag], axis=0))
        m = nn(jnp.concatenate([high, rest], axis=0), decay)
        m = m[0 : 4 * count] + m[4 * count : 8 * count]
        m0 = jnp.where(low, m[0:count], m[count : 2 * count])
        m1 = jnp.where(low, m[2 * count : 3 * count], m[3 * count : 4 * count]) + block * m0
        s0_ref[0, pl.ds(p, 1), :] = jnp.sum(far * m0, axis=0, keepdims=True)
        s1_ref[0, pl.ds(p, 1), :] = jnp.sum(far * m1, axis=0, keepdims=True)
        return carry

    lax.fori_loop(0, cc // 2, one, 0, unroll=4)


def moments(ld, gh, back):
    ch = gh.shape[2]
    cc = chunk_of(ch, 128)
    row = pl.BlockSpec((1, cc // 2, BLK), lambda k, i: (k, i, 0))
    return pl.pallas_call(
        partial(moments_body, cc),
        grid=(2, ch // cc),
        in_specs=[
            row,
            pl.BlockSpec((1, LAGS, cc, 2 * BIG), lambda k, i: (k, 0, i, 0)),
            pl.BlockSpec((2 * BIG, BIG), lambda k, i: (0, 0)),
        ],
        out_specs=[row, row, pl.BlockSpec((1, cc, BLK), lambda k, i: (k, i, 0))],
        out_shape=[jax.ShapeDtypeStruct((2, ch // 2, BLK), f32)] * 2
        + [jax.ShapeDtypeStruct((2, ch, BLK), f32)],
        scratch_shapes=[pltpu.VMEM((2 * LAGS * cc, BLK), f32)],
        compiler_params=params(40),
        cost_estimate=cost(2 * ch * 40e6, 2 * ch * LAGS * 2 * BIG * 4),
    )(ld, gh, back)


def ssm_body(
    nb, nseq, cc, rg, tab_ref, seq_ref, u_ref, v_ref, kh_ref, wave_ref, back_ref, gg_ref, gq_ref, da_ref,
    mix_ref, gpg_ref, gp_ref, gh_ref, bs_ref, in_s, uh_s, vh_s, ph_s, qh_s, p_s, q_s,
):
    pieces = (nb + nseq) // 2

    def load(src, dst):
        for h in range(pieces):
            first = tab_ref[0, h]
            whole = tab_ref[1, h].astype(f32)
            in_s[pl.ds(h * cc, cc), 0:BLK] = src[0, first]
            after = src[0, jnp.minimum(first + 1, nb - 1)].astype(f32) * whole
            in_s[pl.ds(h * cc, cc), BLK:BIG] = after.astype(bf16)
        for h in range(pieces):
            at = pl.ds(h * cc, cc)
            dst[at, :] = nn(in_s[at, :], wave_ref[...])

    load(u_ref, uh_s)
    load(v_ref, vh_s)
    qh_s[...] = jnp.zeros_like(qh_s)
    gh_ref[...] = jnp.zeros_like(gh_ref)
    zero = jnp.zeros((rg, BIG), f32)

    def group(r, carry):
        off = pl.multiple_of(r * rg, rg)
        for s in range(nseq):
            base = seq_ref[0, s]
            count = seq_ref[1, s]

            def outer(i, carry):
                at = pl.ds(pl.multiple_of((base + i) * cc + off, rg), rg)
                vc = vh_s[at, :BIG]
                vs = vh_s[at, BIG:]

                def inner(j, acc):
                    pc, ps = acc
                    m = pl.ds(pl.multiple_of((base + i - j) * cc + off, rg), rg)
                    rows = pl.ds(off, rg)
                    uc = uh_s[m, :BIG]
                    us = uh_s[m, BIG:]
                    kc = kh_ref[0, j, rows, :BIG]
                    ks = kh_ref[0, j, rows, BIG:]
                    pc = pc + kc * uc - ks * us
                    ps = ps + kc * us + ks * uc
                    qh_s[m, :BIG] += kc * vc + ks * vs
                    qh_s[m, BIG:] += kc * vs - ks * vc
                    gh_ref[0, j, rows, :BIG] += uc * vc + us * vs
                    gh_ref[0, j, rows, BIG:] += uc * vs - us * vc
                    return (pc, ps)

                pc, ps = lax.fori_loop(0, i + 1, inner, (zero, zero))
                ph_s[at, :BIG] = pc.astype(bf16)
                ph_s[at, BIG:] = ps.astype(bf16)
                return carry

            lax.fori_loop(0, count, outer, 0)
        return carry

    lax.fori_loop(0, cc // rg, group, 0)

    for h in range(pieces):
        at = pl.ds(h * cc, cc)
        p_s[at, :] = nn(ph_s[at, :], back_ref[...])
        q_s[at, :] = nn(qh_s[at, :].astype(bf16), back_ref[...])

    none = jnp.zeros((cc, BLK), f32)

    def finish(y_s, gx_s):
        def one(b, y, gx, carry):
            s0, s1 = carry
            mix_ref[0, b] = (y * gg_ref[0, b].astype(f32)).astype(bf16)
            gpg = (y * gq_ref[0, b].astype(f32)).astype(bf16)
            gpg_ref[0, b] = gpg
            gp = (gx * da_ref[0, b].astype(f32)).astype(bf16)
            gp_ref[0, b] = gp
            return (s0 + gpg.astype(f32), s1 + gp.astype(f32))

        def last(h, carry):
            b = tab_ref[0, h]
            at = pl.ds(pl.multiple_of(h * cc, cc), cc)
            carry = one(b, y_s[at, 0:BLK], gx_s[at, 0:BLK], carry)

            def more(kept):
                return one(b + 1, y_s[at, BLK:], gx_s[at, BLK:], kept)

            return lax.cond(tab_ref[1, h] == 1, more, lambda kept: kept, carry)

        s0, s1 = lax.fori_loop(0, seq_ref[1, nseq], last, (none, none))
        bs_ref[0, :, 0:BLK] = s0
        bs_ref[0, :, BLK:] = s1

    @pl.when(pl.program_id(0) == 0)
    def _():
        finish(p_s, q_s)

    @pl.when(pl.program_id(0) == 1)
    def _():
        finish(q_s, p_s)

    nothing = jnp.zeros((cc, BLK), bf16)

    def fill(b, carry):
        mix_ref[0, b] = nothing
        gpg_ref[0, b] = nothing
        gp_ref[0, b] = nothing
        return carry

    lax.fori_loop(seq_ref[0, nseq], nb, fill, 0)


def ssm(tab, seq, u, v, kh, wave, back, gg, gq, da):
    _, nb, ch, _ = u.shape
    nseq = seq.shape[1] - 1
    pieces = (nb + nseq) // 2
    cc = chunk_of(ch, 128 if nb <= 32 else 64)
    rg = 16
    size = pieces * cc
    big = pl.BlockSpec((1, nb, cc, BLK), lambda k, i: (k, 0, i, 0))
    spec = pl.BlockSpec((1, LAGS, cc, 2 * BIG), lambda k, i: (k, 0, i, 0))
    smem = pl.BlockSpec(memory_space=pltpu.SMEM)
    pairs = 2 * LAGS * (LAGS + 1) // 2
    return pl.pallas_call(
        partial(ssm_body, nb, nseq, cc, rg),
        grid=(2, ch // cc),
        in_specs=[
            smem,
            smem,
            big,
            big,
            spec,
            pl.BlockSpec((BIG, 2 * BIG), lambda k, i: (0, 0)),
            pl.BlockSpec((2 * BIG, BIG), lambda k, i: (0, 0)),
            big,
            big,
            big,
        ],
        out_specs=[big, big, big, spec, pl.BlockSpec((1, cc, 2 * BLK), lambda k, i: (k, i, 0))],
        out_shape=[jax.ShapeDtypeStruct(u.shape, bf16)] * 3
        + [
            jax.ShapeDtypeStruct((2, LAGS, ch, 2 * BIG), f32),
            jax.ShapeDtypeStruct((2, ch, 2 * BLK), f32),
        ],
        scratch_shapes=[
            pltpu.VMEM((size, BIG), bf16),
            pltpu.VMEM((size, 2 * BIG), f32),
            pltpu.VMEM((size, 2 * BIG), f32),
            pltpu.VMEM((size, 2 * BIG), bf16),
            pltpu.VMEM((size, 2 * BIG), f32),
            pltpu.VMEM((size, BIG), f32),
            pltpu.VMEM((size, BIG), f32),
        ],
        compiler_params=params(60),
        cost_estimate=cost(2 * ch * pairs * BIG * 300, 2 * ch * nb * BLK * 16),
    )(tab, seq, u, v, kh, wave, back, gg, gq, da)


def stack_pair(refs):
    return jnp.concatenate(
        [jnp.concatenate([ref[k, 0], ref[k, 1]], axis=1) for ref in refs for k in range(2)], axis=0
    )


def mul_body(count, w_ref, *refs):
    out = nn(w_ref[...], stack_pair(refs[:count])).astype(bf16)
    refs[count][0] = out[:, :BLK]
    refs[count][1] = out[:, BLK:]


def mul_rows(w, arrays):
    width, deep = w.shape
    _, nb, ch, _ = arrays[0].shape
    count = len(arrays)
    return pl.pallas_call(
        partial(mul_body, count),
        grid=(nb // 2,),
        in_specs=[pl.BlockSpec((width, deep), lambda i: (0, 0))]
        + [pl.BlockSpec((2, 2, ch, BLK), lambda i: (0, i, 0, 0))] * count,
        out_specs=pl.BlockSpec((2, width, BLK), lambda i: (i, 0, 0)),
        out_shape=jax.ShapeDtypeStruct((nb, width, BLK), bf16),
        compiler_params=params(40),
        cost_estimate=cost(2 * nb * BLK * width * deep, 2 * nb * BLK * (width + deep)),
    )(w, *arrays)


def outer_body(ch, many, x_ref, g_ref, gp_ref, gpg_ref, mix_ref, o_ref, acc_s):
    step = pl.program_id(0)

    def flat(ref):
        return jnp.concatenate([ref[b] for b in range(many)], axis=1)

    def part(ref, k):
        return jnp.concatenate([ref[k, b] for b in range(many)], axis=1)

    @pl.when(step == 0)
    def _():
        acc_s[...] = jnp.zeros_like(acc_s)

    x = flat(x_ref)
    g = flat(g_ref)
    for at, (left, ref, k) in enumerate(
        [(x, gp_ref, 0), (x, gp_ref, 1), (x, gpg_ref, 0), (x, gpg_ref, 1), (g, mix_ref, 0), (g, mix_ref, 1)]
    ):
        acc_s[at] += nt(left, part(ref, k))

    @pl.when(step == pl.num_programs(0) - 1)
    def _():
        for at in range(6):
            o_ref[at] = acc_s[at].astype(bf16)


def outer_sums(xt, gt, gp, gpg, mix):
    nb, width, _ = xt.shape
    ch = gp.shape[2]
    many = 8
    rows = pl.BlockSpec((many, width, BLK), lambda i: (i, 0, 0))
    chan = pl.BlockSpec((2, many, ch, BLK), lambda i: (0, i, 0, 0))
    tok = nb * BLK
    return pl.pallas_call(
        partial(outer_body, ch, many),
        grid=(nb // many,),
        in_specs=[rows, rows, chan, chan, chan],
        out_specs=pl.BlockSpec((6, width, ch), lambda i: (0, 0, 0)),
        out_shape=jax.ShapeDtypeStruct((6, width, ch), bf16),
        scratch_shapes=[pltpu.VMEM((6, width, ch), f32)],
        compiler_params=params(56),
        cost_estimate=cost(12 * tok * width * ch, tok * (4 * width + 12 * ch)),
    )(xt, gt, gp, gpg, mix)


def sequence_tables(lens, nb):
    nseq = lens.shape[0]
    blocks = (lens + BLK - 1) // BLK
    start = jnp.cumsum(blocks) - blocks
    bigs = (blocks + 1) // 2
    first_big = jnp.cumsum(bigs) - bigs
    h = jnp.arange((nb + nseq) // 2, dtype=jnp.int32)
    owner = (h[:, None] >= first_big[None, :]).astype(jnp.int32).sum(axis=1) - 1
    mine = owner[:, None] == jnp.arange(nseq, dtype=jnp.int32)[None, :]

    def at_owner(values):
        return jnp.sum(jnp.where(mine, values[None, :], 0), axis=1)

    rel = h - at_owner(first_big)
    first = jnp.minimum(at_owner(start) + 2 * rel, nb - 1)
    whole = (2 * rel + 1 < at_owner(blocks)).astype(jnp.int32)
    tab = jnp.stack([first, whole]).astype(jnp.int32)
    seq = jnp.stack(
        [jnp.append(first_big, jnp.sum(blocks)), jnp.append(bigs, jnp.sum(bigs))]
    ).astype(jnp.int32)
    return tab, seq


def live_rows(lens, rows):
    slot = (lens + BLK - 1) // BLK * BLK
    begin = jnp.cumsum(slot) - slot
    pos = jnp.arange(rows, dtype=jnp.int32)
    inside = (pos[:, None] >= begin[None, :]) & (pos[:, None] < (begin + lens)[None, :])
    return jnp.sum(inside.astype(f32), axis=1)


def rank_of(keys):
    return jnp.sum((keys[None, :] < keys[:, None]).astype(jnp.int32), axis=1)


def local(
    n_dp, n_t, wave, tokens, cotangent, source, target, lengths, ln_gain, ln_bias, w_fwd, b_fwd, w_bwd, b_bwd,
    w_gate, b_gate, w_out, b_out, log_dt, log_rate, ssm_b, ssm_c, ssm_d,
):
    rows, width = tokens.shape
    share = lax.axis_index("tensor")
    group = rows * n_t
    nb = group // BLK
    ch = w_fwd.shape[1]
    own = b_fwd.shape[0]
    both = ("dp", "tensor")
    back = (wave.T / BIG).astype(bf16)
    wave = wave.astype(bf16)

    rank = rank_of(target)
    sender = source // group
    place = rank_of(sender * rows + jnp.arange(rows, dtype=jnp.int32))
    sent_x, sent_g = permute_to(rank, [tokens, cotangent])

    def swap(x):
        return lax.all_to_all(x, "dp", split_axis=0, concat_axis=0, tiled=True)

    got_x = swap(sent_x)
    got_g = swap(sent_g)

    perm = [(f, (f % n_dp) * n_t + f // n_dp) for f in range(n_dp * n_t)]
    unperm = [(b, a) for a, b in perm]
    chan = jnp.concatenate(
        [log_rate[0], log_rate[1], ssm_b[0], ssm_b[1], ssm_c[0], ssm_c[1]]
        + [jnp.stack([log_dt[0], log_dt[1], ssm_d[0], ssm_d[1], b_fwd, b_bwd, b_gate[0], b_gate[1]], axis=1)],
        axis=1,
    )
    chan = lax.ppermute(chan, both, perm)
    norm = lax.all_gather(jnp.stack([ln_gain, ln_bias, b_out]), "tensor", axis=1, tiled=True)
    flat = jnp.concatenate([chan.reshape(-1), norm.reshape(-1)])
    flat = lax.all_gather(flat.reshape(1, -1), "dp", axis=0, tiled=True)
    chan_all = flat[:, : chan.size].reshape(n_dp * own, chan.shape[1])
    norm_all = flat[:, chan.size :].reshape(n_dp, 3, width // n_dp).transpose(1, 0, 2).reshape(3, width)

    def lanes(column):
        return jnp.broadcast_to(column[..., None], column.shape + (BLK,))

    gain = lanes(norm_all[0])
    shift = lanes(norm_all[1])
    bias_out = lanes(norm_all[2])
    small = chan_all[:, 6 * STATE :]
    bias_in = lanes(small[:, 4:8].T.reshape(-1))

    def pick(at):
        return jnp.stack([chan_all[:, at * STATE : (at + 1) * STATE], chan_all[:, (at + 1) * STATE : (at + 2) * STATE]])

    def decays(log_dt, log_rate, ssm_b):
        rate = jnp.exp(log_rate)
        ld = -jnp.exp(log_dt)[..., None] * rate
        return rate, ld, (1.0 - jnp.exp(ld)) / rate * ssm_b

    _, ld_all, drive_all = decays(small[:, 0:2].T, pick(0), pick(2))
    ld_pairs = (ld_all * log2e).reshape(2, ch // 2, 2 * STATE)
    w_pairs = (pick(4) * drive_all).reshape(2, ch // 2, 2 * STATE)
    kh = spectra(ld_pairs, w_pairs, lanes(small[:, 2:4].T), wave)

    pack = jnp.concatenate(
        [w_fwd, w_bwd, w_gate.reshape(-1, 2 * ch), w_out.transpose(2, 0, 1).reshape(-1, 2 * ch)], axis=1
    )
    w_all = lax.all_gather(pack, "dp", axis=0, tiled=True)
    w_t = w_all.T

    live = live_rows(lengths[0], group)
    live_own = lax.dynamic_slice_in_dim(live, share * rows, rows, 0).reshape(rows // BLK, 1, BLK)
    tab, seq = sequence_tables(lengths[0], nb)

    xt, gt, xd, gd, g_bias_out = deal_rows(place, got_x, got_g, live_own, gain, shift)
    xt_all = lax.all_gather(xt, "tensor", axis=0, tiled=True)
    gt_all = lax.all_gather(gt, "tensor", axis=0, tiled=True)
    u, v, gg, gq, da = project(xt_all, gt_all, live.reshape(nb // 2, 1, BIG), w_t, bias_in)
    mix, gpg, gp, gh, bsum = ssm(tab, seq, u, v, kh, wave, back, gg, gq, da)

    def to_owner(x):
        return lax.psum_scatter(x, "tensor", scatter_dimension=0, tiled=True)

    g_normed = to_owner(mul_rows(w_all[:, : 4 * ch], [gp, gpg]))
    branch = to_owner(mul_rows(w_all[:, 4 * ch :], [mix]))
    gw = outer_sums(xt_all, gt_all, gp, gpg, mix)
    gw = gw.reshape(6, n_dp, width // n_dp, ch).transpose(1, 0, 2, 3)
    gw = lax.psum_scatter(gw, "dp", scatter_dimension=0, tiled=True)[0].astype(f32)
    s0, s1, g0 = moments(ld_pairs, gh, back)

    sent_in, norm_sums = input_rows(place, g_normed, xd, gd, gain)
    in_grad = permute_from(rank, swap(sent_in))
    sent_out = layer_rows(place, branch, xd, live_own, bias_out)
    layer_out = permute_from(rank, swap(sent_out))

    s0 = s0.reshape(2, ch, STATE)
    s1 = s1.reshape(2, ch, STATE)
    gb_gate = jnp.sum(bsum[:, :, :BLK], axis=2)
    gb_in = jnp.sum(bsum[:, :, BLK:], axis=2)
    sums = jnp.concatenate(
        [s0[0], s0[1], s1[0], s1[1], jnp.concatenate([g0[:, :, 0], gb_gate, gb_in], axis=0).T], axis=1
    )
    norm_sums = jnp.sum(jnp.concatenate([norm_sums, g_bias_out[None]], axis=0), axis=2)
    norm_sums = norm_sums.reshape(3, n_dp, width // n_dp).transpose(1, 0, 2).reshape(n_dp, -1)
    flat = jnp.concatenate([sums.reshape(n_dp, -1), norm_sums], axis=1)
    flat = lax.psum_scatter(flat, "dp", scatter_dimension=0, tiled=True)[0]
    cut = own * sums.shape[1]
    norm_sums = lax.psum_scatter(
        flat[cut:].reshape(3, width // n_dp), "tensor", scatter_dimension=1, tiled=True
    )
    sums = lax.ppermute(flat[:cut].reshape(own, -1), both, unperm)
    s0 = jnp.stack([sums[:, :STATE], sums[:, STATE : 2 * STATE]])
    s1 = jnp.stack([sums[:, 2 * STATE : 3 * STATE], sums[:, 3 * STATE : 4 * STATE]])
    tail = sums[:, 4 * STATE :].T
    step = jnp.exp(log_dt)[..., None]
    rate, ld, drive = decays(log_dt, log_rate, ssm_b)
    g_c = s0 * drive
    g_drive = s0 * ssm_c
    g_b = g_drive * (1.0 - jnp.exp(ld)) / rate
    g_ld = s1 * ssm_c * drive - g_drive * ssm_b / rate * jnp.exp(ld)
    g_rate = -g_drive * drive / rate - g_ld * step
    g_dt = jnp.sum(g_ld * ld, axis=2)
    return (
        layer_out,
        in_grad,
        norm_sums[0],
        norm_sums[1],
        gw[0],
        tail[4],
        gw[1],
        tail[5],
        jnp.stack([gw[2], gw[3]], axis=1),
        tail[2:4],
        jnp.stack([gw[4].T, gw[5].T]),
        norm_sums[2],
        g_dt,
        g_rate * rate,
        g_b,
        g_c,
        tail[0:2],
    )


def solution(mesh):
    n_dp, n_t = mesh.shape["dp"], mesh.shape["tensor"]
    both = P(("dp", "tensor"))
    rows = P(("dp", "tensor"), None)
    pair = P(None, ("dp", "tensor"))
    state = P(None, ("dp", "tensor"), None)
    proj = P("dp", "tensor")
    gate = P("dp", None, "tensor")
    out = P(None, "tensor", "dp")
    wave = wave_table()

    def run(*args):
        return local(n_dp, n_t, jnp.asarray(wave), *args)

    return jax.shard_map(
        run,
        mesh=mesh,
        in_specs=(
            rows, rows, both, both, P("dp", None), both, both, proj, both, proj, both, gate, pair, out, both,
            pair, state, state, state, pair,
        ),
        out_specs=(
            rows, rows, both, both, proj, both, proj, both, gate, pair, out, both, pair, state, state, state, pair,
        ),
        check_vma=False,
    )
```

```python
from functools import partial

import jax
import jax.numpy as jnp
import numpy as np
from jax import lax
from jax.experimental import pallas as pl
from jax.experimental.pallas import tpu as pltpu
from jax.sharding import PartitionSpec as P

BLK = 128
BIG = 256
MOST = 2048
LAGS = MOST // BIG
STATE = 64
epsilon = 1e-05
log2e = 1.4426950408889634
f32 = jnp.float32
bf16 = jnp.bfloat16
MIB = 2**20


def nn(a, b):
    return lax.dot_general(a, b, (((1,), (0,)), ((), ())), preferred_element_type=f32)


def nt(a, b):
    return lax.dot_general(a, b, (((1,), (1,)), ((), ())), preferred_element_type=f32)


def params(limit):
    return pltpu.CompilerParams(vmem_limit_bytes=limit * MIB)


def cost(flops, moved, trans=0):
    return pl.CostEstimate(flops=int(flops), bytes_accessed=int(moved), transcendentals=int(trans))


def halves(x):
    high = x.astype(bf16)
    return high, (x - high.astype(f32)).astype(bf16)


def wave_table():
    pos = np.arange(BIG)[:, None]
    freq = np.arange(BIG)[None, :]
    angle = 2 * np.pi * ((2 * freq + 1) * pos % (4 * BIG)) / (4 * BIG)
    return np.concatenate([np.cos(angle), np.sin(angle)], 1).astype(np.float32)


def chunk_of(channels, most):
    best = 16
    for size in range(16, most + 1, 16):
        if channels % size == 0:
            best = size
    return best


def permute_row_body(count, rank_ref, *refs):
    rows = rank_ref.shape[1]
    spot = lax.broadcasted_iota(jnp.int32, (rows, rows), 0)
    pick = jnp.where(spot == rank_ref[...], 1.0, 0.0).astype(bf16)
    for at in range(count):
        refs[count + at][...] = nn(pick, refs[at][...]).astype(bf16)


def permute_to(rank, arrays):
    rows, width = arrays[0].shape
    count = len(arrays)
    return pl.pallas_call(
        partial(permute_row_body, count),
        out_shape=[jax.ShapeDtypeStruct((rows, width), bf16)] * count,
        compiler_params=params(48),
        cost_estimate=cost(2 * count * rows * rows * width, 4 * count * rows * width),
    )(rank.reshape(1, rows), *arrays)


def permute_col_body(rank_ref, x_ref, o_ref):
    rows = x_ref.shape[0]
    spot = lax.broadcasted_iota(jnp.int32, (rows, rows), 1)
    pick = jnp.where(spot == rank_ref[...], 1.0, 0.0).astype(bf16)
    o_ref[...] = nn(pick, x_ref[...]).astype(bf16)


def permute_from(rank, x):
    rows, width = x.shape
    return pl.pallas_call(
        permute_col_body,
        out_shape=jax.ShapeDtypeStruct((rows, width), bf16),
        compiler_params=params(48),
        cost_estimate=cost(2 * rows * rows * width, 4 * rows * width),
    )(rank.reshape(rows, 1), x)


def pick_rows(place_ref, x_ref):
    spot = lax.broadcasted_iota(jnp.int32, (BLK, x_ref.shape[0]), 1)
    pick = jnp.where(spot == place_ref[...], 1.0, 0.0).astype(bf16)
    return nn(pick, x_ref[...]).T


def deal_x_body(place_ref, x_ref, gain_ref, shift_ref, xt_ref, xd_ref):
    x = pick_rows(place_ref, x_ref)
    xd_ref[0] = x.astype(bf16)
    centred = x - jnp.mean(x, axis=0, keepdims=True)
    inv_std = lax.rsqrt(jnp.mean(centred * centred, axis=0, keepdims=True) + epsilon)
    xt_ref[0] = (centred * inv_std * gain_ref[...] + shift_ref[...]).astype(bf16)


def deal_g_body(place_ref, g_ref, live_ref, gt_ref, gd_ref, bo_ref):
    g = pick_rows(place_ref, g_ref)
    gd_ref[0] = g.astype(bf16)
    g = g * live_ref[0]
    gt_ref[0] = g.astype(bf16)

    @pl.when(pl.program_id(0) == 0)
    def _():
        bo_ref[...] = jnp.zeros_like(bo_ref)

    bo_ref[...] += g


def deal_specs(rows, width):
    place = pl.BlockSpec((BLK, 1), lambda i: (i, 0))
    whole = pl.BlockSpec((rows, width), lambda i: (0, 0))
    wide = pl.BlockSpec((width, BLK), lambda i: (0, 0))
    out = pl.BlockSpec((1, width, BLK), lambda i: (i, 0, 0))
    return place, whole, wide, out


def deal_x(place, x, gain, shift):
    rows, width = x.shape
    blocks = rows // BLK
    spot, whole, wide, out = deal_specs(rows, width)
    return pl.pallas_call(
        deal_x_body,
        grid=(blocks,),
        in_specs=[spot, whole, wide, wide],
        out_specs=[out, out],
        out_shape=[jax.ShapeDtypeStruct((blocks, width, BLK), bf16)] * 2,
        compiler_params=params(40),
        cost_estimate=cost(2 * rows * rows * width, 6 * rows * width),
    )(place.reshape(rows, 1), x, gain, shift)


def deal_g(place, g, live):
    rows, width = g.shape
    blocks = rows // BLK
    spot, whole, wide, out = deal_specs(rows, width)
    return pl.pallas_call(
        deal_g_body,
        grid=(blocks,),
        in_specs=[spot, whole, pl.BlockSpec((1, 1, BLK), lambda i: (i, 0, 0))],
        out_specs=[out, out, wide],
        out_shape=[jax.ShapeDtypeStruct((blocks, width, BLK), bf16)] * 2
        + [jax.ShapeDtypeStruct((width, BLK), f32)],
        compiler_params=params(40),
        cost_estimate=cost(2 * rows * rows * width, 6 * rows * width),
    )(place.reshape(rows, 1), g, live)


def send_back(place_ref, out_s, o_ref):
    rows = out_s.shape[0]
    spot = lax.broadcasted_iota(jnp.int32, (rows, rows), 0)
    pick = jnp.where(spot == place_ref[...], 1.0, 0.0).astype(bf16)
    o_ref[...] = nn(pick, out_s[...]).astype(bf16)


def total(refs, at):
    value = refs[0][at].astype(f32)
    for ref in refs[1:]:
        value = value + ref[at].astype(f32)
    return value


def layer_body(place_ref, xd_ref, live_ref, bias_ref, *refs):
    o_ref, out_s = refs[-2:]
    for at in range(xd_ref.shape[0]):
        y = xd_ref[at].astype(f32) + live_ref[at] * (total(refs[:-2], at) + bias_ref[...])
        out_s[at * BLK : (at + 1) * BLK, :] = y.T.astype(bf16)
    send_back(place_ref, out_s, o_ref)


def layer_rows(place, parts, xd, live, bias):
    blocks, width, _ = xd.shape
    rows = blocks * BLK
    return pl.pallas_call(
        layer_body,
        out_shape=jax.ShapeDtypeStruct((rows, width), bf16),
        scratch_shapes=[pltpu.VMEM((rows, width), bf16)],
        compiler_params=params(48),
        cost_estimate=cost(2 * rows * rows * width, 6 * rows * width),
    )(place.reshape(1, rows), xd, live, bias, *parts)


def input_body(place_ref, xd_ref, gd_ref, gain_ref, *refs):
    o_ref, sums_ref, out_s = refs[-3:]
    g_gain = jnp.zeros(gain_ref.shape, f32)
    g_shift = jnp.zeros(gain_ref.shape, f32)
    for at in range(xd_ref.shape[0]):
        x = xd_ref[at].astype(f32)
        centred = x - jnp.mean(x, axis=0, keepdims=True)
        inv_std = lax.rsqrt(jnp.mean(centred * centred, axis=0, keepdims=True) + epsilon)
        x_hat = centred * inv_std
        g = total(refs[:-3], at)
        g_gain = g_gain + g * x_hat
        g_shift = g_shift + g
        hat = g * gain_ref[...]
        back = inv_std * (
            hat
            - jnp.mean(hat, axis=0, keepdims=True)
            - x_hat * jnp.mean(hat * x_hat, axis=0, keepdims=True)
        )
        out_s[at * BLK : (at + 1) * BLK, :] = (gd_ref[at].astype(f32) + back).T.astype(bf16)
    sums_ref[0] = g_gain
    sums_ref[1] = g_shift
    send_back(place_ref, out_s, o_ref)


def input_rows(place, parts, xd, gd, gain):
    blocks, width, _ = xd.shape
    rows = blocks * BLK
    return pl.pallas_call(
        input_body,
        out_shape=[
            jax.ShapeDtypeStruct((rows, width), bf16),
            jax.ShapeDtypeStruct((2, width, BLK), f32),
        ],
        scratch_shapes=[pltpu.VMEM((rows, width), bf16)],
        compiler_params=params(48),
        cost_estimate=cost(2 * rows * rows * width, 8 * rows * width),
    )(place.reshape(1, rows), xd, gd, gain, *parts)


def project_body(ch, many, start_ref, x_ref, live_ref, wt_ref, bias_ref, *refs):
    a_ref, da_ref, gg_ref, dg_ref, pre_s = refs[-5:]
    x = jnp.concatenate([x_ref[0], x_ref[1]], axis=1)
    pre_s[...] = nn(wt_ref[...], x)
    live = live_ref[0]
    step = 32
    root = 0.7978845608028654

    def act(pre):
        square = pre * pre
        bent = jnp.tanh(root * pre * (1.0 + 0.044715 * square))
        rise = 0.5 + 0.5 * bent
        slope = rise + (0.5 * root) * pre * (1.0 - bent * bent) * (1.0 + 0.134145 * square)
        return pre * rise, slope

    def put(ref, k, at, value):
        value = value.astype(bf16)
        ref[k, 0, at, :] = value[:, :BLK]
        ref[k, 1, at, :] = value[:, BLK:]

    def chunk(i, carry):
        at = pl.ds(pl.multiple_of(i * step, step), step)
        for k in range(2):
            row = pl.ds(pl.multiple_of(k * ch + i * step, step), step)
            gate = pl.ds(pl.multiple_of((2 + k) * ch + i * step, step), step)
            bias = bias_ref[row, :]
            value, slope = act(pre_s[row, :] + jnp.concatenate([bias, bias], axis=1))
            put(a_ref, k, at, live * value)
            put(da_ref, k, at, live * slope)
            bias = bias_ref[gate, :]
            value, slope = act(pre_s[gate, :] + jnp.concatenate([bias, bias], axis=1))
            put(gg_ref, k, at, value)
            put(dg_ref, k, at, slope)
        return carry

    lax.fori_loop(0, ch // step, chunk, 0)


def chained(body, grid, in_specs, out_specs, shapes, scratch, limit, estimate, start, operands, kept):
    kept = [] if kept is None else list(kept)
    specs = list(in_specs) + [pl.BlockSpec(memory_space=pl.ANY)] * len(kept)
    first = 1 + len(operands)
    return pl.pallas_call(
        body,
        grid_spec=pltpu.PrefetchScalarGridSpec(
            num_scalar_prefetch=1, grid=grid, in_specs=specs, out_specs=out_specs, scratch_shapes=scratch
        ),
        out_shape=shapes,
        input_output_aliases={first + at: at for at in range(len(kept))},
        compiler_params=params(limit),
        cost_estimate=estimate,
    )(start, *operands, *kept)


def project(xt, start, nb, live, wt, bias, kept):
    many, width, _ = xt.shape
    ch = wt.shape[0] // 4
    out = pl.BlockSpec((2, 2, ch, BLK), lambda i, at: (0, at[0] + i, 0, 0))
    tok = many * BLK
    return chained(
        partial(project_body, ch, many),
        (many // 2,),
        [
            pl.BlockSpec((2, width, BLK), lambda i, at: (i, 0, 0)),
            pl.BlockSpec((1, 1, BIG), lambda i, at: (at[0] + i, 0, 0)),
            pl.BlockSpec((4 * ch, width), lambda i, at: (0, 0)),
            pl.BlockSpec((4 * ch, BLK), lambda i, at: (0, 0)),
        ],
        [out] * 4,
        [jax.ShapeDtypeStruct((2, nb, ch, BLK), bf16)] * 4,
        [pltpu.VMEM((4 * ch, BIG), f32)],
        48,
        cost(8 * tok * width * ch, 2 * tok * width + 16 * tok * ch, 4 * tok * ch),
        start // 2,
        [xt, live, wt, bias],
        kept,
    )


def gate_grad_body(ch, start_ref, g_ref, wt_ref, *refs):
    o_ref = refs[-1]
    gm = nn(wt_ref[...], jnp.concatenate([g_ref[0], g_ref[1]], axis=1)).astype(bf16)
    for k in range(2):
        for h in range(2):
            o_ref[k, h] = gm[k * ch : (k + 1) * ch, h * BLK : (h + 1) * BLK]


def gate_grad(gt, start, nb, wt, kept):
    many, width, _ = gt.shape
    ch = wt.shape[0] // 2
    tok = many * BLK
    return chained(
        partial(gate_grad_body, ch),
        (many // 2,),
        [
            pl.BlockSpec((2, width, BLK), lambda i, at: (i, 0, 0)),
            pl.BlockSpec((2 * ch, width), lambda i, at: (0, 0)),
        ],
        [pl.BlockSpec((2, 2, ch, BLK), lambda i, at: (0, at[0] + i, 0, 0))],
        [jax.ShapeDtypeStruct((2, nb, ch, BLK), bf16)],
        [],
        40,
        cost(4 * tok * width * ch, 2 * tok * width + 4 * tok * ch),
        start // 2,
        [gt, wt],
        kept,
    )


def spectra_body(cc, ld_ref, w_ref, d_ref, wave_ref, kh_ref, k_s):
    t = lax.broadcasted_iota(jnp.int32, (BLK, BLK), 0).astype(f32)
    block = lax.broadcasted_iota(jnp.int32, (2 * LAGS, BLK), 0).astype(f32) * float(BLK)
    low = lax.broadcasted_iota(jnp.int32, (2 * LAGS, BLK), 1) < STATE
    count = 2 * LAGS

    def one(p, carry):
        ld = ld_ref[0, pl.ds(p, 1), :]
        decay = jnp.exp2(t * ld)
        scale = w_ref[0, pl.ds(p, 1), :] * jnp.exp2(block * ld)
        lhs = jnp.concatenate([jnp.where(low, scale, 0.0), jnp.where(low, 0.0, scale)], axis=0)
        lhs_high, lhs_low = halves(lhs)
        high, rest = halves(decay)
        k = nt(jnp.concatenate([lhs_high, lhs_low], axis=0), high)
        k = k[0 : 2 * count] + k[2 * count : 4 * count] + nt(lhs_high, rest)
        k_s[pl.ds(2 * p, count, stride=cc), :] = k[0:count]
        k_s[pl.ds(2 * p + 1, count, stride=cc), :] = k[count : 2 * count]
        return carry

    lax.fori_loop(0, cc // 2, one, 0, unroll=4)
    sign = jnp.where(lax.broadcasted_iota(jnp.int32, (cc, BIG), 1) % 2 == 0, 1.0, -1.0)
    before = None
    for big in range(LAGS):
        rows = jnp.concatenate(
            [k_s[pl.ds(2 * big * cc, cc), :], k_s[pl.ds((2 * big + 1) * cc, cc), :]], axis=1
        )
        high, rest = halves(rows)
        x = nn(high, wave_ref[...]) + nn(rest, wave_ref[...])
        xc, xs = x[:, :BIG], x[:, BIG:]
        if big == 0:
            kh_ref[0, 0, :, :BIG] = xc + d_ref[0][:, 0:1]
            kh_ref[0, 0, :, BIG:] = xs
        else:
            kh_ref[0, big, :, :BIG] = xc + sign * before[1]
            kh_ref[0, big, :, BIG:] = xs - sign * before[0]
        before = (xc, xs)


def spectra(ld, w, d, wave):
    ch = 2 * ld.shape[1]
    cc = chunk_of(ch, 128)
    return pl.pallas_call(
        partial(spectra_body, cc),
        grid=(2, ch // cc),
        in_specs=[pl.BlockSpec((1, cc // 2, BLK), lambda k, i: (k, i, 0))] * 2
        + [
            pl.BlockSpec((1, cc, BLK), lambda k, i: (k, i, 0)),
            pl.BlockSpec((BIG, 2 * BIG), lambda k, i: (0, 0)),
        ],
        out_specs=pl.BlockSpec((1, LAGS, cc, 2 * BIG), lambda k, i: (k, 0, i, 0)),
        out_shape=jax.ShapeDtypeStruct((2, LAGS, ch, 2 * BIG), f32),
        scratch_shapes=[pltpu.VMEM((2 * LAGS * cc, BLK), f32)],
        compiler_params=params(40),
        cost_estimate=cost(2 * ch * 40e6, 2 * ch * LAGS * 2 * BIG * 4),
    )(ld, w, d, wave)


def moments_body(cc, ld_ref, gh_ref, back_ref, s0_ref, s1_ref, g0_ref, g_s):
    sign = jnp.where(lax.broadcasted_iota(jnp.int32, (cc, BIG), 1) % 2 == 0, 1.0, -1.0)
    count = 2 * LAGS
    for big in range(LAGS):
        c = gh_ref[0, big, :, :BIG]
        s = gh_ref[0, big, :, BIG:]
        if big < LAGS - 1:
            c, s = c - sign * gh_ref[0, big + 1, :, BIG:], s + sign * gh_ref[0, big + 1, :, :BIG]
        high, rest = halves(jnp.concatenate([c, s], axis=1))
        g = nn(high, back_ref[...]) + nn(rest, back_ref[...])
        g_s[pl.ds(2 * big * cc, cc), :] = g[:, :BLK]
        g_s[pl.ds((2 * big + 1) * cc, cc), :] = g[:, BLK:]
        if big == 0:
            g0_ref[0] = g[:, :BLK]
    t = lax.broadcasted_iota(jnp.int32, (BLK, BLK), 0).astype(f32)
    lane = lax.broadcasted_iota(jnp.int32, (count, BLK), 1)
    lag = lane.astype(f32)
    block = lax.broadcasted_iota(jnp.int32, (count, BLK), 0).astype(f32) * float(BLK)
    low = lane < STATE

    def one(p, carry):
        ld = ld_ref[0, pl.ds(p, 1), :]
        decay = jnp.exp2(t * ld).astype(bf16)
        far = jnp.exp2(block * ld)
        ga = g_s[pl.ds(2 * p, count, stride=cc), :]
        gb = g_s[pl.ds(2 * p + 1, count, stride=cc), :]
        high, rest = halves(jnp.concatenate([ga, gb, ga * lag, gb * lag], axis=0))
        m = nn(jnp.concatenate([high, rest], axis=0), decay)
        m = m[0 : 4 * count] + m[4 * count : 8 * count]
        m0 = jnp.where(low, m[0:count], m[count : 2 * count])
        m1 = jnp.where(low, m[2 * count : 3 * count], m[3 * count : 4 * count]) + block * m0
        s0_ref[0, pl.ds(p, 1), :] = jnp.sum(far * m0, axis=0, keepdims=True)
        s1_ref[0, pl.ds(p, 1), :] = jnp.sum(far * m1, axis=0, keepdims=True)
        return carry

    lax.fori_loop(0, cc // 2, one, 0, unroll=4)


def moments(ld, gh, back):
    ch = gh.shape[2]
    cc = chunk_of(ch, 128)
    row = pl.BlockSpec((1, cc // 2, BLK), lambda k, i: (k, i, 0))
    return pl.pallas_call(
        partial(moments_body, cc),
        grid=(2, ch // cc),
        in_specs=[
            row,
            pl.BlockSpec((1, LAGS, cc, 2 * BIG), lambda k, i: (k, 0, i, 0)),
            pl.BlockSpec((2 * BIG, BIG), lambda k, i: (0, 0)),
        ],
        out_specs=[row, row, pl.BlockSpec((1, cc, BLK), lambda k, i: (k, i, 0))],
        out_shape=[jax.ShapeDtypeStruct((2, ch // 2, BLK), f32)] * 2
        + [jax.ShapeDtypeStruct((2, ch, BLK), f32)],
        scratch_shapes=[pltpu.VMEM((2 * LAGS * cc, BLK), f32)],
        compiler_params=params(40),
        cost_estimate=cost(2 * ch * 40e6, 2 * ch * LAGS * 2 * BIG * 4),
    )(ld, gh, back)


def load_pieces(nb, pieces, cc, tab_ref, block, in_s, wave_ref, dst):
    for h in range(pieces):
        first = tab_ref[0, h]
        whole = tab_ref[1, h].astype(f32)
        in_s[pl.ds(h * cc, cc), 0:BLK] = block(first).astype(bf16)
        in_s[pl.ds(h * cc, cc), BLK:BIG] = (block(jnp.minimum(first + 1, nb - 1)) * whole).astype(bf16)
    for h in range(pieces):
        at = pl.ds(h * cc, cc)
        dst[at, :] = nn(in_s[at, :], wave_ref[...])


def over_pieces(nseq, cc, rg, seq_ref, piece):
    def group(r, carry):
        off = pl.multiple_of(r * rg, rg)
        for s in range(nseq):
            base = seq_ref[0, s]
            count = seq_ref[1, s]

            def outer(i, carry):
                piece(i, count, base, off)
                return carry

            lax.fori_loop(0, count, outer, 0)
        return carry

    lax.fori_loop(0, cc // rg, group, 0)


def scan_body(
    nb, nseq, cc, rg, tab_ref, seq_ref, a_ref, kh_ref, wave_ref, back_ref, gg_ref, y_ref, mix_ref, in_s, ah_s, yh_s, y_s
):
    pieces = (nb + nseq) // 2
    load_pieces(nb, pieces, cc, tab_ref, lambda b: a_ref[0, b].astype(f32), in_s, wave_ref, ah_s)
    zero = jnp.zeros((rg, BIG), f32)

    def products(flip):
        def piece(i, count, base, off):
            def inner(j, acc):
                yc, ys = acc
                other = (base + i + j) if flip else (base + i - j)
                m = pl.ds(pl.multiple_of(other * cc + off, rg), rg)
                rows = pl.ds(off, rg)
                ac = ah_s[m, :BIG]
                as_ = ah_s[m, BIG:]
                kc = kh_ref[0, j, rows, :BIG]
                ks = kh_ref[0, j, rows, BIG:]
                if flip:
                    return (yc + kc * ac + ks * as_, ys + kc * as_ - ks * ac)
                return (yc + kc * ac - ks * as_, ys + kc * as_ + ks * ac)

            yc, ys = lax.fori_loop(0, (count - i) if flip else (i + 1), inner, (zero, zero))
            at = pl.ds(pl.multiple_of((base + i) * cc + off, rg), rg)
            yh_s[at, :BIG] = yc.astype(bf16)
            yh_s[at, BIG:] = ys.astype(bf16)

        over_pieces(nseq, cc, rg, seq_ref, piece)

    @pl.when(pl.program_id(0) == 0)
    def _():
        products(False)

    @pl.when(pl.program_id(0) == 1)
    def _():
        products(True)

    for h in range(pieces):
        at = pl.ds(h * cc, cc)
        y_s[at, :] = nn(yh_s[at, :], back_ref[...])

    def one(b, y):
        y_ref[0, b] = y.astype(bf16)
        mix_ref[0, b] = (y * gg_ref[0, b].astype(f32)).astype(bf16)

    def last(h, carry):
        b = tab_ref[0, h]
        at = pl.ds(pl.multiple_of(h * cc, cc), cc)
        one(b, y_s[at, 0:BLK])

        @pl.when(tab_ref[1, h] == 1)
        def _():
            one(b + 1, y_s[at, BLK:])

        return carry

    lax.fori_loop(0, seq_ref[1, nseq], last, 0)
    nothing = jnp.zeros((cc, BLK), bf16)

    def fill(b, carry):
        y_ref[0, b] = nothing
        mix_ref[0, b] = nothing
        return carry

    lax.fori_loop(seq_ref[0, nseq], nb, fill, 0)


def back_body(
    nb, nseq, cc, rg, tab_ref, seq_ref, a_ref, gm_ref, kh_ref, wave_ref, back_ref, gg_ref, y_ref, dg_ref, da_ref,
    gpg_ref, gp_ref, gh_ref, bs_ref, in_s, ah_s, gh_s, xh_s, x_s,
):
    pieces = (nb + nseq) // 2
    load_pieces(nb, pieces, cc, tab_ref, lambda b: a_ref[0, b].astype(f32), in_s, wave_ref, ah_s)
    load_pieces(
        nb, pieces, cc, tab_ref, lambda b: gm_ref[0, b].astype(f32) * gg_ref[0, b].astype(f32), in_s, wave_ref, gh_s
    )
    gh_ref[...] = jnp.zeros_like(gh_ref)
    zero = jnp.zeros((rg, BIG), f32)

    def products(flip):
        def piece(i, count, base, off):
            at = pl.ds(pl.multiple_of((base + i) * cc + off, rg), rg)
            ac = ah_s[at, :BIG]
            as_ = ah_s[at, BIG:]

            def inner(j, acc):
                xc, xs = acc
                other = (base + i - j) if flip else (base + i + j)
                m = pl.ds(pl.multiple_of(other * cc + off, rg), rg)
                rows = pl.ds(off, rg)
                gc = gh_s[m, :BIG]
                gs = gh_s[m, BIG:]
                kc = kh_ref[0, j, rows, :BIG]
                ks = kh_ref[0, j, rows, BIG:]
                gh_ref[0, j, rows, :BIG] += ac * gc + as_ * gs
                if flip:
                    gh_ref[0, j, rows, BIG:] += gc * as_ - gs * ac
                    return (xc + kc * gc - ks * gs, xs + kc * gs + ks * gc)
                gh_ref[0, j, rows, BIG:] += ac * gs - as_ * gc
                return (xc + kc * gc + ks * gs, xs + kc * gs - ks * gc)

            xc, xs = lax.fori_loop(0, (i + 1) if flip else (count - i), inner, (zero, zero))
            xh_s[at, :BIG] = xc.astype(bf16)
            xh_s[at, BIG:] = xs.astype(bf16)

        over_pieces(nseq, cc, rg, seq_ref, piece)

    @pl.when(pl.program_id(0) == 0)
    def _():
        products(False)

    @pl.when(pl.program_id(0) == 1)
    def _():
        products(True)

    for h in range(pieces):
        at = pl.ds(h * cc, cc)
        x_s[at, :] = nn(xh_s[at, :], back_ref[...])

    none = jnp.zeros((cc, BLK), f32)

    def one(b, gx, carry):
        s0, s1 = carry
        gpg = (y_ref[0, b].astype(f32) * gm_ref[0, b].astype(f32) * dg_ref[0, b].astype(f32)).astype(bf16)
        gpg_ref[0, b] = gpg
        gp = (gx * da_ref[0, b].astype(f32)).astype(bf16)
        gp_ref[0, b] = gp
        return (s0 + gpg.astype(f32), s1 + gp.astype(f32))

    def last(h, carry):
        b = tab_ref[0, h]
        at = pl.ds(pl.multiple_of(h * cc, cc), cc)
        carry = one(b, x_s[at, 0:BLK], carry)

        def more(kept):
            return one(b + 1, x_s[at, BLK:], kept)

        return lax.cond(tab_ref[1, h] == 1, more, lambda kept: kept, carry)

    s0, s1 = lax.fori_loop(0, seq_ref[1, nseq], last, (none, none))
    bs_ref[0, :, 0:BLK] = s0
    bs_ref[0, :, BLK:] = s1
    nothing = jnp.zeros((cc, BLK), bf16)

    def fill(b, carry):
        gpg_ref[0, b] = nothing
        gp_ref[0, b] = nothing
        return carry

    lax.fori_loop(seq_ref[0, nseq], nb, fill, 0)


def ssm_specs(shape, seq):
    _, nb, ch, _ = shape
    nseq = seq.shape[1] - 1
    pieces = (nb + nseq) // 2
    cc = chunk_of(ch, 128 if nb <= 32 else 64)
    big = pl.BlockSpec((1, nb, cc, BLK), lambda k, i: (k, 0, i, 0))
    spec = pl.BlockSpec((1, LAGS, cc, 2 * BIG), lambda k, i: (k, 0, i, 0))
    smem = pl.BlockSpec(memory_space=pltpu.SMEM)
    head = [smem, smem]
    tables = [pl.BlockSpec((BIG, 2 * BIG), lambda k, i: (0, 0)), pl.BlockSpec((2 * BIG, BIG), lambda k, i: (0, 0))]
    return nb, nseq, ch, cc, pieces * cc, big, spec, head, tables


def ssm_scan(tab, seq, a, kh, wave, back, gg):
    nb, nseq, ch, cc, size, big, spec, head, tables = ssm_specs(a.shape, seq)
    return pl.pallas_call(
        partial(scan_body, nb, nseq, cc, 32),
        grid=(2, ch // cc),
        in_specs=head + [big, spec] + tables + [big],
        out_specs=[big, big],
        out_shape=[jax.ShapeDtypeStruct(a.shape, bf16)] * 2,
        scratch_shapes=[
            pltpu.VMEM((size, BIG), bf16),
            pltpu.VMEM((size, 2 * BIG), f32),
            pltpu.VMEM((size, 2 * BIG), bf16),
            pltpu.VMEM((size, BIG), f32),
        ],
        compiler_params=params(56),
        cost_estimate=cost(2 * ch * 50e6, 2 * ch * nb * BLK * 8),
    )(tab, seq, a, kh, wave, back, gg)


def ssm_back(tab, seq, a, gm, kh, wave, back, gg, y, dg, da):
    nb, nseq, ch, cc, size, big, spec, head, tables = ssm_specs(a.shape, seq)
    return pl.pallas_call(
        partial(back_body, nb, nseq, cc, 16),
        grid=(2, ch // cc),
        in_specs=head + [big, big, spec] + tables + [big] * 4,
        out_specs=[big, big, spec, pl.BlockSpec((1, cc, 2 * BLK), lambda k, i: (k, i, 0))],
        out_shape=[jax.ShapeDtypeStruct(a.shape, bf16)] * 2
        + [
            jax.ShapeDtypeStruct((2, LAGS, ch, 2 * BIG), f32),
            jax.ShapeDtypeStruct((2, ch, 2 * BLK), f32),
        ],
        scratch_shapes=[
            pltpu.VMEM((size, BIG), bf16),
            pltpu.VMEM((size, 2 * BIG), f32),
            pltpu.VMEM((size, 2 * BIG), f32),
            pltpu.VMEM((size, 2 * BIG), bf16),
            pltpu.VMEM((size, BIG), f32),
        ],
        compiler_params=params(60),
        cost_estimate=cost(2 * ch * 80e6, 2 * ch * nb * BLK * 16),
    )(tab, seq, a, gm, kh, wave, back, gg, y, dg, da)


def stack_pair(refs):
    return jnp.concatenate(
        [jnp.concatenate([ref[k, 0], ref[k, 1]], axis=1) for ref in refs for k in range(2)], axis=0
    )


def mul_body(count, more, start_ref, w_ref, *refs):
    out = nn(w_ref[...], stack_pair(refs[:count]))
    o_ref = refs[-1]
    for h in range(2):
        part = out[:, h * BLK : (h + 1) * BLK]
        if more:
            part = part + refs[count][h].astype(f32)
        o_ref[h] = part.astype(o_ref.dtype)


def mul_rows(w, arrays, start, many, dtype=bf16, extra=None):
    width, deep = w.shape
    ch = arrays[0].shape[2]
    count = len(arrays)
    out = pl.BlockSpec((2, width, BLK), lambda i, at: (i, 0, 0))
    return pl.pallas_call(
        partial(mul_body, count, extra is not None),
        grid_spec=pltpu.PrefetchScalarGridSpec(
            num_scalar_prefetch=1,
            grid=(many // 2,),
            in_specs=[pl.BlockSpec((width, deep), lambda i, at: (0, 0))]
            + [pl.BlockSpec((2, 2, ch, BLK), lambda i, at: (0, at[0] + i, 0, 0))] * count
            + ([] if extra is None else [out]),
            out_specs=out,
        ),
        out_shape=jax.ShapeDtypeStruct((many, width, BLK), dtype),
        compiler_params=params(40),
        cost_estimate=cost(2 * many * BLK * width * deep, 2 * many * BLK * (2 * width + deep)),
    )(start // 2, w, *arrays, *([] if extra is None else [extra]))


def outer_body(ch, many, cuts, at_ref, x_ref, g_ref, gp_ref, gpg_ref, mix_ref, *refs):
    step = pl.program_id(0)
    acc_s = refs[-1]

    def flat(ref):
        return jnp.concatenate([ref[b] for b in range(many)], axis=1)

    def part(ref, k):
        return jnp.concatenate([ref[k, b] for b in range(many)], axis=1)

    @pl.when(step == 0)
    def _():
        acc_s[...] = jnp.zeros_like(acc_s)

    x = flat(x_ref)
    g = flat(g_ref)
    for at, (left, ref, k) in enumerate(
        [(x, gp_ref, 0), (x, gp_ref, 1), (x, gpg_ref, 0), (x, gpg_ref, 1), (g, mix_ref, 0), (g, mix_ref, 1)]
    ):
        acc_s[at] += nt(left, part(ref, k))

    @pl.when(step == pl.num_programs(0) - 1)
    def _():
        deep = acc_s.shape[1] // cuts
        for cut in range(cuts):
            start = pl.multiple_of(at_ref[pl.num_programs(0) + cut] * deep, 8)
            for at in range(6):
                refs[cut][at] = acc_s[at, pl.ds(start, deep), :].astype(bf16)


def outer_sums(order, cuts, xt, gt, gp, gpg, mix):
    nb, width, _ = xt.shape
    ch = gp.shape[2]
    many = 8
    rows = pl.BlockSpec((many, width, BLK), lambda i, at: (i, 0, 0))
    chan = pl.BlockSpec((2, many, ch, BLK), lambda i, at: (0, at[i], 0, 0))
    tok = nb * BLK
    return pl.pallas_call(
        partial(outer_body, ch, many, cuts),
        grid_spec=pltpu.PrefetchScalarGridSpec(
            num_scalar_prefetch=1,
            grid=(nb // many,),
            in_specs=[rows, rows, chan, chan, chan],
            out_specs=[pl.BlockSpec((6, width // cuts, ch), lambda i, at: (0, 0, 0))] * cuts,
            scratch_shapes=[pltpu.VMEM((6, width, ch), f32)],
        ),
        out_shape=[jax.ShapeDtypeStruct((6, width // cuts, ch), bf16)] * cuts,
        compiler_params=params(56),
        cost_estimate=cost(12 * tok * width * ch, tok * (4 * width + 12 * ch)),
    )(order, xt, gt, gp, gpg, mix)


def sequence_tables(lens, nb):
    nseq = lens.shape[0]
    blocks = (lens + BLK - 1) // BLK
    start = jnp.cumsum(blocks) - blocks
    bigs = (blocks + 1) // 2
    first_big = jnp.cumsum(bigs) - bigs
    h = jnp.arange((nb + nseq) // 2, dtype=jnp.int32)
    owner = (h[:, None] >= first_big[None, :]).astype(jnp.int32).sum(axis=1) - 1
    mine = owner[:, None] == jnp.arange(nseq, dtype=jnp.int32)[None, :]

    def at_owner(values):
        return jnp.sum(jnp.where(mine, values[None, :], 0), axis=1)

    rel = h - at_owner(first_big)
    first = jnp.minimum(at_owner(start) + 2 * rel, nb - 1)
    whole = (2 * rel + 1 < at_owner(blocks)).astype(jnp.int32)
    tab = jnp.stack([first, whole]).astype(jnp.int32)
    seq = jnp.stack(
        [jnp.append(first_big, jnp.sum(blocks)), jnp.append(bigs, jnp.sum(bigs))]
    ).astype(jnp.int32)
    return tab, seq


def live_rows(lens, rows):
    slot = (lens + BLK - 1) // BLK * BLK
    begin = jnp.cumsum(slot) - slot
    pos = jnp.arange(rows, dtype=jnp.int32)
    inside = (pos[:, None] >= begin[None, :]) & (pos[:, None] < (begin + lens)[None, :])
    return jnp.sum(inside.astype(f32), axis=1)


def rank_of(keys):
    return jnp.sum((keys[None, :] < keys[:, None]).astype(jnp.int32), axis=1)


class Line:
    def __init__(self, n_dp, n_t):
        self.n_dp, self.n_t = n_dp, n_t
        self.axes = {"dp": n_dp, "tensor": n_t}
        self.both = ("dp", "tensor")
        self.cuts = 1

    def place_of_group(self):
        return lax.axis_index("tensor")

    def regroup(self, x):
        return x

    def deal(self, x):
        return lax.all_to_all(x, "dp", split_axis=0, concat_axis=0, tiled=True)

    def undeal(self, x):
        return self.deal(x)

    def gather_rows(self, x):
        return [(lax.all_gather(x, "tensor", axis=0, tiled=True), jnp.zeros((1,), jnp.int32))]

    def scatter_rows(self, w, arrays, many):
        whole = mul_rows(w, arrays, jnp.zeros((1,), jnp.int32), many * self.n_t)
        return [lax.psum_scatter(whole, "tensor", scatter_dimension=0, tiled=True)]

    def order(self, pieces):
        return jnp.append(jnp.arange(pieces * self.n_t, dtype=jnp.int32), 0)

    def gather_channels(self, chan, norm):
        perm = [(f, (f % self.n_dp) * self.n_t + f // self.n_dp) for f in range(self.n_dp * self.n_t)]
        chan = lax.ppermute(chan, self.both, perm)
        norm = lax.all_gather(norm, self.both, axis=1, tiled=True)
        return lax.all_gather(chan, "dp", axis=0, tiled=True), norm

    def gather_weights(self, pack):
        return lax.all_gather(pack, "dp", axis=0, tiled=True)

    def scatter_weights(self, gw):
        six, width, ch = gw[0].shape
        gw = gw[0].reshape(six, self.n_dp, width // self.n_dp, ch).transpose(1, 0, 2, 3)
        return lax.psum_scatter(gw, "dp", scatter_dimension=0, tiled=True)[0].astype(f32)

    def scatter_channels(self, sums):
        sums = lax.psum_scatter(sums, "dp", scatter_dimension=0, tiled=True)
        perm = [((f % self.n_dp) * self.n_t + f // self.n_dp, f) for f in range(self.n_dp * self.n_t)]
        return lax.ppermute(sums, self.both, perm)

    def scatter_norm(self, sums):
        return lax.psum_scatter(sums, self.both, scatter_dimension=1, tiled=True)


class Pairs:
    def __init__(self, n_dp, n_t):
        self.quads = n_dp // 2
        self.axes = {"q": self.quads, "c": 2, "h": 2, "w": 2}
        self.both = ("q", "c", "h", "w")
        self.cuts = self.quads
        self.other = [(0, 1), (1, 0)]
        self.crossed = [(2 * c + h, 2 * h + c) for c in range(2) for h in range(2)]

    def flip(self, x, axis, bit=1):
        return lax.ppermute(x, axis, [(i, i ^ bit) for i in range(self.axes[axis])])

    def place_of_group(self):
        return 2 * lax.axis_index("c") + lax.axis_index("w")

    def regroup(self, x):
        return lax.ppermute(x, ("c", "h"), self.crossed)

    def deal(self, x):
        return self.regroup(lax.all_to_all(x, ("q", "c"), split_axis=0, concat_axis=0, tiled=True))

    def undeal(self, x):
        return lax.all_to_all(self.regroup(x), ("q", "c"), split_axis=0, concat_axis=0, tiled=True)

    def places(self):
        c, w = lax.axis_index("c"), lax.axis_index("w")
        return [2 * c + w, 2 * (1 - c) + w, 2 * c + 1 - w, 2 * (1 - c) + 1 - w]

    def starts(self, many):
        return [(place * many).astype(jnp.int32).reshape(1) for place in self.places()]

    def gather_rows(self, x):
        beside = self.flip(x, "c")
        near = self.flip(x, "w")
        far = self.flip(near, "c")
        return list(zip([x, beside, near, far], self.starts(x.shape[0])))

    def scatter_rows(self, w, arrays, many):
        own, beside, near, far = self.starts(many)
        give = self.flip(mul_rows(w, arrays, far, many), "c")
        send = self.flip(mul_rows(w, arrays, near, many, extra=give), "w")
        give = self.flip(mul_rows(w, arrays, beside, many), "c")
        return [mul_rows(w, arrays, own, many, dtype=f32), give, send]

    def order(self, pieces):
        place = jnp.stack(self.places())[:, None] * pieces + jnp.arange(pieces)[None, :]
        cut = lax.axis_index("q") ^ jnp.arange(self.quads)
        return jnp.concatenate([place.reshape(-1), cut]).astype(jnp.int32)

    def steps(self):
        bit = self.quads // 2
        while bit:
            yield "q", bit
            bit //= 2
        yield "h", 1

    def spot(self):
        return 2 * lax.axis_index("q") + lax.axis_index("h")

    def gather_channels(self, chan, norm):
        count = 2 * self.quads
        perm = []
        for f in range(4 * count):
            place, at = f // count, f % count
            q, h, c, w = at // 2, at % 2, place // 2, place % 2
            perm.append((f, ((2 * q + c) * 2 + h) * 2 + w))
        chan = lax.ppermute(chan, self.both, perm)
        norm = norm.reshape(1, -1)
        for axis in ("c", "w"):
            norm = jnp.concatenate([norm, self.flip(norm, axis)], axis=0)
        c, w = lax.axis_index("c"), lax.axis_index("w")
        at = jnp.arange(4)
        norm = jnp.take(norm, 2 * ((at % 2) ^ w) + ((at // 2) ^ c), axis=0)
        flat = jnp.concatenate([chan.reshape(1, -1), norm.reshape(1, -1)], axis=1)
        for axis, bit in reversed(list(self.steps())):
            flat = jnp.concatenate([flat, self.flip(flat, axis, bit)], axis=0)
        flat = jnp.take(flat, jnp.arange(count) ^ self.spot(), axis=0)
        rows, wide = chan.shape
        chan = flat[:, : rows * wide].reshape(count * rows, wide)
        norm = flat[:, rows * wide :].reshape(self.quads, 2, 2, 2, 3, -1)
        norm = norm.transpose(4, 0, 2, 1, 3, 5).reshape(3, -1)
        return chan, norm

    def gather_weights(self, pack):
        h = lax.axis_index("h")
        first = self.regroup(pack)
        back = [(2 * (1 - h) + c, 2 * c + h) for c in range(2) for h in range(2)]
        second = lax.ppermute(pack, ("c", "h"), back)
        pair = jnp.concatenate([jnp.where(h == 0, first, second), jnp.where(h == 0, second, first)], axis=0)
        deep, wide = pair.shape
        q = lax.axis_index("q")
        whole = jnp.zeros((self.quads * deep, wide), pack.dtype)
        for bit in range(self.quads):
            part = self.flip(pair, "q", bit) if bit else pair
            whole = lax.dynamic_update_slice_in_dim(whole, part, (q ^ bit) * deep, 0)
        return whole

    def scatter_weights(self, gw):
        total = gw[0].astype(f32)
        for bit in range(1, self.quads):
            total = total + self.flip(gw[bit], "q", bit).astype(f32)
        total = total.astype(bf16)
        six, deep, ch = total.shape
        total = total.reshape(six, 2, deep // 2, ch)
        h = lax.axis_index("h")
        first = jnp.where(h == 0, total[:, 0], total[:, 1])
        second = jnp.where(h == 0, total[:, 1], total[:, 0])
        there = [(2 * c + h, 2 * (1 - h) + c) for c in range(2) for h in range(2)]
        return self.regroup(first).astype(f32) + lax.ppermute(second, ("c", "h"), there).astype(f32)

    def scatter_channels(self, sums):
        count = 2 * self.quads
        rows, wide = sums.shape
        part = jnp.take(sums.reshape(count, rows // count * wide), jnp.arange(count) ^ self.spot(), axis=0)
        for axis, bit in self.steps():
            half = part.shape[0] // 2
            part = part[:half] + self.flip(part[half:], axis, bit)
        perm = []
        for f in range(4 * count):
            place, at = f // count, f % count
            q, h, c, w = at // 2, at % 2, place // 2, place % 2
            perm.append((((2 * q + c) * 2 + h) * 2 + w, f))
        return lax.ppermute(part.reshape(rows // count, wide), self.both, perm)

    def scatter_norm(self, sums):
        count = 8 * self.quads
        mine = lax.axis_index(self.both)
        part = jnp.take(sums.reshape(3, count, -1), jnp.arange(count) ^ mine, axis=1)
        bits = [("q", 1 << at) for at in reversed(range(self.quads.bit_length() - 1))]
        for axis, bit in bits + [("c", 1), ("h", 1), ("w", 1)]:
            half = part.shape[1] // 2
            part = part[:, :half] + self.flip(part[:, half:], axis, bit)
        return part[:, 0]


def local(
    net, wave, tokens, cotangent, source, target, lengths, ln_gain, ln_bias, w_fwd, b_fwd, w_bwd, b_bwd,
    w_gate, b_gate, w_out, b_out, log_dt, log_rate, ssm_b, ssm_c, ssm_d,
):
    rows, width = tokens.shape
    many = rows // BLK
    n_t = net.n_t
    group = rows * n_t
    nb = group // BLK
    ch = w_fwd.shape[1]
    back = (wave.T / BIG).astype(bf16)
    wave = wave.astype(bf16)

    rank = rank_of(target)
    sender = source // group
    place = rank_of(sender * rows + jnp.arange(rows, dtype=jnp.int32))
    (sent_x,) = permute_to(rank, [tokens])
    got_x = net.deal(sent_x)
    (sent_g,) = permute_to(rank, [cotangent])
    got_g = net.deal(sent_g)
    table = net.regroup(jnp.concatenate([place, lengths[0]]))
    place, lens = table[:rows], table[rows:]

    chan = jnp.concatenate(
        [log_rate[0], log_rate[1], ssm_b[0], ssm_b[1], ssm_c[0], ssm_c[1]]
        + [jnp.stack([log_dt[0], log_dt[1], ssm_d[0], ssm_d[1], b_fwd, b_bwd, b_gate[0], b_gate[1]], axis=1)],
        axis=1,
    )
    chan_all, norm_all = net.gather_channels(chan, jnp.stack([ln_gain, ln_bias, b_out]))

    def lanes(column):
        return jnp.broadcast_to(column[..., None], column.shape + (BLK,))

    gain = lanes(norm_all[0])
    shift = lanes(norm_all[1])
    bias_out = lanes(norm_all[2])
    small = chan_all[:, 6 * STATE :]
    bias_in = lanes(small[:, 4:8].T.reshape(-1))

    def pick(at):
        return jnp.stack([chan_all[:, at * STATE : (at + 1) * STATE], chan_all[:, (at + 1) * STATE : (at + 2) * STATE]])

    def decays(log_dt, log_rate, ssm_b):
        rate = jnp.exp(log_rate)
        ld = -jnp.exp(log_dt)[..., None] * rate
        return rate, ld, (1.0 - jnp.exp(ld)) / rate * ssm_b

    _, ld_all, drive_all = decays(small[:, 0:2].T, pick(0), pick(2))
    ld_pairs = (ld_all * log2e).reshape(2, ch // 2, 2 * STATE)
    w_pairs = (pick(4) * drive_all).reshape(2, ch // 2, 2 * STATE)
    kh = spectra(ld_pairs, w_pairs, lanes(small[:, 2:4].T), wave)

    pack = jnp.concatenate(
        [w_fwd, w_bwd, w_gate.reshape(-1, 2 * ch), w_out.transpose(2, 0, 1).reshape(-1, 2 * ch)], axis=1
    )
    w_all = net.gather_weights(pack)
    w_in, w_back = w_all[:, : 4 * ch], w_all[:, 4 * ch :]
    w_in_t, w_back_t = w_in.T, w_back.T

    live = live_rows(lens, group)
    live_own = lax.dynamic_slice_in_dim(live, net.place_of_group() * rows, rows, 0).reshape(many, 1, BLK)
    live = live.reshape(nb // 2, 1, BIG)
    tab, seq = sequence_tables(lens, nb)

    xt, xd = deal_x(place, got_x, gain, shift)
    xs = net.gather_rows(xt)
    kept = None
    for part, start in xs:
        kept = project(part, start, nb, live, w_in_t, bias_in, kept)
    a, da, gg, dg = kept
    y, mix = ssm_scan(tab, seq, a, kh, wave, back, gg)

    gt, gd, g_bias_out = deal_g(place, got_g, live_own)
    gs = net.gather_rows(gt)
    kept = None
    for part, start in gs:
        kept = gate_grad(part, start, nb, w_back_t, kept)
    (gm,) = kept

    branch = net.scatter_rows(w_back, [mix], many)
    sent_out = layer_rows(place, branch, xd, live_own, bias_out)
    layer_out = permute_from(rank, net.undeal(sent_out))

    gpg, gp, gh, bsum = ssm_back(tab, seq, a, gm, kh, wave, back, gg, y, dg, da)
    g_normed = net.scatter_rows(w_in, [gp, gpg], many)
    gw = outer_sums(
        net.order(many // 8),
        net.cuts,
        jnp.concatenate([part for part, _ in xs], axis=0),
        jnp.concatenate([part for part, _ in gs], axis=0),
        gp,
        gpg,
        mix,
    )
    gw = net.scatter_weights(gw)
    s0, s1, g0 = moments(ld_pairs, gh, back)

    sent_in, norm_sums = input_rows(place, g_normed, xd, gd, gain)
    in_grad = permute_from(rank, net.undeal(sent_in))

    s0 = s0.reshape(2, ch, STATE)
    s1 = s1.reshape(2, ch, STATE)
    gb_gate = jnp.sum(bsum[:, :, :BLK], axis=2)
    gb_in = jnp.sum(bsum[:, :, BLK:], axis=2)
    sums = jnp.concatenate(
        [s0[0], s0[1], s1[0], s1[1], jnp.concatenate([g0[:, :, 0], gb_gate, gb_in], axis=0).T], axis=1
    )
    sums = net.scatter_channels(sums)
    norm_sums = net.scatter_norm(jnp.sum(jnp.concatenate([norm_sums, g_bias_out[None]], axis=0), axis=2))
    s0 = jnp.stack([sums[:, :STATE], sums[:, STATE : 2 * STATE]])
    s1 = jnp.stack([sums[:, 2 * STATE : 3 * STATE], sums[:, 3 * STATE : 4 * STATE]])
    tail = sums[:, 4 * STATE :].T
    step = jnp.exp(log_dt)[..., None]
    rate, ld, drive = decays(log_dt, log_rate, ssm_b)
    g_c = s0 * drive
    g_drive = s0 * ssm_c
    g_b = g_drive * (1.0 - jnp.exp(ld)) / rate
    g_ld = s1 * ssm_c * drive - g_drive * ssm_b / rate * jnp.exp(ld)
    g_rate = -g_drive * drive / rate - g_ld * step
    g_dt = jnp.sum(g_ld * ld, axis=2)
    return (
        layer_out,
        in_grad,
        norm_sums[0],
        norm_sums[1],
        gw[0],
        tail[4],
        gw[1],
        tail[5],
        jnp.stack([gw[2], gw[3]], axis=1),
        tail[2:4],
        jnp.stack([gw[4].T, gw[5].T]),
        norm_sums[2],
        g_dt,
        g_rate * rate,
        g_b,
        g_c,
        tail[0:2],
    )


def solution(mesh):
    n_dp, n_t = mesh.shape["dp"], mesh.shape["tensor"]
    if n_t == 4 and n_dp == 8:
        net = Pairs(n_dp, n_t)
        dp, tensor = ("q", "c"), ("h", "w")
    else:
        net = Line(n_dp, n_t)
        dp, tensor = ("dp",), ("tensor",)
    net.n_t = n_t
    mesh = jax.sharding.Mesh(mesh.devices.reshape(tuple(net.axes.values())), tuple(net.axes))
    both = P(dp + tensor)
    rows = P(dp + tensor, None)
    pair = P(None, dp + tensor)
    state = P(None, dp + tensor, None)
    proj = P(dp, tensor)
    gate = P(dp, None, tensor)
    out = P(None, tensor, dp)
    wave = wave_table()

    def run(*args):
        return local(net, jnp.asarray(wave), *args)

    return jax.shard_map(
        run,
        mesh=mesh,
        in_specs=(
            rows, rows, both, both, P(dp, None), both, both, proj, both, proj, both, gate, pair, out, both,
            pair, state, state, state, pair,
        ),
        out_specs=(
            rows, rows, both, both, proj, both, proj, both, gate, pair, out, both, pair, state, state, state, pair,
        ),
        check_vma=False,
    )
```

```python
from functools import partial

import jax
import jax.numpy as jnp
import numpy as np
from jax import lax
from jax.experimental import pallas as pl
from jax.experimental.pallas import tpu as pltpu
from jax.sharding import PartitionSpec as P

BLK = 128
BIG = 256
MOST = 2048
LAGS = MOST // BIG
STATE = 64
epsilon = 1e-05
log2e = 1.4426950408889634
f32 = jnp.float32
bf16 = jnp.bfloat16
MIB = 2**20


def nn(a, b):
    return lax.dot_general(a, b, (((1,), (0,)), ((), ())), preferred_element_type=f32)


def nt(a, b):
    return lax.dot_general(a, b, (((1,), (1,)), ((), ())), preferred_element_type=f32)


def params(limit):
    return pltpu.CompilerParams(vmem_limit_bytes=limit * MIB)


def cost(flops, moved, trans=0):
    return pl.CostEstimate(flops=int(flops), bytes_accessed=int(moved), transcendentals=int(trans))


def halves(x):
    high = x.astype(bf16)
    return high, (x - high.astype(f32)).astype(bf16)


def wave_table():
    pos = np.arange(BIG)[:, None]
    freq = np.arange(BIG)[None, :]
    angle = 2 * np.pi * ((2 * freq + 1) * pos % (4 * BIG)) / (4 * BIG)
    return np.concatenate([np.cos(angle), np.sin(angle)], 1).astype(np.float32)


def chunk_of(channels, most):
    best = 16
    for size in range(16, most + 1, 16):
        if channels % size == 0:
            best = size
    return best


def permute_row_body(count, rank_ref, *refs):
    rows = rank_ref.shape[1]
    spot = lax.broadcasted_iota(jnp.int32, (rows, rows), 0)
    pick = jnp.where(spot == rank_ref[...], 1.0, 0.0).astype(bf16)
    for at in range(count):
        refs[count + at][...] = nn(pick, refs[at][...]).astype(bf16)


def permute_to(rank, arrays):
    rows, width = arrays[0].shape
    count = len(arrays)
    return pl.pallas_call(
        partial(permute_row_body, count),
        out_shape=[jax.ShapeDtypeStruct((rows, width), bf16)] * count,
        compiler_params=params(48),
        cost_estimate=cost(2 * count * rows * rows * width, 4 * count * rows * width),
    )(rank.reshape(1, rows), *arrays)


def permute_col_body(rank_ref, x_ref, o_ref):
    rows = x_ref.shape[0]
    spot = lax.broadcasted_iota(jnp.int32, (rows, rows), 1)
    pick = jnp.where(spot == rank_ref[...], 1.0, 0.0).astype(bf16)
    o_ref[...] = nn(pick, x_ref[...]).astype(bf16)


def permute_from(rank, x):
    rows, width = x.shape
    return pl.pallas_call(
        permute_col_body,
        out_shape=jax.ShapeDtypeStruct((rows, width), bf16),
        compiler_params=params(48),
        cost_estimate=cost(2 * rows * rows * width, 4 * rows * width),
    )(rank.reshape(rows, 1), x)


def pick_rows(place_ref, x_ref):
    spot = lax.broadcasted_iota(jnp.int32, (BLK, x_ref.shape[0]), 1)
    pick = jnp.where(spot == place_ref[...], 1.0, 0.0).astype(bf16)
    return nn(pick, x_ref[...]).T


def deal_x_body(place_ref, x_ref, gain_ref, shift_ref, xt_ref, xd_ref):
    x = pick_rows(place_ref, x_ref)
    xd_ref[0] = x.astype(bf16)
    centred = x - jnp.mean(x, axis=0, keepdims=True)
    inv_std = lax.rsqrt(jnp.mean(centred * centred, axis=0, keepdims=True) + epsilon)
    xt_ref[0] = (centred * inv_std * gain_ref[...] + shift_ref[...]).astype(bf16)


def deal_g_body(place_ref, g_ref, live_ref, gt_ref, gd_ref, bo_ref):
    g = pick_rows(place_ref, g_ref)
    gd_ref[0] = g.astype(bf16)
    g = g * live_ref[0]
    gt_ref[0] = g.astype(bf16)

    @pl.when(pl.program_id(0) == 0)
    def _():
        bo_ref[...] = jnp.zeros_like(bo_ref)

    bo_ref[...] += g


def deal_specs(rows, width):
    place = pl.BlockSpec((BLK, 1), lambda i: (i, 0))
    whole = pl.BlockSpec((rows, width), lambda i: (0, 0))
    wide = pl.BlockSpec((width, BLK), lambda i: (0, 0))
    out = pl.BlockSpec((1, width, BLK), lambda i: (i, 0, 0))
    return place, whole, wide, out


def deal_x(place, x, gain, shift):
    rows, width = x.shape
    blocks = rows // BLK
    spot, whole, wide, out = deal_specs(rows, width)
    return pl.pallas_call(
        deal_x_body,
        grid=(blocks,),
        in_specs=[spot, whole, wide, wide],
        out_specs=[out, out],
        out_shape=[jax.ShapeDtypeStruct((blocks, width, BLK), bf16)] * 2,
        compiler_params=params(40),
        cost_estimate=cost(2 * rows * rows * width, 6 * rows * width),
    )(place.reshape(rows, 1), x, gain, shift)


def deal_g(place, g, live):
    rows, width = g.shape
    blocks = rows // BLK
    spot, whole, wide, out = deal_specs(rows, width)
    return pl.pallas_call(
        deal_g_body,
        grid=(blocks,),
        in_specs=[spot, whole, pl.BlockSpec((1, 1, BLK), lambda i: (i, 0, 0))],
        out_specs=[out, out, wide],
        out_shape=[jax.ShapeDtypeStruct((blocks, width, BLK), bf16)] * 2
        + [jax.ShapeDtypeStruct((width, BLK), f32)],
        compiler_params=params(40),
        cost_estimate=cost(2 * rows * rows * width, 6 * rows * width),
    )(place.reshape(rows, 1), g, live)


def send_back(place_ref, out_s, o_ref):
    rows = out_s.shape[0]
    spot = lax.broadcasted_iota(jnp.int32, (rows, rows), 0)
    pick = jnp.where(spot == place_ref[...], 1.0, 0.0).astype(bf16)
    o_ref[...] = nn(pick, out_s[...]).astype(bf16)


def total(refs, at):
    value = refs[0][at].astype(f32)
    for ref in refs[1:]:
        value = value + ref[at].astype(f32)
    return value


def layer_body(place_ref, xd_ref, live_ref, bias_ref, *refs):
    o_ref, out_s = refs[-2:]
    for at in range(xd_ref.shape[0]):
        y = xd_ref[at].astype(f32) + live_ref[at] * (total(refs[:-2], at) + bias_ref[...])
        out_s[at * BLK : (at + 1) * BLK, :] = y.T.astype(bf16)
    send_back(place_ref, out_s, o_ref)


def layer_rows(place, parts, xd, live, bias):
    blocks, width, _ = xd.shape
    rows = blocks * BLK
    return pl.pallas_call(
        layer_body,
        out_shape=jax.ShapeDtypeStruct((rows, width), bf16),
        scratch_shapes=[pltpu.VMEM((rows, width), bf16)],
        compiler_params=params(48),
        cost_estimate=cost(2 * rows * rows * width, 6 * rows * width),
    )(place.reshape(1, rows), xd, live, bias, *parts)


def input_body(place_ref, xd_ref, gd_ref, gain_ref, *refs):
    o_ref, sums_ref, out_s = refs[-3:]
    g_gain = jnp.zeros(gain_ref.shape, f32)
    g_shift = jnp.zeros(gain_ref.shape, f32)
    for at in range(xd_ref.shape[0]):
        x = xd_ref[at].astype(f32)
        centred = x - jnp.mean(x, axis=0, keepdims=True)
        inv_std = lax.rsqrt(jnp.mean(centred * centred, axis=0, keepdims=True) + epsilon)
        x_hat = centred * inv_std
        g = total(refs[:-3], at)
        g_gain = g_gain + g * x_hat
        g_shift = g_shift + g
        hat = g * gain_ref[...]
        back = inv_std * (
            hat
            - jnp.mean(hat, axis=0, keepdims=True)
            - x_hat * jnp.mean(hat * x_hat, axis=0, keepdims=True)
        )
        out_s[at * BLK : (at + 1) * BLK, :] = (gd_ref[at].astype(f32) + back).T.astype(bf16)
    sums_ref[0] = g_gain
    sums_ref[1] = g_shift
    send_back(place_ref, out_s, o_ref)


def input_rows(place, parts, xd, gd, gain):
    blocks, width, _ = xd.shape
    rows = blocks * BLK
    return pl.pallas_call(
        input_body,
        out_shape=[
            jax.ShapeDtypeStruct((rows, width), bf16),
            jax.ShapeDtypeStruct((2, width, BLK), f32),
        ],
        scratch_shapes=[pltpu.VMEM((rows, width), bf16)],
        compiler_params=params(48),
        cost_estimate=cost(2 * rows * rows * width, 8 * rows * width),
    )(place.reshape(1, rows), xd, gd, gain, *parts)


def project_body(ch, many, start_ref, x_ref, live_ref, wt_ref, bias_ref, *refs):
    a_ref, da_ref, gg_ref, dg_ref, pre_s = refs[-5:]
    x = jnp.concatenate([x_ref[0], x_ref[1]], axis=1)
    pre_s[...] = nn(wt_ref[...], x)
    live = live_ref[0]
    step = 32
    root = 0.7978845608028654

    def act(pre):
        square = pre * pre
        bent = jnp.tanh(root * pre * (1.0 + 0.044715 * square))
        rise = 0.5 + 0.5 * bent
        slope = rise + (0.5 * root) * pre * (1.0 - bent * bent) * (1.0 + 0.134145 * square)
        return pre * rise, slope

    def put(ref, k, at, value):
        value = value.astype(bf16)
        ref[k, 0, at, :] = value[:, :BLK]
        ref[k, 1, at, :] = value[:, BLK:]

    def chunk(i, carry):
        at = pl.ds(pl.multiple_of(i * step, step), step)
        for k in range(2):
            row = pl.ds(pl.multiple_of(k * ch + i * step, step), step)
            gate = pl.ds(pl.multiple_of((2 + k) * ch + i * step, step), step)
            bias = bias_ref[row, :]
            value, slope = act(pre_s[row, :] + jnp.concatenate([bias, bias], axis=1))
            put(a_ref, k, at, live * value)
            put(da_ref, k, at, live * slope)
            bias = bias_ref[gate, :]
            value, slope = act(pre_s[gate, :] + jnp.concatenate([bias, bias], axis=1))
            put(gg_ref, k, at, value)
            put(dg_ref, k, at, slope)
        return carry

    lax.fori_loop(0, ch // step, chunk, 0)


def chained(body, grid, in_specs, out_specs, shapes, scratch, limit, estimate, start, operands, kept):
    kept = [] if kept is None else list(kept)
    specs = list(in_specs) + [pl.BlockSpec(memory_space=pl.ANY)] * len(kept)
    first = 1 + len(operands)
    return pl.pallas_call(
        body,
        grid_spec=pltpu.PrefetchScalarGridSpec(
            num_scalar_prefetch=1, grid=grid, in_specs=specs, out_specs=out_specs, scratch_shapes=scratch
        ),
        out_shape=shapes,
        input_output_aliases={first + at: at for at in range(len(kept))},
        compiler_params=params(limit),
        cost_estimate=estimate,
    )(start, *operands, *kept)


def project(xt, start, nb, live, wt, bias, kept):
    many, width, _ = xt.shape
    ch = wt.shape[0] // 4
    out = pl.BlockSpec((2, 2, ch, BLK), lambda i, at: (0, at[0] + i, 0, 0))
    tok = many * BLK
    return chained(
        partial(project_body, ch, many),
        (many // 2,),
        [
            pl.BlockSpec((2, width, BLK), lambda i, at: (i, 0, 0)),
            pl.BlockSpec((1, 1, BIG), lambda i, at: (at[0] + i, 0, 0)),
            pl.BlockSpec((4 * ch, width), lambda i, at: (0, 0)),
            pl.BlockSpec((4 * ch, BLK), lambda i, at: (0, 0)),
        ],
        [out] * 4,
        [jax.ShapeDtypeStruct((2, nb, ch, BLK), bf16)] * 4,
        [pltpu.VMEM((4 * ch, BIG), f32)],
        48,
        cost(8 * tok * width * ch, 2 * tok * width + 16 * tok * ch, 4 * tok * ch),
        start // 2,
        [xt, live, wt, bias],
        kept,
    )


def gate_grad_body(ch, start_ref, g_ref, wt_ref, *refs):
    o_ref = refs[-1]
    gm = nn(wt_ref[...], jnp.concatenate([g_ref[0], g_ref[1]], axis=1)).astype(bf16)
    for k in range(2):
        for h in range(2):
            o_ref[k, h] = gm[k * ch : (k + 1) * ch, h * BLK : (h + 1) * BLK]


def gate_grad(gt, start, nb, wt, kept):
    many, width, _ = gt.shape
    ch = wt.shape[0] // 2
    tok = many * BLK
    return chained(
        partial(gate_grad_body, ch),
        (many // 2,),
        [
            pl.BlockSpec((2, width, BLK), lambda i, at: (i, 0, 0)),
            pl.BlockSpec((2 * ch, width), lambda i, at: (0, 0)),
        ],
        [pl.BlockSpec((2, 2, ch, BLK), lambda i, at: (0, at[0] + i, 0, 0))],
        [jax.ShapeDtypeStruct((2, nb, ch, BLK), bf16)],
        [],
        40,
        cost(4 * tok * width * ch, 2 * tok * width + 4 * tok * ch),
        start // 2,
        [gt, wt],
        kept,
    )


def spectra_body(cc, ld_ref, w_ref, d_ref, wave_ref, kh_ref, k_s):
    t = lax.broadcasted_iota(jnp.int32, (BLK, BLK), 0).astype(f32)
    block = lax.broadcasted_iota(jnp.int32, (2 * LAGS, BLK), 0).astype(f32) * float(BLK)
    low = lax.broadcasted_iota(jnp.int32, (2 * LAGS, BLK), 1) < STATE
    count = 2 * LAGS

    def one(p, carry):
        ld = ld_ref[0, pl.ds(p, 1), :]
        decay = jnp.exp2(t * ld)
        scale = w_ref[0, pl.ds(p, 1), :] * jnp.exp2(block * ld)
        lhs = jnp.concatenate([jnp.where(low, scale, 0.0), jnp.where(low, 0.0, scale)], axis=0)
        lhs_high, lhs_low = halves(lhs)
        high, rest = halves(decay)
        k = nt(jnp.concatenate([lhs_high, lhs_low], axis=0), high)
        k = k[0 : 2 * count] + k[2 * count : 4 * count] + nt(lhs_high, rest)
        k_s[pl.ds(2 * p, count, stride=cc), :] = k[0:count]
        k_s[pl.ds(2 * p + 1, count, stride=cc), :] = k[count : 2 * count]
        return carry

    lax.fori_loop(0, cc // 2, one, 0, unroll=4)
    sign = jnp.where(lax.broadcasted_iota(jnp.int32, (cc, BIG), 1) % 2 == 0, 1.0, -1.0)
    before = None
    for big in range(LAGS):
        rows = jnp.concatenate(
            [k_s[pl.ds(2 * big * cc, cc), :], k_s[pl.ds((2 * big + 1) * cc, cc), :]], axis=1
        )
        high, rest = halves(rows)
        x = nn(high, wave_ref[...]) + nn(rest, wave_ref[...])
        xc, xs = x[:, :BIG], x[:, BIG:]
        if big == 0:
            kh_ref[0, 0, :, :BIG] = xc + d_ref[0][:, 0:1]
            kh_ref[0, 0, :, BIG:] = xs
        else:
            kh_ref[0, big, :, :BIG] = xc + sign * before[1]
            kh_ref[0, big, :, BIG:] = xs - sign * before[0]
        before = (xc, xs)


def spectra(ld, w, d, wave):
    ch = 2 * ld.shape[1]
    cc = chunk_of(ch, 128)
    return pl.pallas_call(
        partial(spectra_body, cc),
        grid=(2, ch // cc),
        in_specs=[pl.BlockSpec((1, cc // 2, BLK), lambda k, i: (k, i, 0))] * 2
        + [
            pl.BlockSpec((1, cc, BLK), lambda k, i: (k, i, 0)),
            pl.BlockSpec((BIG, 2 * BIG), lambda k, i: (0, 0)),
        ],
        out_specs=pl.BlockSpec((1, LAGS, cc, 2 * BIG), lambda k, i: (k, 0, i, 0)),
        out_shape=jax.ShapeDtypeStruct((2, LAGS, ch, 2 * BIG), f32),
        scratch_shapes=[pltpu.VMEM((2 * LAGS * cc, BLK), f32)],
        compiler_params=params(40),
        cost_estimate=cost(2 * ch * 40e6, 2 * ch * LAGS * 2 * BIG * 4),
    )(ld, w, d, wave)


def moments_body(cc, ld_ref, gh_ref, back_ref, s0_ref, s1_ref, g0_ref, g_s):
    sign = jnp.where(lax.broadcasted_iota(jnp.int32, (cc, BIG), 1) % 2 == 0, 1.0, -1.0)
    count = 2 * LAGS
    for big in range(LAGS):
        c = gh_ref[0, big, :, :BIG]
        s = gh_ref[0, big, :, BIG:]
        if big < LAGS - 1:
            c, s = c - sign * gh_ref[0, big + 1, :, BIG:], s + sign * gh_ref[0, big + 1, :, :BIG]
        high, rest = halves(jnp.concatenate([c, s], axis=1))
        g = nn(high, back_ref[...]) + nn(rest, back_ref[...])
        g_s[pl.ds(2 * big * cc, cc), :] = g[:, :BLK]
        g_s[pl.ds((2 * big + 1) * cc, cc), :] = g[:, BLK:]
        if big == 0:
            g0_ref[0] = g[:, :BLK]
    t = lax.broadcasted_iota(jnp.int32, (BLK, BLK), 0).astype(f32)
    lane = lax.broadcasted_iota(jnp.int32, (count, BLK), 1)
    lag = lane.astype(f32)
    block = lax.broadcasted_iota(jnp.int32, (count, BLK), 0).astype(f32) * float(BLK)
    low = lane < STATE

    def one(p, carry):
        ld = ld_ref[0, pl.ds(p, 1), :]
        decay = jnp.exp2(t * ld).astype(bf16)
        far = jnp.exp2(block * ld)
        ga = g_s[pl.ds(2 * p, count, stride=cc), :]
        gb = g_s[pl.ds(2 * p + 1, count, stride=cc), :]
        high, rest = halves(jnp.concatenate([ga, gb, ga * lag, gb * lag], axis=0))
        m = nn(jnp.concatenate([high, rest], axis=0), decay)
        m = m[0 : 4 * count] + m[4 * count : 8 * count]
        m0 = jnp.where(low, m[0:count], m[count : 2 * count])
        m1 = jnp.where(low, m[2 * count : 3 * count], m[3 * count : 4 * count]) + block * m0
        s0_ref[0, pl.ds(p, 1), :] = jnp.sum(far * m0, axis=0, keepdims=True)
        s1_ref[0, pl.ds(p, 1), :] = jnp.sum(far * m1, axis=0, keepdims=True)
        return carry

    lax.fori_loop(0, cc // 2, one, 0, unroll=4)


def moments(ld, gh, back):
    ch = gh.shape[2]
    cc = chunk_of(ch, 128)
    row = pl.BlockSpec((1, cc // 2, BLK), lambda k, i: (k, i, 0))
    return pl.pallas_call(
        partial(moments_body, cc),
        grid=(2, ch // cc),
        in_specs=[
            row,
            pl.BlockSpec((1, LAGS, cc, 2 * BIG), lambda k, i: (k, 0, i, 0)),
            pl.BlockSpec((2 * BIG, BIG), lambda k, i: (0, 0)),
        ],
        out_specs=[row, row, pl.BlockSpec((1, cc, BLK), lambda k, i: (k, i, 0))],
        out_shape=[jax.ShapeDtypeStruct((2, ch // 2, BLK), f32)] * 2
        + [jax.ShapeDtypeStruct((2, ch, BLK), f32)],
        scratch_shapes=[pltpu.VMEM((2 * LAGS * cc, BLK), f32)],
        compiler_params=params(40),
        cost_estimate=cost(2 * ch * 40e6, 2 * ch * LAGS * 2 * BIG * 4),
    )(ld, gh, back)


def load_pieces(nb, pieces, cc, tab_ref, block, in_s, wave_ref, dst):
    for h in range(pieces):
        first = tab_ref[0, h]
        whole = tab_ref[1, h].astype(f32)
        in_s[pl.ds(h * cc, cc), 0:BLK] = block(first).astype(bf16)
        in_s[pl.ds(h * cc, cc), BLK:BIG] = (block(jnp.minimum(first + 1, nb - 1)) * whole).astype(bf16)
    for h in range(pieces):
        at = pl.ds(h * cc, cc)
        dst[at, :] = nn(in_s[at, :], wave_ref[...])


def over_pieces(nseq, cc, rg, seq_ref, piece):
    def group(r, carry):
        off = pl.multiple_of(r * rg, rg)
        for s in range(nseq):
            base = seq_ref[0, s]
            count = seq_ref[1, s]

            def outer(i, carry):
                piece(i, count, base, off)
                return carry

            lax.fori_loop(0, count, outer, 0)
        return carry

    lax.fori_loop(0, cc // rg, group, 0)


def scan_body(
    nb, nseq, cc, rg, tab_ref, seq_ref, a_ref, kh_ref, wave_ref, back_ref, gg_ref, y_ref, mix_ref, in_s, ah_s, yh_s, y_s
):
    pieces = (nb + nseq) // 2
    load_pieces(nb, pieces, cc, tab_ref, lambda b: a_ref[0, b].astype(f32), in_s, wave_ref, ah_s)
    zero = jnp.zeros((rg, BIG), f32)

    def products(flip):
        def piece(i, count, base, off):
            def inner(j, acc):
                yc, ys = acc
                other = (base + i + j) if flip else (base + i - j)
                m = pl.ds(pl.multiple_of(other * cc + off, rg), rg)
                rows = pl.ds(off, rg)
                ac = ah_s[m, :BIG]
                as_ = ah_s[m, BIG:]
                kc = kh_ref[0, j, rows, :BIG]
                ks = kh_ref[0, j, rows, BIG:]
                if flip:
                    return (yc + kc * ac + ks * as_, ys + kc * as_ - ks * ac)
                return (yc + kc * ac - ks * as_, ys + kc * as_ + ks * ac)

            yc, ys = lax.fori_loop(0, (count - i) if flip else (i + 1), inner, (zero, zero))
            at = pl.ds(pl.multiple_of((base + i) * cc + off, rg), rg)
            yh_s[at, :BIG] = yc.astype(bf16)
            yh_s[at, BIG:] = ys.astype(bf16)

        over_pieces(nseq, cc, rg, seq_ref, piece)

    @pl.when(pl.program_id(0) == 0)
    def _():
        products(False)

    @pl.when(pl.program_id(0) == 1)
    def _():
        products(True)

    for h in range(pieces):
        at = pl.ds(h * cc, cc)
        y_s[at, :] = nn(yh_s[at, :], back_ref[...])

    def one(b, y):
        y_ref[0, b] = y.astype(bf16)
        mix_ref[0, b] = (y * gg_ref[0, b].astype(f32)).astype(bf16)

    def last(h, carry):
        b = tab_ref[0, h]
        at = pl.ds(pl.multiple_of(h * cc, cc), cc)
        one(b, y_s[at, 0:BLK])

        @pl.when(tab_ref[1, h] == 1)
        def _():
            one(b + 1, y_s[at, BLK:])

        return carry

    lax.fori_loop(0, seq_ref[1, nseq], last, 0)
    nothing = jnp.zeros((cc, BLK), bf16)

    def fill(b, carry):
        y_ref[0, b] = nothing
        mix_ref[0, b] = nothing
        return carry

    lax.fori_loop(seq_ref[0, nseq], nb, fill, 0)


def back_body(
    nb, nseq, cc, rg, tab_ref, seq_ref, a_ref, gm_ref, kh_ref, wave_ref, back_ref, gg_ref, y_ref, dg_ref, da_ref,
    gpg_ref, gp_ref, gh_ref, bs_ref, in_s, ah_s, gh_s, xh_s, x_s,
):
    pieces = (nb + nseq) // 2
    load_pieces(nb, pieces, cc, tab_ref, lambda b: a_ref[0, b].astype(f32), in_s, wave_ref, ah_s)
    load_pieces(
        nb, pieces, cc, tab_ref, lambda b: gm_ref[0, b].astype(f32) * gg_ref[0, b].astype(f32), in_s, wave_ref, gh_s
    )
    gh_ref[...] = jnp.zeros_like(gh_ref)
    zero = jnp.zeros((rg, BIG), f32)

    def products(flip):
        def piece(i, count, base, off):
            at = pl.ds(pl.multiple_of((base + i) * cc + off, rg), rg)
            ac = ah_s[at, :BIG]
            as_ = ah_s[at, BIG:]

            def inner(j, acc):
                xc, xs = acc
                other = (base + i - j) if flip else (base + i + j)
                m = pl.ds(pl.multiple_of(other * cc + off, rg), rg)
                rows = pl.ds(off, rg)
                gc = gh_s[m, :BIG]
                gs = gh_s[m, BIG:]
                kc = kh_ref[0, j, rows, :BIG]
                ks = kh_ref[0, j, rows, BIG:]
                gh_ref[0, j, rows, :BIG] += ac * gc + as_ * gs
                if flip:
                    gh_ref[0, j, rows, BIG:] += gc * as_ - gs * ac
                    return (xc + kc * gc - ks * gs, xs + kc * gs + ks * gc)
                gh_ref[0, j, rows, BIG:] += ac * gs - as_ * gc
                return (xc + kc * gc + ks * gs, xs + kc * gs - ks * gc)

            xc, xs = lax.fori_loop(0, (i + 1) if flip else (count - i), inner, (zero, zero))
            xh_s[at, :BIG] = xc.astype(bf16)
            xh_s[at, BIG:] = xs.astype(bf16)

        over_pieces(nseq, cc, rg, seq_ref, piece)

    @pl.when(pl.program_id(0) == 0)
    def _():
        products(False)

    @pl.when(pl.program_id(0) == 1)
    def _():
        products(True)

    for h in range(pieces):
        at = pl.ds(h * cc, cc)
        x_s[at, :] = nn(xh_s[at, :], back_ref[...])

    none = jnp.zeros((cc, BLK), f32)

    def one(b, gx, carry):
        s0, s1 = carry
        gpg = (y_ref[0, b].astype(f32) * gm_ref[0, b].astype(f32) * dg_ref[0, b].astype(f32)).astype(bf16)
        gpg_ref[0, b] = gpg
        gp = (gx * da_ref[0, b].astype(f32)).astype(bf16)
        gp_ref[0, b] = gp
        return (s0 + gpg.astype(f32), s1 + gp.astype(f32))

    def last(h, carry):
        b = tab_ref[0, h]
        at = pl.ds(pl.multiple_of(h * cc, cc), cc)
        carry = one(b, x_s[at, 0:BLK], carry)

        def more(kept):
            return one(b + 1, x_s[at, BLK:], kept)

        return lax.cond(tab_ref[1, h] == 1, more, lambda kept: kept, carry)

    s0, s1 = lax.fori_loop(0, seq_ref[1, nseq], last, (none, none))
    bs_ref[0, :, 0:BLK] = s0
    bs_ref[0, :, BLK:] = s1
    nothing = jnp.zeros((cc, BLK), bf16)

    def fill(b, carry):
        gpg_ref[0, b] = nothing
        gp_ref[0, b] = nothing
        return carry

    lax.fori_loop(seq_ref[0, nseq], nb, fill, 0)


def ssm_specs(shape, seq):
    _, nb, ch, _ = shape
    nseq = seq.shape[1] - 1
    pieces = (nb + nseq) // 2
    cc = chunk_of(ch, 128 if nb <= 32 else 64)
    big = pl.BlockSpec((1, nb, cc, BLK), lambda k, i: (k, 0, i, 0))
    spec = pl.BlockSpec((1, LAGS, cc, 2 * BIG), lambda k, i: (k, 0, i, 0))
    smem = pl.BlockSpec(memory_space=pltpu.SMEM)
    head = [smem, smem]
    tables = [pl.BlockSpec((BIG, 2 * BIG), lambda k, i: (0, 0)), pl.BlockSpec((2 * BIG, BIG), lambda k, i: (0, 0))]
    return nb, nseq, ch, cc, pieces * cc, big, spec, head, tables


def ssm_scan(tab, seq, a, kh, wave, back, gg):
    nb, nseq, ch, cc, size, big, spec, head, tables = ssm_specs(a.shape, seq)
    return pl.pallas_call(
        partial(scan_body, nb, nseq, cc, 32),
        grid=(2, ch // cc),
        in_specs=head + [big, spec] + tables + [big],
        out_specs=[big, big],
        out_shape=[jax.ShapeDtypeStruct(a.shape, bf16)] * 2,
        scratch_shapes=[
            pltpu.VMEM((size, BIG), bf16),
            pltpu.VMEM((size, 2 * BIG), f32),
            pltpu.VMEM((size, 2 * BIG), bf16),
            pltpu.VMEM((size, BIG), f32),
        ],
        compiler_params=params(56),
        cost_estimate=cost(2 * ch * 50e6, 2 * ch * nb * BLK * 8),
    )(tab, seq, a, kh, wave, back, gg)


def ssm_back(tab, seq, a, gm, kh, wave, back, gg, y, dg, da):
    nb, nseq, ch, cc, size, big, spec, head, tables = ssm_specs(a.shape, seq)
    return pl.pallas_call(
        partial(back_body, nb, nseq, cc, 16),
        grid=(2, ch // cc),
        in_specs=head + [big, big, spec] + tables + [big] * 4,
        out_specs=[big, big, spec, pl.BlockSpec((1, cc, 2 * BLK), lambda k, i: (k, i, 0))],
        out_shape=[jax.ShapeDtypeStruct(a.shape, bf16)] * 2
        + [
            jax.ShapeDtypeStruct((2, LAGS, ch, 2 * BIG), f32),
            jax.ShapeDtypeStruct((2, ch, 2 * BLK), f32),
        ],
        scratch_shapes=[
            pltpu.VMEM((size, BIG), bf16),
            pltpu.VMEM((size, 2 * BIG), f32),
            pltpu.VMEM((size, 2 * BIG), f32),
            pltpu.VMEM((size, 2 * BIG), bf16),
            pltpu.VMEM((size, BIG), f32),
        ],
        compiler_params=params(60),
        cost_estimate=cost(2 * ch * 80e6, 2 * ch * nb * BLK * 16),
    )(tab, seq, a, gm, kh, wave, back, gg, y, dg, da)


def stack_pair(refs):
    return jnp.concatenate(
        [jnp.concatenate([ref[k, 0], ref[k, 1]], axis=1) for ref in refs for k in range(2)], axis=0
    )


def mul_body(count, more, start_ref, w_ref, *refs):
    out = nn(w_ref[...], stack_pair(refs[:count]))
    o_ref = refs[-1]
    for h in range(2):
        part = out[:, h * BLK : (h + 1) * BLK]
        if more:
            part = part + refs[count][h].astype(f32)
        o_ref[h] = part.astype(o_ref.dtype)


def mul_rows(w, arrays, start, many, dtype=bf16, extra=None):
    width, deep = w.shape
    ch = arrays[0].shape[2]
    count = len(arrays)
    out = pl.BlockSpec((2, width, BLK), lambda i, at: (i, 0, 0))
    return pl.pallas_call(
        partial(mul_body, count, extra is not None),
        grid_spec=pltpu.PrefetchScalarGridSpec(
            num_scalar_prefetch=1,
            grid=(many // 2,),
            in_specs=[pl.BlockSpec((width, deep), lambda i, at: (0, 0))]
            + [pl.BlockSpec((2, 2, ch, BLK), lambda i, at: (0, at[0] + i, 0, 0))] * count
            + ([] if extra is None else [out]),
            out_specs=out,
        ),
        out_shape=jax.ShapeDtypeStruct((many, width, BLK), dtype),
        compiler_params=params(40),
        cost_estimate=cost(2 * many * BLK * width * deep, 2 * many * BLK * (2 * width + deep)),
    )(start // 2, w, *arrays, *([] if extra is None else [extra]))


def outer_body(ch, many, cuts, parts, at_ref, *refs):
    step = pl.program_id(0)
    xs, gs = refs[:parts], refs[parts : 2 * parts]
    gp_ref, gpg_ref, mix_ref = refs[2 * parts : 2 * parts + 3]
    outs = refs[2 * parts + 3 : 2 * parts + 3 + cuts]
    acc_s, x_s, g_s = refs[-3:]

    def fill(at):
        for b in range(many):
            x_s[:, b * BLK : (b + 1) * BLK] = xs[at][b]
            g_s[:, b * BLK : (b + 1) * BLK] = gs[at][b]

    if parts == 1:
        fill(0)
    else:
        for at in range(parts):

            @pl.when(step == at)
            def _(at=at):
                fill(at)

    def part(ref, k):
        return jnp.concatenate([ref[k, b] for b in range(many)], axis=1)

    @pl.when(step == 0)
    def _():
        acc_s[...] = jnp.zeros_like(acc_s)

    for at, (left, ref, k) in enumerate(
        [(x_s, gp_ref, 0), (x_s, gp_ref, 1), (x_s, gpg_ref, 0), (x_s, gpg_ref, 1), (g_s, mix_ref, 0), (g_s, mix_ref, 1)]
    ):
        acc_s[at] += nt(left[...], part(ref, k))

    @pl.when(step == pl.num_programs(0) - 1)
    def _():
        deep = acc_s.shape[1] // cuts
        for cut in range(cuts):
            start = pl.multiple_of(at_ref[pl.num_programs(0) + cut] * deep, 8)
            for at in range(6):
                outs[cut][at] = acc_s[at, pl.ds(start, deep), :].astype(bf16)


def outer_sums(order, cuts, xs, gs, gp, gpg, mix):
    width = xs[0].shape[1]
    _, nb, ch, _ = gp.shape
    many = 8
    parts = len(xs)
    if parts == 1:
        rows = pl.BlockSpec((many, width, BLK), lambda i, at: (i, 0, 0))
    else:
        rows = pl.BlockSpec((many, width, BLK), lambda i, at: (0, 0, 0), pipeline_mode=pl.Buffered(1))
    chan = pl.BlockSpec((2, many, ch, BLK), lambda i, at: (0, at[i], 0, 0))
    tok = nb * BLK
    return pl.pallas_call(
        partial(outer_body, ch, many, cuts, parts),
        grid_spec=pltpu.PrefetchScalarGridSpec(
            num_scalar_prefetch=1,
            grid=(nb // many,),
            in_specs=[rows] * (2 * parts) + [chan, chan, chan],
            out_specs=[pl.BlockSpec((6, width // cuts, ch), lambda i, at: (0, 0, 0))] * cuts,
            scratch_shapes=[
                pltpu.VMEM((6, width, ch), f32),
                pltpu.VMEM((width, many * BLK), bf16),
                pltpu.VMEM((width, many * BLK), bf16),
            ],
        ),
        out_shape=[jax.ShapeDtypeStruct((6, width // cuts, ch), bf16)] * cuts,
        compiler_params=params(60),
        cost_estimate=cost(12 * tok * width * ch, tok * (4 * width + 12 * ch)),
    )(order, *xs, *gs, gp, gpg, mix)


def meet_body(axes, rank_ref, x_ref, chan_ref, norm_ref, got_ref, call_ref, nall_ref, send_s, *sems):
    xs_sem, xr_sem, cs_sem, cr_sem, ns_sem, nr_sem, own_sem = sems
    q, c, h, w = (lax.axis_index(name) for name in axes)
    rows = x_ref.shape[0]
    piece = rows // 8
    flat = ((2 * q + c) * 2 + h) * 2 + w

    def peer(bits):
        return (q ^ (bits // 8), c ^ (bits // 4 % 2), h ^ (bits // 2 % 2), w ^ (bits % 2))

    barrier = pltpu.get_barrier_semaphore()
    for bits in range(1, 32):
        pl.semaphore_signal(barrier, inc=1, device_id=peer(bits), device_id_type=pl.DeviceIdType.MESH)
    pl.semaphore_wait(barrier, 31)

    def remote(src, dst, send, recv, to):
        return pltpu.make_async_remote_copy(
            src_ref=src, dst_ref=dst, send_sem=send, recv_sem=recv, device_id=to, device_id_type=pl.DeviceIdType.MESH
        )

    nall_ref[flat] = norm_ref[...]

    def norm_copy(bits):
        return remote(norm_ref, nall_ref.at[flat], ns_sem.at[bits], nr_sem.at[bits], peer(bits))

    for bits in range(1, 32):
        norm_copy(bits).start()

    pieces = [(kq, kh) for kh in (1, 0) for kq in (1, 2, 3, 0)]
    spot = lax.broadcasted_iota(jnp.int32, (piece, rows), 0)

    def row_copy(kq, kh):
        at = 2 * kq + kh
        return remote(
            send_s.at[at], got_ref.at[2 * q + c], xs_sem.at[at], xr_sem.at[2 * kq + c], (q ^ kq, h, h ^ kh, w)
        )

    def own_copy():
        return pltpu.make_async_copy(send_s.at[0], got_ref.at[2 * q + c], own_sem.at[0])

    for kq, kh in pieces:
        chunk = 2 * (q ^ kq) + (h ^ kh)
        pick = jnp.where(spot + chunk * piece == rank_ref[...], 1.0, 0.0).astype(bf16)
        send_s[2 * kq + kh] = nn(pick, x_ref[...]).astype(bf16)
        if (kq, kh) == (0, 0):

            @pl.when(c == h)
            def _():
                own_copy().start()

            @pl.when(c != h)
            def _():
                row_copy(0, 0).start()

        else:
            row_copy(kq, kh).start()

    place = 2 * c + w
    spot_c = 4 * c + 2 * h + w

    def chan_copy(kq, kh):
        at = 2 * kq + kh
        return remote(
            chan_ref, call_ref.at[spot_c], cs_sem.at[at], cr_sem.at[spot_c], (q ^ kq, q // 2, h ^ kh, q % 2)
        )

    def own_chan():
        return pltpu.make_async_copy(chan_ref, call_ref.at[spot_c], own_sem.at[1])

    for kq, kh in pieces:
        if (kq, kh) == (0, 0):

            @pl.when(place == q)
            def _():
                own_chan().start()

            @pl.when(place != q)
            def _():
                chan_copy(0, 0).start()

        else:
            chan_copy(kq, kh).start()

    for bits in range(1, 32):
        norm_copy(bits).wait()
    for at in range(8):

        @pl.when((c == h) & (at == c))
        def _():
            own_copy().wait()

        @pl.when(jnp.logical_not((c == h) & (at == c)))
        def _(at=at):
            remote(send_s.at[at], got_ref.at[at], xs_sem.at[at], xr_sem.at[at], peer(1)).wait_recv()

    for at in range(8):

        @pl.when((place == q) & (at == spot_c))
        def _():
            own_chan().wait()

        @pl.when(jnp.logical_not((place == q) & (at == spot_c)))
        def _(at=at):
            remote(chan_ref, call_ref.at[at], cs_sem.at[at], cr_sem.at[at], peer(1)).wait_recv()

    for kq, kh in pieces:
        if (kq, kh) == (0, 0):

            @pl.when(c != h)
            def _():
                row_copy(0, 0).wait_send()

            @pl.when(place != q)
            def _():
                chan_copy(0, 0).wait_send()

        else:
            row_copy(kq, kh).wait_send()
            chan_copy(kq, kh).wait_send()


def meet(axes, rank, x, chan, norm):
    rows, width = x.shape
    vmem = pl.BlockSpec(memory_space=pltpu.VMEM)
    sem = pltpu.SemaphoreType.DMA
    return pl.pallas_call(
        partial(meet_body, axes),
        in_specs=[vmem] * 4,
        out_specs=[vmem] * 3,
        out_shape=[
            jax.ShapeDtypeStruct((8, rows // 8, width), bf16),
            jax.ShapeDtypeStruct((8,) + chan.shape, f32),
            jax.ShapeDtypeStruct((32,) + norm.shape, f32),
        ],
        scratch_shapes=[pltpu.VMEM((8, rows // 8, width), bf16)]
        + [sem((8,)), sem((8,)), sem((8,)), sem((8,)), sem((32,)), sem((32,)), sem((2,))],
        compiler_params=pltpu.CompilerParams(collective_id=1, has_side_effects=True, vmem_limit_bytes=32 * MIB),
        cost_estimate=cost(2 * rows * rows * width, 100 * rows * width),
    )(rank.reshape(1, rows), x, chan, norm)


def sequence_tables(lens, nb):
    nseq = lens.shape[0]
    blocks = (lens + BLK - 1) // BLK
    start = jnp.cumsum(blocks) - blocks
    bigs = (blocks + 1) // 2
    first_big = jnp.cumsum(bigs) - bigs
    h = jnp.arange((nb + nseq) // 2, dtype=jnp.int32)
    owner = (h[:, None] >= first_big[None, :]).astype(jnp.int32).sum(axis=1) - 1
    mine = owner[:, None] == jnp.arange(nseq, dtype=jnp.int32)[None, :]

    def at_owner(values):
        return jnp.sum(jnp.where(mine, values[None, :], 0), axis=1)

    rel = h - at_owner(first_big)
    first = jnp.minimum(at_owner(start) + 2 * rel, nb - 1)
    whole = (2 * rel + 1 < at_owner(blocks)).astype(jnp.int32)
    tab = jnp.stack([first, whole]).astype(jnp.int32)
    seq = jnp.stack(
        [jnp.append(first_big, jnp.sum(blocks)), jnp.append(bigs, jnp.sum(bigs))]
    ).astype(jnp.int32)
    return tab, seq


def live_rows(lens, rows):
    slot = (lens + BLK - 1) // BLK * BLK
    begin = jnp.cumsum(slot) - slot
    pos = jnp.arange(rows, dtype=jnp.int32)
    inside = (pos[:, None] >= begin[None, :]) & (pos[:, None] < (begin + lens)[None, :])
    return jnp.sum(inside.astype(f32), axis=1)


def after(values):
    return lax.optimization_barrier(values)


def rank_of(keys):
    return jnp.sum((keys[None, :] < keys[:, None]).astype(jnp.int32), axis=1)


class Line:
    def __init__(self, n_dp, n_t):
        self.n_dp, self.n_t = n_dp, n_t
        self.axes = {"dp": n_dp, "tensor": n_t}
        self.both = ("dp", "tensor")
        self.cuts = 1

    def place_of_group(self):
        return lax.axis_index("tensor")

    def regroup(self, x):
        return x

    def deal(self, x):
        return lax.all_to_all(x, "dp", split_axis=0, concat_axis=0, tiled=True)

    def undeal(self, x):
        return self.deal(x)

    def gather_rows(self, x):
        return [(lax.all_gather(x, "tensor", axis=0, tiled=True), jnp.zeros((1,), jnp.int32))]

    def scatter_rows(self, w, arrays, many):
        whole = mul_rows(w, arrays, jnp.zeros((1,), jnp.int32), many * self.n_t)
        return [lax.psum_scatter(whole, "tensor", scatter_dimension=0, tiled=True)]

    def order(self, pieces):
        return jnp.append(jnp.arange(pieces * self.n_t, dtype=jnp.int32), 0)

    def enter(self, rank, x, chan, norm):
        (sent,) = permute_to(rank, [x])
        return (self.deal(sent),) + self.gather_channels(chan, norm)

    def gather_channels(self, chan, norm):
        perm = [(f, (f % self.n_dp) * self.n_t + f // self.n_dp) for f in range(self.n_dp * self.n_t)]
        chan = lax.ppermute(chan, self.both, perm)
        norm = lax.all_gather(norm, self.both, axis=1, tiled=True)
        return lax.all_gather(chan, "dp", axis=0, tiled=True), norm

    def gather_weights(self, pack):
        return lax.all_gather(pack, "dp", axis=0, tiled=True)

    def scatter_weights(self, gw):
        six, width, ch = gw[0].shape
        gw = gw[0].reshape(six, self.n_dp, width // self.n_dp, ch).transpose(1, 0, 2, 3)
        return lax.psum_scatter(gw, "dp", scatter_dimension=0, tiled=True)[0].astype(f32)

    def scatter_channels(self, sums):
        sums = lax.psum_scatter(sums, "dp", scatter_dimension=0, tiled=True)
        perm = [((f % self.n_dp) * self.n_t + f // self.n_dp, f) for f in range(self.n_dp * self.n_t)]
        return lax.ppermute(sums, self.both, perm)

    def scatter_norm(self, sums):
        return lax.psum_scatter(sums, self.both, scatter_dimension=1, tiled=True)


class Pairs:
    def __init__(self, n_dp, n_t):
        self.quads = n_dp // 2
        self.axes = {"q": self.quads, "c": 2, "h": 2, "w": 2}
        self.both = ("q", "c", "h", "w")
        self.cuts = self.quads
        self.other = [(0, 1), (1, 0)]
        self.crossed = [(2 * c + h, 2 * h + c) for c in range(2) for h in range(2)]

    def flip(self, x, axis, bit=1):
        return lax.ppermute(x, axis, [(i, i ^ bit) for i in range(self.axes[axis])])

    def place_of_group(self):
        return 2 * lax.axis_index("c") + lax.axis_index("w")

    def regroup(self, x):
        return lax.ppermute(x, ("c", "h"), self.crossed)

    def deal(self, x):
        return self.regroup(lax.all_to_all(x, ("q", "c"), split_axis=0, concat_axis=0, tiled=True))

    def undeal(self, x):
        return lax.all_to_all(self.regroup(x), ("q", "c"), split_axis=0, concat_axis=0, tiled=True)

    def places(self):
        c, w = lax.axis_index("c"), lax.axis_index("w")
        return [2 * c + w, 2 * (1 - c) + w, 2 * c + 1 - w, 2 * (1 - c) + 1 - w]

    def starts(self, many):
        return [(place * many).astype(jnp.int32).reshape(1) for place in self.places()]

    def gather_rows(self, x):
        beside = self.flip(x, "c")
        near = self.flip(x, "w")
        far = self.flip(near, "c")
        return list(zip([x, beside, near, far], self.starts(x.shape[0])))

    def scatter_rows(self, w, arrays, many):
        own, beside, near, far = self.starts(many)
        first = mul_rows(w, arrays, far, many)
        give = self.flip(first, "c")
        beside, first = after((beside, first))
        second = mul_rows(w, arrays, beside, many)
        second, give = after((second, give))
        third = mul_rows(w, arrays, near, many, extra=give)
        send = self.flip(third, "w")
        own, third = after((own, third))
        return [mul_rows(w, arrays, own, many, dtype=f32), self.flip(second, "c"), send]

    def order(self, pieces):
        place = jnp.stack(self.places())[:, None] * pieces + jnp.arange(pieces)[None, :]
        cut = lax.axis_index("q") ^ jnp.arange(self.quads)
        return jnp.concatenate([place.reshape(-1), cut]).astype(jnp.int32)

    def steps(self):
        bit = self.quads // 2
        while bit:
            yield "q", bit
            bit //= 2
        yield "h", 1

    def spot(self):
        return 2 * lax.axis_index("q") + lax.axis_index("h")

    def enter(self, rank, x, chan, norm):
        own, wide = chan.shape
        small = norm.shape[1]
        rows = -(-own * wide // 1024) * 8
        chan = jnp.pad(chan.reshape(-1), (0, rows * BLK - own * wide)).reshape(rows, BLK)
        norm = jnp.pad(norm, ((0, 5), (0, BLK - small)))
        got, chan, norm = meet(self.both, rank, x, chan, norm)
        chan = chan.reshape(8, -1)[:, : own * wide].reshape(8 * own, wide)
        norm = norm[:, :3, :small].transpose(1, 0, 2).reshape(3, -1)
        return got.reshape(x.shape), chan, norm

    def gather_weights(self, pack):
        h = lax.axis_index("h")
        first = self.regroup(pack)
        back = [(2 * (1 - h) + c, 2 * c + h) for c in range(2) for h in range(2)]
        second = lax.ppermute(pack, ("c", "h"), back)
        pair = jnp.concatenate([jnp.where(h == 0, first, second), jnp.where(h == 0, second, first)], axis=0)
        deep, wide = pair.shape
        q = lax.axis_index("q")
        whole = jnp.zeros((self.quads * deep, wide), pack.dtype)
        for bit in range(self.quads):
            part = self.flip(pair, "q", bit) if bit else pair
            whole = lax.dynamic_update_slice_in_dim(whole, part, (q ^ bit) * deep, 0)
        return whole

    def scatter_weights(self, gw):
        total = gw[0].astype(f32)
        for bit in range(1, self.quads):
            total = total + self.flip(gw[bit], "q", bit).astype(f32)
        total = total.astype(bf16)
        six, deep, ch = total.shape
        total = total.reshape(six, 2, deep // 2, ch)
        h = lax.axis_index("h")
        first = jnp.where(h == 0, total[:, 0], total[:, 1])
        second = jnp.where(h == 0, total[:, 1], total[:, 0])
        there = [(2 * c + h, 2 * (1 - h) + c) for c in range(2) for h in range(2)]
        return self.regroup(first).astype(f32) + lax.ppermute(second, ("c", "h"), there).astype(f32)

    def scatter_channels(self, sums):
        count = 2 * self.quads
        rows, wide = sums.shape
        part = jnp.take(sums.reshape(count, rows // count * wide), jnp.arange(count) ^ self.spot(), axis=0)
        for axis, bit in self.steps():
            half = part.shape[0] // 2
            part = part[:half] + self.flip(part[half:], axis, bit)
        perm = []
        for f in range(4 * count):
            place, at = f // count, f % count
            q, h, c, w = at // 2, at % 2, place // 2, place % 2
            perm.append((((2 * q + c) * 2 + h) * 2 + w, f))
        return lax.ppermute(part.reshape(rows // count, wide), self.both, perm)

    def scatter_norm(self, sums):
        count = 8 * self.quads
        mine = lax.axis_index(self.both)
        part = jnp.take(sums.reshape(3, count, -1), jnp.arange(count) ^ mine, axis=1)
        bits = [("q", 1 << at) for at in reversed(range(self.quads.bit_length() - 1))]
        for axis, bit in bits + [("c", 1), ("h", 1), ("w", 1)]:
            half = part.shape[1] // 2
            part = part[:, :half] + self.flip(part[:, half:], axis, bit)
        return part[:, 0]


def local(
    net, wave, tokens, cotangent, source, target, lengths, ln_gain, ln_bias, w_fwd, b_fwd, w_bwd, b_bwd,
    w_gate, b_gate, w_out, b_out, log_dt, log_rate, ssm_b, ssm_c, ssm_d,
):
    rows, width = tokens.shape
    many = rows // BLK
    n_t = net.n_t
    group = rows * n_t
    nb = group // BLK
    ch = w_fwd.shape[1]
    back = (wave.T / BIG).astype(bf16)
    wave = wave.astype(bf16)

    rank = rank_of(target)
    sender = source // group
    place = rank_of(sender * rows + jnp.arange(rows, dtype=jnp.int32))
    table = net.regroup(jnp.concatenate([place, lengths[0]]))
    place, lens = table[:rows], table[rows:]

    chan = jnp.concatenate(
        [log_rate[0], log_rate[1], ssm_b[0], ssm_b[1], ssm_c[0], ssm_c[1]]
        + [jnp.stack([log_dt[0], log_dt[1], ssm_d[0], ssm_d[1], b_fwd, b_bwd, b_gate[0], b_gate[1]], axis=1)],
        axis=1,
    )
    got_x, chan_all, norm_all = net.enter(rank, tokens, chan, jnp.stack([ln_gain, ln_bias, b_out]))

    def lanes(column):
        return jnp.broadcast_to(column[..., None], column.shape + (BLK,))

    gain = lanes(norm_all[0])
    shift = lanes(norm_all[1])
    bias_out = lanes(norm_all[2])
    small = chan_all[:, 6 * STATE :]
    bias_in = lanes(small[:, 4:8].T.reshape(-1))

    def pick(at):
        return jnp.stack([chan_all[:, at * STATE : (at + 1) * STATE], chan_all[:, (at + 1) * STATE : (at + 2) * STATE]])

    def decays(log_dt, log_rate, ssm_b):
        rate = jnp.exp(log_rate)
        ld = -jnp.exp(log_dt)[..., None] * rate
        return rate, ld, (1.0 - jnp.exp(ld)) / rate * ssm_b

    _, ld_all, drive_all = decays(small[:, 0:2].T, pick(0), pick(2))
    ld_pairs = (ld_all * log2e).reshape(2, ch // 2, 2 * STATE)
    w_pairs = (pick(4) * drive_all).reshape(2, ch // 2, 2 * STATE)
    kh = spectra(ld_pairs, w_pairs, lanes(small[:, 2:4].T), wave)

    pack = jnp.concatenate(
        [w_fwd, w_bwd, w_gate.reshape(-1, 2 * ch), w_out.transpose(2, 0, 1).reshape(-1, 2 * ch)], axis=1
    )
    pack, cotangent, got_x = after((pack, cotangent, got_x))
    w_all = net.gather_weights(pack)
    (sent_g,) = permute_to(rank, [cotangent])
    got_g = net.deal(sent_g)
    w_in, w_back = w_all[:, : 4 * ch], w_all[:, 4 * ch :]
    w_in_t, w_back_t = w_in.T, w_back.T

    live = live_rows(lens, group)
    live_own = lax.dynamic_slice_in_dim(live, net.place_of_group() * rows, rows, 0).reshape(many, 1, BLK)
    live = live.reshape(nb // 2, 1, BIG)
    tab, seq = sequence_tables(lens, nb)

    xt, xd = deal_x(place, got_x, gain, shift)
    xs = net.gather_rows(xt)
    kept = None
    for part, start in xs:
        kept = project(part, start, nb, live, w_in_t, bias_in, kept)
    a, da, gg, dg = kept
    y, mix = ssm_scan(tab, seq, a, kh, wave, back, gg)

    gt, gd, g_bias_out = deal_g(place, got_g, live_own)
    gs = net.gather_rows(gt)
    kept = None
    for part, start in gs:
        kept = gate_grad(part, start, nb, w_back_t, kept)
    (gm,) = kept

    branch = net.scatter_rows(w_back, [mix], many)
    sent_out = layer_rows(place, branch, xd, live_own, bias_out)
    layer_out = permute_from(rank, net.undeal(sent_out))

    gpg, gp, gh, bsum = ssm_back(tab, seq, a, gm, kh, wave, back, gg, y, dg, da)
    g_normed = net.scatter_rows(w_in, [gp, gpg], many)
    mix, own_part = after((mix, g_normed[0]))
    g_normed[0] = own_part
    gw = outer_sums(net.order(many // 8), net.cuts, [part for part, _ in xs], [part for part, _ in gs], gp, gpg, mix)
    gh, gw = after((gh, gw))
    gw = net.scatter_weights(gw)

    sent_in, norm_sums = input_rows(place, g_normed, xd, gd, gain)
    gh, sent_in = after((gh, sent_in))
    s0, s1, g0 = moments(ld_pairs, gh, back)
    in_grad = permute_from(rank, net.undeal(sent_in))

    s0 = s0.reshape(2, ch, STATE)
    s1 = s1.reshape(2, ch, STATE)
    gb_gate = jnp.sum(bsum[:, :, :BLK], axis=2)
    gb_in = jnp.sum(bsum[:, :, BLK:], axis=2)
    sums = jnp.concatenate(
        [s0[0], s0[1], s1[0], s1[1], jnp.concatenate([g0[:, :, 0], gb_gate, gb_in], axis=0).T], axis=1
    )
    sums = net.scatter_channels(sums)
    norm_sums = net.scatter_norm(jnp.sum(jnp.concatenate([norm_sums, g_bias_out[None]], axis=0), axis=2))
    s0 = jnp.stack([sums[:, :STATE], sums[:, STATE : 2 * STATE]])
    s1 = jnp.stack([sums[:, 2 * STATE : 3 * STATE], sums[:, 3 * STATE : 4 * STATE]])
    tail = sums[:, 4 * STATE :].T
    step = jnp.exp(log_dt)[..., None]
    rate, ld, drive = decays(log_dt, log_rate, ssm_b)
    g_c = s0 * drive
    g_drive = s0 * ssm_c
    g_b = g_drive * (1.0 - jnp.exp(ld)) / rate
    g_ld = s1 * ssm_c * drive - g_drive * ssm_b / rate * jnp.exp(ld)
    g_rate = -g_drive * drive / rate - g_ld * step
    g_dt = jnp.sum(g_ld * ld, axis=2)
    return (
        layer_out,
        in_grad,
        norm_sums[0],
        norm_sums[1],
        gw[0],
        tail[4],
        gw[1],
        tail[5],
        jnp.stack([gw[2], gw[3]], axis=1),
        tail[2:4],
        jnp.stack([gw[4].T, gw[5].T]),
        norm_sums[2],
        g_dt,
        g_rate * rate,
        g_b,
        g_c,
        tail[0:2],
    )


def solution(mesh):
    n_dp, n_t = mesh.shape["dp"], mesh.shape["tensor"]
    if n_t == 4 and n_dp == 8:
        net = Pairs(n_dp, n_t)
        dp, tensor = ("q", "c"), ("h", "w")
    else:
        net = Line(n_dp, n_t)
        dp, tensor = ("dp",), ("tensor",)
    net.n_t = n_t
    mesh = jax.sharding.Mesh(mesh.devices.reshape(tuple(net.axes.values())), tuple(net.axes))
    both = P(dp + tensor)
    rows = P(dp + tensor, None)
    pair = P(None, dp + tensor)
    state = P(None, dp + tensor, None)
    proj = P(dp, tensor)
    gate = P(dp, None, tensor)
    out = P(None, tensor, dp)
    wave = wave_table()

    def run(*args):
        return local(net, jnp.asarray(wave), *args)

    return jax.shard_map(
        run,
        mesh=mesh,
        in_specs=(
            rows, rows, both, both, P(dp, None), both, both, proj, both, proj, both, gate, pair, out, both,
            pair, state, state, state, pair,
        ),
        out_specs=(
            rows, rows, both, both, proj, both, proj, both, gate, pair, out, both, pair, state, state, state, pair,
        ),
        check_vma=False,
    )
```

```python
from functools import partial

import jax
import jax.numpy as jnp
import numpy as np
from jax import lax
from jax.experimental import pallas as pl
from jax.experimental.pallas import tpu as pltpu
from jax.sharding import PartitionSpec as P

BLK = 128
BIG = 256
MOST = 2048
LAGS = MOST // BIG
STATE = 64
epsilon = 1e-05
log2e = 1.4426950408889634
f32 = jnp.float32
bf16 = jnp.bfloat16
MIB = 2**20


def nn(a, b):
    return lax.dot_general(a, b, (((1,), (0,)), ((), ())), preferred_element_type=f32)


def nt(a, b):
    return lax.dot_general(a, b, (((1,), (1,)), ((), ())), preferred_element_type=f32)


def params(limit):
    return pltpu.CompilerParams(vmem_limit_bytes=limit * MIB)


def cost(flops, moved, trans=0):
    scale = 0.05
    return pl.CostEstimate(
        flops=int(scale * flops), bytes_accessed=int(scale * moved), transcendentals=int(scale * trans)
    )


def halves(x):
    high = x.astype(bf16)
    return high, (x - high.astype(f32)).astype(bf16)


def wave_table():
    pos = np.arange(BIG)[:, None]
    freq = np.arange(BIG)[None, :]
    angle = 2 * np.pi * ((2 * freq + 1) * pos % (4 * BIG)) / (4 * BIG)
    return np.concatenate([np.cos(angle), np.sin(angle)], 1).astype(np.float32)


def chunk_of(channels, most):
    best = 16
    for size in range(16, most + 1, 16):
        if channels % size == 0:
            best = size
    return best


def permute_row_body(count, rank_ref, *refs):
    rows = rank_ref.shape[1]
    spot = lax.broadcasted_iota(jnp.int32, (rows, rows), 0)
    pick = jnp.where(spot == rank_ref[...], 1.0, 0.0).astype(bf16)
    for at in range(count):
        refs[count + at][...] = nn(pick, refs[at][...]).astype(bf16)


def permute_to(rank, arrays):
    rows, width = arrays[0].shape
    count = len(arrays)
    return pl.pallas_call(
        partial(permute_row_body, count),
        out_shape=[jax.ShapeDtypeStruct((rows, width), bf16)] * count,
        compiler_params=params(48),
        cost_estimate=cost(2 * count * rows * rows * width, 4 * count * rows * width),
    )(rank.reshape(1, rows), *arrays)


def permute_col_body(rank_ref, x_ref, o_ref):
    rows = x_ref.shape[0]
    spot = lax.broadcasted_iota(jnp.int32, (rows, rows), 1)
    pick = jnp.where(spot == rank_ref[...], 1.0, 0.0).astype(bf16)
    o_ref[...] = nn(pick, x_ref[...]).astype(bf16)


def permute_from(rank, x):
    rows, width = x.shape
    return pl.pallas_call(
        permute_col_body,
        out_shape=jax.ShapeDtypeStruct((rows, width), bf16),
        compiler_params=params(48),
        cost_estimate=cost(2 * rows * rows * width, 4 * rows * width),
    )(rank.reshape(rows, 1), x)


def pick_rows(place_ref, x_ref):
    spot = lax.broadcasted_iota(jnp.int32, (BLK, x_ref.shape[0]), 1)
    pick = jnp.where(spot == place_ref[...], 1.0, 0.0).astype(bf16)
    return nn(pick, x_ref[...]).T


def deal_x_body(place_ref, x_ref, gain_ref, shift_ref, xt_ref, xd_ref):
    x = pick_rows(place_ref, x_ref)
    xd_ref[0] = x.astype(bf16)
    centred = x - jnp.mean(x, axis=0, keepdims=True)
    inv_std = lax.rsqrt(jnp.mean(centred * centred, axis=0, keepdims=True) + epsilon)
    xt_ref[0] = (centred * inv_std * gain_ref[...] + shift_ref[...]).astype(bf16)


def deal_g_body(place_ref, g_ref, live_ref, gt_ref, gd_ref, bo_ref):
    g = pick_rows(place_ref, g_ref)
    gd_ref[0] = g.astype(bf16)
    g = g * live_ref[0]
    gt_ref[0] = g.astype(bf16)

    @pl.when(pl.program_id(0) == 0)
    def _():
        bo_ref[...] = jnp.zeros_like(bo_ref)

    bo_ref[...] += g


def deal_specs(rows, width):
    place = pl.BlockSpec((BLK, 1), lambda i: (i, 0))
    whole = pl.BlockSpec((rows, width), lambda i: (0, 0))
    wide = pl.BlockSpec((width, BLK), lambda i: (0, 0))
    out = pl.BlockSpec((1, width, BLK), lambda i: (i, 0, 0))
    return place, whole, wide, out


def deal_x(place, x, gain, shift):
    rows, width = x.shape
    blocks = rows // BLK
    spot, whole, wide, out = deal_specs(rows, width)
    return pl.pallas_call(
        deal_x_body,
        grid=(blocks,),
        in_specs=[spot, whole, wide, wide],
        out_specs=[out, out],
        out_shape=[jax.ShapeDtypeStruct((blocks, width, BLK), bf16)] * 2,
        compiler_params=params(40),
        cost_estimate=cost(2 * rows * rows * width, 6 * rows * width),
    )(place.reshape(rows, 1), x, gain, shift)


def deal_g(place, g, live):
    rows, width = g.shape
    blocks = rows // BLK
    spot, whole, wide, out = deal_specs(rows, width)
    return pl.pallas_call(
        deal_g_body,
        grid=(blocks,),
        in_specs=[spot, whole, pl.BlockSpec((1, 1, BLK), lambda i: (i, 0, 0))],
        out_specs=[out, out, wide],
        out_shape=[jax.ShapeDtypeStruct((blocks, width, BLK), bf16)] * 2
        + [jax.ShapeDtypeStruct((width, BLK), f32)],
        compiler_params=params(40),
        cost_estimate=cost(2 * rows * rows * width, 6 * rows * width),
    )(place.reshape(rows, 1), g, live)


def send_back(place_ref, out_s, o_ref):
    rows = out_s.shape[0]
    spot = lax.broadcasted_iota(jnp.int32, (rows, rows), 0)
    pick = jnp.where(spot == place_ref[...], 1.0, 0.0).astype(bf16)
    o_ref[...] = nn(pick, out_s[...]).astype(bf16)


def total(refs, at):
    value = refs[0][at].astype(f32)
    for ref in refs[1:]:
        value = value + ref[at].astype(f32)
    return value


def layer_body(place_ref, xd_ref, live_ref, bias_ref, *refs):
    o_ref, out_s = refs[-2:]
    for at in range(xd_ref.shape[0]):
        y = xd_ref[at].astype(f32) + live_ref[at] * (total(refs[:-2], at) + bias_ref[...])
        out_s[at * BLK : (at + 1) * BLK, :] = y.T.astype(bf16)
    send_back(place_ref, out_s, o_ref)


def layer_rows(place, parts, xd, live, bias):
    blocks, width, _ = xd.shape
    rows = blocks * BLK
    return pl.pallas_call(
        layer_body,
        out_shape=jax.ShapeDtypeStruct((rows, width), bf16),
        scratch_shapes=[pltpu.VMEM((rows, width), bf16)],
        compiler_params=params(48),
        cost_estimate=cost(2 * rows * rows * width, 6 * rows * width),
    )(place.reshape(1, rows), xd, live, bias, *parts)


def input_body(place_ref, xd_ref, gd_ref, gain_ref, *refs):
    o_ref, sums_ref, out_s = refs[-3:]
    g_gain = jnp.zeros(gain_ref.shape, f32)
    g_shift = jnp.zeros(gain_ref.shape, f32)
    for at in range(xd_ref.shape[0]):
        x = xd_ref[at].astype(f32)
        centred = x - jnp.mean(x, axis=0, keepdims=True)
        inv_std = lax.rsqrt(jnp.mean(centred * centred, axis=0, keepdims=True) + epsilon)
        x_hat = centred * inv_std
        g = total(refs[:-3], at)
        g_gain = g_gain + g * x_hat
        g_shift = g_shift + g
        hat = g * gain_ref[...]
        back = inv_std * (
            hat
            - jnp.mean(hat, axis=0, keepdims=True)
            - x_hat * jnp.mean(hat * x_hat, axis=0, keepdims=True)
        )
        out_s[at * BLK : (at + 1) * BLK, :] = (gd_ref[at].astype(f32) + back).T.astype(bf16)
    sums_ref[0] = g_gain
    sums_ref[1] = g_shift
    send_back(place_ref, out_s, o_ref)


def input_rows(place, parts, xd, gd, gain):
    blocks, width, _ = xd.shape
    rows = blocks * BLK
    return pl.pallas_call(
        input_body,
        out_shape=[
            jax.ShapeDtypeStruct((rows, width), bf16),
            jax.ShapeDtypeStruct((2, width, BLK), f32),
        ],
        scratch_shapes=[pltpu.VMEM((rows, width), bf16)],
        compiler_params=params(48),
        cost_estimate=cost(2 * rows * rows * width, 8 * rows * width),
    )(place.reshape(1, rows), xd, gd, gain, *parts)


def project_body(ch, many, start_ref, x_ref, live_ref, wt_ref, bias_ref, *refs):
    a_ref, da_ref, gg_ref, dg_ref, pre_s = refs[-5:]
    x = jnp.concatenate([x_ref[0], x_ref[1]], axis=1)
    pre_s[...] = nn(wt_ref[...], x)
    live = live_ref[0]
    step = 32
    root = 0.7978845608028654

    def act(pre):
        square = pre * pre
        bent = jnp.tanh(root * pre * (1.0 + 0.044715 * square))
        rise = 0.5 + 0.5 * bent
        slope = rise + (0.5 * root) * pre * (1.0 - bent * bent) * (1.0 + 0.134145 * square)
        return pre * rise, slope

    def put(ref, k, at, value):
        value = value.astype(bf16)
        ref[k, 0, at, :] = value[:, :BLK]
        ref[k, 1, at, :] = value[:, BLK:]

    def chunk(i, carry):
        at = pl.ds(pl.multiple_of(i * step, step), step)
        for k in range(2):
            row = pl.ds(pl.multiple_of(k * ch + i * step, step), step)
            gate = pl.ds(pl.multiple_of((2 + k) * ch + i * step, step), step)
            bias = bias_ref[row, :]
            value, slope = act(pre_s[row, :] + jnp.concatenate([bias, bias], axis=1))
            put(a_ref, k, at, live * value)
            put(da_ref, k, at, live * slope)
            bias = bias_ref[gate, :]
            value, slope = act(pre_s[gate, :] + jnp.concatenate([bias, bias], axis=1))
            put(gg_ref, k, at, value)
            put(dg_ref, k, at, slope)
        return carry

    lax.fori_loop(0, ch // step, chunk, 0)


def chained(body, grid, in_specs, out_specs, shapes, scratch, limit, estimate, start, operands, kept):
    kept = [] if kept is None else list(kept)
    specs = list(in_specs) + [pl.BlockSpec(memory_space=pl.ANY)] * len(kept)
    first = 1 + len(operands)
    return pl.pallas_call(
        body,
        grid_spec=pltpu.PrefetchScalarGridSpec(
            num_scalar_prefetch=1, grid=grid, in_specs=specs, out_specs=out_specs, scratch_shapes=scratch
        ),
        out_shape=shapes,
        input_output_aliases={first + at: at for at in range(len(kept))},
        compiler_params=params(limit),
        cost_estimate=estimate,
    )(start, *operands, *kept)


def project(xt, start, nb, live, wt, bias, kept):
    many, width, _ = xt.shape
    ch = wt.shape[0] // 4
    out = pl.BlockSpec((2, 2, ch, BLK), lambda i, at: (0, at[0] + i, 0, 0))
    tok = many * BLK
    return chained(
        partial(project_body, ch, many),
        (many // 2,),
        [
            pl.BlockSpec((2, width, BLK), lambda i, at: (i, 0, 0)),
            pl.BlockSpec((1, 1, BIG), lambda i, at: (at[0] + i, 0, 0)),
            pl.BlockSpec((4 * ch, width), lambda i, at: (0, 0)),
            pl.BlockSpec((4 * ch, BLK), lambda i, at: (0, 0)),
        ],
        [out] * 4,
        [jax.ShapeDtypeStruct((2, nb, ch, BLK), bf16)] * 4,
        [pltpu.VMEM((4 * ch, BIG), f32)],
        48,
        cost(8 * tok * width * ch, 2 * tok * width + 16 * tok * ch, 4 * tok * ch),
        start // 2,
        [xt, live, wt, bias],
        kept,
    )


def gate_grad_body(ch, start_ref, g_ref, wt_ref, *refs):
    o_ref = refs[-1]
    gm = nn(wt_ref[...], jnp.concatenate([g_ref[0], g_ref[1]], axis=1)).astype(bf16)
    for k in range(2):
        for h in range(2):
            o_ref[k, h] = gm[k * ch : (k + 1) * ch, h * BLK : (h + 1) * BLK]


def gate_grad(gt, start, nb, wt, kept):
    many, width, _ = gt.shape
    ch = wt.shape[0] // 2
    tok = many * BLK
    return chained(
        partial(gate_grad_body, ch),
        (many // 2,),
        [
            pl.BlockSpec((2, width, BLK), lambda i, at: (i, 0, 0)),
            pl.BlockSpec((2 * ch, width), lambda i, at: (0, 0)),
        ],
        [pl.BlockSpec((2, 2, ch, BLK), lambda i, at: (0, at[0] + i, 0, 0))],
        [jax.ShapeDtypeStruct((2, nb, ch, BLK), bf16)],
        [],
        40,
        cost(4 * tok * width * ch, 2 * tok * width + 4 * tok * ch),
        start // 2,
        [gt, wt],
        kept,
    )


def spectra_body(cc, ld_ref, w_ref, d_ref, wave_ref, kh_ref, k_s):
    t = lax.broadcasted_iota(jnp.int32, (BLK, BLK), 0).astype(f32)
    block = lax.broadcasted_iota(jnp.int32, (2 * LAGS, BLK), 0).astype(f32) * float(BLK)
    low = lax.broadcasted_iota(jnp.int32, (2 * LAGS, BLK), 1) < STATE
    count = 2 * LAGS

    def one(p, carry):
        ld = ld_ref[0, pl.ds(p, 1), :]
        decay = jnp.exp2(t * ld)
        scale = w_ref[0, pl.ds(p, 1), :] * jnp.exp2(block * ld)
        lhs = jnp.concatenate([jnp.where(low, scale, 0.0), jnp.where(low, 0.0, scale)], axis=0)
        lhs_high, lhs_low = halves(lhs)
        high, rest = halves(decay)
        k = nt(jnp.concatenate([lhs_high, lhs_low], axis=0), high)
        k = k[0 : 2 * count] + k[2 * count : 4 * count] + nt(lhs_high, rest)
        k_s[pl.ds(2 * p, count, stride=cc), :] = k[0:count]
        k_s[pl.ds(2 * p + 1, count, stride=cc), :] = k[count : 2 * count]
        return carry

    lax.fori_loop(0, cc // 2, one, 0, unroll=4)
    sign = jnp.where(lax.broadcasted_iota(jnp.int32, (cc, BIG), 1) % 2 == 0, 1.0, -1.0)
    before = None
    for big in range(LAGS):
        rows = jnp.concatenate(
            [k_s[pl.ds(2 * big * cc, cc), :], k_s[pl.ds((2 * big + 1) * cc, cc), :]], axis=1
        )
        high, rest = halves(rows)
        x = nn(high, wave_ref[...]) + nn(rest, wave_ref[...])
        xc, xs = x[:, :BIG], x[:, BIG:]
        if big == 0:
            kh_ref[0, 0, :, :BIG] = xc + d_ref[0][:, 0:1]
            kh_ref[0, 0, :, BIG:] = xs
        else:
            kh_ref[0, big, :, :BIG] = xc + sign * before[1]
            kh_ref[0, big, :, BIG:] = xs - sign * before[0]
        before = (xc, xs)


def spectra(ld, w, d, wave):
    ch = 2 * ld.shape[1]
    cc = chunk_of(ch, 128)
    return pl.pallas_call(
        partial(spectra_body, cc),
        grid=(2, ch // cc),
        in_specs=[pl.BlockSpec((1, cc // 2, BLK), lambda k, i: (k, i, 0))] * 2
        + [
            pl.BlockSpec((1, cc, BLK), lambda k, i: (k, i, 0)),
            pl.BlockSpec((BIG, 2 * BIG), lambda k, i: (0, 0)),
        ],
        out_specs=pl.BlockSpec((1, LAGS, cc, 2 * BIG), lambda k, i: (k, 0, i, 0)),
        out_shape=jax.ShapeDtypeStruct((2, LAGS, ch, 2 * BIG), f32),
        scratch_shapes=[pltpu.VMEM((2 * LAGS * cc, BLK), f32)],
        compiler_params=params(40),
        cost_estimate=cost(2 * ch * 40e6, 2 * ch * LAGS * 2 * BIG * 4),
    )(ld, w, d, wave)


def moments_body(cc, ld_ref, gh_ref, back_ref, s0_ref, s1_ref, g0_ref, g_s):
    sign = jnp.where(lax.broadcasted_iota(jnp.int32, (cc, BIG), 1) % 2 == 0, 1.0, -1.0)
    count = 2 * LAGS
    for big in range(LAGS):
        c = gh_ref[0, big, :, :BIG]
        s = gh_ref[0, big, :, BIG:]
        if big < LAGS - 1:
            c, s = c - sign * gh_ref[0, big + 1, :, BIG:], s + sign * gh_ref[0, big + 1, :, :BIG]
        high, rest = halves(jnp.concatenate([c, s], axis=1))
        g = nn(high, back_ref[...]) + nn(rest, back_ref[...])
        g_s[pl.ds(2 * big * cc, cc), :] = g[:, :BLK]
        g_s[pl.ds((2 * big + 1) * cc, cc), :] = g[:, BLK:]
        if big == 0:
            g0_ref[0] = g[:, :BLK]
    t = lax.broadcasted_iota(jnp.int32, (BLK, BLK), 0).astype(f32)
    lane = lax.broadcasted_iota(jnp.int32, (count, BLK), 1)
    lag = lane.astype(f32)
    block = lax.broadcasted_iota(jnp.int32, (count, BLK), 0).astype(f32) * float(BLK)
    low = lane < STATE

    def one(p, carry):
        ld = ld_ref[0, pl.ds(p, 1), :]
        decay = jnp.exp2(t * ld).astype(bf16)
        far = jnp.exp2(block * ld)
        ga = g_s[pl.ds(2 * p, count, stride=cc), :]
        gb = g_s[pl.ds(2 * p + 1, count, stride=cc), :]
        high, rest = halves(jnp.concatenate([ga, gb, ga * lag, gb * lag], axis=0))
        m = nn(jnp.concatenate([high, rest], axis=0), decay)
        m = m[0 : 4 * count] + m[4 * count : 8 * count]
        m0 = jnp.where(low, m[0:count], m[count : 2 * count])
        m1 = jnp.where(low, m[2 * count : 3 * count], m[3 * count : 4 * count]) + block * m0
        s0_ref[0, pl.ds(p, 1), :] = jnp.sum(far * m0, axis=0, keepdims=True)
        s1_ref[0, pl.ds(p, 1), :] = jnp.sum(far * m1, axis=0, keepdims=True)
        return carry

    lax.fori_loop(0, cc // 2, one, 0, unroll=4)


def moments(k, ld, gh, back):
    ch = gh.shape[2]
    cc = chunk_of(ch, 128)
    row = pl.BlockSpec((1, cc // 2, BLK), lambda i: (0, i, 0))
    return pl.pallas_call(
        partial(moments_body, cc),
        grid=(ch // cc,),
        in_specs=[
            pl.BlockSpec((1, cc // 2, BLK), lambda i: (k, i, 0)),
            pl.BlockSpec((1, LAGS, cc, 2 * BIG), lambda i: (0, 0, i, 0)),
            pl.BlockSpec((2 * BIG, BIG), lambda i: (0, 0)),
        ],
        out_specs=[row, row, pl.BlockSpec((1, cc, BLK), lambda i: (0, i, 0))],
        out_shape=[jax.ShapeDtypeStruct((1, ch // 2, BLK), f32)] * 2
        + [jax.ShapeDtypeStruct((1, ch, BLK), f32)],
        scratch_shapes=[pltpu.VMEM((2 * LAGS * cc, BLK), f32)],
        compiler_params=params(40),
        cost_estimate=cost(ch * 40e6, ch * LAGS * 2 * BIG * 4),
    )(ld, gh, back)


def load_pieces(nb, pieces, cc, tab_ref, block, in_s, wave_ref, dst):
    for h in range(pieces):
        first = tab_ref[0, h]
        whole = tab_ref[1, h].astype(f32)
        in_s[pl.ds(h * cc, cc), 0:BLK] = block(first).astype(bf16)
        in_s[pl.ds(h * cc, cc), BLK:BIG] = (block(jnp.minimum(first + 1, nb - 1)) * whole).astype(bf16)
    for h in range(pieces):
        at = pl.ds(h * cc, cc)
        dst[at, :] = nn(in_s[at, :], wave_ref[...])


def over_pieces(nseq, cc, rg, seq_ref, piece):
    def group(r, carry):
        off = pl.multiple_of(r * rg, rg)
        for s in range(nseq):
            base = seq_ref[0, s]
            count = seq_ref[1, s]

            def outer(i, carry):
                piece(i, count, base, off)
                return carry

            lax.fori_loop(0, count, outer, 0)
        return carry

    lax.fori_loop(0, cc // rg, group, 0)


def scan_body(
    nb, nseq, cc, rg, tab_ref, seq_ref, a_ref, kh_ref, wave_ref, back_ref, gg_ref, y_ref, mix_ref, in_s, ah_s, yh_s, y_s
):
    pieces = (nb + nseq) // 2
    load_pieces(nb, pieces, cc, tab_ref, lambda b: a_ref[0, b].astype(f32), in_s, wave_ref, ah_s)
    zero = jnp.zeros((rg, BIG), f32)

    def products(flip):
        def piece(i, count, base, off):
            def inner(j, acc):
                yc, ys = acc
                other = (base + i + j) if flip else (base + i - j)
                m = pl.ds(pl.multiple_of(other * cc + off, rg), rg)
                rows = pl.ds(off, rg)
                ac = ah_s[m, :BIG]
                as_ = ah_s[m, BIG:]
                kc = kh_ref[0, j, rows, :BIG]
                ks = kh_ref[0, j, rows, BIG:]
                if flip:
                    return (yc + kc * ac + ks * as_, ys + kc * as_ - ks * ac)
                return (yc + kc * ac - ks * as_, ys + kc * as_ + ks * ac)

            yc, ys = lax.fori_loop(0, (count - i) if flip else (i + 1), inner, (zero, zero))
            at = pl.ds(pl.multiple_of((base + i) * cc + off, rg), rg)
            yh_s[at, :BIG] = yc.astype(bf16)
            yh_s[at, BIG:] = ys.astype(bf16)

        over_pieces(nseq, cc, rg, seq_ref, piece)

    @pl.when(pl.program_id(0) == 0)
    def _():
        products(False)

    @pl.when(pl.program_id(0) == 1)
    def _():
        products(True)

    for h in range(pieces):
        at = pl.ds(h * cc, cc)
        y_s[at, :] = nn(yh_s[at, :], back_ref[...])

    def one(b, y):
        y_ref[0, b] = y.astype(bf16)
        mix_ref[0, b] = (y * gg_ref[0, b].astype(f32)).astype(bf16)

    def last(h, carry):
        b = tab_ref[0, h]
        at = pl.ds(pl.multiple_of(h * cc, cc), cc)
        one(b, y_s[at, 0:BLK])

        @pl.when(tab_ref[1, h] == 1)
        def _():
            one(b + 1, y_s[at, BLK:])

        return carry

    lax.fori_loop(0, seq_ref[1, nseq], last, 0)
    nothing = jnp.zeros((cc, BLK), bf16)

    def fill(b, carry):
        y_ref[0, b] = nothing
        mix_ref[0, b] = nothing
        return carry

    lax.fori_loop(seq_ref[0, nseq], nb, fill, 0)


def back_body(
    nb, nseq, cc, rg, flip, tab_ref, seq_ref, a_ref, gm_ref, kh_ref, wave_ref, back_ref, gg_ref, y_ref, dg_ref, da_ref,
    gpg_ref, gp_ref, gh_ref, bs_ref, in_s, ah_s, gh_s, xh_s, x_s,
):
    pieces = (nb + nseq) // 2
    load_pieces(nb, pieces, cc, tab_ref, lambda b: a_ref[0, b].astype(f32), in_s, wave_ref, ah_s)
    load_pieces(
        nb, pieces, cc, tab_ref, lambda b: gm_ref[0, b].astype(f32) * gg_ref[0, b].astype(f32), in_s, wave_ref, gh_s
    )
    gh_ref[...] = jnp.zeros_like(gh_ref)
    zero = jnp.zeros((rg, BIG), f32)

    def piece(i, count, base, off):
        at = pl.ds(pl.multiple_of((base + i) * cc + off, rg), rg)
        ac = ah_s[at, :BIG]
        as_ = ah_s[at, BIG:]

        def inner(j, acc):
            xc, xs = acc
            other = (base + i - j) if flip else (base + i + j)
            m = pl.ds(pl.multiple_of(other * cc + off, rg), rg)
            rows = pl.ds(off, rg)
            gc = gh_s[m, :BIG]
            gs = gh_s[m, BIG:]
            kc = kh_ref[0, j, rows, :BIG]
            ks = kh_ref[0, j, rows, BIG:]
            gh_ref[0, j, rows, :BIG] += ac * gc + as_ * gs
            if flip:
                gh_ref[0, j, rows, BIG:] += gc * as_ - gs * ac
                return (xc + kc * gc - ks * gs, xs + kc * gs + ks * gc)
            gh_ref[0, j, rows, BIG:] += ac * gs - as_ * gc
            return (xc + kc * gc + ks * gs, xs + kc * gs - ks * gc)

        xc, xs = lax.fori_loop(0, (i + 1) if flip else (count - i), inner, (zero, zero))
        xh_s[at, :BIG] = xc.astype(bf16)
        xh_s[at, BIG:] = xs.astype(bf16)

    over_pieces(nseq, cc, rg, seq_ref, piece)

    for h in range(pieces):
        at = pl.ds(h * cc, cc)
        x_s[at, :] = nn(xh_s[at, :], back_ref[...])

    none = jnp.zeros((cc, BLK), f32)

    def one(b, gx, carry):
        s0, s1 = carry
        gpg = (y_ref[0, b].astype(f32) * gm_ref[0, b].astype(f32) * dg_ref[0, b].astype(f32)).astype(bf16)
        gpg_ref[0, b] = gpg
        gp = (gx * da_ref[0, b].astype(f32)).astype(bf16)
        gp_ref[0, b] = gp
        return (s0 + gpg.astype(f32), s1 + gp.astype(f32))

    def last(h, carry):
        b = tab_ref[0, h]
        at = pl.ds(pl.multiple_of(h * cc, cc), cc)
        carry = one(b, x_s[at, 0:BLK], carry)

        def more(kept):
            return one(b + 1, x_s[at, BLK:], kept)

        return lax.cond(tab_ref[1, h] == 1, more, lambda kept: kept, carry)

    s0, s1 = lax.fori_loop(0, seq_ref[1, nseq], last, (none, none))
    bs_ref[0, :, 0:BLK] = s0
    bs_ref[0, :, BLK:] = s1
    nothing = jnp.zeros((cc, BLK), bf16)

    def fill(b, carry):
        gpg_ref[0, b] = nothing
        gp_ref[0, b] = nothing
        return carry

    lax.fori_loop(seq_ref[0, nseq], nb, fill, 0)


def ssm_specs(shape, seq):
    _, nb, ch, _ = shape
    nseq = seq.shape[1] - 1
    pieces = (nb + nseq) // 2
    cc = chunk_of(ch, 128 if nb <= 32 else 64)
    big = pl.BlockSpec((1, nb, cc, BLK), lambda k, i: (k, 0, i, 0))
    spec = pl.BlockSpec((1, LAGS, cc, 2 * BIG), lambda k, i: (k, 0, i, 0))
    smem = pl.BlockSpec(memory_space=pltpu.SMEM)
    head = [smem, smem]
    tables = [pl.BlockSpec((BIG, 2 * BIG), lambda k, i: (0, 0)), pl.BlockSpec((2 * BIG, BIG), lambda k, i: (0, 0))]
    return nb, nseq, ch, cc, pieces * cc, big, spec, head, tables


def ssm_scan(tab, seq, a, kh, wave, back, gg):
    nb, nseq, ch, cc, size, big, spec, head, tables = ssm_specs(a.shape, seq)
    return pl.pallas_call(
        partial(scan_body, nb, nseq, cc, 32),
        grid=(2, ch // cc),
        in_specs=head + [big, spec] + tables + [big],
        out_specs=[big, big],
        out_shape=[jax.ShapeDtypeStruct(a.shape, bf16)] * 2,
        scratch_shapes=[
            pltpu.VMEM((size, BIG), bf16),
            pltpu.VMEM((size, 2 * BIG), f32),
            pltpu.VMEM((size, 2 * BIG), bf16),
            pltpu.VMEM((size, BIG), f32),
        ],
        compiler_params=params(56),
        cost_estimate=cost(2 * ch * 50e6, 2 * ch * nb * BLK * 8),
    )(tab, seq, a, kh, wave, back, gg)


def ssm_back(k, tab, seq, a, gm, kh, wave, back, gg, y, dg, da):
    nb, nseq, ch, cc, size, _, _, head, tables = ssm_specs(a.shape, seq)
    big = pl.BlockSpec((1, nb, cc, BLK), lambda i: (k, 0, i, 0))
    spec = pl.BlockSpec((1, LAGS, cc, 2 * BIG), lambda i: (k, 0, i, 0))
    out = pl.BlockSpec((1, nb, cc, BLK), lambda i: (0, 0, i, 0))
    out_spec = pl.BlockSpec((1, LAGS, cc, 2 * BIG), lambda i: (0, 0, i, 0))
    tables = [
        pl.BlockSpec((BIG, 2 * BIG), lambda i: (0, 0)),
        pl.BlockSpec((2 * BIG, BIG), lambda i: (0, 0)),
    ]
    return pl.pallas_call(
        partial(back_body, nb, nseq, cc, 16, k == 1),
        grid=(ch // cc,),
        in_specs=head + [big, big, spec] + tables + [big] * 4,
        out_specs=[out, out, out_spec, pl.BlockSpec((1, cc, 2 * BLK), lambda i: (0, i, 0))],
        out_shape=[jax.ShapeDtypeStruct((1,) + a.shape[1:], bf16)] * 2
        + [
            jax.ShapeDtypeStruct((1, LAGS, ch, 2 * BIG), f32),
            jax.ShapeDtypeStruct((1, ch, 2 * BLK), f32),
        ],
        scratch_shapes=[
            pltpu.VMEM((size, BIG), bf16),
            pltpu.VMEM((size, 2 * BIG), f32),
            pltpu.VMEM((size, 2 * BIG), f32),
            pltpu.VMEM((size, 2 * BIG), bf16),
            pltpu.VMEM((size, BIG), f32),
        ],
        compiler_params=params(60),
        cost_estimate=cost(ch * 80e6, ch * nb * BLK * 16),
    )(tab, seq, a, gm, kh, wave, back, gg, y, dg, da)


def stack_pair(refs):
    return jnp.concatenate(
        [jnp.concatenate([ref[k, 0], ref[k, 1]], axis=1) for ref in refs for k in range(ref.shape[0])], axis=0
    )


def mul_body(count, more, start_ref, w_ref, *refs):
    out = nn(w_ref[...], stack_pair(refs[:count]))
    o_ref = refs[-1]
    for h in range(2):
        part = out[:, h * BLK : (h + 1) * BLK]
        if more:
            part = part + refs[count][h].astype(f32)
        o_ref[h] = part.astype(o_ref.dtype)


def mul_rows(w, arrays, start, many, dtype=bf16, extra=None):
    width, deep = w.shape
    ch = arrays[0].shape[2]
    count = len(arrays)
    out = pl.BlockSpec((2, width, BLK), lambda i, at: (i, 0, 0))
    return pl.pallas_call(
        partial(mul_body, count, extra is not None),
        grid_spec=pltpu.PrefetchScalarGridSpec(
            num_scalar_prefetch=1,
            grid=(many // 2,),
            in_specs=[pl.BlockSpec((width, deep), lambda i, at: (0, 0))]
            + [pl.BlockSpec((x.shape[0], 2, ch, BLK), lambda i, at: (0, at[0] + i, 0, 0)) for x in arrays]
            + ([] if extra is None else [out]),
            out_specs=out,
        ),
        out_shape=jax.ShapeDtypeStruct((many, width, BLK), dtype),
        compiler_params=params(40),
        cost_estimate=cost(2 * many * BLK * width * deep, 2 * many * BLK * (2 * width + deep)),
    )(start // 2, w, *arrays, *([] if extra is None else [extra]))


def outer_body(ch, many, cuts, parts, at_ref, *refs):
    step = pl.program_id(0)
    xs, gs = refs[:parts], refs[parts : 2 * parts]
    gp_refs, gpg_refs, mix_ref = refs[2 * parts : 2 * parts + 2], refs[2 * parts + 2 : 2 * parts + 4], refs[2 * parts + 4]
    outs = refs[2 * parts + 5 : 2 * parts + 5 + cuts]
    acc_s, x_s, g_s = refs[-3:]

    def fill(at):
        for b in range(many):
            x_s[:, b * BLK : (b + 1) * BLK] = xs[at][b]
            g_s[:, b * BLK : (b + 1) * BLK] = gs[at][b]

    if parts == 1:
        fill(0)
    else:
        for at in range(parts):

            @pl.when(step == at)
            def _(at=at):
                fill(at)

    def part(ref, k):
        return jnp.concatenate([ref[k, b] for b in range(many)], axis=1)

    @pl.when(step == 0)
    def _():
        acc_s[...] = jnp.zeros_like(acc_s)

    for at, (left, ref, k) in enumerate(
        [(x_s, gp_refs[0], 0), (x_s, gp_refs[1], 0), (x_s, gpg_refs[0], 0), (x_s, gpg_refs[1], 0)]
        + [(g_s, mix_ref, 0), (g_s, mix_ref, 1)]
    ):
        acc_s[at] += nt(left[...], part(ref, k))

    @pl.when(step == pl.num_programs(0) - 1)
    def _():
        deep = acc_s.shape[1] // cuts
        for cut in range(cuts):
            start = pl.multiple_of(at_ref[pl.num_programs(0) + cut] * deep, 8)
            for at in range(6):
                outs[cut][at] = acc_s[at, pl.ds(start, deep), :].astype(bf16)


def outer_sums(order, cuts, xs, gs, gp, gpg, mix):
    width = xs[0].shape[1]
    _, nb, ch, _ = mix.shape
    many = 8
    parts = len(xs)
    if parts == 1:
        rows = pl.BlockSpec((many, width, BLK), lambda i, at: (i, 0, 0))
    else:
        rows = pl.BlockSpec((many, width, BLK), lambda i, at: (0, 0, 0), pipeline_mode=pl.Buffered(1))
    chan = pl.BlockSpec((2, many, ch, BLK), lambda i, at: (0, at[i], 0, 0))
    one = pl.BlockSpec((1, many, ch, BLK), lambda i, at: (0, at[i], 0, 0))
    tok = nb * BLK
    return pl.pallas_call(
        partial(outer_body, ch, many, cuts, parts),
        grid_spec=pltpu.PrefetchScalarGridSpec(
            num_scalar_prefetch=1,
            grid=(nb // many,),
            in_specs=[rows] * (2 * parts) + [one] * 4 + [chan],
            out_specs=[pl.BlockSpec((6, width // cuts, ch), lambda i, at: (0, 0, 0))] * cuts,
            scratch_shapes=[
                pltpu.VMEM((6, width, ch), f32),
                pltpu.VMEM((width, many * BLK), bf16),
                pltpu.VMEM((width, many * BLK), bf16),
            ],
        ),
        out_shape=[jax.ShapeDtypeStruct((6, width // cuts, ch), bf16)] * cuts,
        compiler_params=params(60),
        cost_estimate=cost(12 * tok * width * ch, tok * (4 * width + 12 * ch)),
    )(order, *xs, *gs, *gp, *gpg, mix)


def meet_body(axes, rank_ref, x_ref, chan_ref, norm_ref, got_ref, call_ref, nall_ref, send_s, *sems):
    xs_sem, xr_sem, cs_sem, cr_sem, ns_sem, nr_sem, own_sem = sems
    q, c, h, w = (lax.axis_index(name) for name in axes)
    rows = x_ref.shape[0]
    piece = rows // 8
    flat = ((2 * q + c) * 2 + h) * 2 + w

    def peer(bits):
        return (q ^ (bits // 8), c ^ (bits // 4 % 2), h ^ (bits // 2 % 2), w ^ (bits % 2))

    barrier = pltpu.get_barrier_semaphore()
    for bits in range(1, 32):
        pl.semaphore_signal(barrier, inc=1, device_id=peer(bits), device_id_type=pl.DeviceIdType.MESH)
    pl.semaphore_wait(barrier, 31)

    def remote(src, dst, send, recv, to):
        return pltpu.make_async_remote_copy(
            src_ref=src, dst_ref=dst, send_sem=send, recv_sem=recv, device_id=to, device_id_type=pl.DeviceIdType.MESH
        )

    nall_ref[flat] = norm_ref[...]

    def norm_copy(bits):
        return remote(norm_ref, nall_ref.at[flat], ns_sem.at[bits], nr_sem.at[bits], peer(bits))

    for bits in range(1, 32):
        norm_copy(bits).start()

    pieces = [(kq, kh) for kh in (1, 0) for kq in (1, 2, 3, 0)]
    spot = lax.broadcasted_iota(jnp.int32, (piece, rows), 0)

    def row_copy(kq, kh):
        at = 2 * kq + kh
        return remote(
            send_s.at[at], got_ref.at[2 * q + c], xs_sem.at[at], xr_sem.at[2 * kq + c], (q ^ kq, h, h ^ kh, w)
        )

    def own_copy():
        return pltpu.make_async_copy(send_s.at[0], got_ref.at[2 * q + c], own_sem.at[0])

    for kq, kh in pieces:
        chunk = 2 * (q ^ kq) + (h ^ kh)
        pick = jnp.where(spot + chunk * piece == rank_ref[...], 1.0, 0.0).astype(bf16)
        send_s[2 * kq + kh] = nn(pick, x_ref[...]).astype(bf16)
        if (kq, kh) == (0, 0):

            @pl.when(c == h)
            def _():
                own_copy().start()

            @pl.when(c != h)
            def _():
                row_copy(0, 0).start()

        else:
            row_copy(kq, kh).start()

    place = 2 * c + w
    spot_c = 4 * c + 2 * h + w

    def chan_copy(kq, kh):
        at = 2 * kq + kh
        return remote(
            chan_ref, call_ref.at[spot_c], cs_sem.at[at], cr_sem.at[spot_c], (q ^ kq, q // 2, h ^ kh, q % 2)
        )

    def own_chan():
        return pltpu.make_async_copy(chan_ref, call_ref.at[spot_c], own_sem.at[1])

    for kq, kh in pieces:
        if (kq, kh) == (0, 0):

            @pl.when(place == q)
            def _():
                own_chan().start()

            @pl.when(place != q)
            def _():
                chan_copy(0, 0).start()

        else:
            chan_copy(kq, kh).start()

    for bits in range(1, 32):
        norm_copy(bits).wait()
    for at in range(8):

        @pl.when((c == h) & (at == c))
        def _():
            own_copy().wait()

        @pl.when(jnp.logical_not((c == h) & (at == c)))
        def _(at=at):
            remote(send_s.at[at], got_ref.at[at], xs_sem.at[at], xr_sem.at[at], peer(1)).wait_recv()

    for at in range(8):

        @pl.when((place == q) & (at == spot_c))
        def _():
            own_chan().wait()

        @pl.when(jnp.logical_not((place == q) & (at == spot_c)))
        def _(at=at):
            remote(chan_ref, call_ref.at[at], cs_sem.at[at], cr_sem.at[at], peer(1)).wait_recv()

    for kq, kh in pieces:
        if (kq, kh) == (0, 0):

            @pl.when(c != h)
            def _():
                row_copy(0, 0).wait_send()

            @pl.when(place != q)
            def _():
                chan_copy(0, 0).wait_send()

        else:
            row_copy(kq, kh).wait_send()
            chan_copy(kq, kh).wait_send()


def meet(axes, rank, x, chan, norm):
    rows, width = x.shape
    vmem = pl.BlockSpec(memory_space=pltpu.VMEM)
    sem = pltpu.SemaphoreType.DMA
    return pl.pallas_call(
        partial(meet_body, axes),
        in_specs=[vmem] * 4,
        out_specs=[vmem] * 3,
        out_shape=[
            jax.ShapeDtypeStruct((8, rows // 8, width), bf16),
            jax.ShapeDtypeStruct((8,) + chan.shape, f32),
            jax.ShapeDtypeStruct((32,) + norm.shape, f32),
        ],
        scratch_shapes=[pltpu.VMEM((8, rows // 8, width), bf16)]
        + [sem((8,)), sem((8,)), sem((8,)), sem((8,)), sem((32,)), sem((32,)), sem((2,))],
        compiler_params=pltpu.CompilerParams(collective_id=1, has_side_effects=True, vmem_limit_bytes=32 * MIB),
        cost_estimate=cost(2 * rows * rows * width, 100 * rows * width),
    )(rank.reshape(1, rows), x, chan, norm)


def sequence_tables(lens, nb):
    nseq = lens.shape[0]
    blocks = (lens + BLK - 1) // BLK
    start = jnp.cumsum(blocks) - blocks
    bigs = (blocks + 1) // 2
    first_big = jnp.cumsum(bigs) - bigs
    h = jnp.arange((nb + nseq) // 2, dtype=jnp.int32)
    owner = (h[:, None] >= first_big[None, :]).astype(jnp.int32).sum(axis=1) - 1
    mine = owner[:, None] == jnp.arange(nseq, dtype=jnp.int32)[None, :]

    def at_owner(values):
        return jnp.sum(jnp.where(mine, values[None, :], 0), axis=1)

    rel = h - at_owner(first_big)
    first = jnp.minimum(at_owner(start) + 2 * rel, nb - 1)
    whole = (2 * rel + 1 < at_owner(blocks)).astype(jnp.int32)
    tab = jnp.stack([first, whole]).astype(jnp.int32)
    seq = jnp.stack(
        [jnp.append(first_big, jnp.sum(blocks)), jnp.append(bigs, jnp.sum(bigs))]
    ).astype(jnp.int32)
    return tab, seq


def live_rows(lens, rows):
    slot = (lens + BLK - 1) // BLK * BLK
    begin = jnp.cumsum(slot) - slot
    pos = jnp.arange(rows, dtype=jnp.int32)
    inside = (pos[:, None] >= begin[None, :]) & (pos[:, None] < (begin + lens)[None, :])
    return jnp.sum(inside.astype(f32), axis=1)


def after(values):
    return lax.optimization_barrier(values)


def rank_of(keys):
    return jnp.sum((keys[None, :] < keys[:, None]).astype(jnp.int32), axis=1)


class Line:
    def __init__(self, n_dp, n_t):
        self.n_dp, self.n_t = n_dp, n_t
        self.axes = {"dp": n_dp, "tensor": n_t}
        self.both = ("dp", "tensor")
        self.cuts = 1

    def place_of_group(self):
        return lax.axis_index("tensor")

    def regroup(self, x):
        return x

    def gather_first(self, x):
        return [lax.all_gather(x, "tensor", axis=0, tiled=True)]

    def gather_last(self, x, got):
        return [(got[0], jnp.zeros((1,), jnp.int32))]

    def scatter_first(self, w, arrays, many):
        return [mul_rows(w, arrays, jnp.zeros((1,), jnp.int32), many * self.n_t)]

    def scatter_send(self, parts):
        return [lax.psum_scatter(parts[0], "tensor", scatter_dimension=0, tiled=True)]

    def scatter_own(self, w, arrays, many):
        return []

    def swap(self, x):
        return x

    def spread(self, x):
        return lax.all_to_all(x, "dp", split_axis=0, concat_axis=0, tiled=True)

    def order(self, pieces):
        return jnp.append(jnp.arange(pieces * self.n_t, dtype=jnp.int32), 0)

    def enter(self, rank, x, chan, norm):
        (sent,) = permute_to(rank, [x])
        return (self.spread(sent),) + self.gather_channels(chan, norm)

    def gather_channels(self, chan, norm):
        perm = [(f, (f % self.n_dp) * self.n_t + f // self.n_dp) for f in range(self.n_dp * self.n_t)]
        chan = lax.ppermute(chan, self.both, perm)
        norm = lax.all_gather(norm, self.both, axis=1, tiled=True)
        return lax.all_gather(chan, "dp", axis=0, tiled=True), norm

    def weights_first(self, pack):
        return [pack]

    def weights_send(self, packs):
        return [lax.all_gather(packs[0], "dp", axis=0, tiled=True)]

    def weights_last(self, parts):
        return parts[0]

    def grads_send(self, gw):
        six, width, ch = gw[0].shape
        gw = gw[0].reshape(six, self.n_dp, width // self.n_dp, ch).transpose(1, 0, 2, 3)
        return [lax.psum_scatter(gw, "dp", scatter_dimension=0, tiled=True)[0]]

    def grads_last(self, parts):
        return parts[0].astype(f32)

    def scatter_channels(self, sums):
        sums = lax.psum_scatter(sums, "dp", scatter_dimension=0, tiled=True)
        perm = [((f % self.n_dp) * self.n_t + f // self.n_dp, f) for f in range(self.n_dp * self.n_t)]
        return lax.ppermute(sums, self.both, perm)

    def scatter_norm(self, sums):
        return lax.psum_scatter(sums, self.both, scatter_dimension=1, tiled=True)


class Pairs:
    def __init__(self, n_dp, n_t):
        self.quads = n_dp // 2
        self.axes = {"q": self.quads, "c": 2, "h": 2, "w": 2}
        self.both = ("q", "c", "h", "w")
        self.cuts = self.quads
        self.other = [(0, 1), (1, 0)]
        self.crossed = [(2 * c + h, 2 * h + c) for c in range(2) for h in range(2)]

    def flip(self, x, axis, bit=1):
        return lax.ppermute(x, axis, [(i, i ^ bit) for i in range(self.axes[axis])])

    def place_of_group(self):
        return 2 * lax.axis_index("c") + lax.axis_index("w")

    def regroup(self, x):
        return lax.ppermute(x, ("c", "h"), self.crossed)

    def swap(self, x):
        return self.regroup(x)

    def spread(self, x):
        return lax.all_to_all(x, ("q", "c"), split_axis=0, concat_axis=0, tiled=True)

    def places(self):
        c, w = lax.axis_index("c"), lax.axis_index("w")
        return [2 * c + w, 2 * (1 - c) + w, 2 * c + 1 - w, 2 * (1 - c) + 1 - w]

    def starts(self, many):
        return [(place * many).astype(jnp.int32).reshape(1) for place in self.places()]

    def gather_first(self, x):
        return [self.flip(x, "c"), self.flip(x, "w")]

    def gather_last(self, x, got):
        beside, near = got
        return list(zip([x, beside, near, self.flip(near, "c")], self.starts(x.shape[0])))

    def scatter_first(self, w, arrays, many):
        _, beside, near, far = self.starts(many)
        first = mul_rows(w, arrays, far, many)
        give = self.flip(first, "c")
        beside, first = after((beside, first))
        second = mul_rows(w, arrays, beside, many)
        second, give = after((second, give))
        return [second, mul_rows(w, arrays, near, many, extra=give)]

    def scatter_send(self, parts):
        return [self.flip(parts[0], "c"), self.flip(parts[1], "w")]

    def scatter_own(self, w, arrays, many):
        return [mul_rows(w, arrays, self.starts(many)[0], many, dtype=f32)]

    def order(self, pieces):
        place = jnp.stack(self.places())[:, None] * pieces + jnp.arange(pieces)[None, :]
        cut = lax.axis_index("q") ^ jnp.arange(self.quads)
        return jnp.concatenate([place.reshape(-1), cut]).astype(jnp.int32)

    def steps(self):
        bit = self.quads // 2
        while bit:
            yield "q", bit
            bit //= 2
        yield "h", 1

    def spot(self):
        return 2 * lax.axis_index("q") + lax.axis_index("h")

    def enter(self, rank, x, chan, norm):
        own, wide = chan.shape
        small = norm.shape[1]
        rows = -(-own * wide // 1024) * 8
        chan = jnp.pad(chan.reshape(-1), (0, rows * BLK - own * wide)).reshape(rows, BLK)
        norm = jnp.pad(norm, ((0, 5), (0, BLK - small)))
        got, chan, norm = meet(self.both, rank, x, chan, norm)
        chan = chan.reshape(8, -1)[:, : own * wide].reshape(8 * own, wide)
        norm = norm[:, :3, :small].transpose(1, 0, 2).reshape(3, -1)
        return got.reshape(x.shape), chan, norm

    def weights_first(self, pack):
        back = [(2 * (1 - h) + c, 2 * c + h) for c in range(2) for h in range(2)]
        return [self.regroup(pack), lax.ppermute(pack, ("c", "h"), back)]

    def weights_send(self, packs):
        h = lax.axis_index("h")
        first, second = packs
        pair = jnp.concatenate([jnp.where(h == 0, first, second), jnp.where(h == 0, second, first)], axis=0)
        return [pair] + [self.flip(pair, "q", bit) for bit in range(1, self.quads)]

    def weights_last(self, parts):
        deep, wide = parts[0].shape
        q = lax.axis_index("q")
        whole = jnp.zeros((self.quads * deep, wide), parts[0].dtype)
        for bit in range(self.quads):
            whole = lax.dynamic_update_slice_in_dim(whole, parts[bit], (q ^ bit) * deep, 0)
        return whole

    def grads_send(self, gw):
        return [gw[0]] + [self.flip(gw[bit], "q", bit) for bit in range(1, self.quads)]

    def grads_last(self, parts):
        total = parts[0].astype(f32)
        for part in parts[1:]:
            total = total + part.astype(f32)
        total = total.astype(bf16)
        six, deep, ch = total.shape
        total = total.reshape(six, 2, deep // 2, ch)
        h = lax.axis_index("h")
        first = jnp.where(h == 0, total[:, 0], total[:, 1])
        second = jnp.where(h == 0, total[:, 1], total[:, 0])
        there = [(2 * c + h, 2 * (1 - h) + c) for c in range(2) for h in range(2)]
        return self.regroup(first).astype(f32) + lax.ppermute(second, ("c", "h"), there).astype(f32)

    def scatter_channels(self, sums):
        count = 2 * self.quads
        rows, wide = sums.shape
        part = jnp.take(sums.reshape(count, rows // count * wide), jnp.arange(count) ^ self.spot(), axis=0)
        for axis, bit in self.steps():
            half = part.shape[0] // 2
            part = part[:half] + self.flip(part[half:], axis, bit)
        perm = []
        for f in range(4 * count):
            place, at = f // count, f % count
            q, h, c, w = at // 2, at % 2, place // 2, place % 2
            perm.append((((2 * q + c) * 2 + h) * 2 + w, f))
        return lax.ppermute(part.reshape(rows // count, wide), self.both, perm)

    def scatter_norm(self, sums):
        count = 8 * self.quads
        mine = lax.axis_index(self.both)
        part = jnp.take(sums.reshape(3, count, -1), jnp.arange(count) ^ mine, axis=1)
        bits = [("q", 1 << at) for at in reversed(range(self.quads.bit_length() - 1))]
        for axis, bit in bits + [("c", 1), ("h", 1), ("w", 1)]:
            half = part.shape[1] // 2
            part = part[:, :half] + self.flip(part[:, half:], axis, bit)
        return part[:, 0]


def local(
    net, wave, tokens, cotangent, source, target, lengths, ln_gain, ln_bias, w_fwd, b_fwd, w_bwd, b_bwd,
    w_gate, b_gate, w_out, b_out, log_dt, log_rate, ssm_b, ssm_c, ssm_d,
):
    rows, width = tokens.shape
    many = rows // BLK
    n_t = net.n_t
    group = rows * n_t
    nb = group // BLK
    ch = w_fwd.shape[1]
    back = (wave.T / BIG).astype(bf16)
    wave = wave.astype(bf16)

    def lanes(column):
        return jnp.broadcast_to(column[..., None], column.shape + (BLK,))

    def decays(log_dt, log_rate, ssm_b):
        rate = jnp.exp(log_rate)
        ld = -jnp.exp(log_dt)[..., None] * rate
        return rate, ld, (1.0 - jnp.exp(ld)) / rate * ssm_b

    rank = rank_of(target)
    sender = source // group
    place = rank_of(sender * rows + jnp.arange(rows, dtype=jnp.int32))
    pack = jnp.concatenate(
        [w_fwd, w_bwd, w_gate.reshape(-1, 2 * ch), w_out.transpose(2, 0, 1).reshape(-1, 2 * ch)], axis=1
    )
    packs = net.weights_first(pack)
    table = net.regroup(jnp.concatenate([place, lengths[0]]))
    rate, ld, drive = decays(log_dt, log_rate, ssm_b)
    scale = ssm_c * drive
    chan = jnp.concatenate(
        [ld[0] * log2e, ld[1] * log2e, scale[0], scale[1]]
        + [jnp.stack([ssm_d[0], ssm_d[1], b_fwd, b_bwd, b_gate[0], b_gate[1]], axis=1)],
        axis=1,
    )
    got_x, chan_all, norm_all = net.enter(rank, tokens, chan, jnp.stack([ln_gain, ln_bias, b_out]))
    got_x, chan_all, norm_all, packs, table, cotangent = after((got_x, chan_all, norm_all, packs, table, cotangent))

    place, lens = table[:rows], table[rows:]
    gain = lanes(norm_all[0])
    shift = lanes(norm_all[1])
    bias_out = lanes(norm_all[2])
    small = chan_all[:, 4 * STATE :]
    bias_in = lanes(small[:, 2:6].T.reshape(-1))

    def pairs(at):
        both = jnp.stack([chan_all[:, (at + k) * STATE : (at + k + 1) * STATE] for k in range(2)])
        return both.reshape(2, ch // 2, 2 * STATE)

    ld_pairs = pairs(0)
    w_pairs = pairs(2)
    skip = lanes(small[:, 0:2].T)
    live = live_rows(lens, group)
    live_own = lax.dynamic_slice_in_dim(live, net.place_of_group() * rows, rows, 0).reshape(many, 1, BLK)
    live = live.reshape(nb // 2, 1, BIG)
    tab, seq = sequence_tables(lens, nb)

    w_parts = net.weights_send(packs)
    xt, xd = deal_x(place, got_x, gain, shift)
    xt, ld_pairs, cotangent = after((xt, ld_pairs, cotangent))
    x_got = net.gather_first(xt)
    (sent_g,) = permute_to(rank, [cotangent])
    got_g = net.spread(sent_g)
    kh = spectra(ld_pairs, w_pairs, skip, wave)
    w_parts, x_got, kh = after((w_parts, x_got, kh))

    w_all = net.weights_last(w_parts)
    w_in, w_back = w_all[:, : 4 * ch], w_all[:, 4 * ch :]
    w_in_t, w_back_t = w_in.T, w_back.T
    xs = net.gather_last(xt, x_got)
    got_g = net.swap(got_g)
    kept = None
    for part, start in xs:
        kept = project(part, start, nb, live, w_in_t, bias_in, kept)
    kept, got_g = after((kept, got_g))
    a, da, gg, dg = kept
    gt, gd, g_bias_out = deal_g(place, got_g, live_own)
    gt, a = after((gt, a))
    g_got = net.gather_first(gt)
    y, mix = ssm_scan(tab, seq, a, kh, wave, back, gg)
    g_got, y, mix = after((g_got, y, mix))
    gs = net.gather_last(gt, g_got)
    kept = None
    for part, start in gs:
        kept = gate_grad(part, start, nb, w_back_t, kept)
    (gm,) = kept
    branch = net.scatter_first(w_back, [mix], many)
    branch, gm = after((branch, gm))

    branch = net.scatter_send(branch)
    branch = net.scatter_own(w_back, [mix], many) + branch
    first = ssm_back(0, tab, seq, a, gm, kh, wave, back, gg, y, dg, da)
    branch, first, a = after((branch, first, a))
    sent_out = layer_rows(place, branch, xd, live_own, bias_out)
    sent_out, a = after((sent_out, a))
    sent_out = net.swap(sent_out)
    second = ssm_back(1, tab, seq, a, gm, kh, wave, back, gg, y, dg, da)
    sent_out, first, second = after((sent_out, first, second))
    gpg, gp, gh, bsum = zip(first, second)
    sent_out = net.spread(sent_out)
    back_list = [gp[0], gp[1], gpg[0], gpg[1]]
    g_normed = net.scatter_first(w_in, back_list, many)
    g_normed, back_list, mix = after((g_normed, back_list, mix))
    gp, gpg = back_list[:2], back_list[2:]
    g_normed = net.scatter_send(g_normed)
    g_normed = net.scatter_own(w_in, back_list, many) + g_normed
    gw = outer_sums(net.order(many // 8), net.cuts, [part for part, _ in xs], [part for part, _ in gs], gp, gpg, mix)
    g_normed, gw, gh, sent_out = after((g_normed, gw, gh, sent_out))
    sent_in, norm_sums = input_rows(place, g_normed, xd, gd, gain)
    sent_in, gh, gw, norm_sums = after((sent_in, gh, gw, norm_sums))
    sent_in = net.swap(sent_in)
    gw = net.grads_send(gw)
    s0, s1, g0 = [jnp.concatenate(part) for part in zip(*[moments(k, ld_pairs, gh[k], back) for k in range(2)])]
    layer_out = permute_from(rank, sent_out)
    sent_in, gw, s0, s1, g0 = after((sent_in, gw, s0, s1, g0))
    gw = net.grads_last(gw)
    in_grad = permute_from(rank, net.spread(sent_in))

    s0 = s0.reshape(2, ch, STATE)
    s1 = s1.reshape(2, ch, STATE)
    bsum = jnp.concatenate(bsum)
    gb_gate = jnp.sum(bsum[:, :, :BLK], axis=2)
    gb_in = jnp.sum(bsum[:, :, BLK:], axis=2)
    sums = jnp.concatenate(
        [s0[0], s0[1], s1[0], s1[1], jnp.concatenate([g0[:, :, 0], gb_gate, gb_in], axis=0).T], axis=1
    )
    sums = net.scatter_channels(sums)
    norm_sums = net.scatter_norm(jnp.sum(jnp.concatenate([norm_sums, g_bias_out[None]], axis=0), axis=2))
    s0 = jnp.stack([sums[:, :STATE], sums[:, STATE : 2 * STATE]])
    s1 = jnp.stack([sums[:, 2 * STATE : 3 * STATE], sums[:, 3 * STATE : 4 * STATE]])
    tail = sums[:, 4 * STATE :].T
    step = jnp.exp(log_dt)[..., None]
    g_c = s0 * drive
    g_drive = s0 * ssm_c
    g_b = g_drive * (1.0 - jnp.exp(ld)) / rate
    g_ld = s1 * ssm_c * drive - g_drive * ssm_b / rate * jnp.exp(ld)
    g_rate = -g_drive * drive / rate - g_ld * step
    g_dt = jnp.sum(g_ld * ld, axis=2)
    return (
        layer_out,
        in_grad,
        norm_sums[0],
        norm_sums[1],
        gw[0],
        tail[4],
        gw[1],
        tail[5],
        jnp.stack([gw[2], gw[3]], axis=1),
        tail[2:4],
        jnp.stack([gw[4].T, gw[5].T]),
        norm_sums[2],
        g_dt,
        g_rate * rate,
        g_b,
        g_c,
        tail[0:2],
    )


def solution(mesh):
    n_dp, n_t = mesh.shape["dp"], mesh.shape["tensor"]
    if n_t == 4 and n_dp == 8:
        net = Pairs(n_dp, n_t)
        dp, tensor = ("q", "c"), ("h", "w")
    else:
        net = Line(n_dp, n_t)
        dp, tensor = ("dp",), ("tensor",)
    net.n_t = n_t
    mesh = jax.sharding.Mesh(mesh.devices.reshape(tuple(net.axes.values())), tuple(net.axes))
    both = P(dp + tensor)
    rows = P(dp + tensor, None)
    pair = P(None, dp + tensor)
    state = P(None, dp + tensor, None)
    proj = P(dp, tensor)
    gate = P(dp, None, tensor)
    out = P(None, tensor, dp)
    wave = wave_table()

    def run(*args):
        return local(net, jnp.asarray(wave), *args)

    return jax.shard_map(
        run,
        mesh=mesh,
        in_specs=(
            rows, rows, both, both, P(dp, None), both, both, proj, both, proj, both, gate, pair, out, both,
            pair, state, state, state, pair,
        ),
        out_specs=(
            rows, rows, both, both, proj, both, proj, both, gate, pair, out, both, pair, state, state, state, pair,
        ),
        check_vma=False,
    )
```

```python
from functools import partial

import jax
import jax.numpy as jnp
import numpy as np
from jax import lax
from jax.experimental import pallas as pl
from jax.experimental.pallas import tpu as pltpu
from jax.sharding import PartitionSpec as P

BLK = 128
BIG = 256
MOST = 2048
LAGS = MOST // BIG
STATE = 64
epsilon = 1e-05
log2e = 1.4426950408889634
f32 = jnp.float32
bf16 = jnp.bfloat16
MIB = 2**20


def nn(a, b):
    return lax.dot_general(a, b, (((1,), (0,)), ((), ())), preferred_element_type=f32)


def nt(a, b):
    return lax.dot_general(a, b, (((1,), (1,)), ((), ())), preferred_element_type=f32)


def params(limit):
    return pltpu.CompilerParams(vmem_limit_bytes=limit * MIB)


def cost(flops, moved, trans=0):
    scale = 0.05
    return pl.CostEstimate(
        flops=int(scale * flops), bytes_accessed=int(scale * moved), transcendentals=int(scale * trans)
    )


def halves(x):
    high = x.astype(bf16)
    return high, (x - high.astype(f32)).astype(bf16)


def wave_table():
    pos = np.arange(BIG)[:, None]
    freq = np.arange(BIG)[None, :]
    angle = 2 * np.pi * ((2 * freq + 1) * pos % (4 * BIG)) / (4 * BIG)
    return np.concatenate([np.cos(angle), np.sin(angle)], 1).astype(np.float32)


def chunk_of(channels, most):
    best = 16
    for size in range(16, most + 1, 16):
        if channels % size == 0:
            best = size
    return best


def permute_row_body(count, rank_ref, *refs):
    rows = rank_ref.shape[1]
    spot = lax.broadcasted_iota(jnp.int32, (rows, rows), 0)
    pick = jnp.where(spot == rank_ref[...], 1.0, 0.0).astype(bf16)
    for at in range(count):
        refs[count + at][...] = nn(pick, refs[at][...]).astype(bf16)


def permute_to(rank, arrays):
    rows, width = arrays[0].shape
    count = len(arrays)
    return pl.pallas_call(
        partial(permute_row_body, count),
        out_shape=[jax.ShapeDtypeStruct((rows, width), bf16)] * count,
        compiler_params=params(48),
        cost_estimate=cost(2 * count * rows * rows * width, 4 * count * rows * width),
    )(rank.reshape(1, rows), *arrays)


def permute_col_body(rank_ref, x_ref, o_ref):
    rows = x_ref.shape[0]
    spot = lax.broadcasted_iota(jnp.int32, (rows, rows), 1)
    pick = jnp.where(spot == rank_ref[...], 1.0, 0.0).astype(bf16)
    o_ref[...] = nn(pick, x_ref[...]).astype(bf16)


def permute_from(rank, x):
    rows, width = x.shape
    return pl.pallas_call(
        permute_col_body,
        out_shape=jax.ShapeDtypeStruct((rows, width), bf16),
        compiler_params=params(48),
        cost_estimate=cost(2 * rows * rows * width, 4 * rows * width),
    )(rank.reshape(rows, 1), x)


def pick_rows(place_ref, x_ref):
    spot = lax.broadcasted_iota(jnp.int32, (BLK, x_ref.shape[0]), 1)
    pick = jnp.where(spot == place_ref[...], 1.0, 0.0).astype(bf16)
    return nn(pick, x_ref[...]).T


def deal_x_body(place_ref, x_ref, gain_ref, shift_ref, xt_ref, xd_ref):
    x = pick_rows(place_ref, x_ref)
    xd_ref[0] = x.astype(bf16)
    centred = x - jnp.mean(x, axis=0, keepdims=True)
    inv_std = lax.rsqrt(jnp.mean(centred * centred, axis=0, keepdims=True) + epsilon)
    xt_ref[0] = (centred * inv_std * gain_ref[...] + shift_ref[...]).astype(bf16)


def deal_g_body(place_ref, g_ref, live_ref, gt_ref, gd_ref, bo_ref):
    g = pick_rows(place_ref, g_ref)
    gd_ref[0] = g.astype(bf16)
    g = g * live_ref[0]
    gt_ref[0] = g.astype(bf16)

    @pl.when(pl.program_id(0) == 0)
    def _():
        bo_ref[...] = jnp.zeros_like(bo_ref)

    bo_ref[...] += g


def deal_specs(rows, width):
    place = pl.BlockSpec((BLK, 1), lambda i: (i, 0))
    whole = pl.BlockSpec((rows, width), lambda i: (0, 0))
    wide = pl.BlockSpec((width, BLK), lambda i: (0, 0))
    out = pl.BlockSpec((1, width, BLK), lambda i: (i, 0, 0))
    return place, whole, wide, out


def deal_x(place, x, gain, shift):
    rows, width = x.shape
    blocks = rows // BLK
    spot, whole, wide, out = deal_specs(rows, width)
    return pl.pallas_call(
        deal_x_body,
        grid=(blocks,),
        in_specs=[spot, whole, wide, wide],
        out_specs=[out, out],
        out_shape=[jax.ShapeDtypeStruct((blocks, width, BLK), bf16)] * 2,
        compiler_params=params(40),
        cost_estimate=cost(2 * rows * rows * width, 6 * rows * width),
    )(place.reshape(rows, 1), x, gain, shift)


def deal_g(place, g, live):
    rows, width = g.shape
    blocks = rows // BLK
    spot, whole, wide, out = deal_specs(rows, width)
    return pl.pallas_call(
        deal_g_body,
        grid=(blocks,),
        in_specs=[spot, whole, pl.BlockSpec((1, 1, BLK), lambda i: (i, 0, 0))],
        out_specs=[out, out, wide],
        out_shape=[jax.ShapeDtypeStruct((blocks, width, BLK), bf16)] * 2
        + [jax.ShapeDtypeStruct((width, BLK), f32)],
        compiler_params=params(40),
        cost_estimate=cost(2 * rows * rows * width, 6 * rows * width),
    )(place.reshape(rows, 1), g, live)


def send_back(place_ref, out_s, o_ref):
    rows = out_s.shape[0]
    spot = lax.broadcasted_iota(jnp.int32, (rows, rows), 0)
    pick = jnp.where(spot == place_ref[...], 1.0, 0.0).astype(bf16)
    o_ref[...] = nn(pick, out_s[...]).astype(bf16)


def total(refs, at):
    value = refs[0][at].astype(f32)
    for ref in refs[1:]:
        value = value + ref[at].astype(f32)
    return value


def layer_body(place_ref, xd_ref, live_ref, bias_ref, *refs):
    o_ref, out_s = refs[-2:]
    for at in range(xd_ref.shape[0]):
        y = xd_ref[at].astype(f32) + live_ref[at] * (total(refs[:-2], at) + bias_ref[...])
        out_s[at * BLK : (at + 1) * BLK, :] = y.T.astype(bf16)
    send_back(place_ref, out_s, o_ref)


def layer_rows(place, parts, xd, live, bias):
    blocks, width, _ = xd.shape
    rows = blocks * BLK
    return pl.pallas_call(
        layer_body,
        out_shape=jax.ShapeDtypeStruct((rows, width), bf16),
        scratch_shapes=[pltpu.VMEM((rows, width), bf16)],
        compiler_params=params(48),
        cost_estimate=cost(2 * rows * rows * width, 6 * rows * width),
    )(place.reshape(1, rows), xd, live, bias, *parts)


def input_body(place_ref, xd_ref, gd_ref, gain_ref, *refs):
    o_ref, sums_ref, out_s = refs[-3:]
    g_gain = jnp.zeros(gain_ref.shape, f32)
    g_shift = jnp.zeros(gain_ref.shape, f32)
    for at in range(xd_ref.shape[0]):
        x = xd_ref[at].astype(f32)
        centred = x - jnp.mean(x, axis=0, keepdims=True)
        inv_std = lax.rsqrt(jnp.mean(centred * centred, axis=0, keepdims=True) + epsilon)
        x_hat = centred * inv_std
        g = total(refs[:-3], at)
        g_gain = g_gain + g * x_hat
        g_shift = g_shift + g
        hat = g * gain_ref[...]
        back = inv_std * (
            hat
            - jnp.mean(hat, axis=0, keepdims=True)
            - x_hat * jnp.mean(hat * x_hat, axis=0, keepdims=True)
        )
        out_s[at * BLK : (at + 1) * BLK, :] = (gd_ref[at].astype(f32) + back).T.astype(bf16)
    sums_ref[0] = g_gain
    sums_ref[1] = g_shift
    send_back(place_ref, out_s, o_ref)


def input_rows(place, parts, xd, gd, gain):
    blocks, width, _ = xd.shape
    rows = blocks * BLK
    return pl.pallas_call(
        input_body,
        out_shape=[
            jax.ShapeDtypeStruct((rows, width), bf16),
            jax.ShapeDtypeStruct((2, width, BLK), f32),
        ],
        scratch_shapes=[pltpu.VMEM((rows, width), bf16)],
        compiler_params=params(48),
        cost_estimate=cost(2 * rows * rows * width, 8 * rows * width),
    )(place.reshape(1, rows), xd, gd, gain, *parts)


def project_body(ch, many, start_ref, x_ref, live_ref, wt_ref, bias_ref, *refs):
    a_ref, da_ref, gg_ref, dg_ref, pre_s = refs[-5:]
    x = jnp.concatenate([x_ref[0], x_ref[1]], axis=1)
    pre_s[...] = nn(wt_ref[...], x)
    live = live_ref[0]
    step = 32
    root = 0.7978845608028654

    def act(pre):
        square = pre * pre
        bent = jnp.tanh(root * pre * (1.0 + 0.044715 * square))
        rise = 0.5 + 0.5 * bent
        slope = rise + (0.5 * root) * pre * (1.0 - bent * bent) * (1.0 + 0.134145 * square)
        return pre * rise, slope

    def put(ref, k, at, value):
        value = value.astype(bf16)
        ref[k, 0, at, :] = value[:, :BLK]
        ref[k, 1, at, :] = value[:, BLK:]

    def chunk(i, carry):
        at = pl.ds(pl.multiple_of(i * step, step), step)
        for k in range(2):
            row = pl.ds(pl.multiple_of(k * ch + i * step, step), step)
            gate = pl.ds(pl.multiple_of((2 + k) * ch + i * step, step), step)
            bias = bias_ref[row, :]
            value, slope = act(pre_s[row, :] + jnp.concatenate([bias, bias], axis=1))
            put(a_ref, k, at, live * value)
            put(da_ref, k, at, live * slope)
            bias = bias_ref[gate, :]
            value, slope = act(pre_s[gate, :] + jnp.concatenate([bias, bias], axis=1))
            put(gg_ref, k, at, value)
            put(dg_ref, k, at, slope)
        return carry

    lax.fori_loop(0, ch // step, chunk, 0)


def chained(body, grid, in_specs, out_specs, shapes, scratch, limit, estimate, start, operands, kept):
    kept = [] if kept is None else list(kept)
    specs = list(in_specs) + [pl.BlockSpec(memory_space=pl.ANY)] * len(kept)
    first = 1 + len(operands)
    return pl.pallas_call(
        body,
        grid_spec=pltpu.PrefetchScalarGridSpec(
            num_scalar_prefetch=1, grid=grid, in_specs=specs, out_specs=out_specs, scratch_shapes=scratch
        ),
        out_shape=shapes,
        input_output_aliases={first + at: at for at in range(len(kept))},
        compiler_params=params(limit),
        cost_estimate=estimate,
    )(start, *operands, *kept)


def project(xt, start, nb, live, wt, bias, kept):
    many, width, _ = xt.shape
    ch = wt.shape[0] // 4
    out = pl.BlockSpec((2, 2, ch, BLK), lambda i, at: (0, at[0] + i, 0, 0))
    tok = many * BLK
    return chained(
        partial(project_body, ch, many),
        (many // 2,),
        [
            pl.BlockSpec((2, width, BLK), lambda i, at: (i, 0, 0)),
            pl.BlockSpec((1, 1, BIG), lambda i, at: (at[0] + i, 0, 0)),
            pl.BlockSpec((4 * ch, width), lambda i, at: (0, 0)),
            pl.BlockSpec((4 * ch, BLK), lambda i, at: (0, 0)),
        ],
        [out] * 4,
        [jax.ShapeDtypeStruct((2, nb, ch, BLK), bf16)] * 4,
        [pltpu.VMEM((4 * ch, BIG), f32)],
        48,
        cost(8 * tok * width * ch, 2 * tok * width + 16 * tok * ch, 4 * tok * ch),
        start // 2,
        [xt, live, wt, bias],
        kept,
    )


def gate_grad_body(ch, start_ref, g_ref, wt_ref, *refs):
    o_ref = refs[-1]
    gm = nn(wt_ref[...], jnp.concatenate([g_ref[0], g_ref[1]], axis=1)).astype(bf16)
    for k in range(2):
        for h in range(2):
            o_ref[k, h] = gm[k * ch : (k + 1) * ch, h * BLK : (h + 1) * BLK]


def gate_grad(gt, start, nb, wt, kept):
    many, width, _ = gt.shape
    ch = wt.shape[0] // 2
    tok = many * BLK
    return chained(
        partial(gate_grad_body, ch),
        (many // 2,),
        [
            pl.BlockSpec((2, width, BLK), lambda i, at: (i, 0, 0)),
            pl.BlockSpec((2 * ch, width), lambda i, at: (0, 0)),
        ],
        [pl.BlockSpec((2, 2, ch, BLK), lambda i, at: (0, at[0] + i, 0, 0))],
        [jax.ShapeDtypeStruct((2, nb, ch, BLK), bf16)],
        [],
        40,
        cost(4 * tok * width * ch, 2 * tok * width + 4 * tok * ch),
        start // 2,
        [gt, wt],
        kept,
    )


def spectra_body(cc, ld_ref, w_ref, d_ref, wave_ref, kh_ref, k_s):
    t = lax.broadcasted_iota(jnp.int32, (BLK, BLK), 0).astype(f32)
    block = lax.broadcasted_iota(jnp.int32, (2 * LAGS, BLK), 0).astype(f32) * float(BLK)
    low = lax.broadcasted_iota(jnp.int32, (2 * LAGS, BLK), 1) < STATE
    count = 2 * LAGS

    def one(p, carry):
        ld = ld_ref[0, pl.ds(p, 1), :]
        decay = jnp.exp2(t * ld)
        scale = w_ref[0, pl.ds(p, 1), :] * jnp.exp2(block * ld)
        lhs = jnp.concatenate([jnp.where(low, scale, 0.0), jnp.where(low, 0.0, scale)], axis=0)
        lhs_high, lhs_low = halves(lhs)
        high, rest = halves(decay)
        k = nt(jnp.concatenate([lhs_high, lhs_low], axis=0), high)
        k = k[0 : 2 * count] + k[2 * count : 4 * count] + nt(lhs_high, rest)
        k_s[pl.ds(2 * p, count, stride=cc), :] = k[0:count]
        k_s[pl.ds(2 * p + 1, count, stride=cc), :] = k[count : 2 * count]
        return carry

    lax.fori_loop(0, cc // 2, one, 0, unroll=4)
    sign = jnp.where(lax.broadcasted_iota(jnp.int32, (cc, BIG), 1) % 2 == 0, 1.0, -1.0)
    before = None
    for big in range(LAGS):
        rows = jnp.concatenate(
            [k_s[pl.ds(2 * big * cc, cc), :], k_s[pl.ds((2 * big + 1) * cc, cc), :]], axis=1
        )
        high, rest = halves(rows)
        x = nn(high, wave_ref[...]) + nn(rest, wave_ref[...])
        xc, xs = x[:, :BIG], x[:, BIG:]
        if big == 0:
            kh_ref[0, 0, :, :BIG] = xc + d_ref[0][:, 0:1]
            kh_ref[0, 0, :, BIG:] = xs
        else:
            kh_ref[0, big, :, :BIG] = xc + sign * before[1]
            kh_ref[0, big, :, BIG:] = xs - sign * before[0]
        before = (xc, xs)


def spectra(ld, w, d, wave):
    ch = 2 * ld.shape[1]
    cc = chunk_of(ch, 128)
    return pl.pallas_call(
        partial(spectra_body, cc),
        grid=(2, ch // cc),
        in_specs=[pl.BlockSpec((1, cc // 2, BLK), lambda k, i: (k, i, 0))] * 2
        + [
            pl.BlockSpec((1, cc, BLK), lambda k, i: (k, i, 0)),
            pl.BlockSpec((BIG, 2 * BIG), lambda k, i: (0, 0)),
        ],
        out_specs=pl.BlockSpec((1, LAGS, cc, 2 * BIG), lambda k, i: (k, 0, i, 0)),
        out_shape=jax.ShapeDtypeStruct((2, LAGS, ch, 2 * BIG), f32),
        scratch_shapes=[pltpu.VMEM((2 * LAGS * cc, BLK), f32)],
        compiler_params=params(40),
        cost_estimate=cost(2 * ch * 40e6, 2 * ch * LAGS * 2 * BIG * 4),
    )(ld, w, d, wave)


def moments_body(cc, ld_ref, gh_ref, back_ref, s0_ref, s1_ref, g0_ref, g_s):
    sign = jnp.where(lax.broadcasted_iota(jnp.int32, (cc, BIG), 1) % 2 == 0, 1.0, -1.0)
    count = 2 * LAGS
    for big in range(LAGS):
        c = gh_ref[0, big, :, :BIG]
        s = gh_ref[0, big, :, BIG:]
        if big < LAGS - 1:
            c, s = c - sign * gh_ref[0, big + 1, :, BIG:], s + sign * gh_ref[0, big + 1, :, :BIG]
        high, rest = halves(jnp.concatenate([c, s], axis=1))
        g = nn(high, back_ref[...]) + nn(rest, back_ref[...])
        g_s[pl.ds(2 * big * cc, cc), :] = g[:, :BLK]
        g_s[pl.ds((2 * big + 1) * cc, cc), :] = g[:, BLK:]
        if big == 0:
            g0_ref[0] = g[:, :BLK]
    t = lax.broadcasted_iota(jnp.int32, (BLK, BLK), 0).astype(f32)
    lane = lax.broadcasted_iota(jnp.int32, (count, BLK), 1)
    lag = lane.astype(f32)
    block = lax.broadcasted_iota(jnp.int32, (count, BLK), 0).astype(f32) * float(BLK)
    low = lane < STATE

    def one(p, carry):
        ld = ld_ref[0, pl.ds(p, 1), :]
        decay = jnp.exp2(t * ld).astype(bf16)
        far = jnp.exp2(block * ld)
        ga = g_s[pl.ds(2 * p, count, stride=cc), :]
        gb = g_s[pl.ds(2 * p + 1, count, stride=cc), :]
        high, rest = halves(jnp.concatenate([ga, gb, ga * lag, gb * lag], axis=0))
        m = nn(jnp.concatenate([high, rest], axis=0), decay)
        m = m[0 : 4 * count] + m[4 * count : 8 * count]
        m0 = jnp.where(low, m[0:count], m[count : 2 * count])
        m1 = jnp.where(low, m[2 * count : 3 * count], m[3 * count : 4 * count]) + block * m0
        s0_ref[0, pl.ds(p, 1), :] = jnp.sum(far * m0, axis=0, keepdims=True)
        s1_ref[0, pl.ds(p, 1), :] = jnp.sum(far * m1, axis=0, keepdims=True)
        return carry

    lax.fori_loop(0, cc // 2, one, 0, unroll=4)


def moments(k, ld, gh, back):
    ch = gh.shape[2]
    cc = chunk_of(ch, 128)
    row = pl.BlockSpec((1, cc // 2, BLK), lambda i: (0, i, 0))
    return pl.pallas_call(
        partial(moments_body, cc),
        grid=(ch // cc,),
        in_specs=[
            pl.BlockSpec((1, cc // 2, BLK), lambda i: (k, i, 0)),
            pl.BlockSpec((1, LAGS, cc, 2 * BIG), lambda i: (0, 0, i, 0)),
            pl.BlockSpec((2 * BIG, BIG), lambda i: (0, 0)),
        ],
        out_specs=[row, row, pl.BlockSpec((1, cc, BLK), lambda i: (0, i, 0))],
        out_shape=[jax.ShapeDtypeStruct((1, ch // 2, BLK), f32)] * 2
        + [jax.ShapeDtypeStruct((1, ch, BLK), f32)],
        scratch_shapes=[pltpu.VMEM((2 * LAGS * cc, BLK), f32)],
        compiler_params=params(40),
        cost_estimate=cost(ch * 40e6, ch * LAGS * 2 * BIG * 4),
    )(ld, gh, back)


def load_pieces(nb, pieces, cc, tab_ref, block, in_s, wave_ref, dst):
    for h in range(pieces):
        first = tab_ref[0, h]
        whole = tab_ref[1, h].astype(f32)
        in_s[pl.ds(h * cc, cc), 0:BLK] = block(first).astype(bf16)
        in_s[pl.ds(h * cc, cc), BLK:BIG] = (block(jnp.minimum(first + 1, nb - 1)) * whole).astype(bf16)
    for h in range(pieces):
        at = pl.ds(h * cc, cc)
        dst[at, :] = nn(in_s[at, :], wave_ref[...])


def over_pieces(nseq, cc, rg, seq_ref, piece):
    def group(r, carry):
        off = pl.multiple_of(r * rg, rg)
        for s in range(nseq):
            base = seq_ref[0, s]
            count = seq_ref[1, s]

            def outer(i, carry):
                piece(i, count, base, off)
                return carry

            lax.fori_loop(0, count, outer, 0)
        return carry

    lax.fori_loop(0, cc // rg, group, 0)


def scan_body(
    nb, nseq, cc, rg, tab_ref, seq_ref, a_ref, kh_ref, wave_ref, back_ref, gg_ref, y_ref, mix_ref, in_s, ah_s, yh_s, y_s
):
    pieces = (nb + nseq) // 2
    load_pieces(nb, pieces, cc, tab_ref, lambda b: a_ref[0, b].astype(f32), in_s, wave_ref, ah_s)
    zero = jnp.zeros((rg, BIG), f32)

    def products(flip):
        def piece(i, count, base, off):
            def inner(j, acc):
                yc, ys = acc
                other = (base + i + j) if flip else (base + i - j)
                m = pl.ds(pl.multiple_of(other * cc + off, rg), rg)
                rows = pl.ds(off, rg)
                ac = ah_s[m, :BIG]
                as_ = ah_s[m, BIG:]
                kc = kh_ref[0, j, rows, :BIG]
                ks = kh_ref[0, j, rows, BIG:]
                if flip:
                    return (yc + kc * ac + ks * as_, ys + kc * as_ - ks * ac)
                return (yc + kc * ac - ks * as_, ys + kc * as_ + ks * ac)

            yc, ys = lax.fori_loop(0, (count - i) if flip else (i + 1), inner, (zero, zero))
            at = pl.ds(pl.multiple_of((base + i) * cc + off, rg), rg)
            yh_s[at, :BIG] = yc.astype(bf16)
            yh_s[at, BIG:] = ys.astype(bf16)

        over_pieces(nseq, cc, rg, seq_ref, piece)

    @pl.when(pl.program_id(0) == 0)
    def _():
        products(False)

    @pl.when(pl.program_id(0) == 1)
    def _():
        products(True)

    for h in range(pieces):
        at = pl.ds(h * cc, cc)
        y_s[at, :] = nn(yh_s[at, :], back_ref[...])

    def one(b, y):
        y_ref[0, b] = y.astype(bf16)
        mix_ref[0, b] = (y * gg_ref[0, b].astype(f32)).astype(bf16)

    def last(h, carry):
        b = tab_ref[0, h]
        at = pl.ds(pl.multiple_of(h * cc, cc), cc)
        one(b, y_s[at, 0:BLK])

        @pl.when(tab_ref[1, h] == 1)
        def _():
            one(b + 1, y_s[at, BLK:])

        return carry

    lax.fori_loop(0, seq_ref[1, nseq], last, 0)
    nothing = jnp.zeros((cc, BLK), bf16)

    def fill(b, carry):
        y_ref[0, b] = nothing
        mix_ref[0, b] = nothing
        return carry

    lax.fori_loop(seq_ref[0, nseq], nb, fill, 0)


def back_body(
    nb, nseq, cc, rg, flip, tab_ref, seq_ref, a_ref, gm_ref, kh_ref, wave_ref, back_ref, gg_ref, y_ref, dg_ref, da_ref,
    gpg_ref, gp_ref, gh_ref, bs_ref, in_s, ah_s, gh_s, xh_s, x_s,
):
    pieces = (nb + nseq) // 2
    load_pieces(nb, pieces, cc, tab_ref, lambda b: a_ref[0, b].astype(f32), in_s, wave_ref, ah_s)
    load_pieces(
        nb, pieces, cc, tab_ref, lambda b: gm_ref[0, b].astype(f32) * gg_ref[0, b].astype(f32), in_s, wave_ref, gh_s
    )
    gh_ref[...] = jnp.zeros_like(gh_ref)
    zero = jnp.zeros((rg, BIG), f32)

    def piece(i, count, base, off):
        at = pl.ds(pl.multiple_of((base + i) * cc + off, rg), rg)
        ac = ah_s[at, :BIG]
        as_ = ah_s[at, BIG:]

        def inner(j, acc):
            xc, xs = acc
            other = (base + i - j) if flip else (base + i + j)
            m = pl.ds(pl.multiple_of(other * cc + off, rg), rg)
            rows = pl.ds(off, rg)
            gc = gh_s[m, :BIG]
            gs = gh_s[m, BIG:]
            kc = kh_ref[0, j, rows, :BIG]
            ks = kh_ref[0, j, rows, BIG:]
            gh_ref[0, j, rows, :BIG] += ac * gc + as_ * gs
            if flip:
                gh_ref[0, j, rows, BIG:] += gc * as_ - gs * ac
                return (xc + kc * gc - ks * gs, xs + kc * gs + ks * gc)
            gh_ref[0, j, rows, BIG:] += ac * gs - as_ * gc
            return (xc + kc * gc + ks * gs, xs + kc * gs - ks * gc)

        xc, xs = lax.fori_loop(0, (i + 1) if flip else (count - i), inner, (zero, zero))
        xh_s[at, :BIG] = xc.astype(bf16)
        xh_s[at, BIG:] = xs.astype(bf16)

    over_pieces(nseq, cc, rg, seq_ref, piece)

    for h in range(pieces):
        at = pl.ds(h * cc, cc)
        x_s[at, :] = nn(xh_s[at, :], back_ref[...])

    none = jnp.zeros((cc, BLK), f32)

    def one(b, gx, carry):
        s0, s1 = carry
        gpg = (y_ref[0, b].astype(f32) * gm_ref[0, b].astype(f32) * dg_ref[0, b].astype(f32)).astype(bf16)
        gpg_ref[0, b] = gpg
        gp = (gx * da_ref[0, b].astype(f32)).astype(bf16)
        gp_ref[0, b] = gp
        return (s0 + gpg.astype(f32), s1 + gp.astype(f32))

    def last(h, carry):
        b = tab_ref[0, h]
        at = pl.ds(pl.multiple_of(h * cc, cc), cc)
        carry = one(b, x_s[at, 0:BLK], carry)

        def more(kept):
            return one(b + 1, x_s[at, BLK:], kept)

        return lax.cond(tab_ref[1, h] == 1, more, lambda kept: kept, carry)

    s0, s1 = lax.fori_loop(0, seq_ref[1, nseq], last, (none, none))
    bs_ref[0, :, 0:BLK] = s0
    bs_ref[0, :, BLK:] = s1
    nothing = jnp.zeros((cc, BLK), bf16)

    def fill(b, carry):
        gpg_ref[0, b] = nothing
        gp_ref[0, b] = nothing
        return carry

    lax.fori_loop(seq_ref[0, nseq], nb, fill, 0)


def ssm_specs(shape, seq):
    _, nb, ch, _ = shape
    nseq = seq.shape[1] - 1
    pieces = (nb + nseq) // 2
    cc = chunk_of(ch, 128 if nb <= 32 else 64)
    big = pl.BlockSpec((1, nb, cc, BLK), lambda k, i: (k, 0, i, 0))
    spec = pl.BlockSpec((1, LAGS, cc, 2 * BIG), lambda k, i: (k, 0, i, 0))
    smem = pl.BlockSpec(memory_space=pltpu.SMEM)
    head = [smem, smem]
    tables = [pl.BlockSpec((BIG, 2 * BIG), lambda k, i: (0, 0)), pl.BlockSpec((2 * BIG, BIG), lambda k, i: (0, 0))]
    return nb, nseq, ch, cc, pieces * cc, big, spec, head, tables


def ssm_scan(tab, seq, a, kh, wave, back, gg):
    nb, nseq, ch, cc, size, big, spec, head, tables = ssm_specs(a.shape, seq)
    return pl.pallas_call(
        partial(scan_body, nb, nseq, cc, 32),
        grid=(2, ch // cc),
        in_specs=head + [big, spec] + tables + [big],
        out_specs=[big, big],
        out_shape=[jax.ShapeDtypeStruct(a.shape, bf16)] * 2,
        scratch_shapes=[
            pltpu.VMEM((size, BIG), bf16),
            pltpu.VMEM((size, 2 * BIG), f32),
            pltpu.VMEM((size, 2 * BIG), bf16),
            pltpu.VMEM((size, BIG), f32),
        ],
        compiler_params=params(56),
        cost_estimate=cost(2 * ch * 50e6, 2 * ch * nb * BLK * 8),
    )(tab, seq, a, kh, wave, back, gg)


def ssm_back(k, tab, seq, a, gm, kh, wave, back, gg, y, dg, da):
    nb, nseq, ch, cc, size, _, _, head, tables = ssm_specs(a.shape, seq)
    big = pl.BlockSpec((1, nb, cc, BLK), lambda i: (k, 0, i, 0))
    spec = pl.BlockSpec((1, LAGS, cc, 2 * BIG), lambda i: (k, 0, i, 0))
    out = pl.BlockSpec((1, nb, cc, BLK), lambda i: (0, 0, i, 0))
    out_spec = pl.BlockSpec((1, LAGS, cc, 2 * BIG), lambda i: (0, 0, i, 0))
    tables = [
        pl.BlockSpec((BIG, 2 * BIG), lambda i: (0, 0)),
        pl.BlockSpec((2 * BIG, BIG), lambda i: (0, 0)),
    ]
    return pl.pallas_call(
        partial(back_body, nb, nseq, cc, 64, k == 1),
        grid=(ch // cc,),
        in_specs=head + [big, big, spec] + tables + [big] * 4,
        out_specs=[out, out, out_spec, pl.BlockSpec((1, cc, 2 * BLK), lambda i: (0, i, 0))],
        out_shape=[jax.ShapeDtypeStruct((1,) + a.shape[1:], bf16)] * 2
        + [
            jax.ShapeDtypeStruct((1, LAGS, ch, 2 * BIG), f32),
            jax.ShapeDtypeStruct((1, ch, 2 * BLK), f32),
        ],
        scratch_shapes=[
            pltpu.VMEM((size, BIG), bf16),
            pltpu.VMEM((size, 2 * BIG), f32),
            pltpu.VMEM((size, 2 * BIG), f32),
            pltpu.VMEM((size, 2 * BIG), bf16),
            pltpu.VMEM((size, BIG), f32),
        ],
        compiler_params=params(60),
        cost_estimate=cost(ch * 80e6, ch * nb * BLK * 16),
    )(tab, seq, a, gm, kh, wave, back, gg, y, dg, da)


def stack_pair(refs):
    return jnp.concatenate(
        [jnp.concatenate([ref[k, 0], ref[k, 1]], axis=1) for ref in refs for k in range(ref.shape[0])], axis=0
    )


def mul_body(count, more, start_ref, w_ref, *refs):
    out = nn(w_ref[...], stack_pair(refs[:count]))
    o_ref = refs[-1]
    for h in range(2):
        part = out[:, h * BLK : (h + 1) * BLK]
        if more:
            part = part + refs[count][h].astype(f32)
        o_ref[h] = part.astype(o_ref.dtype)


def mul_rows(w, arrays, start, many, dtype=bf16, extra=None):
    width, deep = w.shape
    ch = arrays[0].shape[2]
    count = len(arrays)
    out = pl.BlockSpec((2, width, BLK), lambda i, at: (i, 0, 0))
    return pl.pallas_call(
        partial(mul_body, count, extra is not None),
        grid_spec=pltpu.PrefetchScalarGridSpec(
            num_scalar_prefetch=1,
            grid=(many // 2,),
            in_specs=[pl.BlockSpec((width, deep), lambda i, at: (0, 0))]
            + [pl.BlockSpec((x.shape[0], 2, ch, BLK), lambda i, at: (0, at[0] + i, 0, 0)) for x in arrays]
            + ([] if extra is None else [out]),
            out_specs=out,
        ),
        out_shape=jax.ShapeDtypeStruct((many, width, BLK), dtype),
        compiler_params=params(40),
        cost_estimate=cost(2 * many * BLK * width * deep, 2 * many * BLK * (2 * width + deep)),
    )(start // 2, w, *arrays, *([] if extra is None else [extra]))


def outer_body(ch, many, cuts, parts, at_ref, *refs):
    step = pl.program_id(0)
    xs, gs = refs[:parts], refs[parts : 2 * parts]
    gp_refs, gpg_refs, mix_ref = refs[2 * parts : 2 * parts + 2], refs[2 * parts + 2 : 2 * parts + 4], refs[2 * parts + 4]
    outs = refs[2 * parts + 5 : 2 * parts + 5 + cuts]
    acc_s, x_s, g_s = refs[-3:]

    def fill(at):
        for b in range(many):
            x_s[:, b * BLK : (b + 1) * BLK] = xs[at][b]
            g_s[:, b * BLK : (b + 1) * BLK] = gs[at][b]

    if parts == 1:
        fill(0)
    else:
        for at in range(parts):

            @pl.when(step == at)
            def _(at=at):
                fill(at)

    def part(ref, k):
        return jnp.concatenate([ref[k, b] for b in range(many)], axis=1)

    @pl.when(step == 0)
    def _():
        acc_s[...] = jnp.zeros_like(acc_s)

    split = 4 * ch
    left = jnp.concatenate([part(ref, 0) for ref in (*gp_refs, *gpg_refs)], axis=0)
    acc_s[:, :split] += nt(x_s[...], left)
    acc_s[:, split:] += nt(g_s[...], jnp.concatenate([part(mix_ref, 0), part(mix_ref, 1)], axis=0))

    @pl.when(step == pl.num_programs(0) - 1)
    def _():
        deep = acc_s.shape[0] // cuts
        for cut in range(cuts):
            start = pl.multiple_of(at_ref[pl.num_programs(0) + cut] * deep, 8)
            outs[cut][...] = acc_s[pl.ds(start, deep), :].astype(bf16)


def outer_sums(order, cuts, xs, gs, gp, gpg, mix):
    width = xs[0].shape[1]
    _, nb, ch, _ = mix.shape
    many = 8
    parts = len(xs)
    if parts == 1:
        rows = pl.BlockSpec((many, width, BLK), lambda i, at: (i, 0, 0))
    else:
        rows = pl.BlockSpec((many, width, BLK), lambda i, at: (0, 0, 0), pipeline_mode=pl.Buffered(1))
    chan = pl.BlockSpec((2, many, ch, BLK), lambda i, at: (0, at[i], 0, 0))
    one = pl.BlockSpec((1, many, ch, BLK), lambda i, at: (0, at[i], 0, 0))
    tok = nb * BLK
    return pl.pallas_call(
        partial(outer_body, ch, many, cuts, parts),
        grid_spec=pltpu.PrefetchScalarGridSpec(
            num_scalar_prefetch=1,
            grid=(nb // many,),
            in_specs=[rows] * (2 * parts) + [one] * 4 + [chan],
            out_specs=[pl.BlockSpec((width // cuts, 6 * ch), lambda i, at: (0, 0))] * cuts,
            scratch_shapes=[
                pltpu.VMEM((width, 6 * ch), f32),
                pltpu.VMEM((width, many * BLK), bf16),
                pltpu.VMEM((width, many * BLK), bf16),
            ],
        ),
        out_shape=[jax.ShapeDtypeStruct((width // cuts, 6 * ch), bf16)] * cuts,
        compiler_params=params(60),
        cost_estimate=cost(12 * tok * width * ch, tok * (4 * width + 12 * ch)),
    )(order, *xs, *gs, *gp, *gpg, mix)


def join_body(parts, split, at_ref, *refs):
    head_ref, tail_ref, head_t_ref, tail_t_ref = refs[parts:]
    deep = refs[0].shape[0]
    for at in range(parts):
        rows = pl.ds(pl.multiple_of(at_ref[at] * deep, 16), deep)
        head_ref[rows, :] = refs[at][:, :split]
        tail_ref[rows, :] = refs[at][:, split:]
    head_t_ref[...] = head_ref[...].T
    tail_t_ref[...] = tail_ref[...].T


def join_weights(order, parts, split):
    count = len(parts)
    deep, wide = parts[0].shape
    rows = deep * count
    vmem = pl.BlockSpec(memory_space=pltpu.VMEM)
    return pl.pallas_call(
        partial(join_body, count, split),
        in_specs=[pl.BlockSpec(memory_space=pltpu.SMEM)] + [vmem] * count,
        out_specs=[vmem] * 4,
        out_shape=[
            jax.ShapeDtypeStruct(shape, bf16)
            for shape in ((rows, split), (rows, wide - split), (split, rows), (wide - split, rows))
        ],
        compiler_params=params(48),
        cost_estimate=cost(0, 6 * rows * wide),
    )(order, *parts)


def meet_body(axes, rank_ref, x_ref, chan_ref, norm_ref, got_ref, call_ref, nall_ref, send_s, *sems):
    xs_sem, xr_sem, cs_sem, cr_sem, ns_sem, nr_sem, own_sem = sems
    q, c, h, w = (lax.axis_index(name) for name in axes)
    rows = x_ref.shape[0]
    piece = rows // 8
    flat = ((2 * q + c) * 2 + h) * 2 + w

    def peer(bits):
        return (q ^ (bits // 8), c ^ (bits // 4 % 2), h ^ (bits // 2 % 2), w ^ (bits % 2))

    barrier = pltpu.get_barrier_semaphore()
    for bits in range(1, 32):
        pl.semaphore_signal(barrier, inc=1, device_id=peer(bits), device_id_type=pl.DeviceIdType.MESH)
    pl.semaphore_wait(barrier, 31)

    def remote(src, dst, send, recv, to):
        return pltpu.make_async_remote_copy(
            src_ref=src, dst_ref=dst, send_sem=send, recv_sem=recv, device_id=to, device_id_type=pl.DeviceIdType.MESH
        )

    nall_ref[flat] = norm_ref[...]

    def norm_copy(bits):
        return remote(norm_ref, nall_ref.at[flat], ns_sem.at[bits], nr_sem.at[bits], peer(bits))

    for bits in range(1, 32):
        norm_copy(bits).start()

    pieces = [(kq, kh) for kh in (1, 0) for kq in (1, 2, 3, 0)]
    spot = lax.broadcasted_iota(jnp.int32, (piece, rows), 0)

    def row_copy(kq, kh):
        at = 2 * kq + kh
        return remote(
            send_s.at[at], got_ref.at[2 * q + c], xs_sem.at[at], xr_sem.at[2 * kq + c], (q ^ kq, 1 - h, h ^ kh, w)
        )

    def own_copy():
        return pltpu.make_async_copy(send_s.at[0], got_ref.at[2 * q + c], own_sem.at[0])

    for kq, kh in pieces:
        chunk = 2 * (q ^ kq) + (h ^ kh)
        pick = jnp.where(spot + chunk * piece == rank_ref[...], 1.0, 0.0).astype(bf16)
        send_s[2 * kq + kh] = nn(pick, x_ref[...]).astype(bf16)
        if (kq, kh) == (0, 0):

            @pl.when(c != h)
            def _():
                own_copy().start()

            @pl.when(c == h)
            def _():
                row_copy(0, 0).start()

        else:
            row_copy(kq, kh).start()

    place = 2 * (1 - c) + w
    spot_c = 4 * c + 2 * h + w

    def chan_copy(kq, kh):
        at = 2 * kq + kh
        return remote(
            chan_ref, call_ref.at[spot_c], cs_sem.at[at], cr_sem.at[spot_c], (q ^ kq, 1 - q // 2, h ^ kh, q % 2)
        )

    def own_chan():
        return pltpu.make_async_copy(chan_ref, call_ref.at[spot_c], own_sem.at[1])

    for kq, kh in pieces:
        if (kq, kh) == (0, 0):

            @pl.when(place == q)
            def _():
                own_chan().start()

            @pl.when(place != q)
            def _():
                chan_copy(0, 0).start()

        else:
            chan_copy(kq, kh).start()

    for bits in range(1, 32):
        norm_copy(bits).wait()
    for at in range(8):

        @pl.when((c != h) & (at == c))
        def _():
            own_copy().wait()

        @pl.when(jnp.logical_not((c != h) & (at == c)))
        def _(at=at):
            remote(send_s.at[at], got_ref.at[at], xs_sem.at[at], xr_sem.at[at], peer(1)).wait_recv()

    for at in range(8):

        @pl.when((place == q) & (at == spot_c))
        def _():
            own_chan().wait()

        @pl.when(jnp.logical_not((place == q) & (at == spot_c)))
        def _(at=at):
            remote(chan_ref, call_ref.at[at], cs_sem.at[at], cr_sem.at[at], peer(1)).wait_recv()

    for kq, kh in pieces:
        if (kq, kh) == (0, 0):

            @pl.when(c == h)
            def _():
                row_copy(0, 0).wait_send()

            @pl.when(place != q)
            def _():
                chan_copy(0, 0).wait_send()

        else:
            row_copy(kq, kh).wait_send()
            chan_copy(kq, kh).wait_send()


def meet(axes, rank, x, chan, norm):
    rows, width = x.shape
    vmem = pl.BlockSpec(memory_space=pltpu.VMEM)
    sem = pltpu.SemaphoreType.DMA
    return pl.pallas_call(
        partial(meet_body, axes),
        in_specs=[vmem] * 4,
        out_specs=[vmem] * 3,
        out_shape=[
            jax.ShapeDtypeStruct((8, rows // 8, width), bf16),
            jax.ShapeDtypeStruct((8,) + chan.shape, f32),
            jax.ShapeDtypeStruct((32,) + norm.shape, f32),
        ],
        scratch_shapes=[pltpu.VMEM((8, rows // 8, width), bf16)]
        + [sem((8,)), sem((8,)), sem((8,)), sem((8,)), sem((32,)), sem((32,)), sem((2,))],
        compiler_params=pltpu.CompilerParams(collective_id=1, has_side_effects=True, vmem_limit_bytes=32 * MIB),
        cost_estimate=cost(2 * rows * rows * width, 100 * rows * width),
    )(rank.reshape(1, rows), x, chan, norm)


def sequence_tables(lens, nb):
    nseq = lens.shape[0]
    blocks = (lens + BLK - 1) // BLK
    start = jnp.cumsum(blocks) - blocks
    bigs = (blocks + 1) // 2
    first_big = jnp.cumsum(bigs) - bigs
    h = jnp.arange((nb + nseq) // 2, dtype=jnp.int32)
    owner = (h[:, None] >= first_big[None, :]).astype(jnp.int32).sum(axis=1) - 1
    mine = owner[:, None] == jnp.arange(nseq, dtype=jnp.int32)[None, :]

    def at_owner(values):
        return jnp.sum(jnp.where(mine, values[None, :], 0), axis=1)

    rel = h - at_owner(first_big)
    first = jnp.minimum(at_owner(start) + 2 * rel, nb - 1)
    whole = (2 * rel + 1 < at_owner(blocks)).astype(jnp.int32)
    tab = jnp.stack([first, whole]).astype(jnp.int32)
    seq = jnp.stack(
        [jnp.append(first_big, jnp.sum(blocks)), jnp.append(bigs, jnp.sum(bigs))]
    ).astype(jnp.int32)
    return tab, seq


def live_rows(lens, rows):
    slot = (lens + BLK - 1) // BLK * BLK
    begin = jnp.cumsum(slot) - slot
    pos = jnp.arange(rows, dtype=jnp.int32)
    inside = (pos[:, None] >= begin[None, :]) & (pos[:, None] < (begin + lens)[None, :])
    return jnp.sum(inside.astype(f32), axis=1)


def after(values):
    return lax.optimization_barrier(values)


def rank_of(keys):
    return jnp.sum((keys[None, :] < keys[:, None]).astype(jnp.int32), axis=1)


class Line:
    def __init__(self, n_dp, n_t):
        self.n_dp, self.n_t = n_dp, n_t
        self.axes = {"dp": n_dp, "tensor": n_t}
        self.both = ("dp", "tensor")
        self.cuts = 1

    def place_of_group(self):
        return lax.axis_index("tensor")

    def regroup(self, x):
        return x

    def gather_first(self, x):
        return [lax.all_gather(x, "tensor", axis=0, tiled=True)]

    def gather_last(self, x, got):
        return [(got[0], jnp.zeros((1,), jnp.int32))]

    def scatter_first(self, w, arrays, many):
        return [mul_rows(w, arrays, jnp.zeros((1,), jnp.int32), many * self.n_t)]

    def scatter_send(self, parts):
        return [lax.psum_scatter(parts[0], "tensor", scatter_dimension=0, tiled=True)]

    def scatter_own(self, w, arrays, many):
        return []

    def ungroup(self, x):
        return x

    def spread(self, x):
        return lax.all_to_all(x, "dp", split_axis=0, concat_axis=0, tiled=True)

    def order(self, pieces):
        return jnp.append(jnp.arange(pieces * self.n_t, dtype=jnp.int32), 0)

    def enter(self, rank, x, chan, norm):
        (sent,) = permute_to(rank, [x])
        return (self.spread(sent),) + self.gather_channels(chan, norm)

    def gather_channels(self, chan, norm):
        perm = [(f, (f % self.n_dp) * self.n_t + f // self.n_dp) for f in range(self.n_dp * self.n_t)]
        chan = lax.ppermute(chan, self.both, perm)
        norm = lax.all_gather(norm, self.both, axis=1, tiled=True)
        return lax.all_gather(chan[None], "dp", axis=0, tiled=True), norm

    def weights_first(self, pack):
        return [pack]

    def weights_send(self, packs):
        return [lax.all_gather(packs[0], "dp", axis=0, tiled=True)]

    def cut_order(self):
        return jnp.zeros((1,), jnp.int32)

    def grads_send(self, gw):
        return [lax.psum_scatter(gw[0], "dp", scatter_dimension=0, tiled=True)]

    def grads_last(self, parts):
        return parts[0].astype(f32)

    def scatter_channels(self, sums):
        sums = lax.psum_scatter(sums, "dp", scatter_dimension=0, tiled=True)
        perm = [((f % self.n_dp) * self.n_t + f // self.n_dp, f) for f in range(self.n_dp * self.n_t)]
        return lax.ppermute(sums, self.both, perm)

    def scatter_norm(self, sums):
        return lax.psum_scatter(sums, self.both, scatter_dimension=1, tiled=True)


class Pairs:
    def __init__(self, n_dp, n_t):
        self.quads = n_dp // 2
        self.axes = {"q": self.quads, "c": 2, "h": 2, "w": 2}
        self.both = ("q", "c", "h", "w")
        self.cuts = self.quads
        self.other = [(0, 1), (1, 0)]
        self.there = [(2 * c + h, 2 * (1 - h) + c) for c in range(2) for h in range(2)]
        self.back = [(b, a) for a, b in self.there]
        self.turned = [(2 * c + h, 2 * (1 - h) + 1 - c) for c in range(2) for h in range(2)]

    def flip(self, x, axis, bit=1):
        return lax.ppermute(x, axis, [(i, i ^ bit) for i in range(self.axes[axis])])

    def place_of_group(self):
        return 2 * (1 - lax.axis_index("c")) + lax.axis_index("w")

    def regroup(self, x):
        return lax.ppermute(x, ("c", "h"), self.there)

    def ungroup(self, x):
        return lax.ppermute(x, ("c", "h"), self.back)

    def spread(self, x):
        return lax.all_to_all(x, ("q", "c"), split_axis=0, concat_axis=0, tiled=True)

    def places(self):
        c, w = lax.axis_index("c"), lax.axis_index("w")
        return [2 * (1 - c) + w, 2 * c + w, 2 * (1 - c) + 1 - w, 2 * c + 1 - w]

    def starts(self, many):
        return [(place * many).astype(jnp.int32).reshape(1) for place in self.places()]

    def gather_first(self, x):
        return [self.flip(x, "c"), self.flip(x, "w")]

    def gather_last(self, x, got):
        beside, near = got
        return list(zip([x, beside, near, self.flip(near, "c")], self.starts(x.shape[0])))

    def scatter_first(self, w, arrays, many):
        _, beside, near, far = self.starts(many)
        first = mul_rows(w, arrays, far, many)
        give = self.flip(first, "c")
        beside, first = after((beside, first))
        second = mul_rows(w, arrays, beside, many)
        second, give = after((second, give))
        return [second, mul_rows(w, arrays, near, many, extra=give)]

    def scatter_send(self, parts):
        return [self.flip(parts[0], "c"), self.flip(parts[1], "w")]

    def scatter_own(self, w, arrays, many):
        return [mul_rows(w, arrays, self.starts(many)[0], many, dtype=f32)]

    def order(self, pieces):
        place = jnp.stack(self.places())[:, None] * pieces + jnp.arange(pieces)[None, :]
        return jnp.concatenate([place.reshape(-1).astype(jnp.int32), self.cut_order()])

    def steps(self):
        bit = self.quads // 2
        while bit:
            yield "q", bit
            bit //= 2
        yield "h", 1

    def spot(self):
        return 2 * lax.axis_index("q") + lax.axis_index("h")

    def enter(self, rank, x, chan, norm):
        small = norm.shape[1]
        norm = jnp.pad(norm, ((0, 5), (0, BLK - small)))
        got, chan, norm = meet(self.both, rank, x, chan, norm)
        norm = norm[:, :3, :small].transpose(1, 0, 2).reshape(3, -1)
        return got.reshape(x.shape), chan, norm

    def weights_first(self, pack):
        return [self.regroup(pack), lax.ppermute(pack, ("c", "h"), self.turned)]

    def weights_send(self, packs):
        h = lax.axis_index("h")
        first, second = packs
        pair = jnp.concatenate([jnp.where(h == 0, first, second), jnp.where(h == 0, second, first)], axis=0)
        return [pair] + [self.flip(pair, "q", bit) for bit in range(1, self.quads)]

    def grads_send(self, gw):
        return [gw[0]] + [self.flip(gw[bit], "q", bit) for bit in range(1, self.quads)]

    def grads_last(self, parts):
        total = parts[0].astype(f32)
        for part in parts[1:]:
            total = total + part.astype(f32)
        total = total.astype(bf16)
        half = total.shape[0] // 2
        h = lax.axis_index("h")
        first = jnp.where(h == 0, total[:half], total[half:])
        second = jnp.where(h == 0, total[half:], total[:half])
        return self.ungroup(first).astype(f32) + lax.ppermute(second, ("c", "h"), self.turned).astype(f32)

    def cut_order(self):
        return (lax.axis_index("q") ^ jnp.arange(self.quads)).astype(jnp.int32)

    def scatter_channels(self, sums):
        count = 2 * self.quads
        rows, wide = sums.shape
        part = jnp.take(sums.reshape(count, rows // count * wide), jnp.arange(count) ^ self.spot(), axis=0)
        for axis, bit in self.steps():
            half = part.shape[0] // 2
            part = part[:half] + self.flip(part[half:], axis, bit)
        perm = []
        for f in range(4 * count):
            place, at = f // count, f % count
            q, h, c, w = at // 2, at % 2, 1 - place // 2, place % 2
            perm.append((((2 * q + c) * 2 + h) * 2 + w, f))
        return lax.ppermute(part.reshape(rows // count, wide), self.both, perm)

    def scatter_norm(self, sums):
        count = 8 * self.quads
        mine = lax.axis_index(self.both)
        part = jnp.take(sums.reshape(3, count, -1), jnp.arange(count) ^ mine, axis=1)
        bits = [("q", 1 << at) for at in reversed(range(self.quads.bit_length() - 1))]
        for axis, bit in bits + [("c", 1), ("h", 1), ("w", 1)]:
            half = part.shape[1] // 2
            part = part[:, :half] + self.flip(part[:, half:], axis, bit)
        return part[:, 0]


def local(
    net, wave, tokens, cotangent, source, target, lengths, ln_gain, ln_bias, w_fwd, b_fwd, w_bwd, b_bwd,
    w_gate, b_gate, w_out, b_out, log_dt, log_rate, ssm_b, ssm_c, ssm_d,
):
    rows, width = tokens.shape
    many = rows // BLK
    n_t = net.n_t
    group = rows * n_t
    nb = group // BLK
    ch = w_fwd.shape[1]
    back = (wave.T / BIG).astype(bf16)
    wave = wave.astype(bf16)

    def lanes(column):
        return jnp.broadcast_to(column[..., None], column.shape + (BLK,))

    def decays(log_dt, log_rate, ssm_b):
        rate = jnp.exp(log_rate)
        ld = -jnp.exp(log_dt)[..., None] * rate
        return rate, ld, (1.0 - jnp.exp(ld)) / rate * ssm_b

    rank = rank_of(target)
    sender = source // group
    place = rank_of(sender * rows + jnp.arange(rows, dtype=jnp.int32))
    pack = jnp.concatenate(
        [w_fwd, w_bwd, w_gate.reshape(-1, 2 * ch), w_out.transpose(2, 0, 1).reshape(-1, 2 * ch)], axis=1
    )
    table = net.regroup(jnp.concatenate([place, lengths[0]]))
    rate, ld, drive = decays(log_dt, log_rate, ssm_b)
    own = b_fwd.shape[0]
    small = jnp.concatenate([ssm_d, b_fwd[None], b_bwd[None], b_gate])
    chan = jnp.concatenate(
        [
            (ld * log2e).reshape(own, 2 * STATE),
            (ssm_c * drive).reshape(own, 2 * STATE),
            jnp.pad(small, ((0, -(2 * own + 6) % 8 + 0), (0, 2 * STATE - own))),
        ]
    )
    got_x, chan_all, norm_all = net.enter(rank, tokens, chan, jnp.stack([ln_gain, ln_bias, b_out]))
    got_x, chan_all, norm_all, table, cotangent, pack = after((got_x, chan_all, norm_all, table, cotangent, pack))

    packs = net.weights_first(pack)
    place, lens = table[:rows], table[rows:]
    gain = lanes(norm_all[0])
    shift = lanes(norm_all[1])
    small = chan_all[:, 2 * own : 2 * own + 6, :own].transpose(1, 0, 2).reshape(6, ch)

    def pairs(at):
        both = chan_all[:, at : at + own].reshape(-1, 2, own // 2, 2 * STATE)
        return both.transpose(1, 0, 2, 3).reshape(2, ch // 2, 2 * STATE)

    ld_pairs = pairs(0)
    w_pairs = pairs(own)
    skip = lanes(small[0:2])
    live = live_rows(lens, group)
    live_own = lax.dynamic_slice_in_dim(live, net.place_of_group() * rows, rows, 0).reshape(many, 1, BLK)
    live = live.reshape(nb // 2, 1, BIG)
    tab, seq = sequence_tables(lens, nb)

    xt, xd = deal_x(place, got_x, gain, shift)
    xt, cotangent, packs, ld_pairs, w_pairs, skip = after((xt, cotangent, packs, ld_pairs, w_pairs, skip))
    x_got = net.gather_first(xt)
    w_parts = net.weights_send(packs)
    (sent_g,) = permute_to(rank, [cotangent])
    got_g = net.spread(sent_g)
    kh = spectra(ld_pairs, w_pairs, skip, wave)
    w_parts, x_got, kh, norm_all, small = after((w_parts, x_got, kh, norm_all, small))
    bias_in = lanes(small[2:6].reshape(-1))
    bias_out = lanes(norm_all[2])
    w_in, w_back, w_in_t, w_back_t = join_weights(net.cut_order(), w_parts, 4 * ch)
    xs = net.gather_last(xt, x_got)
    got_g = net.regroup(got_g)
    kept = None
    for part, start in xs:
        kept = project(part, start, nb, live, w_in_t, bias_in, kept)
    kept, got_g = after((kept, got_g))
    a, da, gg, dg = kept
    gt, gd, g_bias_out = deal_g(place, got_g, live_own)
    gt, a = after((gt, a))
    g_got = net.gather_first(gt)
    y, mix = ssm_scan(tab, seq, a, kh, wave, back, gg)
    g_got, y, mix = after((g_got, y, mix))
    gs = net.gather_last(gt, g_got)
    kept = None
    for part, start in gs:
        kept = gate_grad(part, start, nb, w_back_t, kept)
    (gm,) = kept
    branch = net.scatter_first(w_back, [mix], many)
    branch, gm = after((branch, gm))

    branch = net.scatter_send(branch)
    branch = net.scatter_own(w_back, [mix], many) + branch
    first = ssm_back(0, tab, seq, a, gm, kh, wave, back, gg, y, dg, da)
    branch, first, a = after((branch, first, a))
    sent_out = layer_rows(place, branch, xd, live_own, bias_out)
    sent_out, a = after((sent_out, a))
    sent_out = net.ungroup(sent_out)
    second = ssm_back(1, tab, seq, a, gm, kh, wave, back, gg, y, dg, da)
    sent_out, first, second = after((sent_out, first, second))
    gpg, gp, gh, bsum = zip(first, second)
    sent_out = net.spread(sent_out)
    back_list = [gp[0], gp[1], gpg[0], gpg[1]]
    g_normed = net.scatter_first(w_in, back_list, many)
    g_normed, back_list, mix = after((g_normed, back_list, mix))
    gp, gpg = back_list[:2], back_list[2:]
    g_normed = net.scatter_send(g_normed)
    g_normed = net.scatter_own(w_in, back_list, many) + g_normed
    gw = outer_sums(net.order(many // 8), net.cuts, [part for part, _ in xs], [part for part, _ in gs], gp, gpg, mix)
    first = moments(0, ld_pairs, gh[0], back)
    g_normed, gw, gh, sent_out, first = after((g_normed, gw, gh, sent_out, first))
    sent_in, norm_sums = input_rows(place, g_normed, xd, gd, gain)
    sent_in, gh, gw, norm_sums, sent_out = after((sent_in, gh, gw, norm_sums, sent_out))
    sent_in = net.ungroup(sent_in)
    gw = net.grads_send(gw)
    s0, s1, g0 = [jnp.concatenate(part) for part in zip(first, moments(1, ld_pairs, gh[1], back))]
    layer_out = permute_from(rank, sent_out)

    s0 = s0.reshape(2, ch, STATE)
    s1 = s1.reshape(2, ch, STATE)
    bsum = jnp.concatenate(bsum)
    gb_gate = jnp.sum(bsum[:, :, :BLK], axis=2)
    gb_in = jnp.sum(bsum[:, :, BLK:], axis=2)
    sums = jnp.concatenate(
        [s0[0], s0[1], s1[0], s1[1], jnp.concatenate([g0[:, :, 0], gb_gate, gb_in], axis=0).T], axis=1
    )
    sums = net.scatter_channels(sums)
    norm_sums = net.scatter_norm(jnp.sum(jnp.concatenate([norm_sums, g_bias_out[None]], axis=0), axis=2))
    sent_in, gw, sums, norm_sums, layer_out = after((sent_in, gw, sums, norm_sums, layer_out))
    in_grad = permute_from(rank, net.spread(sent_in))
    gw = net.grads_last(gw)
    s0 = jnp.stack([sums[:, :STATE], sums[:, STATE : 2 * STATE]])
    s1 = jnp.stack([sums[:, 2 * STATE : 3 * STATE], sums[:, 3 * STATE : 4 * STATE]])
    tail = sums[:, 4 * STATE :].T
    step = jnp.exp(log_dt)[..., None]
    g_c = s0 * drive
    g_drive = s0 * ssm_c
    g_b = g_drive * (1.0 - jnp.exp(ld)) / rate
    g_ld = s1 * ssm_c * drive - g_drive * ssm_b / rate * jnp.exp(ld)
    g_rate = -g_drive * drive / rate - g_ld * step
    g_dt = jnp.sum(g_ld * ld, axis=2)
    return (
        layer_out,
        in_grad,
        norm_sums[0],
        norm_sums[1],
        gw[:, :ch],
        tail[4],
        gw[:, ch : 2 * ch],
        tail[5],
        gw[:, 2 * ch : 4 * ch].reshape(-1, 2, ch),
        tail[2:4],
        gw[:, 4 * ch :].T.reshape(2, ch, -1),
        norm_sums[2],
        g_dt,
        g_rate * rate,
        g_b,
        g_c,
        tail[0:2],
    )


def solution(mesh):
    n_dp, n_t = mesh.shape["dp"], mesh.shape["tensor"]
    if n_t == 4 and n_dp == 8:
        net = Pairs(n_dp, n_t)
        dp, tensor = ("q", "c"), ("h", "w")
    else:
        net = Line(n_dp, n_t)
        dp, tensor = ("dp",), ("tensor",)
    net.n_t = n_t
    mesh = jax.sharding.Mesh(mesh.devices.reshape(tuple(net.axes.values())), tuple(net.axes))
    both = P(dp + tensor)
    rows = P(dp + tensor, None)
    pair = P(None, dp + tensor)
    state = P(None, dp + tensor, None)
    proj = P(dp, tensor)
    gate = P(dp, None, tensor)
    out = P(None, tensor, dp)
    wave = wave_table()

    def run(*args):
        return local(net, jnp.asarray(wave), *args)

    return jax.shard_map(
        run,
        mesh=mesh,
        in_specs=(
            rows, rows, both, both, P(dp, None), both, both, proj, both, proj, both, gate, pair, out, both,
            pair, state, state, state, pair,
        ),
        out_specs=(
            rows, rows, both, both, proj, both, proj, both, gate, pair, out, both, pair, state, state, state, pair,
        ),
        check_vma=False,
    )
```

```python
from functools import partial

import jax
import jax.numpy as jnp
import numpy as np
from jax import lax
from jax.experimental import pallas as pl
from jax.experimental.pallas import tpu as pltpu
from jax.sharding import PartitionSpec as P

BLK = 128
BIG = 256
MOST = 2048
LAGS = MOST // BIG
STATE = 64
epsilon = 1e-05
log2e = 1.4426950408889634
f32 = jnp.float32
bf16 = jnp.bfloat16
MIB = 2**20


def nn(a, b):
    return lax.dot_general(a, b, (((1,), (0,)), ((), ())), preferred_element_type=f32)


def nt(a, b):
    return lax.dot_general(a, b, (((1,), (1,)), ((), ())), preferred_element_type=f32)


def params(limit):
    return pltpu.CompilerParams(vmem_limit_bytes=60 * MIB)


def cost(flops, moved, trans=0):
    scale = 0.05
    return pl.CostEstimate(
        flops=int(scale * flops), bytes_accessed=int(scale * moved), transcendentals=int(scale * trans)
    )


def halves(x):
    high = x.astype(bf16)
    return high, (x - high.astype(f32)).astype(bf16)


def wave_table():
    pos = np.arange(BIG)[:, None]
    freq = np.arange(BIG)[None, :]
    angle = 2 * np.pi * ((2 * freq + 1) * pos % (4 * BIG)) / (4 * BIG)
    return np.concatenate([np.cos(angle), np.sin(angle)], 1).astype(np.float32)


def chunk_of(channels, most):
    best = 16
    for size in range(16, most + 1, 16):
        if channels % size == 0:
            best = size
    return best


def permute_row_body(count, rank_ref, *refs):
    rows = rank_ref.shape[1]
    spot = lax.broadcasted_iota(jnp.int32, (rows, rows), 0)
    pick = jnp.where(spot == rank_ref[...], 1.0, 0.0).astype(bf16)
    for at in range(count):
        refs[count + at][...] = nn(pick, refs[at][...]).astype(bf16)


def permute_to(rank, arrays):
    rows, width = arrays[0].shape
    count = len(arrays)
    return pl.pallas_call(
        partial(permute_row_body, count),
        out_shape=[jax.ShapeDtypeStruct((rows, width), bf16)] * count,
        compiler_params=params(48),
        cost_estimate=cost(2 * count * rows * rows * width, 4 * count * rows * width),
    )(rank.reshape(1, rows), *arrays)


def permute_col_body(rank_ref, x_ref, o_ref):
    rows = x_ref.shape[0]
    spot = lax.broadcasted_iota(jnp.int32, (rows, rows), 1)
    pick = jnp.where(spot == rank_ref[...], 1.0, 0.0).astype(bf16)
    o_ref[...] = nn(pick, x_ref[...]).astype(bf16)


def permute_from(rank, x):
    rows, width = x.shape
    return pl.pallas_call(
        permute_col_body,
        out_shape=jax.ShapeDtypeStruct((rows, width), bf16),
        compiler_params=params(48),
        cost_estimate=cost(2 * rows * rows * width, 4 * rows * width),
    )(rank.reshape(rows, 1), x)


def pick_rows(place_ref, x_ref):
    spot = lax.broadcasted_iota(jnp.int32, (BLK, x_ref.shape[0]), 1)
    pick = jnp.where(spot == place_ref[...], 1.0, 0.0).astype(bf16)
    return nn(pick, x_ref[...]).T


def deal_x_body(place_ref, x_ref, gain_ref, shift_ref, xt_ref, xd_ref):
    x = pick_rows(place_ref, x_ref)
    xd_ref[0] = x.astype(bf16)
    centred = x - jnp.mean(x, axis=0, keepdims=True)
    inv_std = lax.rsqrt(jnp.mean(centred * centred, axis=0, keepdims=True) + epsilon)
    xt_ref[0] = (centred * inv_std * gain_ref[...] + shift_ref[...]).astype(bf16)


def deal_g_body(place_ref, g_ref, live_ref, gt_ref, gd_ref, bo_ref):
    g = pick_rows(place_ref, g_ref)
    gd_ref[0] = g.astype(bf16)
    g = g * live_ref[0]
    gt_ref[0] = g.astype(bf16)

    @pl.when(pl.program_id(0) == 0)
    def _():
        bo_ref[...] = jnp.zeros_like(bo_ref)

    bo_ref[...] += g


def deal_specs(rows, width):
    place = pl.BlockSpec((BLK, 1), lambda i: (i, 0))
    whole = pl.BlockSpec((rows, width), lambda i: (0, 0))
    wide = pl.BlockSpec((width, BLK), lambda i: (0, 0))
    out = pl.BlockSpec((1, width, BLK), lambda i: (i, 0, 0))
    return place, whole, wide, out


def deal_x(place, x, gain, shift):
    rows, width = x.shape
    blocks = rows // BLK
    spot, whole, wide, out = deal_specs(rows, width)
    return pl.pallas_call(
        deal_x_body,
        grid=(blocks,),
        in_specs=[spot, whole, wide, wide],
        out_specs=[out, out],
        out_shape=[jax.ShapeDtypeStruct((blocks, width, BLK), bf16)] * 2,
        compiler_params=params(40),
        cost_estimate=cost(2 * rows * rows * width, 6 * rows * width),
    )(place.reshape(rows, 1), x, gain, shift)


def deal_g(place, g, live):
    rows, width = g.shape
    blocks = rows // BLK
    spot, whole, wide, out = deal_specs(rows, width)
    return pl.pallas_call(
        deal_g_body,
        grid=(blocks,),
        in_specs=[spot, whole, pl.BlockSpec((1, 1, BLK), lambda i: (i, 0, 0))],
        out_specs=[out, out, wide],
        out_shape=[jax.ShapeDtypeStruct((blocks, width, BLK), bf16)] * 2
        + [jax.ShapeDtypeStruct((width, BLK), f32)],
        compiler_params=params(40),
        cost_estimate=cost(2 * rows * rows * width, 6 * rows * width),
    )(place.reshape(rows, 1), g, live)


def send_back(place_ref, out_s, o_ref):
    rows = out_s.shape[0]
    spot = lax.broadcasted_iota(jnp.int32, (rows, rows), 0)
    pick = jnp.where(spot == place_ref[...], 1.0, 0.0).astype(bf16)
    o_ref[...] = nn(pick, out_s[...]).astype(bf16)


def total(refs, at):
    value = refs[0][at].astype(f32)
    for ref in refs[1:]:
        value = value + ref[at].astype(f32)
    return value


def layer_body(place_ref, xd_ref, live_ref, bias_ref, *refs):
    o_ref, out_s = refs[-2:]
    for at in range(xd_ref.shape[0]):
        y = xd_ref[at].astype(f32) + live_ref[at] * (total(refs[:-2], at) + bias_ref[...])
        out_s[at * BLK : (at + 1) * BLK, :] = y.T.astype(bf16)
    send_back(place_ref, out_s, o_ref)


def layer_rows(place, parts, xd, live, bias):
    blocks, width, _ = xd.shape
    rows = blocks * BLK
    return pl.pallas_call(
        layer_body,
        out_shape=jax.ShapeDtypeStruct((rows, width), bf16),
        scratch_shapes=[pltpu.VMEM((rows, width), bf16)],
        compiler_params=params(48),
        cost_estimate=cost(2 * rows * rows * width, 6 * rows * width),
    )(place.reshape(1, rows), xd, live, bias, *parts)


def input_body(place_ref, xd_ref, gd_ref, gain_ref, *refs):
    o_ref, sums_ref, out_s = refs[-3:]
    g_gain = jnp.zeros(gain_ref.shape, f32)
    g_shift = jnp.zeros(gain_ref.shape, f32)
    for at in range(xd_ref.shape[0]):
        x = xd_ref[at].astype(f32)
        centred = x - jnp.mean(x, axis=0, keepdims=True)
        inv_std = lax.rsqrt(jnp.mean(centred * centred, axis=0, keepdims=True) + epsilon)
        x_hat = centred * inv_std
        g = total(refs[:-3], at)
        g_gain = g_gain + g * x_hat
        g_shift = g_shift + g
        hat = g * gain_ref[...]
        back = inv_std * (
            hat
            - jnp.mean(hat, axis=0, keepdims=True)
            - x_hat * jnp.mean(hat * x_hat, axis=0, keepdims=True)
        )
        out_s[at * BLK : (at + 1) * BLK, :] = (gd_ref[at].astype(f32) + back).T.astype(bf16)
    sums_ref[0] = g_gain
    sums_ref[1] = g_shift
    send_back(place_ref, out_s, o_ref)


def input_rows(place, parts, xd, gd, gain):
    blocks, width, _ = xd.shape
    rows = blocks * BLK
    return pl.pallas_call(
        input_body,
        out_shape=[
            jax.ShapeDtypeStruct((rows, width), bf16),
            jax.ShapeDtypeStruct((2, width, BLK), f32),
        ],
        scratch_shapes=[pltpu.VMEM((rows, width), bf16)],
        compiler_params=params(48),
        cost_estimate=cost(2 * rows * rows * width, 8 * rows * width),
    )(place.reshape(1, rows), xd, gd, gain, *parts)


def project_body(ch, many, start_ref, x_ref, live_ref, wt_ref, bias_ref, *refs):
    a_ref, da_ref, gg_ref, dg_ref = refs[-4:]
    x = jnp.concatenate([x_ref[0], x_ref[1]], axis=1)
    live = live_ref[0]
    root = 0.7978845608028654
    step = 64 if ch % 128 else 128

    def act(pre):
        square = pre * pre
        rise = 0.5 + 0.5 * jnp.tanh(pre * (root + (0.044715 * root) * square))
        value = pre * rise
        slope = rise + rise * (pre - value) * (2.0 * root + (6.0 * 0.044715 * root) * square)
        return value, slope

    def put(ref, k, at, value):
        value = value.astype(bf16)
        ref[k, 0, at, :] = value[:, :BLK]
        ref[k, 1, at, :] = value[:, BLK:]

    for k in range(2):
        for first, value_ref, slope_ref in ((k * ch, a_ref, da_ref), ((2 + k) * ch, gg_ref, dg_ref)):
            for at in range(0, ch, step):
                rows = pl.ds(first + at, step)
                bias = bias_ref[rows, :]
                pre = nn(wt_ref[rows, :], x) + jnp.concatenate([bias, bias], axis=1)
                value, slope = act(pre)
                if value_ref is a_ref:
                    value, slope = live * value, live * slope
                put(value_ref, k, pl.ds(at, step), value)
                put(slope_ref, k, pl.ds(at, step), slope)


def chained(body, grid, in_specs, out_specs, shapes, scratch, limit, estimate, start, operands, kept):
    kept = [] if kept is None else list(kept)
    specs = list(in_specs) + [pl.BlockSpec(memory_space=pl.ANY)] * len(kept)
    first = 1 + len(operands)
    return pl.pallas_call(
        body,
        grid_spec=pltpu.PrefetchScalarGridSpec(
            num_scalar_prefetch=1, grid=grid, in_specs=specs, out_specs=out_specs, scratch_shapes=scratch
        ),
        out_shape=shapes,
        input_output_aliases={first + at: at for at in range(len(kept))},
        compiler_params=params(limit),
        cost_estimate=estimate,
    )(start, *operands, *kept)


def project(xt, start, nb, live, wt, bias, kept):
    many, width, _ = xt.shape
    ch = wt.shape[0] // 4
    out = pl.BlockSpec((2, 2, ch, BLK), lambda i, at: (0, at[0] + i, 0, 0))
    tok = many * BLK
    return chained(
        partial(project_body, ch, many),
        (many // 2,),
        [
            pl.BlockSpec((2, width, BLK), lambda i, at: (i, 0, 0)),
            pl.BlockSpec((1, 1, BIG), lambda i, at: (at[0] + i, 0, 0)),
            pl.BlockSpec((4 * ch, width), lambda i, at: (0, 0)),
            pl.BlockSpec((4 * ch, BLK), lambda i, at: (0, 0)),
        ],
        [out] * 4,
        [jax.ShapeDtypeStruct((2, nb, ch, BLK), bf16)] * 4,
        [],
        48,
        cost(8 * tok * width * ch, 2 * tok * width + 16 * tok * ch, 4 * tok * ch),
        start // 2,
        [xt, live, wt, bias],
        kept,
    )


def gate_grad_body(ch, start_ref, g_ref, wt_ref, *refs):
    o_ref = refs[-1]
    gm = nn(wt_ref[...], jnp.concatenate([g_ref[0], g_ref[1]], axis=1)).astype(bf16)
    for k in range(2):
        for h in range(2):
            o_ref[k, h] = gm[k * ch : (k + 1) * ch, h * BLK : (h + 1) * BLK]


def gate_grad(gt, start, nb, wt, kept):
    many, width, _ = gt.shape
    ch = wt.shape[0] // 2
    tok = many * BLK
    return chained(
        partial(gate_grad_body, ch),
        (many // 2,),
        [
            pl.BlockSpec((2, width, BLK), lambda i, at: (i, 0, 0)),
            pl.BlockSpec((2 * ch, width), lambda i, at: (0, 0)),
        ],
        [pl.BlockSpec((2, 2, ch, BLK), lambda i, at: (0, at[0] + i, 0, 0))],
        [jax.ShapeDtypeStruct((2, nb, ch, BLK), bf16)],
        [],
        40,
        cost(4 * tok * width * ch, 2 * tok * width + 4 * tok * ch),
        start // 2,
        [gt, wt],
        kept,
    )


def spectra_body(cc, ld_ref, w_ref, d_ref, wave_ref, kh_ref, k_s):
    t = lax.broadcasted_iota(jnp.int32, (BLK, BLK), 0).astype(f32)
    block = lax.broadcasted_iota(jnp.int32, (2 * LAGS, BLK), 0).astype(f32) * float(BLK)
    low = lax.broadcasted_iota(jnp.int32, (2 * LAGS, BLK), 1) < STATE
    count = 2 * LAGS

    def one(p, carry):
        ld = ld_ref[0, pl.ds(p, 1), :]
        decay = jnp.exp2(t * ld)
        scale = w_ref[0, pl.ds(p, 1), :] * jnp.exp2(block * ld)
        lhs = jnp.concatenate([jnp.where(low, scale, 0.0), jnp.where(low, 0.0, scale)], axis=0)
        lhs_high, lhs_low = halves(lhs)
        k = nt(jnp.concatenate([lhs_high, lhs_low], axis=0), decay.astype(bf16))
        k = k[0 : 2 * count] + k[2 * count : 4 * count]
        k_s[pl.ds(2 * p, count, stride=cc), :] = k[0:count]
        k_s[pl.ds(2 * p + 1, count, stride=cc), :] = k[count : 2 * count]
        return carry

    lax.fori_loop(0, cc // 2, one, 0, unroll=16)
    sign = jnp.where(lax.broadcasted_iota(jnp.int32, (cc, BIG), 1) % 2 == 0, 1.0, -1.0)
    before = None
    for big in range(LAGS):
        rows = jnp.concatenate(
            [k_s[pl.ds(2 * big * cc, cc), :], k_s[pl.ds((2 * big + 1) * cc, cc), :]], axis=1
        )
        high, rest = halves(rows)
        x = nn(high, wave_ref[...]) + nn(rest, wave_ref[...])
        xc, xs = x[:, :BIG], x[:, BIG:]
        if big == 0:
            kh_ref[0, 0, :, :BIG] = xc + d_ref[0][:, 0:1]
            kh_ref[0, 0, :, BIG:] = xs
        else:
            kh_ref[0, big, :, :BIG] = xc + sign * before[1]
            kh_ref[0, big, :, BIG:] = xs - sign * before[0]
        before = (xc, xs)


def spectra(ld, w, d, wave):
    ch = 2 * ld.shape[1]
    cc = chunk_of(ch, 128)
    return pl.pallas_call(
        partial(spectra_body, cc),
        grid=(2, ch // cc),
        in_specs=[pl.BlockSpec((1, cc // 2, BLK), lambda k, i: (k, i, 0))] * 2
        + [
            pl.BlockSpec((1, cc, BLK), lambda k, i: (k, i, 0)),
            pl.BlockSpec((BIG, 2 * BIG), lambda k, i: (0, 0)),
        ],
        out_specs=pl.BlockSpec((1, LAGS, cc, 2 * BIG), lambda k, i: (k, 0, i, 0)),
        out_shape=jax.ShapeDtypeStruct((2, LAGS, ch, 2 * BIG), f32),
        scratch_shapes=[pltpu.VMEM((2 * LAGS * cc, BLK), f32)],
        compiler_params=params(40),
        cost_estimate=cost(2 * ch * 40e6, 2 * ch * LAGS * 2 * BIG * 4),
    )(ld, w, d, wave)


def moments_body(cc, ld_ref, gh_ref, back_ref, s0_ref, s1_ref, g0_ref, g_s):
    sign = jnp.where(lax.broadcasted_iota(jnp.int32, (cc, BIG), 1) % 2 == 0, 1.0, -1.0)
    count = 2 * LAGS
    for big in range(LAGS):
        c = gh_ref[0, big, :, :BIG]
        s = gh_ref[0, big, :, BIG:]
        if big < LAGS - 1:
            c, s = c - sign * gh_ref[0, big + 1, :, BIG:], s + sign * gh_ref[0, big + 1, :, :BIG]
        high, rest = halves(jnp.concatenate([c, s], axis=1))
        g = nn(high, back_ref[...]) + nn(rest, back_ref[...])
        g_s[pl.ds(2 * big * cc, cc), :] = g[:, :BLK]
        g_s[pl.ds((2 * big + 1) * cc, cc), :] = g[:, BLK:]
        if big == 0:
            g0_ref[0] = g[:, :BLK]
    t = lax.broadcasted_iota(jnp.int32, (BLK, BLK), 0).astype(f32)
    lane = lax.broadcasted_iota(jnp.int32, (count, BLK), 1)
    lag = lane.astype(f32)
    block = lax.broadcasted_iota(jnp.int32, (count, BLK), 0).astype(f32) * float(BLK)
    low = lane < STATE

    def one(p, carry):
        ld = ld_ref[0, pl.ds(p, 1), :]
        decay = jnp.exp2(t * ld).astype(bf16)
        far = jnp.exp2(block * ld)
        ga = g_s[pl.ds(2 * p, count, stride=cc), :]
        gb = g_s[pl.ds(2 * p + 1, count, stride=cc), :]
        high, rest = halves(jnp.concatenate([ga, gb, ga * lag, gb * lag], axis=0))
        m = nn(jnp.concatenate([high, rest], axis=0), decay)
        m = m[0 : 4 * count] + m[4 * count : 8 * count]
        m0 = jnp.where(low, m[0:count], m[count : 2 * count])
        m1 = jnp.where(low, m[2 * count : 3 * count], m[3 * count : 4 * count]) + block * m0
        s0_ref[0, pl.ds(p, 1), :] = jnp.sum(far * m0, axis=0, keepdims=True)
        s1_ref[0, pl.ds(p, 1), :] = jnp.sum(far * m1, axis=0, keepdims=True)
        return carry

    lax.fori_loop(0, cc // 2, one, 0, unroll=16)


def moments(k, ld, gh, back):
    ch = gh.shape[2]
    cc = chunk_of(ch, 128)
    row = pl.BlockSpec((1, cc // 2, BLK), lambda i: (0, i, 0))
    return pl.pallas_call(
        partial(moments_body, cc),
        grid=(ch // cc,),
        in_specs=[
            pl.BlockSpec((1, cc // 2, BLK), lambda i: (k, i, 0)),
            pl.BlockSpec((1, LAGS, cc, 2 * BIG), lambda i: (0, 0, i, 0)),
            pl.BlockSpec((2 * BIG, BIG), lambda i: (0, 0)),
        ],
        out_specs=[row, row, pl.BlockSpec((1, cc, BLK), lambda i: (0, i, 0))],
        out_shape=[jax.ShapeDtypeStruct((1, ch // 2, BLK), f32)] * 2
        + [jax.ShapeDtypeStruct((1, ch, BLK), f32)],
        scratch_shapes=[pltpu.VMEM((2 * LAGS * cc, BLK), f32)],
        compiler_params=params(40),
        cost_estimate=cost(ch * 40e6, ch * LAGS * 2 * BIG * 4),
    )(ld, gh, back)


def load_pieces(nb, pieces, cc, tab_ref, block, in_s, wave_ref, dst):
    for h in range(pieces):
        first = tab_ref[0, h]
        whole = tab_ref[1, h].astype(f32)
        in_s[pl.ds(h * cc, cc), 0:BLK] = block(first).astype(bf16)
        in_s[pl.ds(h * cc, cc), BLK:BIG] = (block(jnp.minimum(first + 1, nb - 1)) * whole).astype(bf16)
    for h in range(pieces):
        at = pl.ds(h * cc, cc)
        dst[at, :] = nn(in_s[at, :], wave_ref[...])


def over_pieces(nseq, cc, rg, seq_ref, piece):
    def group(r, carry):
        off = pl.multiple_of(r * rg, rg)
        for s in range(nseq):
            base = seq_ref[0, s]
            count = seq_ref[1, s]

            def outer(i, carry):
                piece(i, count, base, off)
                return carry

            lax.fori_loop(0, count, outer, 0)
        return carry

    lax.fori_loop(0, cc // rg, group, 0)


def scan_body(
    nb, nseq, cc, rg, tab_ref, seq_ref, a_ref, kh_ref, wave_ref, back_ref, gg_ref, y_ref, mix_ref, in_s, ah_s, yh_s, y_s
):
    pieces = (nb + nseq) // 2
    load_pieces(nb, pieces, cc, tab_ref, lambda b: a_ref[0, b].astype(f32), in_s, wave_ref, ah_s)
    zero = jnp.zeros((rg, BIG), f32)

    def products(flip):
        def piece(i, count, base, off):
            def inner(j, acc):
                yc, ys = acc
                other = (base + i + j) if flip else (base + i - j)
                m = pl.ds(pl.multiple_of(other * cc + off, rg), rg)
                rows = pl.ds(off, rg)
                ac = ah_s[m, :BIG]
                as_ = ah_s[m, BIG:]
                kc = kh_ref[0, j, rows, :BIG]
                ks = kh_ref[0, j, rows, BIG:]
                if flip:
                    return (yc + kc * ac + ks * as_, ys + kc * as_ - ks * ac)
                return (yc + kc * ac - ks * as_, ys + kc * as_ + ks * ac)

            yc, ys = lax.fori_loop(0, (count - i) if flip else (i + 1), inner, (zero, zero))
            at = pl.ds(pl.multiple_of((base + i) * cc + off, rg), rg)
            yh_s[at, :BIG] = yc.astype(bf16)
            yh_s[at, BIG:] = ys.astype(bf16)

        over_pieces(nseq, cc, rg, seq_ref, piece)

    @pl.when(pl.program_id(0) == 0)
    def _():
        products(False)

    @pl.when(pl.program_id(0) == 1)
    def _():
        products(True)

    for h in range(pieces):
        at = pl.ds(h * cc, cc)
        y_s[at, :] = nn(yh_s[at, :], back_ref[...])

    def one(b, y):
        y_ref[0, b] = y.astype(bf16)
        mix_ref[0, b] = (y * gg_ref[0, b].astype(f32)).astype(bf16)

    def last(h, carry):
        b = tab_ref[0, h]
        at = pl.ds(pl.multiple_of(h * cc, cc), cc)
        one(b, y_s[at, 0:BLK])

        @pl.when(tab_ref[1, h] == 1)
        def _():
            one(b + 1, y_s[at, BLK:])

        return carry

    lax.fori_loop(0, seq_ref[1, nseq], last, 0)
    nothing = jnp.zeros((cc, BLK), bf16)

    def fill(b, carry):
        y_ref[0, b] = nothing
        mix_ref[0, b] = nothing
        return carry

    lax.fori_loop(seq_ref[0, nseq], nb, fill, 0)


def back_body(
    nb, nseq, cc, rg, flip, tab_ref, seq_ref, a_ref, gm_ref, kh_ref, wave_ref, back_ref, gg_ref, y_ref, dg_ref, da_ref,
    gpg_ref, gp_ref, gh_ref, bs_ref, in_s, ah_s, gh_s, xh_s, x_s,
):
    pieces = (nb + nseq) // 2
    load_pieces(nb, pieces, cc, tab_ref, lambda b: a_ref[0, b].astype(f32), in_s, wave_ref, ah_s)
    load_pieces(
        nb, pieces, cc, tab_ref, lambda b: gm_ref[0, b].astype(f32) * gg_ref[0, b].astype(f32), in_s, wave_ref, gh_s
    )
    gh_ref[...] = jnp.zeros_like(gh_ref)
    zero = jnp.zeros((rg, BIG), f32)

    def piece(i, count, base, off):
        at = pl.ds(pl.multiple_of((base + i) * cc + off, rg), rg)
        ac = ah_s[at, :BIG]
        as_ = ah_s[at, BIG:]

        def inner(j, acc):
            xc, xs = acc
            other = (base + i - j) if flip else (base + i + j)
            m = pl.ds(pl.multiple_of(other * cc + off, rg), rg)
            rows = pl.ds(off, rg)
            gc = gh_s[m, :BIG]
            gs = gh_s[m, BIG:]
            kc = kh_ref[0, j, rows, :BIG]
            ks = kh_ref[0, j, rows, BIG:]
            gh_ref[0, j, rows, :BIG] += ac * gc + as_ * gs
            if flip:
                gh_ref[0, j, rows, BIG:] += gc * as_ - gs * ac
                return (xc + kc * gc - ks * gs, xs + kc * gs + ks * gc)
            gh_ref[0, j, rows, BIG:] += ac * gs - as_ * gc
            return (xc + kc * gc + ks * gs, xs + kc * gs - ks * gc)

        xc, xs = lax.fori_loop(0, (i + 1) if flip else (count - i), inner, (zero, zero))
        xh_s[at, :BIG] = xc.astype(bf16)
        xh_s[at, BIG:] = xs.astype(bf16)

    over_pieces(nseq, cc, rg, seq_ref, piece)

    for h in range(pieces):
        at = pl.ds(h * cc, cc)
        x_s[at, :] = nn(xh_s[at, :], back_ref[...])

    none = jnp.zeros((cc, BLK), f32)

    def one(b, gx, carry):
        s0, s1 = carry
        gpg = (y_ref[0, b].astype(f32) * gm_ref[0, b].astype(f32) * dg_ref[0, b].astype(f32)).astype(bf16)
        gpg_ref[0, b] = gpg
        gp = (gx * da_ref[0, b].astype(f32)).astype(bf16)
        gp_ref[0, b] = gp
        return (s0 + gpg.astype(f32), s1 + gp.astype(f32))

    def last(h, carry):
        b = tab_ref[0, h]
        at = pl.ds(pl.multiple_of(h * cc, cc), cc)
        carry = one(b, x_s[at, 0:BLK], carry)

        def more(kept):
            return one(b + 1, x_s[at, BLK:], kept)

        return lax.cond(tab_ref[1, h] == 1, more, lambda kept: kept, carry)

    s0, s1 = lax.fori_loop(0, seq_ref[1, nseq], last, (none, none))
    bs_ref[0, :, 0:BLK] = s0
    bs_ref[0, :, BLK:] = s1
    nothing = jnp.zeros((cc, BLK), bf16)

    def fill(b, carry):
        gpg_ref[0, b] = nothing
        gp_ref[0, b] = nothing
        return carry

    lax.fori_loop(seq_ref[0, nseq], nb, fill, 0)


def ssm_specs(shape, seq):
    _, nb, ch, _ = shape
    nseq = seq.shape[1] - 1
    pieces = (nb + nseq) // 2
    cc = chunk_of(ch, 128 if nb <= 32 else 64)
    big = pl.BlockSpec((1, nb, cc, BLK), lambda k, i: (k, 0, i, 0))
    spec = pl.BlockSpec((1, LAGS, cc, 2 * BIG), lambda k, i: (k, 0, i, 0))
    smem = pl.BlockSpec(memory_space=pltpu.SMEM)
    head = [smem, smem]
    tables = [pl.BlockSpec((BIG, 2 * BIG), lambda k, i: (0, 0)), pl.BlockSpec((2 * BIG, BIG), lambda k, i: (0, 0))]
    return nb, nseq, ch, cc, pieces * cc, big, spec, head, tables


def ssm_scan(tab, seq, a, kh, wave, back, gg):
    nb, nseq, ch, cc, size, big, spec, head, tables = ssm_specs(a.shape, seq)
    return pl.pallas_call(
        partial(scan_body, nb, nseq, cc, 32),
        grid=(2, ch // cc),
        in_specs=head + [big, spec] + tables + [big],
        out_specs=[big, big],
        out_shape=[jax.ShapeDtypeStruct(a.shape, bf16)] * 2,
        scratch_shapes=[
            pltpu.VMEM((size, BIG), bf16),
            pltpu.VMEM((size, 2 * BIG), f32),
            pltpu.VMEM((size, 2 * BIG), bf16),
            pltpu.VMEM((size, BIG), f32),
        ],
        compiler_params=params(56),
        cost_estimate=cost(2 * ch * 50e6, 2 * ch * nb * BLK * 8),
    )(tab, seq, a, kh, wave, back, gg)


def ssm_back(k, tab, seq, a, gm, kh, wave, back, gg, y, dg, da):
    nb, nseq, ch, cc, size, _, _, head, tables = ssm_specs(a.shape, seq)
    big = pl.BlockSpec((1, nb, cc, BLK), lambda i: (k, 0, i, 0))
    spec = pl.BlockSpec((1, LAGS, cc, 2 * BIG), lambda i: (k, 0, i, 0))
    out = pl.BlockSpec((1, nb, cc, BLK), lambda i: (0, 0, i, 0))
    out_spec = pl.BlockSpec((1, LAGS, cc, 2 * BIG), lambda i: (0, 0, i, 0))
    tables = [
        pl.BlockSpec((BIG, 2 * BIG), lambda i: (0, 0)),
        pl.BlockSpec((2 * BIG, BIG), lambda i: (0, 0)),
    ]
    return pl.pallas_call(
        partial(back_body, nb, nseq, cc, 64, k == 1),
        grid=(ch // cc,),
        in_specs=head + [big, big, spec] + tables + [big] * 4,
        out_specs=[out, out, out_spec, pl.BlockSpec((1, cc, 2 * BLK), lambda i: (0, i, 0))],
        out_shape=[jax.ShapeDtypeStruct((1,) + a.shape[1:], bf16)] * 2
        + [
            jax.ShapeDtypeStruct((1, LAGS, ch, 2 * BIG), f32),
            jax.ShapeDtypeStruct((1, ch, 2 * BLK), f32),
        ],
        scratch_shapes=[
            pltpu.VMEM((size, BIG), bf16),
            pltpu.VMEM((size, 2 * BIG), f32),
            pltpu.VMEM((size, 2 * BIG), f32),
            pltpu.VMEM((size, 2 * BIG), bf16),
            pltpu.VMEM((size, BIG), f32),
        ],
        compiler_params=params(60),
        cost_estimate=cost(ch * 80e6, ch * nb * BLK * 16),
    )(tab, seq, a, gm, kh, wave, back, gg, y, dg, da)


def stack_pair(refs):
    return jnp.concatenate(
        [jnp.concatenate([ref[k, 0], ref[k, 1]], axis=1) for ref in refs for k in range(ref.shape[0])], axis=0
    )


def mul_body(count, more, start_ref, w_ref, *refs):
    out = nn(w_ref[...], stack_pair(refs[:count]))
    o_ref = refs[-1]
    for h in range(2):
        part = out[:, h * BLK : (h + 1) * BLK]
        if more:
            part = part + refs[count][h].astype(f32)
        o_ref[h] = part.astype(o_ref.dtype)


def mul_rows(w, arrays, start, many, dtype=bf16, extra=None):
    width, deep = w.shape
    ch = arrays[0].shape[2]
    count = len(arrays)
    out = pl.BlockSpec((2, width, BLK), lambda i, at: (i, 0, 0))
    return pl.pallas_call(
        partial(mul_body, count, extra is not None),
        grid_spec=pltpu.PrefetchScalarGridSpec(
            num_scalar_prefetch=1,
            grid=(many // 2,),
            in_specs=[pl.BlockSpec((width, deep), lambda i, at: (0, 0))]
            + [pl.BlockSpec((x.shape[0], 2, ch, BLK), lambda i, at: (0, at[0] + i, 0, 0)) for x in arrays]
            + ([] if extra is None else [out]),
            out_specs=out,
        ),
        out_shape=jax.ShapeDtypeStruct((many, width, BLK), dtype),
        compiler_params=params(40),
        cost_estimate=cost(2 * many * BLK * width * deep, 2 * many * BLK * (2 * width + deep)),
    )(start // 2, w, *arrays, *([] if extra is None else [extra]))


def outer_body(ch, many, cuts, parts, at_ref, *refs):
    step = pl.program_id(0)
    xs, gs = refs[:parts], refs[parts : 2 * parts]
    gp_refs, gpg_refs, mix_ref = refs[2 * parts : 2 * parts + 2], refs[2 * parts + 2 : 2 * parts + 4], refs[2 * parts + 4]
    outs = refs[2 * parts + 5 : 2 * parts + 5 + cuts]
    acc_s, x_s, g_s = refs[-3:]

    def fill(at):
        for b in range(many):
            x_s[:, b * BLK : (b + 1) * BLK] = xs[at][b]
            g_s[:, b * BLK : (b + 1) * BLK] = gs[at][b]

    if parts == 1:
        fill(0)
    else:
        for at in range(parts):

            @pl.when(step == at)
            def _(at=at):
                fill(at)

    def part(ref, k):
        return jnp.concatenate([ref[k, b] for b in range(many)], axis=1)

    @pl.when(step == 0)
    def _():
        acc_s[...] = jnp.zeros_like(acc_s)

    split = 4 * ch
    left = jnp.concatenate([part(ref, 0) for ref in (*gp_refs, *gpg_refs)], axis=0)
    acc_s[:, :split] += nt(x_s[...], left)
    acc_s[:, split:] += nt(g_s[...], jnp.concatenate([part(mix_ref, 0), part(mix_ref, 1)], axis=0))

    @pl.when(step == pl.num_programs(0) - 1)
    def _():
        deep = acc_s.shape[0] // cuts
        for cut in range(cuts):
            start = pl.multiple_of(at_ref[pl.num_programs(0) + cut] * deep, 8)
            outs[cut][...] = acc_s[pl.ds(start, deep), :].astype(bf16)


def outer_sums(order, cuts, xs, gs, gp, gpg, mix):
    width = xs[0].shape[1]
    _, nb, ch, _ = mix.shape
    many = 8
    parts = len(xs)
    if parts == 1:
        rows = pl.BlockSpec((many, width, BLK), lambda i, at: (i, 0, 0))
    else:
        rows = pl.BlockSpec((many, width, BLK), lambda i, at: (0, 0, 0), pipeline_mode=pl.Buffered(1))
    chan = pl.BlockSpec((2, many, ch, BLK), lambda i, at: (0, at[i], 0, 0))
    one = pl.BlockSpec((1, many, ch, BLK), lambda i, at: (0, at[i], 0, 0))
    tok = nb * BLK
    return pl.pallas_call(
        partial(outer_body, ch, many, cuts, parts),
        grid_spec=pltpu.PrefetchScalarGridSpec(
            num_scalar_prefetch=1,
            grid=(nb // many,),
            in_specs=[rows] * (2 * parts) + [one] * 4 + [chan],
            out_specs=[pl.BlockSpec((width // cuts, 6 * ch), lambda i, at: (0, 0))] * cuts,
            scratch_shapes=[
                pltpu.VMEM((width, 6 * ch), f32),
                pltpu.VMEM((width, many * BLK), bf16),
                pltpu.VMEM((width, many * BLK), bf16),
            ],
        ),
        out_shape=[jax.ShapeDtypeStruct((width // cuts, 6 * ch), bf16)] * cuts,
        compiler_params=params(60),
        cost_estimate=cost(12 * tok * width * ch, tok * (4 * width + 12 * ch)),
    )(order, *xs, *gs, *gp, *gpg, mix)


def join_body(parts, split, at_ref, *refs):
    head_ref, tail_ref, head_t_ref, tail_t_ref = refs[parts:]
    deep = refs[0].shape[0]
    for at in range(parts):
        rows = pl.ds(pl.multiple_of(at_ref[at] * deep, 16), deep)
        head_ref[rows, :] = refs[at][:, :split]
        tail_ref[rows, :] = refs[at][:, split:]
    head_t_ref[...] = head_ref[...].T
    tail_t_ref[...] = tail_ref[...].T


def join_weights(order, parts, split):
    count = len(parts)
    deep, wide = parts[0].shape
    rows = deep * count
    vmem = pl.BlockSpec(memory_space=pltpu.VMEM)
    return pl.pallas_call(
        partial(join_body, count, split),
        in_specs=[pl.BlockSpec(memory_space=pltpu.SMEM)] + [vmem] * count,
        out_specs=[vmem] * 4,
        out_shape=[
            jax.ShapeDtypeStruct(shape, bf16)
            for shape in ((rows, split), (rows, wide - split), (split, rows), (wide - split, rows))
        ],
        compiler_params=params(48),
        cost_estimate=cost(0, 6 * rows * wide),
    )(order, *parts)


def meet_body(axes, rank_ref, x_ref, chan_ref, norm_ref, got_ref, call_ref, nall_ref, send_s, *sems):
    xs_sem, xr_sem, cs_sem, cr_sem, ns_sem, nr_sem, own_sem = sems
    q, c, h, w = (lax.axis_index(name) for name in axes)
    rows = x_ref.shape[0]
    piece = rows // 8
    flat = ((2 * q + c) * 2 + h) * 2 + w

    def peer(bits):
        return (q ^ (bits // 8), c ^ (bits // 4 % 2), h ^ (bits // 2 % 2), w ^ (bits % 2))

    barrier = pltpu.get_barrier_semaphore()
    for bits in range(1, 32):
        pl.semaphore_signal(barrier, inc=1, device_id=peer(bits), device_id_type=pl.DeviceIdType.MESH)
    pl.semaphore_wait(barrier, 31)

    def remote(src, dst, send, recv, to):
        return pltpu.make_async_remote_copy(
            src_ref=src, dst_ref=dst, send_sem=send, recv_sem=recv, device_id=to, device_id_type=pl.DeviceIdType.MESH
        )

    nall_ref[flat] = norm_ref[...]

    def norm_copy(bits):
        return remote(norm_ref, nall_ref.at[flat], ns_sem.at[bits], nr_sem.at[bits], peer(bits))

    for bits in range(1, 32):
        norm_copy(bits).start()

    pieces = [(kq, kh) for kh in (1, 0) for kq in (1, 2, 3, 0)]
    spot = lax.broadcasted_iota(jnp.int32, (piece, rows), 0)

    def row_copy(kq, kh):
        at = 2 * kq + kh
        return remote(
            send_s.at[at], got_ref.at[2 * q + c], xs_sem.at[at], xr_sem.at[2 * kq + c], (q ^ kq, 1 - h, h ^ kh, w)
        )

    def own_copy():
        return pltpu.make_async_copy(send_s.at[0], got_ref.at[2 * q + c], own_sem.at[0])

    for kq, kh in pieces:
        chunk = 2 * (q ^ kq) + (h ^ kh)
        pick = jnp.where(spot + chunk * piece == rank_ref[...], 1.0, 0.0).astype(bf16)
        send_s[2 * kq + kh] = nn(pick, x_ref[...]).astype(bf16)
        if (kq, kh) == (0, 0):

            @pl.when(c != h)
            def _():
                own_copy().start()

            @pl.when(c == h)
            def _():
                row_copy(0, 0).start()

        else:
            row_copy(kq, kh).start()

    place = 2 * (1 - c) + w
    spot_c = 4 * c + 2 * h + w

    def chan_copy(kq, kh):
        at = 2 * kq + kh
        return remote(
            chan_ref, call_ref.at[spot_c], cs_sem.at[at], cr_sem.at[spot_c], (q ^ kq, 1 - q // 2, h ^ kh, q % 2)
        )

    def own_chan():
        return pltpu.make_async_copy(chan_ref, call_ref.at[spot_c], own_sem.at[1])

    for kq, kh in pieces:
        if (kq, kh) == (0, 0):

            @pl.when(place == q)
            def _():
                own_chan().start()

            @pl.when(place != q)
            def _():
                chan_copy(0, 0).start()

        else:
            chan_copy(kq, kh).start()

    for bits in range(1, 32):
        norm_copy(bits).wait()
    for at in range(8):

        @pl.when((c != h) & (at == c))
        def _():
            own_copy().wait()

        @pl.when(jnp.logical_not((c != h) & (at == c)))
        def _(at=at):
            remote(send_s.at[at], got_ref.at[at], xs_sem.at[at], xr_sem.at[at], peer(1)).wait_recv()

    for at in range(8):

        @pl.when((place == q) & (at == spot_c))
        def _():
            own_chan().wait()

        @pl.when(jnp.logical_not((place == q) & (at == spot_c)))
        def _(at=at):
            remote(chan_ref, call_ref.at[at], cs_sem.at[at], cr_sem.at[at], peer(1)).wait_recv()

    for kq, kh in pieces:
        if (kq, kh) == (0, 0):

            @pl.when(c == h)
            def _():
                row_copy(0, 0).wait_send()

            @pl.when(place != q)
            def _():
                chan_copy(0, 0).wait_send()

        else:
            row_copy(kq, kh).wait_send()
            chan_copy(kq, kh).wait_send()


def meet(axes, rank, x, chan, norm):
    rows, width = x.shape
    vmem = pl.BlockSpec(memory_space=pltpu.VMEM)
    sem = pltpu.SemaphoreType.DMA
    return pl.pallas_call(
        partial(meet_body, axes),
        in_specs=[vmem] * 4,
        out_specs=[vmem] * 3,
        out_shape=[
            jax.ShapeDtypeStruct((8, rows // 8, width), bf16),
            jax.ShapeDtypeStruct((8,) + chan.shape, f32),
            jax.ShapeDtypeStruct((32,) + norm.shape, f32),
        ],
        scratch_shapes=[pltpu.VMEM((8, rows // 8, width), bf16)]
        + [sem((8,)), sem((8,)), sem((8,)), sem((8,)), sem((32,)), sem((32,)), sem((2,))],
        compiler_params=pltpu.CompilerParams(collective_id=1, has_side_effects=True, vmem_limit_bytes=32 * MIB),
        cost_estimate=cost(2 * rows * rows * width, 100 * rows * width),
    )(rank.reshape(1, rows), x, chan, norm)


def sequence_tables(lens, nb):
    nseq = lens.shape[0]
    blocks = (lens + BLK - 1) // BLK
    start = jnp.cumsum(blocks) - blocks
    bigs = (blocks + 1) // 2
    first_big = jnp.cumsum(bigs) - bigs
    h = jnp.arange((nb + nseq) // 2, dtype=jnp.int32)
    owner = (h[:, None] >= first_big[None, :]).astype(jnp.int32).sum(axis=1) - 1
    mine = owner[:, None] == jnp.arange(nseq, dtype=jnp.int32)[None, :]

    def at_owner(values):
        return jnp.sum(jnp.where(mine, values[None, :], 0), axis=1)

    rel = h - at_owner(first_big)
    first = jnp.minimum(at_owner(start) + 2 * rel, nb - 1)
    whole = (2 * rel + 1 < at_owner(blocks)).astype(jnp.int32)
    tab = jnp.stack([first, whole]).astype(jnp.int32)
    seq = jnp.stack(
        [jnp.append(first_big, jnp.sum(blocks)), jnp.append(bigs, jnp.sum(bigs))]
    ).astype(jnp.int32)
    return tab, seq


def live_rows(lens, rows):
    slot = (lens + BLK - 1) // BLK * BLK
    begin = jnp.cumsum(slot) - slot
    pos = jnp.arange(rows, dtype=jnp.int32)
    inside = (pos[:, None] >= begin[None, :]) & (pos[:, None] < (begin + lens)[None, :])
    return jnp.sum(inside.astype(f32), axis=1)


def after(values):
    return lax.optimization_barrier(values)


def rank_of(keys):
    return jnp.sum((keys[None, :] < keys[:, None]).astype(jnp.int32), axis=1)


class Line:
    def __init__(self, n_dp, n_t):
        self.n_dp, self.n_t = n_dp, n_t
        self.axes = {"dp": n_dp, "tensor": n_t}
        self.both = ("dp", "tensor")
        self.cuts = 1

    def place_of_group(self):
        return lax.axis_index("tensor")

    def regroup(self, x):
        return x

    def gather_first(self, x):
        return [lax.all_gather(x, "tensor", axis=0, tiled=True)]

    def gather_last(self, x, got):
        return [(got[0], jnp.zeros((1,), jnp.int32))]

    def scatter_first(self, w, arrays, many):
        return [mul_rows(w, arrays, jnp.zeros((1,), jnp.int32), many * self.n_t)]

    def scatter_send(self, parts):
        return [lax.psum_scatter(parts[0], "tensor", scatter_dimension=0, tiled=True)]

    def scatter_own(self, w, arrays, many):
        return []

    def ungroup(self, x):
        return x

    def spread(self, x):
        return lax.all_to_all(x, "dp", split_axis=0, concat_axis=0, tiled=True)

    def order(self, pieces):
        return jnp.append(jnp.arange(pieces * self.n_t, dtype=jnp.int32), 0)

    def enter(self, rank, x, chan, norm):
        (sent,) = permute_to(rank, [x])
        return (self.spread(sent),) + self.gather_channels(chan, norm)

    def gather_channels(self, chan, norm):
        perm = [(f, (f % self.n_dp) * self.n_t + f // self.n_dp) for f in range(self.n_dp * self.n_t)]
        chan = lax.ppermute(chan, self.both, perm)
        norm = lax.all_gather(norm, self.both, axis=1, tiled=True)
        return lax.all_gather(chan[None], "dp", axis=0, tiled=True), norm

    def weights_first(self, pack):
        return [pack]

    def weights_send(self, packs):
        return [lax.all_gather(packs[0], "dp", axis=0, tiled=True)]

    def cut_order(self):
        return jnp.zeros((1,), jnp.int32)

    def grads_send(self, gw):
        return [lax.psum_scatter(gw[0], "dp", scatter_dimension=0, tiled=True)]

    def grads_last(self, parts):
        return parts[0].astype(f32)

    def scatter_channels(self, sums):
        return lax.psum_scatter(sums, "dp", scatter_dimension=0, tiled=True)

    def owner_channels(self, sums):
        perm = [((f % self.n_dp) * self.n_t + f // self.n_dp, f) for f in range(self.n_dp * self.n_t)]
        return lax.ppermute(sums, self.both, perm)

    def scatter_norm(self, sums):
        return lax.psum_scatter(sums, self.both, scatter_dimension=1, tiled=True)


class Pairs:
    def __init__(self, n_dp, n_t):
        self.quads = n_dp // 2
        self.axes = {"q": self.quads, "c": 2, "h": 2, "w": 2}
        self.both = ("q", "c", "h", "w")
        self.cuts = self.quads
        self.other = [(0, 1), (1, 0)]
        self.there = [(2 * c + h, 2 * (1 - h) + c) for c in range(2) for h in range(2)]
        self.back = [(b, a) for a, b in self.there]
        self.turned = [(2 * c + h, 2 * (1 - h) + 1 - c) for c in range(2) for h in range(2)]

    def flip(self, x, axis, bit=1):
        return lax.ppermute(x, axis, [(i, i ^ bit) for i in range(self.axes[axis])])

    def place_of_group(self):
        return 2 * (1 - lax.axis_index("c")) + lax.axis_index("w")

    def regroup(self, x):
        return lax.ppermute(x, ("c", "h"), self.there)

    def ungroup(self, x):
        return lax.ppermute(x, ("c", "h"), self.back)

    def spread(self, x):
        return lax.all_to_all(x, ("q", "c"), split_axis=0, concat_axis=0, tiled=True)

    def places(self):
        c, w = lax.axis_index("c"), lax.axis_index("w")
        return [2 * (1 - c) + w, 2 * c + w, 2 * (1 - c) + 1 - w, 2 * c + 1 - w]

    def starts(self, many):
        return [(place * many).astype(jnp.int32).reshape(1) for place in self.places()]

    def gather_first(self, x):
        return [self.flip(x, "c"), self.flip(x, "w")]

    def gather_last(self, x, got):
        beside, near = got
        return list(zip([x, beside, near, self.flip(near, "c")], self.starts(x.shape[0])))

    def scatter_first(self, w, arrays, many):
        _, beside, near, far = self.starts(many)
        first = mul_rows(w, arrays, far, many)
        give = self.flip(first, "c")
        beside, first = after((beside, first))
        second = mul_rows(w, arrays, beside, many)
        second, give = after((second, give))
        return [second, mul_rows(w, arrays, near, many, extra=give)]

    def scatter_send(self, parts):
        return [self.flip(parts[0], "c"), self.flip(parts[1], "w")]

    def scatter_own(self, w, arrays, many):
        return [mul_rows(w, arrays, self.starts(many)[0], many, dtype=f32)]

    def order(self, pieces):
        place = jnp.stack(self.places())[:, None] * pieces + jnp.arange(pieces)[None, :]
        return jnp.concatenate([place.reshape(-1).astype(jnp.int32), self.cut_order()])

    def steps(self):
        bit = self.quads // 2
        while bit:
            yield "q", bit
            bit //= 2
        yield "h", 1

    def spot(self):
        return 2 * lax.axis_index("q") + lax.axis_index("h")

    def enter(self, rank, x, chan, norm):
        small = norm.shape[1]
        norm = jnp.pad(norm, ((0, 5), (0, BLK - small)))
        got, chan, norm = meet(self.both, rank, x, chan, norm)
        norm = norm[:, :3, :small].transpose(1, 0, 2).reshape(3, -1)
        return got.reshape(x.shape), chan, norm

    def weights_first(self, pack):
        return [self.regroup(pack), lax.ppermute(pack, ("c", "h"), self.turned)]

    def weights_send(self, packs):
        h = lax.axis_index("h")
        first, second = packs
        pair = jnp.concatenate([jnp.where(h == 0, first, second), jnp.where(h == 0, second, first)], axis=0)
        return [pair] + [self.flip(pair, "q", bit) for bit in range(1, self.quads)]

    def grads_send(self, gw):
        return [gw[0]] + [self.flip(gw[bit], "q", bit) for bit in range(1, self.quads)]

    def grads_last(self, parts):
        total = parts[0].astype(f32)
        for part in parts[1:]:
            total = total + part.astype(f32)
        total = total.astype(bf16)
        half = total.shape[0] // 2
        h = lax.axis_index("h")
        first = jnp.where(h == 0, total[:half], total[half:])
        second = jnp.where(h == 0, total[half:], total[:half])
        return self.ungroup(first).astype(f32) + lax.ppermute(second, ("c", "h"), self.turned).astype(f32)

    def cut_order(self):
        return (lax.axis_index("q") ^ jnp.arange(self.quads)).astype(jnp.int32)

    def scatter_channels(self, sums):
        count = 2 * self.quads
        rows, wide = sums.shape[0] // count, sums.shape[1]
        part = jnp.pad(sums, ((0, 0), (0, -wide % 8))).reshape(count, -1, BLK)
        part = lax.all_to_all(part, ("q", "h"), split_axis=0, concat_axis=0, tiled=True)
        return jnp.sum(part, axis=0).reshape(rows, -1)[:, :wide]

    def owner_channels(self, sums):
        count = 2 * self.quads
        perm = []
        for f in range(4 * count):
            place, at = f // count, f % count
            q, h, c, w = at // 2, at % 2, 1 - place // 2, place % 2
            perm.append((((2 * q + c) * 2 + h) * 2 + w, f))
        return lax.ppermute(sums, self.both, perm)

    def scatter_norm(self, sums):
        count = 8 * self.quads
        part = sums.reshape(3, count, -1).transpose(1, 0, 2)
        wide = part.shape[2]
        part = jnp.pad(part, ((0, 0), (0, 5), (0, BLK - wide)))
        part = lax.all_to_all(part, self.both, split_axis=0, concat_axis=0, tiled=True)
        return jnp.sum(part, axis=0)[:3, :wide]


def local(
    net, wave, tokens, cotangent, source, target, lengths, ln_gain, ln_bias, w_fwd, b_fwd, w_bwd, b_bwd,
    w_gate, b_gate, w_out, b_out, log_dt, log_rate, ssm_b, ssm_c, ssm_d,
):
    rows, width = tokens.shape
    many = rows // BLK
    n_t = net.n_t
    group = rows * n_t
    nb = group // BLK
    ch = w_fwd.shape[1]
    back = (wave.T / BIG).astype(bf16)
    wave = wave.astype(bf16)

    def lanes(column):
        return jnp.broadcast_to(column[..., None], column.shape + (BLK,))

    def decays(log_dt, log_rate, ssm_b):
        rate = jnp.exp(log_rate)
        ld = -jnp.exp(log_dt)[..., None] * rate
        return rate, ld, (1.0 - jnp.exp(ld)) / rate * ssm_b

    rank = rank_of(target)
    sender = source // group
    place = rank_of(sender * rows + jnp.arange(rows, dtype=jnp.int32))
    pack = jnp.concatenate(
        [w_fwd, w_bwd, w_gate.reshape(-1, 2 * ch), w_out.transpose(2, 0, 1).reshape(-1, 2 * ch)], axis=1
    )
    table = net.regroup(jnp.concatenate([place, lengths[0]]))
    rate, ld, drive = decays(log_dt, log_rate, ssm_b)
    own = b_fwd.shape[0]
    small = jnp.concatenate([ssm_d, b_fwd[None], b_bwd[None], b_gate])
    chan = jnp.concatenate(
        [
            (ld * log2e).reshape(own, 2 * STATE),
            (ssm_c * drive).reshape(own, 2 * STATE),
            jnp.pad(small, ((0, -(2 * own + 6) % 8 + 0), (0, 2 * STATE - own))),
        ]
    )
    got_x, chan_all, norm_all = net.enter(rank, tokens, chan, jnp.stack([ln_gain, ln_bias, b_out]))
    got_x, chan_all, norm_all, table, cotangent, pack = after((got_x, chan_all, norm_all, table, cotangent, pack))

    packs = net.weights_first(pack)
    place, lens = table[:rows], table[rows:]
    gain = lanes(norm_all[0])
    shift = lanes(norm_all[1])
    small = chan_all[:, 2 * own : 2 * own + 6, :own].transpose(1, 0, 2).reshape(6, ch)

    def pairs(at):
        both = chan_all[:, at : at + own].reshape(-1, 2, own // 2, 2 * STATE)
        return both.transpose(1, 0, 2, 3).reshape(2, ch // 2, 2 * STATE)

    ld_pairs = pairs(0)
    w_pairs = pairs(own)
    skip = lanes(small[0:2])
    live = live_rows(lens, group)
    live_own = lax.dynamic_slice_in_dim(live, net.place_of_group() * rows, rows, 0).reshape(many, 1, BLK)
    live = live.reshape(nb // 2, 1, BIG)
    tab, seq = sequence_tables(lens, nb)

    xt, xd = deal_x(place, got_x, gain, shift)
    xt, cotangent, packs, ld_pairs, w_pairs, skip = after((xt, cotangent, packs, ld_pairs, w_pairs, skip))
    x_got = net.gather_first(xt)
    w_parts = net.weights_send(packs)
    (sent_g,) = permute_to(rank, [cotangent])
    got_g = net.spread(sent_g)
    kh = spectra(ld_pairs, w_pairs, skip, wave)
    w_parts, x_got, kh, norm_all, small = after((w_parts, x_got, kh, norm_all, small))
    bias_in = lanes(small[2:6].reshape(-1))
    bias_out = lanes(norm_all[2])
    w_in, w_back, w_in_t, w_back_t = join_weights(net.cut_order(), w_parts, 4 * ch)
    xs = net.gather_last(xt, x_got)
    got_g = net.regroup(got_g)
    kept = None
    for part, start in xs:
        kept = project(part, start, nb, live, w_in_t, bias_in, kept)
    kept, got_g = after((kept, got_g))
    a, da, gg, dg = kept
    gt, gd, g_bias_out = deal_g(place, got_g, live_own)
    gt, a = after((gt, a))
    g_got = net.gather_first(gt)
    y, mix = ssm_scan(tab, seq, a, kh, wave, back, gg)
    g_got, y, mix = after((g_got, y, mix))
    gs = net.gather_last(gt, g_got)
    kept = None
    for part, start in gs:
        kept = gate_grad(part, start, nb, w_back_t, kept)
    (gm,) = kept
    branch = net.scatter_first(w_back, [mix], many)
    branch, gm = after((branch, gm))

    branch = net.scatter_send(branch)
    branch = net.scatter_own(w_back, [mix], many) + branch
    first = ssm_back(0, tab, seq, a, gm, kh, wave, back, gg, y, dg, da)
    branch, first, a = after((branch, first, a))
    sent_out = layer_rows(place, branch, xd, live_own, bias_out)
    sent_out, a = after((sent_out, a))
    sent_out = net.ungroup(sent_out)
    second = ssm_back(1, tab, seq, a, gm, kh, wave, back, gg, y, dg, da)
    sent_out, first, second = after((sent_out, first, second))
    gpg, gp, gh, bsum = zip(first, second)
    sent_out = net.spread(sent_out)
    back_list = [gp[0], gp[1], gpg[0], gpg[1]]
    g_normed = net.scatter_first(w_in, back_list, many)
    g_normed, back_list, mix = after((g_normed, back_list, mix))
    gp, gpg = back_list[:2], back_list[2:]
    g_normed = net.scatter_send(g_normed)
    g_normed = net.scatter_own(w_in, back_list, many) + g_normed
    gw = outer_sums(net.order(many // 8), net.cuts, [part for part, _ in xs], [part for part, _ in gs], gp, gpg, mix)
    g_normed, gw, gh, sent_out = after((g_normed, gw, gh, sent_out))
    sent_in, norm_sums = input_rows(place, g_normed, xd, gd, gain)
    sent_in, gh, gw, norm_sums, sent_out, bsum = after((sent_in, gh, gw, norm_sums, sent_out, bsum))
    sent_in = net.ungroup(sent_in)
    gw = net.grads_send(gw)
    s0, s1, g0 = [jnp.concatenate(part) for part in zip(*[moments(k, ld_pairs, gh[k], back) for k in range(2)])]
    layer_out = permute_from(rank, sent_out)

    s0 = s0.reshape(2, ch, STATE)
    s1 = s1.reshape(2, ch, STATE)
    bsum = jnp.concatenate(bsum)
    gb_gate = jnp.sum(bsum[:, :, :BLK], axis=2)
    gb_in = jnp.sum(bsum[:, :, BLK:], axis=2)
    sums = jnp.concatenate(
        [s0[0], s0[1], s1[0], s1[1], jnp.concatenate([g0[:, :, 0], gb_gate, gb_in], axis=0).T], axis=1
    )
    sums = net.scatter_channels(sums)
    norm_sums = net.scatter_norm(jnp.sum(jnp.concatenate([norm_sums, g_bias_out[None]], axis=0), axis=2))
    sent_in, gw, sums, norm_sums, layer_out = after((sent_in, gw, sums, norm_sums, layer_out))
    in_grad = permute_from(rank, net.spread(sent_in))
    gw = net.grads_last(gw)
    sums = net.owner_channels(sums)
    s0 = jnp.stack([sums[:, :STATE], sums[:, STATE : 2 * STATE]])
    s1 = jnp.stack([sums[:, 2 * STATE : 3 * STATE], sums[:, 3 * STATE : 4 * STATE]])
    tail = sums[:, 4 * STATE :].T
    step = jnp.exp(log_dt)[..., None]
    g_c = s0 * drive
    g_drive = s0 * ssm_c
    g_b = g_drive * (1.0 - jnp.exp(ld)) / rate
    g_ld = s1 * ssm_c * drive - g_drive * ssm_b / rate * jnp.exp(ld)
    g_rate = -g_drive * drive / rate - g_ld * step
    g_dt = jnp.sum(g_ld * ld, axis=2)
    return (
        layer_out,
        in_grad,
        norm_sums[0],
        norm_sums[1],
        gw[:, :ch],
        tail[4],
        gw[:, ch : 2 * ch],
        tail[5],
        gw[:, 2 * ch : 4 * ch].reshape(-1, 2, ch),
        tail[2:4],
        gw[:, 4 * ch :].T.reshape(2, ch, -1),
        norm_sums[2],
        g_dt,
        g_rate * rate,
        g_b,
        g_c,
        tail[0:2],
    )


def solution(mesh):
    n_dp, n_t = mesh.shape["dp"], mesh.shape["tensor"]
    if n_t == 4 and n_dp == 8:
        net = Pairs(n_dp, n_t)
        dp, tensor = ("q", "c"), ("h", "w")
    else:
        net = Line(n_dp, n_t)
        dp, tensor = ("dp",), ("tensor",)
    net.n_t = n_t
    mesh = jax.sharding.Mesh(mesh.devices.reshape(tuple(net.axes.values())), tuple(net.axes))
    both = P(dp + tensor)
    rows = P(dp + tensor, None)
    pair = P(None, dp + tensor)
    state = P(None, dp + tensor, None)
    proj = P(dp, tensor)
    gate = P(dp, None, tensor)
    out = P(None, tensor, dp)
    wave = wave_table()

    def run(*args):
        return local(net, jnp.asarray(wave), *args)

    return jax.shard_map(
        run,
        mesh=mesh,
        in_specs=(
            rows, rows, both, both, P(dp, None), both, both, proj, both, proj, both, gate, pair, out, both,
            pair, state, state, state, pair,
        ),
        out_specs=(
            rows, rows, both, both, proj, both, proj, both, gate, pair, out, both, pair, state, state, state, pair,
        ),
        check_vma=False,
    )
```

```python
from functools import partial

import jax
import jax.numpy as jnp
import numpy as np
from jax import lax
from jax.experimental import pallas as pl
from jax.experimental.pallas import tpu as pltpu
from jax.sharding import PartitionSpec as P

BLK = 128
BIG = 256
MOST = 2048
LAGS = MOST // BIG
STATE = 64
epsilon = 1e-05
log2e = 1.4426950408889634
f32 = jnp.float32
bf16 = jnp.bfloat16
MIB = 2**20


def nn(a, b):
    return lax.dot_general(a, b, (((1,), (0,)), ((), ())), preferred_element_type=f32)


def nt(a, b):
    return lax.dot_general(a, b, (((1,), (1,)), ((), ())), preferred_element_type=f32)


def params(limit):
    return pltpu.CompilerParams(vmem_limit_bytes=60 * MIB)


def cost(flops, moved, trans=0):
    scale = 0.05
    return pl.CostEstimate(
        flops=int(scale * flops), bytes_accessed=int(scale * moved), transcendentals=int(scale * trans)
    )


def halves(x):
    high = x.astype(bf16)
    return high, (x - high.astype(f32)).astype(bf16)


def wave_table():
    pos = np.arange(BIG)[:, None]
    freq = np.arange(BIG)[None, :]
    angle = 2 * np.pi * ((2 * freq + 1) * pos % (4 * BIG)) / (4 * BIG)
    return np.concatenate([np.cos(angle), np.sin(angle)], 1).astype(np.float32)


def chunk_of(channels, most):
    best = 16
    for size in range(16, most + 1, 16):
        if channels % size == 0:
            best = size
    return best


def permute_row_body(count, rank_ref, *refs):
    rows = rank_ref.shape[1]
    spot = lax.broadcasted_iota(jnp.int32, (rows, rows), 0)
    pick = jnp.where(spot == rank_ref[...], 1.0, 0.0).astype(bf16)
    for at in range(count):
        refs[count + at][...] = nn(pick, refs[at][...]).astype(bf16)


def permute_to(rank, arrays):
    rows, width = arrays[0].shape
    count = len(arrays)
    return pl.pallas_call(
        partial(permute_row_body, count),
        out_shape=[jax.ShapeDtypeStruct((rows, width), bf16)] * count,
        compiler_params=params(48),
        cost_estimate=cost(2 * count * rows * rows * width, 4 * count * rows * width),
    )(rank.reshape(1, rows), *arrays)


def permute_col_body(rank_ref, x_ref, o_ref):
    rows = x_ref.shape[0]
    spot = lax.broadcasted_iota(jnp.int32, (rows, rows), 1)
    pick = jnp.where(spot == rank_ref[...], 1.0, 0.0).astype(bf16)
    o_ref[...] = nn(pick, x_ref[...]).astype(bf16)


def permute_from(rank, x):
    rows, width = x.shape
    return pl.pallas_call(
        permute_col_body,
        out_shape=jax.ShapeDtypeStruct((rows, width), bf16),
        compiler_params=params(48),
        cost_estimate=cost(2 * rows * rows * width, 4 * rows * width),
    )(rank.reshape(rows, 1), x)


def pick_rows(place_ref, x_ref):
    spot = lax.broadcasted_iota(jnp.int32, (BLK, x_ref.shape[0]), 1)
    pick = jnp.where(spot == place_ref[...], 1.0, 0.0).astype(bf16)
    return nn(pick, x_ref[...]).T


def deal_x_body(place_ref, x_ref, gain_ref, shift_ref, xt_ref, xd_ref):
    x = pick_rows(place_ref, x_ref)
    xd_ref[0] = x.astype(bf16)
    centred = x - jnp.mean(x, axis=0, keepdims=True)
    inv_std = lax.rsqrt(jnp.mean(centred * centred, axis=0, keepdims=True) + epsilon)
    xt_ref[0] = (centred * inv_std * gain_ref[...] + shift_ref[...]).astype(bf16)


def deal_g_body(place_ref, g_ref, live_ref, gt_ref, gd_ref, bo_ref):
    g = pick_rows(place_ref, g_ref)
    gd_ref[0] = g.astype(bf16)
    g = g * live_ref[0]
    gt_ref[0] = g.astype(bf16)

    @pl.when(pl.program_id(0) == 0)
    def _():
        bo_ref[...] = jnp.zeros_like(bo_ref)

    bo_ref[...] += g


def deal_specs(rows, width):
    place = pl.BlockSpec((BLK, 1), lambda i: (i, 0))
    whole = pl.BlockSpec((rows, width), lambda i: (0, 0))
    wide = pl.BlockSpec((width, BLK), lambda i: (0, 0))
    out = pl.BlockSpec((1, width, BLK), lambda i: (i, 0, 0))
    return place, whole, wide, out


def deal_x(place, x, gain, shift):
    rows, width = x.shape
    blocks = rows // BLK
    spot, whole, wide, out = deal_specs(rows, width)
    return pl.pallas_call(
        deal_x_body,
        grid=(blocks,),
        in_specs=[spot, whole, wide, wide],
        out_specs=[out, out],
        out_shape=[jax.ShapeDtypeStruct((blocks, width, BLK), bf16)] * 2,
        compiler_params=params(40),
        cost_estimate=cost(2 * rows * rows * width, 6 * rows * width),
    )(place.reshape(rows, 1), x, gain, shift)


def deal_g(place, g, live):
    rows, width = g.shape
    blocks = rows // BLK
    spot, whole, wide, out = deal_specs(rows, width)
    return pl.pallas_call(
        deal_g_body,
        grid=(blocks,),
        in_specs=[spot, whole, pl.BlockSpec((1, 1, BLK), lambda i: (i, 0, 0))],
        out_specs=[out, out, wide],
        out_shape=[jax.ShapeDtypeStruct((blocks, width, BLK), bf16)] * 2
        + [jax.ShapeDtypeStruct((width, BLK), f32)],
        compiler_params=params(40),
        cost_estimate=cost(2 * rows * rows * width, 6 * rows * width),
    )(place.reshape(rows, 1), g, live)


def send_back(place_ref, out_s, o_ref):
    rows = out_s.shape[0]
    spot = lax.broadcasted_iota(jnp.int32, (rows, rows), 0)
    pick = jnp.where(spot == place_ref[...], 1.0, 0.0).astype(bf16)
    o_ref[...] = nn(pick, out_s[...]).astype(bf16)


def total(refs, at):
    value = refs[0][at].astype(f32)
    for ref in refs[1:]:
        value = value + ref[at].astype(f32)
    return value


def layer_body(place_ref, xd_ref, live_ref, bias_ref, *refs):
    o_ref, out_s = refs[-2:]
    for at in range(xd_ref.shape[0]):
        y = xd_ref[at].astype(f32) + live_ref[at] * (total(refs[:-2], at) + bias_ref[...])
        out_s[at * BLK : (at + 1) * BLK, :] = y.T.astype(bf16)
    send_back(place_ref, out_s, o_ref)


def layer_rows(place, parts, xd, live, bias):
    blocks, width, _ = xd.shape
    rows = blocks * BLK
    return pl.pallas_call(
        layer_body,
        out_shape=jax.ShapeDtypeStruct((rows, width), bf16),
        scratch_shapes=[pltpu.VMEM((rows, width), bf16)],
        compiler_params=params(48),
        cost_estimate=cost(2 * rows * rows * width, 6 * rows * width),
    )(place.reshape(1, rows), xd, live, bias, *parts)


def input_body(place_ref, xd_ref, gd_ref, gain_ref, *refs):
    o_ref, sums_ref, out_s = refs[-3:]
    g_gain = jnp.zeros(gain_ref.shape, f32)
    g_shift = jnp.zeros(gain_ref.shape, f32)
    for at in range(xd_ref.shape[0]):
        x = xd_ref[at].astype(f32)
        centred = x - jnp.mean(x, axis=0, keepdims=True)
        inv_std = lax.rsqrt(jnp.mean(centred * centred, axis=0, keepdims=True) + epsilon)
        x_hat = centred * inv_std
        g = total(refs[:-3], at)
        g_gain = g_gain + g * x_hat
        g_shift = g_shift + g
        hat = g * gain_ref[...]
        back = inv_std * (
            hat
            - jnp.mean(hat, axis=0, keepdims=True)
            - x_hat * jnp.mean(hat * x_hat, axis=0, keepdims=True)
        )
        out_s[at * BLK : (at + 1) * BLK, :] = (gd_ref[at].astype(f32) + back).T.astype(bf16)
    sums_ref[0] = g_gain
    sums_ref[1] = g_shift
    send_back(place_ref, out_s, o_ref)


def input_rows(place, parts, xd, gd, gain):
    blocks, width, _ = xd.shape
    rows = blocks * BLK
    return pl.pallas_call(
        input_body,
        out_shape=[
            jax.ShapeDtypeStruct((rows, width), bf16),
            jax.ShapeDtypeStruct((2, width, BLK), f32),
        ],
        scratch_shapes=[pltpu.VMEM((rows, width), bf16)],
        compiler_params=params(48),
        cost_estimate=cost(2 * rows * rows * width, 8 * rows * width),
    )(place.reshape(1, rows), xd, gd, gain, *parts)


def project_body(ch, many, start_ref, x_ref, live_ref, wt_ref, bias_ref, *refs):
    a_ref, da_ref, gg_ref, dg_ref = refs[-4:]
    x = jnp.concatenate([x_ref[0], x_ref[1]], axis=1)
    live = live_ref[0]
    root = 0.7978845608028654
    step = 64 if ch % 128 else 128

    def act(pre):
        square = pre * pre
        rise = 0.5 + 0.5 * jnp.tanh(pre * (root + (0.044715 * root) * square))
        value = pre * rise
        slope = rise + rise * (pre - value) * (2.0 * root + (6.0 * 0.044715 * root) * square)
        return value, slope

    def put(ref, k, at, value):
        value = value.astype(bf16)
        ref[k, 0, at, :] = value[:, :BLK]
        ref[k, 1, at, :] = value[:, BLK:]

    for k in range(2):
        for first, value_ref, slope_ref in ((k * ch, a_ref, da_ref), ((2 + k) * ch, gg_ref, dg_ref)):
            for at in range(0, ch, step):
                rows = pl.ds(first + at, step)
                bias = bias_ref[rows, :]
                pre = nn(wt_ref[rows, :], x) + jnp.concatenate([bias, bias], axis=1)
                value, slope = act(pre)
                if value_ref is a_ref:
                    value, slope = live * value, live * slope
                put(value_ref, k, pl.ds(at, step), value)
                put(slope_ref, k, pl.ds(at, step), slope)


def chained(body, grid, in_specs, out_specs, shapes, scratch, limit, estimate, start, operands, kept):
    kept = [] if kept is None else list(kept)
    specs = list(in_specs) + [pl.BlockSpec(memory_space=pl.ANY)] * len(kept)
    first = 1 + len(operands)
    return pl.pallas_call(
        body,
        grid_spec=pltpu.PrefetchScalarGridSpec(
            num_scalar_prefetch=1, grid=grid, in_specs=specs, out_specs=out_specs, scratch_shapes=scratch
        ),
        out_shape=shapes,
        input_output_aliases={first + at: at for at in range(len(kept))},
        compiler_params=params(limit),
        cost_estimate=estimate,
    )(start, *operands, *kept)


def project(xt, start, nb, live, wt, bias, kept):
    many, width, _ = xt.shape
    ch = wt.shape[0] // 4
    out = pl.BlockSpec((2, 2, ch, BLK), lambda i, at: (0, at[0] + i, 0, 0))
    tok = many * BLK
    return chained(
        partial(project_body, ch, many),
        (many // 2,),
        [
            pl.BlockSpec((2, width, BLK), lambda i, at: (i, 0, 0)),
            pl.BlockSpec((1, 1, BIG), lambda i, at: (at[0] + i, 0, 0)),
            pl.BlockSpec((4 * ch, width), lambda i, at: (0, 0)),
            pl.BlockSpec((4 * ch, BLK), lambda i, at: (0, 0)),
        ],
        [out] * 4,
        [jax.ShapeDtypeStruct((2, nb, ch, BLK), bf16)] * 4,
        [],
        48,
        cost(8 * tok * width * ch, 2 * tok * width + 16 * tok * ch, 4 * tok * ch),
        start // 2,
        [xt, live, wt, bias],
        kept,
    )


def gate_grad_body(ch, parts, at_ref, *refs):
    wt_ref, o_ref = refs[parts:]
    steps = pl.num_programs(0) // parts

    def work(g_ref):
        gm = nn(wt_ref[...], jnp.concatenate([g_ref[0], g_ref[1]], axis=1)).astype(bf16)
        for k in range(2):
            for h in range(2):
                o_ref[k, h] = gm[k * ch : (k + 1) * ch, h * BLK : (h + 1) * BLK]

    for part in range(parts):

        @pl.when(pl.program_id(0) // steps == part)
        def _(part=part):
            work(refs[part])


def gate_grad(gs, nb, wt):
    parts = len(gs)
    many, width, _ = gs[0][0].shape
    steps = many // 2
    ch = wt.shape[0] // 2
    tok = nb * BLK

    def rows(part):
        return pl.BlockSpec((2, width, BLK), lambda i, at: (jnp.clip(i - part * steps, 0, steps - 1), 0, 0))

    order = jnp.concatenate([start // 2 for _, start in gs]).astype(jnp.int32)
    return pl.pallas_call(
        partial(gate_grad_body, ch, parts),
        grid_spec=pltpu.PrefetchScalarGridSpec(
            num_scalar_prefetch=1,
            grid=(parts * steps,),
            in_specs=[rows(part) for part in range(parts)] + [pl.BlockSpec((2 * ch, width), lambda i, at: (0, 0))],
            out_specs=pl.BlockSpec((2, 2, ch, BLK), lambda i, at: (0, at[i // steps] + i % steps, 0, 0)),
        ),
        out_shape=jax.ShapeDtypeStruct((2, nb, ch, BLK), bf16),
        compiler_params=params(40),
        cost_estimate=cost(4 * tok * width * ch, 2 * tok * width + 4 * tok * ch),
    )(order, *[part for part, _ in gs], wt)


def spectra_body(cc, ld_ref, w_ref, d_ref, wave_ref, kh_ref, k_s):
    t = lax.broadcasted_iota(jnp.int32, (BLK, BLK), 0).astype(f32)
    block = lax.broadcasted_iota(jnp.int32, (2 * LAGS, BLK), 0).astype(f32) * float(BLK)
    low = lax.broadcasted_iota(jnp.int32, (2 * LAGS, BLK), 1) < STATE
    count = 2 * LAGS

    def one(p, carry):
        ld = ld_ref[0, pl.ds(p, 1), :]
        decay = jnp.exp2(t * ld)
        scale = w_ref[0, pl.ds(p, 1), :] * jnp.exp2(block * ld)
        lhs = jnp.concatenate([jnp.where(low, scale, 0.0), jnp.where(low, 0.0, scale)], axis=0)
        lhs_high, lhs_low = halves(lhs)
        k = nt(jnp.concatenate([lhs_high, lhs_low], axis=0), decay.astype(bf16))
        k = k[0 : 2 * count] + k[2 * count : 4 * count]
        k_s[pl.ds(2 * p, count, stride=cc), :] = k[0:count]
        k_s[pl.ds(2 * p + 1, count, stride=cc), :] = k[count : 2 * count]
        return carry

    lax.fori_loop(0, cc // 2, one, 0, unroll=16)
    sign = jnp.where(lax.broadcasted_iota(jnp.int32, (cc, BIG), 1) % 2 == 0, 1.0, -1.0)
    before = None
    for big in range(LAGS):
        rows = jnp.concatenate(
            [k_s[pl.ds(2 * big * cc, cc), :], k_s[pl.ds((2 * big + 1) * cc, cc), :]], axis=1
        )
        high, rest = halves(rows)
        x = nn(high, wave_ref[...]) + nn(rest, wave_ref[...])
        xc, xs = x[:, :BIG], x[:, BIG:]
        if big == 0:
            kh_ref[0, 0, :, :BIG] = xc + d_ref[0][:, 0:1]
            kh_ref[0, 0, :, BIG:] = xs
        else:
            kh_ref[0, big, :, :BIG] = xc + sign * before[1]
            kh_ref[0, big, :, BIG:] = xs - sign * before[0]
        before = (xc, xs)


def spectra(ld, w, d, wave):
    ch = 2 * ld.shape[1]
    cc = chunk_of(ch, 128)
    return pl.pallas_call(
        partial(spectra_body, cc),
        grid=(2, ch // cc),
        in_specs=[pl.BlockSpec((1, cc // 2, BLK), lambda k, i: (k, i, 0))] * 2
        + [
            pl.BlockSpec((1, cc, BLK), lambda k, i: (k, i, 0)),
            pl.BlockSpec((BIG, 2 * BIG), lambda k, i: (0, 0)),
        ],
        out_specs=pl.BlockSpec((1, LAGS, cc, 2 * BIG), lambda k, i: (k, 0, i, 0)),
        out_shape=jax.ShapeDtypeStruct((2, LAGS, ch, 2 * BIG), f32),
        scratch_shapes=[pltpu.VMEM((2 * LAGS * cc, BLK), f32)],
        compiler_params=params(40),
        cost_estimate=cost(2 * ch * 40e6, 2 * ch * LAGS * 2 * BIG * 4),
    )(ld, w, d, wave)


def moments_body(cc, ld_ref, gh_ref, back_ref, s0_ref, s1_ref, g0_ref, g_s):
    sign = jnp.where(lax.broadcasted_iota(jnp.int32, (cc, BIG), 1) % 2 == 0, 1.0, -1.0)
    count = 2 * LAGS
    for big in range(LAGS):
        c = gh_ref[0, big, :, :BIG]
        s = gh_ref[0, big, :, BIG:]
        if big < LAGS - 1:
            c, s = c - sign * gh_ref[0, big + 1, :, BIG:], s + sign * gh_ref[0, big + 1, :, :BIG]
        high, rest = halves(jnp.concatenate([c, s], axis=1))
        g = nn(high, back_ref[...]) + nn(rest, back_ref[...])
        g_s[pl.ds(2 * big * cc, cc), :] = g[:, :BLK]
        g_s[pl.ds((2 * big + 1) * cc, cc), :] = g[:, BLK:]
        if big == 0:
            g0_ref[0] = g[:, :BLK]
    t = lax.broadcasted_iota(jnp.int32, (BLK, BLK), 0).astype(f32)
    lane = lax.broadcasted_iota(jnp.int32, (count, BLK), 1)
    lag = lane.astype(f32)
    block = lax.broadcasted_iota(jnp.int32, (count, BLK), 0).astype(f32) * float(BLK)
    low = lane < STATE

    def one(p, carry):
        ld = ld_ref[0, pl.ds(p, 1), :]
        decay = jnp.exp2(t * ld).astype(bf16)
        far = jnp.exp2(block * ld)
        ga = g_s[pl.ds(2 * p, count, stride=cc), :]
        gb = g_s[pl.ds(2 * p + 1, count, stride=cc), :]
        high, rest = halves(jnp.concatenate([ga, gb, ga * lag, gb * lag], axis=0))
        m = nn(jnp.concatenate([high, rest], axis=0), decay)
        m = m[0 : 4 * count] + m[4 * count : 8 * count]
        m0 = jnp.where(low, m[0:count], m[count : 2 * count])
        m1 = jnp.where(low, m[2 * count : 3 * count], m[3 * count : 4 * count]) + block * m0
        s0_ref[0, pl.ds(p, 1), :] = jnp.sum(far * m0, axis=0, keepdims=True)
        s1_ref[0, pl.ds(p, 1), :] = jnp.sum(far * m1, axis=0, keepdims=True)
        return carry

    lax.fori_loop(0, cc // 2, one, 0, unroll=16)


def moments(k, ld, gh, back):
    ch = gh.shape[2]
    cc = chunk_of(ch, 128)
    row = pl.BlockSpec((1, cc // 2, BLK), lambda i: (0, i, 0))
    return pl.pallas_call(
        partial(moments_body, cc),
        grid=(ch // cc,),
        in_specs=[
            pl.BlockSpec((1, cc // 2, BLK), lambda i: (k, i, 0)),
            pl.BlockSpec((1, LAGS, cc, 2 * BIG), lambda i: (0, 0, i, 0)),
            pl.BlockSpec((2 * BIG, BIG), lambda i: (0, 0)),
        ],
        out_specs=[row, row, pl.BlockSpec((1, cc, BLK), lambda i: (0, i, 0))],
        out_shape=[jax.ShapeDtypeStruct((1, ch // 2, BLK), f32)] * 2
        + [jax.ShapeDtypeStruct((1, ch, BLK), f32)],
        scratch_shapes=[pltpu.VMEM((2 * LAGS * cc, BLK), f32)],
        compiler_params=params(40),
        cost_estimate=cost(ch * 40e6, ch * LAGS * 2 * BIG * 4),
    )(ld, gh, back)


def load_pieces(nb, pieces, cc, tab_ref, block, in_s, wave_ref, dst):
    for h in range(pieces):
        first = tab_ref[0, h]
        whole = tab_ref[1, h].astype(f32)
        in_s[pl.ds(h * cc, cc), 0:BLK] = block(first).astype(bf16)
        in_s[pl.ds(h * cc, cc), BLK:BIG] = (block(jnp.minimum(first + 1, nb - 1)) * whole).astype(bf16)
    for h in range(pieces):
        at = pl.ds(h * cc, cc)
        dst[at, :] = nn(in_s[at, :], wave_ref[...])


def over_pieces(nseq, cc, rg, seq_ref, piece):
    def group(r, carry):
        off = pl.multiple_of(r * rg, rg)
        for s in range(nseq):
            base = seq_ref[0, s]
            count = seq_ref[1, s]

            def outer(i, carry):
                piece(i, count, base, off)
                return carry

            lax.fori_loop(0, count, outer, 0)
        return carry

    lax.fori_loop(0, cc // rg, group, 0)


def scan_body(
    nb, nseq, cc, rg, tab_ref, seq_ref, a_ref, kh_ref, wave_ref, back_ref, gg_ref, y_ref, mix_ref, in_s, ah_s, yh_s, y_s
):
    pieces = (nb + nseq) // 2
    load_pieces(nb, pieces, cc, tab_ref, lambda b: a_ref[0, b].astype(f32), in_s, wave_ref, ah_s)
    zero = jnp.zeros((rg, BIG), f32)

    def products(flip):
        def piece(i, count, base, off):
            def inner(j, acc):
                yc, ys = acc
                other = (base + i + j) if flip else (base + i - j)
                m = pl.ds(pl.multiple_of(other * cc + off, rg), rg)
                rows = pl.ds(off, rg)
                ac = ah_s[m, :BIG]
                as_ = ah_s[m, BIG:]
                kc = kh_ref[0, j, rows, :BIG]
                ks = kh_ref[0, j, rows, BIG:]
                if flip:
                    return (yc + kc * ac + ks * as_, ys + kc * as_ - ks * ac)
                return (yc + kc * ac - ks * as_, ys + kc * as_ + ks * ac)

            yc, ys = lax.fori_loop(0, (count - i) if flip else (i + 1), inner, (zero, zero))
            at = pl.ds(pl.multiple_of((base + i) * cc + off, rg), rg)
            yh_s[at, :BIG] = yc.astype(bf16)
            yh_s[at, BIG:] = ys.astype(bf16)

        over_pieces(nseq, cc, rg, seq_ref, piece)

    @pl.when(pl.program_id(0) == 0)
    def _():
        products(False)

    @pl.when(pl.program_id(0) == 1)
    def _():
        products(True)

    for h in range(pieces):
        at = pl.ds(h * cc, cc)
        y_s[at, :] = nn(yh_s[at, :], back_ref[...])

    def one(b, y):
        y_ref[0, b] = y.astype(bf16)
        mix_ref[0, b] = (y * gg_ref[0, b].astype(f32)).astype(bf16)

    def last(h, carry):
        b = tab_ref[0, h]
        at = pl.ds(pl.multiple_of(h * cc, cc), cc)
        one(b, y_s[at, 0:BLK])

        @pl.when(tab_ref[1, h] == 1)
        def _():
            one(b + 1, y_s[at, BLK:])

        return carry

    lax.fori_loop(0, seq_ref[1, nseq], last, 0)
    nothing = jnp.zeros((cc, BLK), bf16)

    def fill(b, carry):
        y_ref[0, b] = nothing
        mix_ref[0, b] = nothing
        return carry

    lax.fori_loop(seq_ref[0, nseq], nb, fill, 0)


def back_body(
    nb, nseq, cc, rg, flip, tab_ref, seq_ref, a_ref, gm_ref, kh_ref, wave_ref, back_ref, gg_ref, y_ref, dg_ref, da_ref,
    gpg_ref, gp_ref, gh_ref, bs_ref, in_s, ah_s, gh_s, xh_s, x_s,
):
    pieces = (nb + nseq) // 2
    load_pieces(nb, pieces, cc, tab_ref, lambda b: a_ref[0, b].astype(f32), in_s, wave_ref, ah_s)
    load_pieces(
        nb, pieces, cc, tab_ref, lambda b: gm_ref[0, b].astype(f32) * gg_ref[0, b].astype(f32), in_s, wave_ref, gh_s
    )
    gh_ref[...] = jnp.zeros_like(gh_ref)
    zero = jnp.zeros((rg, BIG), f32)

    def piece(i, count, base, off):
        at = pl.ds(pl.multiple_of((base + i) * cc + off, rg), rg)
        ac = ah_s[at, :BIG]
        as_ = ah_s[at, BIG:]

        def inner(j, acc):
            xc, xs = acc
            other = (base + i - j) if flip else (base + i + j)
            m = pl.ds(pl.multiple_of(other * cc + off, rg), rg)
            rows = pl.ds(off, rg)
            gc = gh_s[m, :BIG]
            gs = gh_s[m, BIG:]
            kc = kh_ref[0, j, rows, :BIG]
            ks = kh_ref[0, j, rows, BIG:]
            gh_ref[0, j, rows, :BIG] += ac * gc + as_ * gs
            if flip:
                gh_ref[0, j, rows, BIG:] += gc * as_ - gs * ac
                return (xc + kc * gc - ks * gs, xs + kc * gs + ks * gc)
            gh_ref[0, j, rows, BIG:] += ac * gs - as_ * gc
            return (xc + kc * gc + ks * gs, xs + kc * gs - ks * gc)

        xc, xs = lax.fori_loop(0, (i + 1) if flip else (count - i), inner, (zero, zero))
        xh_s[at, :BIG] = xc.astype(bf16)
        xh_s[at, BIG:] = xs.astype(bf16)

    over_pieces(nseq, cc, rg, seq_ref, piece)

    for h in range(pieces):
        at = pl.ds(h * cc, cc)
        x_s[at, :] = nn(xh_s[at, :], back_ref[...])

    none = jnp.zeros((cc, BLK), f32)

    def one(b, gx, carry):
        s0, s1 = carry
        gpg = (y_ref[0, b].astype(f32) * gm_ref[0, b].astype(f32) * dg_ref[0, b].astype(f32)).astype(bf16)
        gpg_ref[0, b] = gpg
        gp = (gx * da_ref[0, b].astype(f32)).astype(bf16)
        gp_ref[0, b] = gp
        return (s0 + gpg.astype(f32), s1 + gp.astype(f32))

    def last(h, carry):
        b = tab_ref[0, h]
        at = pl.ds(pl.multiple_of(h * cc, cc), cc)
        carry = one(b, x_s[at, 0:BLK], carry)

        def more(kept):
            return one(b + 1, x_s[at, BLK:], kept)

        return lax.cond(tab_ref[1, h] == 1, more, lambda kept: kept, carry)

    s0, s1 = lax.fori_loop(0, seq_ref[1, nseq], last, (none, none))
    bs_ref[0, :, 0:BLK] = s0
    bs_ref[0, :, BLK:] = s1
    nothing = jnp.zeros((cc, BLK), bf16)

    def fill(b, carry):
        gpg_ref[0, b] = nothing
        gp_ref[0, b] = nothing
        return carry

    lax.fori_loop(seq_ref[0, nseq], nb, fill, 0)


def ssm_specs(shape, seq):
    _, nb, ch, _ = shape
    nseq = seq.shape[1] - 1
    pieces = (nb + nseq) // 2
    cc = chunk_of(ch, 128 if nb <= 32 else 64)
    big = pl.BlockSpec((1, nb, cc, BLK), lambda k, i: (k, 0, i, 0))
    spec = pl.BlockSpec((1, LAGS, cc, 2 * BIG), lambda k, i: (k, 0, i, 0))
    smem = pl.BlockSpec(memory_space=pltpu.SMEM)
    head = [smem, smem]
    tables = [pl.BlockSpec((BIG, 2 * BIG), lambda k, i: (0, 0)), pl.BlockSpec((2 * BIG, BIG), lambda k, i: (0, 0))]
    return nb, nseq, ch, cc, pieces * cc, big, spec, head, tables


def ssm_scan(tab, seq, a, kh, wave, back, gg):
    nb, nseq, ch, cc, size, big, spec, head, tables = ssm_specs(a.shape, seq)
    return pl.pallas_call(
        partial(scan_body, nb, nseq, cc, 32),
        grid=(2, ch // cc),
        in_specs=head + [big, spec] + tables + [big],
        out_specs=[big, big],
        out_shape=[jax.ShapeDtypeStruct(a.shape, bf16)] * 2,
        scratch_shapes=[
            pltpu.VMEM((size, BIG), bf16),
            pltpu.VMEM((size, 2 * BIG), f32),
            pltpu.VMEM((size, 2 * BIG), bf16),
            pltpu.VMEM((size, BIG), f32),
        ],
        compiler_params=params(56),
        cost_estimate=cost(2 * ch * 50e6, 2 * ch * nb * BLK * 8),
    )(tab, seq, a, kh, wave, back, gg)


def ssm_back(k, tab, seq, a, gm, kh, wave, back, gg, y, dg, da):
    nb, nseq, ch, cc, size, _, _, head, tables = ssm_specs(a.shape, seq)
    big = pl.BlockSpec((1, nb, cc, BLK), lambda i: (k, 0, i, 0))
    spec = pl.BlockSpec((1, LAGS, cc, 2 * BIG), lambda i: (k, 0, i, 0))
    out = pl.BlockSpec((1, nb, cc, BLK), lambda i: (0, 0, i, 0))
    out_spec = pl.BlockSpec((1, LAGS, cc, 2 * BIG), lambda i: (0, 0, i, 0))
    tables = [
        pl.BlockSpec((BIG, 2 * BIG), lambda i: (0, 0)),
        pl.BlockSpec((2 * BIG, BIG), lambda i: (0, 0)),
    ]
    return pl.pallas_call(
        partial(back_body, nb, nseq, cc, 64, k == 1),
        grid=(ch // cc,),
        in_specs=head + [big, big, spec] + tables + [big] * 4,
        out_specs=[out, out, out_spec, pl.BlockSpec((1, cc, 2 * BLK), lambda i: (0, i, 0))],
        out_shape=[jax.ShapeDtypeStruct((1,) + a.shape[1:], bf16)] * 2
        + [
            jax.ShapeDtypeStruct((1, LAGS, ch, 2 * BIG), f32),
            jax.ShapeDtypeStruct((1, ch, 2 * BLK), f32),
        ],
        scratch_shapes=[
            pltpu.VMEM((size, BIG), bf16),
            pltpu.VMEM((size, 2 * BIG), f32),
            pltpu.VMEM((size, 2 * BIG), f32),
            pltpu.VMEM((size, 2 * BIG), bf16),
            pltpu.VMEM((size, BIG), f32),
        ],
        compiler_params=params(60),
        cost_estimate=cost(ch * 80e6, ch * nb * BLK * 16),
    )(tab, seq, a, gm, kh, wave, back, gg, y, dg, da)


def stack_pair(refs):
    return jnp.concatenate(
        [jnp.concatenate([ref[k, 0], ref[k, 1]], axis=1) for ref in refs for k in range(ref.shape[0])], axis=0
    )


def mul_body(count, more, start_ref, w_ref, *refs):
    out = nn(w_ref[...], stack_pair(refs[:count]))
    o_ref = refs[-1]
    for h in range(2):
        part = out[:, h * BLK : (h + 1) * BLK]
        if more:
            part = part + refs[count][h].astype(f32)
        o_ref[h] = part.astype(o_ref.dtype)


def mul_rows(w, arrays, start, many, dtype=bf16, extra=None):
    width, deep = w.shape
    ch = arrays[0].shape[2]
    count = len(arrays)
    out = pl.BlockSpec((2, width, BLK), lambda i, at: (i, 0, 0))
    return pl.pallas_call(
        partial(mul_body, count, extra is not None),
        grid_spec=pltpu.PrefetchScalarGridSpec(
            num_scalar_prefetch=1,
            grid=(many // 2,),
            in_specs=[pl.BlockSpec((width, deep), lambda i, at: (0, 0))]
            + [pl.BlockSpec((x.shape[0], 2, ch, BLK), lambda i, at: (0, at[0] + i, 0, 0)) for x in arrays]
            + ([] if extra is None else [out]),
            out_specs=out,
        ),
        out_shape=jax.ShapeDtypeStruct((many, width, BLK), dtype),
        compiler_params=params(40),
        cost_estimate=cost(2 * many * BLK * width * deep, 2 * many * BLK * (2 * width + deep)),
    )(start // 2, w, *arrays, *([] if extra is None else [extra]))


def outer_body(ch, many, cuts, parts, at_ref, *refs):
    step = pl.program_id(0)
    xs, gs = refs[:parts], refs[parts : 2 * parts]
    gp_refs, gpg_refs, mix_ref = refs[2 * parts : 2 * parts + 2], refs[2 * parts + 2 : 2 * parts + 4], refs[2 * parts + 4]
    outs = refs[2 * parts + 5 : 2 * parts + 5 + cuts]
    acc_s, x_s, g_s = refs[-3:]

    def fill(at):
        for b in range(many):
            x_s[:, b * BLK : (b + 1) * BLK] = xs[at][b]
            g_s[:, b * BLK : (b + 1) * BLK] = gs[at][b]

    if parts == 1:
        fill(0)
    else:
        for at in range(parts):

            @pl.when(step == at)
            def _(at=at):
                fill(at)

    def part(ref, k):
        return jnp.concatenate([ref[k, b] for b in range(many)], axis=1)

    @pl.when(step == 0)
    def _():
        acc_s[...] = jnp.zeros_like(acc_s)

    split = 4 * ch
    left = jnp.concatenate([part(ref, 0) for ref in (*gp_refs, *gpg_refs)], axis=0)
    acc_s[:, :split] += nt(x_s[...], left)
    acc_s[:, split:] += nt(g_s[...], jnp.concatenate([part(mix_ref, 0), part(mix_ref, 1)], axis=0))

    @pl.when(step == pl.num_programs(0) - 1)
    def _():
        deep = acc_s.shape[0] // cuts
        for cut in range(cuts):
            start = pl.multiple_of(at_ref[pl.num_programs(0) + cut] * deep, 8)
            outs[cut][...] = acc_s[pl.ds(start, deep), :].astype(bf16)


def outer_sums(order, cuts, xs, gs, gp, gpg, mix):
    width = xs[0].shape[1]
    _, nb, ch, _ = mix.shape
    many = 8
    parts = len(xs)
    if parts == 1:
        rows = pl.BlockSpec((many, width, BLK), lambda i, at: (i, 0, 0))
    else:
        rows = pl.BlockSpec((many, width, BLK), lambda i, at: (0, 0, 0), pipeline_mode=pl.Buffered(1))
    chan = pl.BlockSpec((2, many, ch, BLK), lambda i, at: (0, at[i], 0, 0))
    one = pl.BlockSpec((1, many, ch, BLK), lambda i, at: (0, at[i], 0, 0))
    tok = nb * BLK
    return pl.pallas_call(
        partial(outer_body, ch, many, cuts, parts),
        grid_spec=pltpu.PrefetchScalarGridSpec(
            num_scalar_prefetch=1,
            grid=(nb // many,),
            in_specs=[rows] * (2 * parts) + [one] * 4 + [chan],
            out_specs=[pl.BlockSpec((width // cuts, 6 * ch), lambda i, at: (0, 0))] * cuts,
            scratch_shapes=[
                pltpu.VMEM((width, 6 * ch), f32),
                pltpu.VMEM((width, many * BLK), bf16),
                pltpu.VMEM((width, many * BLK), bf16),
            ],
        ),
        out_shape=[jax.ShapeDtypeStruct((width // cuts, 6 * ch), bf16)] * cuts,
        compiler_params=params(60),
        cost_estimate=cost(12 * tok * width * ch, tok * (4 * width + 12 * ch)),
    )(order, *xs, *gs, *gp, *gpg, mix)


def join_body(split, w_ref, head_ref, tail_ref, head_t_ref, tail_t_ref):
    head_ref[...] = w_ref[:, :split]
    tail_ref[...] = w_ref[:, split:]
    head_t_ref[...] = w_ref[:, :split].T
    tail_t_ref[...] = w_ref[:, split:].T


def split_weights(w, split):
    rows, wide = w.shape
    vmem = pl.BlockSpec(memory_space=pltpu.VMEM)
    return pl.pallas_call(
        partial(join_body, split),
        in_specs=[vmem],
        out_specs=[vmem] * 4,
        out_shape=[
            jax.ShapeDtypeStruct(shape, bf16)
            for shape in ((rows, split), (rows, wide - split), (split, rows), (wide - split, rows))
        ],
        compiler_params=params(48),
        cost_estimate=cost(0, 6 * rows * wide),
    )(w)


def meet_body(
    axes, rank_ref, x_ref, chan_ref, norm_ref, pack_ref, got_ref, call_ref, nall_ref, wall_ref, send_s, *sems
):
    xs_sem, xr_sem, cs_sem, cr_sem, ns_sem, nr_sem, ws_sem, wr_sem, own_sem = sems
    q, c, h, w = (lax.axis_index(name) for name in axes)
    rows = x_ref.shape[0]
    piece = rows // 8
    flat = ((2 * q + c) * 2 + h) * 2 + w

    def peer(bits):
        return (q ^ (bits // 8), c ^ (bits // 4 % 2), h ^ (bits // 2 % 2), w ^ (bits % 2))

    barrier = pltpu.get_barrier_semaphore()
    for bits in range(1, 32):
        pl.semaphore_signal(barrier, inc=1, device_id=peer(bits), device_id_type=pl.DeviceIdType.MESH)
    pl.semaphore_wait(barrier, 31)

    def remote(src, dst, send, recv, to):
        return pltpu.make_async_remote_copy(
            src_ref=src, dst_ref=dst, send_sem=send, recv_sem=recv, device_id=to, device_id_type=pl.DeviceIdType.MESH
        )

    deep = pack_ref.shape[0]

    def shard(at):
        return wall_ref.at[pl.ds(pl.multiple_of(at * deep, 16), deep)]

    def first_copy():
        return remote(pack_ref, shard(2 * q + c), ws_sem.at[0], wr_sem.at[c], (q, 1 - h, c, w))

    def second_copy():
        return remote(pack_ref, shard(2 * q + c), ws_sem.at[1], wr_sem.at[c], (q, 1 - h, 1 - c, w))

    def own_shard():
        return pltpu.make_async_copy(pack_ref, shard(2 * q + c), own_sem.at[2])

    def shard_came(at):
        return remote(pack_ref, shard(2 * q + at), ws_sem.at[0], wr_sem.at[at], peer(1))

    def pass_on(bits):
        rows = wall_ref.at[pl.ds(pl.multiple_of(q * 2 * deep, 16), 2 * deep)]
        return remote(rows, rows, ws_sem.at[1 + bits], wr_sem.at[1 + bits], (q ^ bits, c, h, w))

    first_copy().start()

    @pl.when(c != h)
    def _():
        own_shard().start()

    @pl.when(c == h)
    def _():
        second_copy().start()

    nall_ref[flat] = norm_ref[...]

    def norm_copy(bits):
        return remote(norm_ref, nall_ref.at[flat], ns_sem.at[bits], nr_sem.at[bits], peer(bits))

    for bits in range(1, 32):
        norm_copy(bits).start()

    pieces = [(kq, kh) for kh in (0, 1) for kq in (1, 2, 3, 0)]
    spot = lax.broadcasted_iota(jnp.int32, (piece, rows), 0)

    def row_copy(kq, kh):
        at = 2 * kq + kh
        return remote(
            send_s.at[at], got_ref.at[2 * q + c], xs_sem.at[at], xr_sem.at[2 * kq + c], (q ^ kq, 1 - h, h ^ kh, w)
        )

    def own_copy():
        return pltpu.make_async_copy(send_s.at[0], got_ref.at[2 * q + c], own_sem.at[0])

    for kq, kh in pieces:
        chunk = 2 * (q ^ kq) + (h ^ kh)
        pick = jnp.where(spot + chunk * piece == rank_ref[...], 1.0, 0.0).astype(bf16)
        send_s[2 * kq + kh] = nn(pick, x_ref[...]).astype(bf16)
        if (kq, kh) == (1, 1):
            for at in range(2):

                @pl.when((c != h) & (at == c))
                def _():
                    own_shard().wait()

                @pl.when(jnp.logical_not((c != h) & (at == c)))
                def _(at=at):
                    shard_came(at).wait_recv()

            for bits in range(1, 4):
                pass_on(bits).start()
        if (kq, kh) == (0, 0):

            @pl.when(c != h)
            def _():
                own_copy().start()

            @pl.when(c == h)
            def _():
                row_copy(0, 0).start()

        else:
            row_copy(kq, kh).start()

    place = 2 * (1 - c) + w
    spot_c = 4 * c + 2 * h + w

    def chan_copy(kq, kh):
        at = 2 * kq + kh
        return remote(
            chan_ref, call_ref.at[spot_c], cs_sem.at[at], cr_sem.at[spot_c], (q ^ kq, 1 - q // 2, h ^ kh, q % 2)
        )

    def own_chan():
        return pltpu.make_async_copy(chan_ref, call_ref.at[spot_c], own_sem.at[1])

    for kq, kh in pieces:
        if (kq, kh) == (0, 0):

            @pl.when(place == q)
            def _():
                own_chan().start()

            @pl.when(place != q)
            def _():
                chan_copy(0, 0).start()

        else:
            chan_copy(kq, kh).start()

    for bits in range(1, 32):
        norm_copy(bits).wait()
    for at in range(8):

        @pl.when((c != h) & (at == c))
        def _():
            own_copy().wait()

        @pl.when(jnp.logical_not((c != h) & (at == c)))
        def _(at=at):
            remote(send_s.at[at], got_ref.at[at], xs_sem.at[at], xr_sem.at[at], peer(1)).wait_recv()

    for at in range(8):

        @pl.when((place == q) & (at == spot_c))
        def _():
            own_chan().wait()

        @pl.when(jnp.logical_not((place == q) & (at == spot_c)))
        def _(at=at):
            remote(chan_ref, call_ref.at[at], cs_sem.at[at], cr_sem.at[at], peer(1)).wait_recv()

    for bits in range(1, 4):
        pass_on(bits).wait()
    first_copy().wait_send()

    @pl.when(c == h)
    def _():
        second_copy().wait_send()

    for kq, kh in pieces:
        if (kq, kh) == (0, 0):

            @pl.when(c == h)
            def _():
                row_copy(0, 0).wait_send()

            @pl.when(place != q)
            def _():
                chan_copy(0, 0).wait_send()

        else:
            row_copy(kq, kh).wait_send()
            chan_copy(kq, kh).wait_send()


def meet(axes, rank, x, chan, norm, pack):
    rows, width = x.shape
    vmem = pl.BlockSpec(memory_space=pltpu.VMEM)
    sem = pltpu.SemaphoreType.DMA
    return pl.pallas_call(
        partial(meet_body, axes),
        in_specs=[vmem] * 5,
        out_specs=[vmem] * 4,
        out_shape=[
            jax.ShapeDtypeStruct((8, rows // 8, width), bf16),
            jax.ShapeDtypeStruct((8,) + chan.shape, f32),
            jax.ShapeDtypeStruct((32,) + norm.shape, f32),
            jax.ShapeDtypeStruct((8 * pack.shape[0], pack.shape[1]), bf16),
        ],
        scratch_shapes=[pltpu.VMEM((8, rows // 8, width), bf16)]
        + [sem((8,)), sem((8,)), sem((8,)), sem((8,)), sem((32,)), sem((32,)), sem((5,)), sem((5,)), sem((3,))],
        compiler_params=pltpu.CompilerParams(collective_id=1, has_side_effects=True, vmem_limit_bytes=60 * MIB),
        cost_estimate=cost(2 * rows * rows * width, 100 * rows * width),
    )(rank.reshape(1, rows), x, chan, norm, pack)


def sequence_tables(lens, nb):
    nseq = lens.shape[0]
    blocks = (lens + BLK - 1) // BLK
    start = jnp.cumsum(blocks) - blocks
    bigs = (blocks + 1) // 2
    first_big = jnp.cumsum(bigs) - bigs
    h = jnp.arange((nb + nseq) // 2, dtype=jnp.int32)
    owner = (h[:, None] >= first_big[None, :]).astype(jnp.int32).sum(axis=1) - 1
    mine = owner[:, None] == jnp.arange(nseq, dtype=jnp.int32)[None, :]

    def at_owner(values):
        return jnp.sum(jnp.where(mine, values[None, :], 0), axis=1)

    rel = h - at_owner(first_big)
    first = jnp.minimum(at_owner(start) + 2 * rel, nb - 1)
    whole = (2 * rel + 1 < at_owner(blocks)).astype(jnp.int32)
    tab = jnp.stack([first, whole]).astype(jnp.int32)
    seq = jnp.stack(
        [jnp.append(first_big, jnp.sum(blocks)), jnp.append(bigs, jnp.sum(bigs))]
    ).astype(jnp.int32)
    return tab, seq


def live_rows(lens, rows):
    slot = (lens + BLK - 1) // BLK * BLK
    begin = jnp.cumsum(slot) - slot
    pos = jnp.arange(rows, dtype=jnp.int32)
    inside = (pos[:, None] >= begin[None, :]) & (pos[:, None] < (begin + lens)[None, :])
    return jnp.sum(inside.astype(f32), axis=1)


def after(values):
    return lax.optimization_barrier(values)


def rank_of(keys):
    return jnp.sum((keys[None, :] < keys[:, None]).astype(jnp.int32), axis=1)


class Line:
    def __init__(self, n_dp, n_t):
        self.n_dp, self.n_t = n_dp, n_t
        self.axes = {"dp": n_dp, "tensor": n_t}
        self.both = ("dp", "tensor")
        self.cuts = 1

    def place_of_group(self):
        return lax.axis_index("tensor")

    def regroup(self, x):
        return x

    def gather_first(self, x):
        return [lax.all_gather(x, "tensor", axis=0, tiled=True)]

    def gather_last(self, x, got):
        return [(got[0], jnp.zeros((1,), jnp.int32))]

    def scatter_first(self, w, arrays, many):
        return [mul_rows(w, arrays, jnp.zeros((1,), jnp.int32), many * self.n_t)]

    def scatter_send(self, parts):
        return [lax.psum_scatter(parts[0], "tensor", scatter_dimension=0, tiled=True)]

    def scatter_own(self, w, arrays, many):
        return []

    def ungroup(self, x):
        return x

    def spread(self, x):
        return lax.all_to_all(x, "dp", split_axis=0, concat_axis=0, tiled=True)

    def order(self, pieces):
        return jnp.append(jnp.arange(pieces * self.n_t, dtype=jnp.int32), 0)

    def enter(self, rank, x, chan, norm, pack):
        (sent,) = permute_to(rank, [x])
        return (self.spread(sent),) + self.gather_channels(chan, norm) + (lax.all_gather(pack, "dp", axis=0, tiled=True),)

    def gather_channels(self, chan, norm):
        perm = [(f, (f % self.n_dp) * self.n_t + f // self.n_dp) for f in range(self.n_dp * self.n_t)]
        chan = lax.ppermute(chan, self.both, perm)
        norm = lax.all_gather(norm, self.both, axis=1, tiled=True)
        return lax.all_gather(chan[None], "dp", axis=0, tiled=True), norm

    def cut_order(self):
        return jnp.zeros((1,), jnp.int32)

    def grads_send(self, gw):
        return [lax.psum_scatter(gw[0], "dp", scatter_dimension=0, tiled=True)]

    def grads_last(self, parts):
        return parts[0].astype(f32)

    def scatter_channels(self, sums):
        return lax.psum_scatter(sums, "dp", scatter_dimension=0, tiled=True)

    def owner_channels(self, sums):
        perm = [((f % self.n_dp) * self.n_t + f // self.n_dp, f) for f in range(self.n_dp * self.n_t)]
        return lax.ppermute(sums, self.both, perm)

    def scatter_norm(self, sums):
        return lax.psum_scatter(sums, self.both, scatter_dimension=1, tiled=True)


class Pairs:
    def __init__(self, n_dp, n_t):
        self.quads = n_dp // 2
        self.axes = {"q": self.quads, "c": 2, "h": 2, "w": 2}
        self.both = ("q", "c", "h", "w")
        self.cuts = self.quads
        self.other = [(0, 1), (1, 0)]
        self.there = [(2 * c + h, 2 * (1 - h) + c) for c in range(2) for h in range(2)]
        self.back = [(b, a) for a, b in self.there]
        self.turned = [(2 * c + h, 2 * (1 - h) + 1 - c) for c in range(2) for h in range(2)]

    def flip(self, x, axis, bit=1):
        return lax.ppermute(x, axis, [(i, i ^ bit) for i in range(self.axes[axis])])

    def place_of_group(self):
        return 2 * (1 - lax.axis_index("c")) + lax.axis_index("w")

    def regroup(self, x):
        return lax.ppermute(x, ("c", "h"), self.there)

    def ungroup(self, x):
        return lax.ppermute(x, ("c", "h"), self.back)

    def spread(self, x):
        return lax.all_to_all(x, ("q", "c"), split_axis=0, concat_axis=0, tiled=True)

    def places(self):
        c, w = lax.axis_index("c"), lax.axis_index("w")
        return [2 * (1 - c) + w, 2 * c + w, 2 * (1 - c) + 1 - w, 2 * c + 1 - w]

    def starts(self, many):
        return [(place * many).astype(jnp.int32).reshape(1) for place in self.places()]

    def gather_first(self, x):
        return [self.flip(x, "c"), self.flip(x, "w")]

    def gather_last(self, x, got):
        beside, near = got
        return list(zip([x, beside, near, self.flip(near, "c")], self.starts(x.shape[0])))

    def scatter_first(self, w, arrays, many):
        _, beside, near, far = self.starts(many)
        first = mul_rows(w, arrays, far, many)
        give = self.flip(first, "c")
        beside, first = after((beside, first))
        second = mul_rows(w, arrays, beside, many)
        second, give = after((second, give))
        return [second, mul_rows(w, arrays, near, many, extra=give)]

    def scatter_send(self, parts):
        return [self.flip(parts[0], "c"), self.flip(parts[1], "w")]

    def scatter_own(self, w, arrays, many):
        return [mul_rows(w, arrays, self.starts(many)[0], many, dtype=f32)]

    def order(self, pieces):
        place = jnp.stack(self.places())[:, None] * pieces + jnp.arange(pieces)[None, :]
        return jnp.concatenate([place.reshape(-1).astype(jnp.int32), self.cut_order()])

    def steps(self):
        bit = self.quads // 2
        while bit:
            yield "q", bit
            bit //= 2
        yield "h", 1

    def spot(self):
        return 2 * lax.axis_index("q") + lax.axis_index("h")

    def enter(self, rank, x, chan, norm, pack):
        small = norm.shape[1]
        norm = jnp.pad(norm, ((0, 5), (0, BLK - small)))
        got, chan, norm, weights = meet(self.both, rank, x, chan, norm, pack)
        norm = norm[:, :3, :small].transpose(1, 0, 2).reshape(3, -1)
        return got.reshape(x.shape), chan, norm, weights

    def grads_send(self, gw):
        return [gw[0]] + [self.flip(gw[bit], "q", bit) for bit in range(1, self.quads)]

    def grads_last(self, parts):
        total = parts[0].astype(f32)
        for part in parts[1:]:
            total = total + part.astype(f32)
        total = total.astype(bf16)
        half = total.shape[0] // 2
        h = lax.axis_index("h")
        first = jnp.where(h == 0, total[:half], total[half:])
        second = jnp.where(h == 0, total[half:], total[:half])
        return self.ungroup(first).astype(f32) + lax.ppermute(second, ("c", "h"), self.turned).astype(f32)

    def cut_order(self):
        return (lax.axis_index("q") ^ jnp.arange(self.quads)).astype(jnp.int32)

    def scatter_channels(self, sums):
        count = 2 * self.quads
        rows, wide = sums.shape[0] // count, sums.shape[1]
        sums = jnp.pad(sums, ((0, 0), (0, -wide % 8))).reshape(count, -1, BLK)
        part = jnp.take(sums, jnp.arange(count) ^ self.spot(), axis=0)
        for axis, bit in self.steps():
            half = part.shape[0] // 2
            part = part[:half] + self.flip(part[half:], axis, bit)
        return part.reshape(rows, -1)[:, :wide]

    def owner_channels(self, sums):
        count = 2 * self.quads
        perm = []
        for f in range(4 * count):
            place, at = f // count, f % count
            q, h, c, w = at // 2, at % 2, 1 - place // 2, place % 2
            perm.append((((2 * q + c) * 2 + h) * 2 + w, f))
        return lax.ppermute(sums, self.both, perm)

    def scatter_norm(self, sums):
        count = 8 * self.quads
        part = sums.reshape(3, count, -1).transpose(1, 0, 2)
        wide = part.shape[2]
        part = jnp.pad(part, ((0, 0), (0, 5), (0, BLK - wide)))
        part = lax.all_to_all(part, self.both, split_axis=0, concat_axis=0, tiled=True)
        return jnp.sum(part, axis=0)[:3, :wide]


def local(
    net, wave, tokens, cotangent, source, target, lengths, ln_gain, ln_bias, w_fwd, b_fwd, w_bwd, b_bwd,
    w_gate, b_gate, w_out, b_out, log_dt, log_rate, ssm_b, ssm_c, ssm_d,
):
    rows, width = tokens.shape
    many = rows // BLK
    n_t = net.n_t
    group = rows * n_t
    nb = group // BLK
    ch = w_fwd.shape[1]
    back = (wave.T / BIG).astype(bf16)
    wave = wave.astype(bf16)

    def lanes(column):
        return jnp.broadcast_to(column[..., None], column.shape + (BLK,))

    def decays(log_dt, log_rate, ssm_b):
        rate = jnp.exp(log_rate)
        ld = -jnp.exp(log_dt)[..., None] * rate
        return rate, ld, (1.0 - jnp.exp(ld)) / rate * ssm_b

    rank = rank_of(target)
    sender = source // group
    place = rank_of(sender * rows + jnp.arange(rows, dtype=jnp.int32))
    pack = jnp.concatenate(
        [w_fwd, w_bwd, w_gate.reshape(-1, 2 * ch), w_out.transpose(2, 0, 1).reshape(-1, 2 * ch)], axis=1
    )
    table = net.regroup(jnp.concatenate([place, lengths[0]]))
    rate, ld, drive = decays(log_dt, log_rate, ssm_b)
    own = b_fwd.shape[0]
    small = jnp.concatenate([ssm_d, b_fwd[None], b_bwd[None], b_gate])
    chan = jnp.concatenate(
        [
            (ld * log2e).reshape(own, 2 * STATE),
            (ssm_c * drive).reshape(own, 2 * STATE),
            jnp.pad(small, ((0, -(2 * own + 6) % 8 + 0), (0, 2 * STATE - own))),
        ]
    )
    norm = jnp.stack([ln_gain, ln_bias, b_out])
    got_x, chan_all, norm_all, w_all = net.enter(rank, tokens, chan, norm, pack)
    got_x, chan_all, norm_all, w_all, table, cotangent = after((got_x, chan_all, norm_all, w_all, table, cotangent))

    place, lens = table[:rows], table[rows:]
    gain = lanes(norm_all[0])
    shift = lanes(norm_all[1])
    small = chan_all[:, 2 * own : 2 * own + 6, :own].transpose(1, 0, 2).reshape(6, ch)

    def pairs(at):
        both = chan_all[:, at : at + own].reshape(-1, 2, own // 2, 2 * STATE)
        return both.transpose(1, 0, 2, 3).reshape(2, ch // 2, 2 * STATE)

    ld_pairs = pairs(0)
    w_pairs = pairs(own)
    skip = lanes(small[0:2])
    live = live_rows(lens, group)
    live_own = lax.dynamic_slice_in_dim(live, net.place_of_group() * rows, rows, 0).reshape(many, 1, BLK)
    live = live.reshape(nb // 2, 1, BIG)
    tab, seq = sequence_tables(lens, nb)

    xt, xd = deal_x(place, got_x, gain, shift)
    xt, cotangent, ld_pairs, w_pairs, skip, w_all = after((xt, cotangent, ld_pairs, w_pairs, skip, w_all))
    x_got = net.gather_first(xt)
    (sent_g,) = permute_to(rank, [cotangent])
    got_g = net.spread(sent_g)
    kh = spectra(ld_pairs, w_pairs, skip, wave)
    w_in, w_back, w_in_t, w_back_t = split_weights(w_all, 4 * ch)
    bias_in = lanes(small[2:6].reshape(-1))
    bias_out = lanes(norm_all[2])
    x_got, got_g, kh, w_in_t, bias_in = after((x_got, got_g, kh, w_in_t, bias_in))
    xs = net.gather_last(xt, x_got)
    got_g = net.regroup(got_g)
    kept = None
    for part, start in xs:
        kept = project(part, start, nb, live, w_in_t, bias_in, kept)
    kept, got_g = after((kept, got_g))
    a, da, gg, dg = kept
    gt, gd, g_bias_out = deal_g(place, got_g, live_own)
    gt, a = after((gt, a))
    g_got = net.gather_first(gt)
    y, mix = ssm_scan(tab, seq, a, kh, wave, back, gg)
    g_got, y, mix = after((g_got, y, mix))
    gs = net.gather_last(gt, g_got)
    branch = net.scatter_first(w_back, [mix], many)
    gm = gate_grad(gs, nb, w_back_t)
    branch, gm = after((branch, gm))

    branch = net.scatter_send(branch)
    branch = net.scatter_own(w_back, [mix], many) + branch
    first = ssm_back(0, tab, seq, a, gm, kh, wave, back, gg, y, dg, da)
    branch, first, a = after((branch, first, a))
    sent_out = layer_rows(place, branch, xd, live_own, bias_out)
    sent_out, a = after((sent_out, a))
    sent_out = net.ungroup(sent_out)
    second = ssm_back(1, tab, seq, a, gm, kh, wave, back, gg, y, dg, da)
    sent_out, first, second = after((sent_out, first, second))
    gpg, gp, gh, bsum = zip(first, second)
    sent_out = net.spread(sent_out)
    back_list = [gp[0], gp[1], gpg[0], gpg[1]]
    g_normed = net.scatter_first(w_in, back_list, many)
    g_normed, back_list, mix = after((g_normed, back_list, mix))
    gp, gpg = back_list[:2], back_list[2:]
    g_normed = net.scatter_send(g_normed)
    g_normed = net.scatter_own(w_in, back_list, many) + g_normed
    gw = outer_sums(net.order(many // 8), net.cuts, [part for part, _ in xs], [part for part, _ in gs], gp, gpg, mix)
    g_normed, gw, gh, sent_out = after((g_normed, gw, gh, sent_out))
    sent_in, norm_sums = input_rows(place, g_normed, xd, gd, gain)
    sent_in, gh, gw, norm_sums, sent_out, bsum = after((sent_in, gh, gw, norm_sums, sent_out, bsum))
    sent_in = net.ungroup(sent_in)
    gw = net.grads_send(gw)
    s0, s1, g0 = [jnp.concatenate(part) for part in zip(*[moments(k, ld_pairs, gh[k], back) for k in range(2)])]
    layer_out = permute_from(rank, sent_out)

    s0 = s0.reshape(2, ch, STATE)
    s1 = s1.reshape(2, ch, STATE)
    bsum = jnp.concatenate(bsum)
    gb_gate = jnp.sum(bsum[:, :, :BLK], axis=2)
    gb_in = jnp.sum(bsum[:, :, BLK:], axis=2)
    sums = jnp.concatenate(
        [s0[0], s0[1], s1[0], s1[1], jnp.concatenate([g0[:, :, 0], gb_gate, gb_in], axis=0).T], axis=1
    )
    norm_sums = net.scatter_norm(jnp.sum(jnp.concatenate([norm_sums, g_bias_out[None]], axis=0), axis=2))
    sent_in, gw, sums, norm_sums, layer_out = after((sent_in, gw, sums, norm_sums, layer_out))
    in_grad = permute_from(rank, net.spread(sent_in))
    sums = net.owner_channels(net.scatter_channels(sums))
    gw = net.grads_last(gw)
    s0 = jnp.stack([sums[:, :STATE], sums[:, STATE : 2 * STATE]])
    s1 = jnp.stack([sums[:, 2 * STATE : 3 * STATE], sums[:, 3 * STATE : 4 * STATE]])
    tail = sums[:, 4 * STATE :].T
    step = jnp.exp(log_dt)[..., None]
    g_c = s0 * drive
    g_drive = s0 * ssm_c
    g_b = g_drive * (1.0 - jnp.exp(ld)) / rate
    g_ld = s1 * ssm_c * drive - g_drive * ssm_b / rate * jnp.exp(ld)
    g_rate = -g_drive * drive / rate - g_ld * step
    g_dt = jnp.sum(g_ld * ld, axis=2)
    return (
        layer_out,
        in_grad,
        norm_sums[0],
        norm_sums[1],
        gw[:, :ch],
        tail[4],
        gw[:, ch : 2 * ch],
        tail[5],
        gw[:, 2 * ch : 4 * ch].reshape(-1, 2, ch),
        tail[2:4],
        gw[:, 4 * ch :].T.reshape(2, ch, -1),
        norm_sums[2],
        g_dt,
        g_rate * rate,
        g_b,
        g_c,
        tail[0:2],
    )


def solution(mesh):
    n_dp, n_t = mesh.shape["dp"], mesh.shape["tensor"]
    if n_t == 4 and n_dp == 8:
        net = Pairs(n_dp, n_t)
        dp, tensor = ("q", "c"), ("h", "w")
    else:
        net = Line(n_dp, n_t)
        dp, tensor = ("dp",), ("tensor",)
    net.n_t = n_t
    mesh = jax.sharding.Mesh(mesh.devices.reshape(tuple(net.axes.values())), tuple(net.axes))
    both = P(dp + tensor)
    rows = P(dp + tensor, None)
    pair = P(None, dp + tensor)
    state = P(None, dp + tensor, None)
    proj = P(dp, tensor)
    gate = P(dp, None, tensor)
    out = P(None, tensor, dp)
    wave = wave_table()

    def run(*args):
        return local(net, jnp.asarray(wave), *args)

    return jax.shard_map(
        run,
        mesh=mesh,
        in_specs=(
            rows, rows, both, both, P(dp, None), both, both, proj, both, proj, both, gate, pair, out, both,
            pair, state, state, state, pair,
        ),
        out_specs=(
            rows, rows, both, both, proj, both, proj, both, gate, pair, out, both, pair, state, state, state, pair,
        ),
        check_vma=False,
    )
```

```python
from functools import partial

import jax
import jax.numpy as jnp
import numpy as np
from jax import lax
from jax.experimental import pallas as pl
from jax.experimental.pallas import tpu as pltpu
from jax.sharding import PartitionSpec as P

BLK = 128
BIG = 256
MOST = 2048
LAGS = MOST // BIG
STATE = 64
epsilon = 1e-05
log2e = 1.4426950408889634
f32 = jnp.float32
bf16 = jnp.bfloat16
MIB = 2**20


def nn(a, b):
    return lax.dot_general(a, b, (((1,), (0,)), ((), ())), preferred_element_type=f32)


def nt(a, b):
    return lax.dot_general(a, b, (((1,), (1,)), ((), ())), preferred_element_type=f32)


def params(limit):
    return pltpu.CompilerParams(vmem_limit_bytes=60 * MIB)


def cost(flops, moved, trans=0):
    scale = 0.05
    return pl.CostEstimate(
        flops=int(scale * flops), bytes_accessed=int(scale * moved), transcendentals=int(scale * trans)
    )


def halves(x):
    high = x.astype(bf16)
    return high, (x - high.astype(f32)).astype(bf16)


def wave_table():
    pos = np.arange(BIG)[:, None]
    freq = np.arange(BIG)[None, :]
    angle = 2 * np.pi * ((2 * freq + 1) * pos % (4 * BIG)) / (4 * BIG)
    return np.concatenate([np.cos(angle), np.sin(angle)], 1).astype(np.float32)


def chunk_of(channels, most):
    best = 16
    for size in range(16, most + 1, 16):
        if channels % size == 0:
            best = size
    return best


def permute_row_body(count, rank_ref, *refs):
    rows = rank_ref.shape[1]
    spot = lax.broadcasted_iota(jnp.int32, (rows, rows), 0)
    pick = jnp.where(spot == rank_ref[...], 1.0, 0.0).astype(bf16)
    for at in range(count):
        refs[count + at][...] = nn(pick, refs[at][...]).astype(bf16)


def permute_to(rank, arrays):
    rows, width = arrays[0].shape
    count = len(arrays)
    return pl.pallas_call(
        partial(permute_row_body, count),
        out_shape=[jax.ShapeDtypeStruct((rows, width), bf16)] * count,
        compiler_params=params(48),
        cost_estimate=cost(2 * count * rows * rows * width, 4 * count * rows * width),
    )(rank.reshape(1, rows), *arrays)


def permute_col_body(rank_ref, x_ref, o_ref):
    rows = x_ref.shape[0]
    spot = lax.broadcasted_iota(jnp.int32, (rows, rows), 1)
    pick = jnp.where(spot == rank_ref[...], 1.0, 0.0).astype(bf16)
    o_ref[...] = nn(pick, x_ref[...]).astype(bf16)


def permute_from(rank, x):
    rows, width = x.shape
    return pl.pallas_call(
        permute_col_body,
        out_shape=jax.ShapeDtypeStruct((rows, width), bf16),
        compiler_params=params(48),
        cost_estimate=cost(2 * rows * rows * width, 4 * rows * width),
    )(rank.reshape(rows, 1), x)


def pick_rows(place_ref, x_ref):
    spot = lax.broadcasted_iota(jnp.int32, (BLK, x_ref.shape[0]), 1)
    pick = jnp.where(spot == place_ref[...], 1.0, 0.0).astype(bf16)
    return nn(pick, x_ref[...]).T


def deal_x_body(place_ref, x_ref, gain_ref, shift_ref, xt_ref, xd_ref):
    x = pick_rows(place_ref, x_ref)
    xd_ref[0] = x.astype(bf16)
    centred = x - jnp.mean(x, axis=0, keepdims=True)
    inv_std = lax.rsqrt(jnp.mean(centred * centred, axis=0, keepdims=True) + epsilon)
    xt_ref[0] = (centred * inv_std * gain_ref[...] + shift_ref[...]).astype(bf16)


def deal_g_body(place_ref, g_ref, live_ref, gt_ref, gd_ref, bo_ref):
    g = pick_rows(place_ref, g_ref)
    gd_ref[0] = g.astype(bf16)
    g = g * live_ref[0]
    gt_ref[0] = g.astype(bf16)

    @pl.when(pl.program_id(0) == 0)
    def _():
        bo_ref[...] = jnp.zeros_like(bo_ref)

    bo_ref[...] += g


def deal_specs(rows, width):
    place = pl.BlockSpec((BLK, 1), lambda i: (i, 0))
    whole = pl.BlockSpec((rows, width), lambda i: (0, 0))
    wide = pl.BlockSpec((width, BLK), lambda i: (0, 0))
    out = pl.BlockSpec((1, width, BLK), lambda i: (i, 0, 0))
    return place, whole, wide, out


def deal_x(place, x, gain, shift):
    rows, width = x.shape
    blocks = rows // BLK
    spot, whole, wide, out = deal_specs(rows, width)
    return pl.pallas_call(
        deal_x_body,
        grid=(blocks,),
        in_specs=[spot, whole, wide, wide],
        out_specs=[out, out],
        out_shape=[jax.ShapeDtypeStruct((blocks, width, BLK), bf16)] * 2,
        compiler_params=params(40),
        cost_estimate=cost(2 * rows * rows * width, 6 * rows * width),
    )(place.reshape(rows, 1), x, gain, shift)


def deal_g(place, g, live):
    rows, width = g.shape
    blocks = rows // BLK
    spot, whole, wide, out = deal_specs(rows, width)
    return pl.pallas_call(
        deal_g_body,
        grid=(blocks,),
        in_specs=[spot, whole, pl.BlockSpec((1, 1, BLK), lambda i: (i, 0, 0))],
        out_specs=[out, out, wide],
        out_shape=[jax.ShapeDtypeStruct((blocks, width, BLK), bf16)] * 2
        + [jax.ShapeDtypeStruct((width, BLK), f32)],
        compiler_params=params(40),
        cost_estimate=cost(2 * rows * rows * width, 6 * rows * width),
    )(place.reshape(rows, 1), g, live)


def send_back(place_ref, out_s, o_ref):
    rows = out_s.shape[0]
    spot = lax.broadcasted_iota(jnp.int32, (rows, rows), 0)
    pick = jnp.where(spot == place_ref[...], 1.0, 0.0).astype(bf16)
    o_ref[...] = nn(pick, out_s[...]).astype(bf16)


def total(refs, at):
    value = refs[0][at].astype(f32)
    for ref in refs[1:]:
        value = value + ref[at].astype(f32)
    return value


def layer_body(place_ref, xd_ref, live_ref, bias_ref, *refs):
    o_ref, out_s = refs[-2:]
    for at in range(xd_ref.shape[0]):
        y = xd_ref[at].astype(f32) + live_ref[at] * (total(refs[:-2], at) + bias_ref[...])
        out_s[at * BLK : (at + 1) * BLK, :] = y.T.astype(bf16)
    send_back(place_ref, out_s, o_ref)


def layer_rows(place, parts, xd, live, bias):
    blocks, width, _ = xd.shape
    rows = blocks * BLK
    return pl.pallas_call(
        layer_body,
        out_shape=jax.ShapeDtypeStruct((rows, width), bf16),
        scratch_shapes=[pltpu.VMEM((rows, width), bf16)],
        compiler_params=params(48),
        cost_estimate=cost(2 * rows * rows * width, 6 * rows * width),
    )(place.reshape(1, rows), xd, live, bias, *parts)


def input_body(place_ref, xd_ref, gd_ref, gain_ref, *refs):
    o_ref, sums_ref, out_s = refs[-3:]
    g_gain = jnp.zeros(gain_ref.shape, f32)
    g_shift = jnp.zeros(gain_ref.shape, f32)
    for at in range(xd_ref.shape[0]):
        x = xd_ref[at].astype(f32)
        centred = x - jnp.mean(x, axis=0, keepdims=True)
        inv_std = lax.rsqrt(jnp.mean(centred * centred, axis=0, keepdims=True) + epsilon)
        x_hat = centred * inv_std
        g = total(refs[:-3], at)
        g_gain = g_gain + g * x_hat
        g_shift = g_shift + g
        hat = g * gain_ref[...]
        back = inv_std * (
            hat
            - jnp.mean(hat, axis=0, keepdims=True)
            - x_hat * jnp.mean(hat * x_hat, axis=0, keepdims=True)
        )
        out_s[at * BLK : (at + 1) * BLK, :] = (gd_ref[at].astype(f32) + back).T.astype(bf16)
    sums_ref[0] = g_gain
    sums_ref[1] = g_shift
    send_back(place_ref, out_s, o_ref)


def input_rows(place, parts, xd, gd, gain):
    blocks, width, _ = xd.shape
    rows = blocks * BLK
    return pl.pallas_call(
        input_body,
        out_shape=[
            jax.ShapeDtypeStruct((rows, width), bf16),
            jax.ShapeDtypeStruct((2, width, BLK), f32),
        ],
        scratch_shapes=[pltpu.VMEM((rows, width), bf16)],
        compiler_params=params(48),
        cost_estimate=cost(2 * rows * rows * width, 8 * rows * width),
    )(place.reshape(1, rows), xd, gd, gain, *parts)


def project_body(ch, many, start_ref, x_ref, live_ref, wt_ref, bias_ref, *refs):
    a_ref, da_ref, gg_ref, dg_ref = refs[-4:]
    x = jnp.concatenate([x_ref[0], x_ref[1]], axis=1)
    live = live_ref[0]
    root = 0.7978845608028654
    step = 64 if ch % 128 else 128

    def act(pre):
        square = pre * pre
        rise = 0.5 + 0.5 * jnp.tanh(pre * (root + (0.044715 * root) * square))
        value = pre * rise
        slope = rise + rise * (pre - value) * (2.0 * root + (6.0 * 0.044715 * root) * square)
        return value, slope

    def put(ref, k, at, value):
        value = value.astype(bf16)
        ref[k, 0, at, :] = value[:, :BLK]
        ref[k, 1, at, :] = value[:, BLK:]

    for k in range(2):
        for first, value_ref, slope_ref in ((k * ch, a_ref, da_ref), ((2 + k) * ch, gg_ref, dg_ref)):
            for at in range(0, ch, step):
                rows = pl.ds(first + at, step)
                bias = bias_ref[rows, :]
                pre = nn(wt_ref[rows, :], x) + jnp.concatenate([bias, bias], axis=1)
                value, slope = act(pre)
                if value_ref is a_ref:
                    value, slope = live * value, live * slope
                put(value_ref, k, pl.ds(at, step), value)
                put(slope_ref, k, pl.ds(at, step), slope)


def chained(body, grid, in_specs, out_specs, shapes, scratch, limit, estimate, start, operands, kept):
    kept = [] if kept is None else list(kept)
    specs = list(in_specs) + [pl.BlockSpec(memory_space=pl.ANY)] * len(kept)
    first = 1 + len(operands)
    return pl.pallas_call(
        body,
        grid_spec=pltpu.PrefetchScalarGridSpec(
            num_scalar_prefetch=1, grid=grid, in_specs=specs, out_specs=out_specs, scratch_shapes=scratch
        ),
        out_shape=shapes,
        input_output_aliases={first + at: at for at in range(len(kept))},
        compiler_params=params(limit),
        cost_estimate=estimate,
    )(start, *operands, *kept)


def project(xt, start, nb, live, wt, bias, kept):
    many, width, _ = xt.shape
    ch = wt.shape[0] // 4
    out = pl.BlockSpec((2, 2, ch, BLK), lambda i, at: (0, at[0] + i, 0, 0))
    tok = many * BLK
    return chained(
        partial(project_body, ch, many),
        (many // 2,),
        [
            pl.BlockSpec((2, width, BLK), lambda i, at: (i, 0, 0)),
            pl.BlockSpec((1, 1, BIG), lambda i, at: (at[0] + i, 0, 0)),
            pl.BlockSpec((4 * ch, width), lambda i, at: (0, 0)),
            pl.BlockSpec((4 * ch, BLK), lambda i, at: (0, 0)),
        ],
        [out] * 4,
        [jax.ShapeDtypeStruct((2, nb, ch, BLK), bf16)] * 4,
        [],
        48,
        cost(8 * tok * width * ch, 2 * tok * width + 16 * tok * ch, 4 * tok * ch),
        start // 2,
        [xt, live, wt, bias],
        kept,
    )


def gate_grad_body(ch, parts, at_ref, *refs):
    wt_ref, o_ref = refs[parts:]
    steps = pl.num_programs(0) // parts

    def work(g_ref):
        gm = nn(wt_ref[...], jnp.concatenate([g_ref[0], g_ref[1]], axis=1)).astype(bf16)
        for k in range(2):
            for h in range(2):
                o_ref[k, h] = gm[k * ch : (k + 1) * ch, h * BLK : (h + 1) * BLK]

    for part in range(parts):

        @pl.when(pl.program_id(0) // steps == part)
        def _(part=part):
            work(refs[part])


def gate_grad(gs, nb, wt):
    parts = len(gs)
    many, width, _ = gs[0][0].shape
    steps = many // 2
    ch = wt.shape[0] // 2
    tok = nb * BLK

    def rows(part):
        return pl.BlockSpec((2, width, BLK), lambda i, at: (jnp.clip(i - part * steps, 0, steps - 1), 0, 0))

    order = jnp.concatenate([start // 2 for _, start in gs]).astype(jnp.int32)
    return pl.pallas_call(
        partial(gate_grad_body, ch, parts),
        grid_spec=pltpu.PrefetchScalarGridSpec(
            num_scalar_prefetch=1,
            grid=(parts * steps,),
            in_specs=[rows(part) for part in range(parts)] + [pl.BlockSpec((2 * ch, width), lambda i, at: (0, 0))],
            out_specs=pl.BlockSpec((2, 2, ch, BLK), lambda i, at: (0, at[i // steps] + i % steps, 0, 0)),
        ),
        out_shape=jax.ShapeDtypeStruct((2, nb, ch, BLK), bf16),
        compiler_params=params(40),
        cost_estimate=cost(4 * tok * width * ch, 2 * tok * width + 4 * tok * ch),
    )(order, *[part for part, _ in gs], wt)


def spectra_body(cc, ld_ref, w_ref, d_ref, wave_ref, kh_ref, k_s):
    t = lax.broadcasted_iota(jnp.int32, (BLK, BLK), 0).astype(f32)
    block = lax.broadcasted_iota(jnp.int32, (2 * LAGS, BLK), 0).astype(f32) * float(BLK)
    low = lax.broadcasted_iota(jnp.int32, (2 * LAGS, BLK), 1) < STATE
    count = 2 * LAGS

    def one(p, carry):
        ld = ld_ref[0, pl.ds(p, 1), :]
        decay = jnp.exp2(t * ld)
        scale = w_ref[0, pl.ds(p, 1), :] * jnp.exp2(block * ld)
        lhs = jnp.concatenate([jnp.where(low, scale, 0.0), jnp.where(low, 0.0, scale)], axis=0)
        lhs_high, lhs_low = halves(lhs)
        k = nt(jnp.concatenate([lhs_high, lhs_low], axis=0), decay.astype(bf16))
        k = k[0 : 2 * count] + k[2 * count : 4 * count]
        k_s[pl.ds(2 * p, count, stride=cc), :] = k[0:count]
        k_s[pl.ds(2 * p + 1, count, stride=cc), :] = k[count : 2 * count]
        return carry

    lax.fori_loop(0, cc // 2, one, 0, unroll=16)
    sign = jnp.where(lax.broadcasted_iota(jnp.int32, (cc, BIG), 1) % 2 == 0, 1.0, -1.0)
    before = None
    for big in range(LAGS):
        rows = jnp.concatenate(
            [k_s[pl.ds(2 * big * cc, cc), :], k_s[pl.ds((2 * big + 1) * cc, cc), :]], axis=1
        )
        high, rest = halves(rows)
        x = nn(high, wave_ref[...]) + nn(rest, wave_ref[...])
        xc, xs = x[:, :BIG], x[:, BIG:]
        if big == 0:
            kh_ref[0, 0, :, :BIG] = xc + d_ref[0][:, 0:1]
            kh_ref[0, 0, :, BIG:] = xs
        else:
            kh_ref[0, big, :, :BIG] = xc + sign * before[1]
            kh_ref[0, big, :, BIG:] = xs - sign * before[0]
        before = (xc, xs)


def spectra(ld, w, d, wave):
    ch = 2 * ld.shape[1]
    cc = chunk_of(ch, 128)
    return pl.pallas_call(
        partial(spectra_body, cc),
        grid=(2, ch // cc),
        in_specs=[pl.BlockSpec((1, cc // 2, BLK), lambda k, i: (k, i, 0))] * 2
        + [
            pl.BlockSpec((1, cc, BLK), lambda k, i: (k, i, 0)),
            pl.BlockSpec((BIG, 2 * BIG), lambda k, i: (0, 0)),
        ],
        out_specs=pl.BlockSpec((1, LAGS, cc, 2 * BIG), lambda k, i: (k, 0, i, 0)),
        out_shape=jax.ShapeDtypeStruct((2, LAGS, ch, 2 * BIG), f32),
        scratch_shapes=[pltpu.VMEM((2 * LAGS * cc, BLK), f32)],
        compiler_params=params(40),
        cost_estimate=cost(2 * ch * 40e6, 2 * ch * LAGS * 2 * BIG * 4),
    )(ld, w, d, wave)


def moments_body(cc, ld_ref, gh_ref, back_ref, s0_ref, s1_ref, g0_ref, g_s):
    sign = jnp.where(lax.broadcasted_iota(jnp.int32, (cc, BIG), 1) % 2 == 0, 1.0, -1.0)
    count = 2 * LAGS
    for big in range(LAGS):
        c = gh_ref[0, big, :, :BIG]
        s = gh_ref[0, big, :, BIG:]
        if big < LAGS - 1:
            c, s = c - sign * gh_ref[0, big + 1, :, BIG:], s + sign * gh_ref[0, big + 1, :, :BIG]
        high, rest = halves(jnp.concatenate([c, s], axis=1))
        g = nn(high, back_ref[...]) + nn(rest, back_ref[...])
        g_s[pl.ds(2 * big * cc, cc), :] = g[:, :BLK]
        g_s[pl.ds((2 * big + 1) * cc, cc), :] = g[:, BLK:]
        if big == 0:
            g0_ref[0] = g[:, :BLK]
    t = lax.broadcasted_iota(jnp.int32, (BLK, BLK), 0).astype(f32)
    lane = lax.broadcasted_iota(jnp.int32, (count, BLK), 1)
    lag = lane.astype(f32)
    block = lax.broadcasted_iota(jnp.int32, (count, BLK), 0).astype(f32) * float(BLK)
    low = lane < STATE

    def one(p, carry):
        ld = ld_ref[0, pl.ds(p, 1), :]
        decay = jnp.exp2(t * ld).astype(bf16)
        far = jnp.exp2(block * ld)
        ga = g_s[pl.ds(2 * p, count, stride=cc), :]
        gb = g_s[pl.ds(2 * p + 1, count, stride=cc), :]
        high, rest = halves(jnp.concatenate([ga, gb, ga * lag, gb * lag], axis=0))
        m = nn(jnp.concatenate([high, rest], axis=0), decay)
        m = m[0 : 4 * count] + m[4 * count : 8 * count]
        m0 = jnp.where(low, m[0:count], m[count : 2 * count])
        m1 = jnp.where(low, m[2 * count : 3 * count], m[3 * count : 4 * count]) + block * m0
        s0_ref[0, pl.ds(p, 1), :] = jnp.sum(far * m0, axis=0, keepdims=True)
        s1_ref[0, pl.ds(p, 1), :] = jnp.sum(far * m1, axis=0, keepdims=True)
        return carry

    lax.fori_loop(0, cc // 2, one, 0, unroll=16)


def moments(k, ld, gh, back):
    ch = gh.shape[2]
    cc = chunk_of(ch, 128)
    row = pl.BlockSpec((1, cc // 2, BLK), lambda i: (0, i, 0))
    return pl.pallas_call(
        partial(moments_body, cc),
        grid=(ch // cc,),
        in_specs=[
            pl.BlockSpec((1, cc // 2, BLK), lambda i: (k, i, 0)),
            pl.BlockSpec((1, LAGS, cc, 2 * BIG), lambda i: (0, 0, i, 0)),
            pl.BlockSpec((2 * BIG, BIG), lambda i: (0, 0)),
        ],
        out_specs=[row, row, pl.BlockSpec((1, cc, BLK), lambda i: (0, i, 0))],
        out_shape=[jax.ShapeDtypeStruct((1, ch // 2, BLK), f32)] * 2
        + [jax.ShapeDtypeStruct((1, ch, BLK), f32)],
        scratch_shapes=[pltpu.VMEM((2 * LAGS * cc, BLK), f32)],
        compiler_params=params(40),
        cost_estimate=cost(ch * 40e6, ch * LAGS * 2 * BIG * 4),
    )(ld, gh, back)


def load_pieces(nb, pieces, cc, tab_ref, block, in_s, wave_ref, dst):
    for h in range(pieces):
        first = tab_ref[0, h]
        whole = tab_ref[1, h].astype(f32)
        in_s[pl.ds(h * cc, cc), 0:BLK] = block(first).astype(bf16)
        in_s[pl.ds(h * cc, cc), BLK:BIG] = (block(jnp.minimum(first + 1, nb - 1)) * whole).astype(bf16)
    for h in range(pieces):
        at = pl.ds(h * cc, cc)
        dst[at, :] = nn(in_s[at, :], wave_ref[...])


def over_pieces(nseq, cc, rg, seq_ref, piece):
    def group(r, carry):
        off = pl.multiple_of(r * rg, rg)
        for s in range(nseq):
            base = seq_ref[0, s]
            count = seq_ref[1, s]

            def outer(i, carry):
                piece(i, count, base, off)
                return carry

            lax.fori_loop(0, count, outer, 0)
        return carry

    lax.fori_loop(0, cc // rg, group, 0)


def scan_body(
    nb, nseq, cc, rg, tab_ref, seq_ref, a_ref, kh_ref, wave_ref, back_ref, gg_ref, y_ref, mix_ref, in_s, ah_s, yh_s, y_s
):
    pieces = (nb + nseq) // 2
    load_pieces(nb, pieces, cc, tab_ref, lambda b: a_ref[0, b].astype(f32), in_s, wave_ref, ah_s)
    zero = jnp.zeros((rg, BIG), f32)

    def products(flip):
        def piece(i, count, base, off):
            def inner(j, acc):
                yc, ys = acc
                other = (base + i + j) if flip else (base + i - j)
                m = pl.ds(pl.multiple_of(other * cc + off, rg), rg)
                rows = pl.ds(off, rg)
                ac = ah_s[m, :BIG]
                as_ = ah_s[m, BIG:]
                kc = kh_ref[0, j, rows, :BIG]
                ks = kh_ref[0, j, rows, BIG:]
                if flip:
                    return (yc + kc * ac + ks * as_, ys + kc * as_ - ks * ac)
                return (yc + kc * ac - ks * as_, ys + kc * as_ + ks * ac)

            yc, ys = lax.fori_loop(0, (count - i) if flip else (i + 1), inner, (zero, zero))
            at = pl.ds(pl.multiple_of((base + i) * cc + off, rg), rg)
            yh_s[at, :BIG] = yc.astype(bf16)
            yh_s[at, BIG:] = ys.astype(bf16)

        over_pieces(nseq, cc, rg, seq_ref, piece)

    @pl.when(pl.program_id(0) == 0)
    def _():
        products(False)

    @pl.when(pl.program_id(0) == 1)
    def _():
        products(True)

    for h in range(pieces):
        at = pl.ds(h * cc, cc)
        y_s[at, :] = nn(yh_s[at, :], back_ref[...])

    def one(b, y):
        y_ref[0, b] = y.astype(bf16)
        mix_ref[0, b] = (y * gg_ref[0, b].astype(f32)).astype(bf16)

    def last(h, carry):
        b = tab_ref[0, h]
        at = pl.ds(pl.multiple_of(h * cc, cc), cc)
        one(b, y_s[at, 0:BLK])

        @pl.when(tab_ref[1, h] == 1)
        def _():
            one(b + 1, y_s[at, BLK:])

        return carry

    lax.fori_loop(0, seq_ref[1, nseq], last, 0)
    nothing = jnp.zeros((cc, BLK), bf16)

    def fill(b, carry):
        y_ref[0, b] = nothing
        mix_ref[0, b] = nothing
        return carry

    lax.fori_loop(seq_ref[0, nseq], nb, fill, 0)


def back_body(
    nb, nseq, cc, rg, flip, tab_ref, seq_ref, a_ref, gm_ref, kh_ref, wave_ref, back_ref, gg_ref, y_ref, dg_ref, da_ref,
    gpg_ref, gp_ref, gh_ref, bs_ref, in_s, ah_s, gh_s, xh_s, x_s,
):
    pieces = (nb + nseq) // 2
    load_pieces(nb, pieces, cc, tab_ref, lambda b: a_ref[0, b].astype(f32), in_s, wave_ref, ah_s)
    load_pieces(
        nb, pieces, cc, tab_ref, lambda b: gm_ref[0, b].astype(f32) * gg_ref[0, b].astype(f32), in_s, wave_ref, gh_s
    )
    gh_ref[...] = jnp.zeros_like(gh_ref)
    zero = jnp.zeros((rg, BIG), f32)

    def piece(i, count, base, off):
        at = pl.ds(pl.multiple_of((base + i) * cc + off, rg), rg)
        ac = ah_s[at, :BIG]
        as_ = ah_s[at, BIG:]

        def inner(j, acc):
            xc, xs = acc
            other = (base + i - j) if flip else (base + i + j)
            m = pl.ds(pl.multiple_of(other * cc + off, rg), rg)
            rows = pl.ds(off, rg)
            gc = gh_s[m, :BIG]
            gs = gh_s[m, BIG:]
            kc = kh_ref[0, j, rows, :BIG]
            ks = kh_ref[0, j, rows, BIG:]
            gh_ref[0, j, rows, :BIG] += ac * gc + as_ * gs
            if flip:
                gh_ref[0, j, rows, BIG:] += gc * as_ - gs * ac
                return (xc + kc * gc - ks * gs, xs + kc * gs + ks * gc)
            gh_ref[0, j, rows, BIG:] += ac * gs - as_ * gc
            return (xc + kc * gc + ks * gs, xs + kc * gs - ks * gc)

        xc, xs = lax.fori_loop(0, (i + 1) if flip else (count - i), inner, (zero, zero))
        xh_s[at, :BIG] = xc.astype(bf16)
        xh_s[at, BIG:] = xs.astype(bf16)

    over_pieces(nseq, cc, rg, seq_ref, piece)

    for h in range(pieces):
        at = pl.ds(h * cc, cc)
        x_s[at, :] = nn(xh_s[at, :], back_ref[...])

    none = jnp.zeros((cc, BLK), f32)

    def one(b, gx, carry):
        s0, s1 = carry
        gpg = (y_ref[0, b].astype(f32) * gm_ref[0, b].astype(f32) * dg_ref[0, b].astype(f32)).astype(bf16)
        gpg_ref[0, b] = gpg
        gp = (gx * da_ref[0, b].astype(f32)).astype(bf16)
        gp_ref[0, b] = gp
        return (s0 + gpg.astype(f32), s1 + gp.astype(f32))

    def last(h, carry):
        b = tab_ref[0, h]
        at = pl.ds(pl.multiple_of(h * cc, cc), cc)
        carry = one(b, x_s[at, 0:BLK], carry)

        def more(kept):
            return one(b + 1, x_s[at, BLK:], kept)

        return lax.cond(tab_ref[1, h] == 1, more, lambda kept: kept, carry)

    s0, s1 = lax.fori_loop(0, seq_ref[1, nseq], last, (none, none))
    bs_ref[0, :, 0:BLK] = s0
    bs_ref[0, :, BLK:] = s1
    nothing = jnp.zeros((cc, BLK), bf16)

    def fill(b, carry):
        gpg_ref[0, b] = nothing
        gp_ref[0, b] = nothing
        return carry

    lax.fori_loop(seq_ref[0, nseq], nb, fill, 0)


def ssm_specs(shape, seq):
    _, nb, ch, _ = shape
    nseq = seq.shape[1] - 1
    pieces = (nb + nseq) // 2
    cc = chunk_of(ch, 128 if nb <= 32 else 64)
    big = pl.BlockSpec((1, nb, cc, BLK), lambda k, i: (k, 0, i, 0))
    spec = pl.BlockSpec((1, LAGS, cc, 2 * BIG), lambda k, i: (k, 0, i, 0))
    smem = pl.BlockSpec(memory_space=pltpu.SMEM)
    head = [smem, smem]
    tables = [pl.BlockSpec((BIG, 2 * BIG), lambda k, i: (0, 0)), pl.BlockSpec((2 * BIG, BIG), lambda k, i: (0, 0))]
    return nb, nseq, ch, cc, pieces * cc, big, spec, head, tables


def ssm_scan(tab, seq, a, kh, wave, back, gg):
    nb, nseq, ch, cc, size, big, spec, head, tables = ssm_specs(a.shape, seq)
    return pl.pallas_call(
        partial(scan_body, nb, nseq, cc, 32),
        grid=(2, ch // cc),
        in_specs=head + [big, spec] + tables + [big],
        out_specs=[big, big],
        out_shape=[jax.ShapeDtypeStruct(a.shape, bf16)] * 2,
        scratch_shapes=[
            pltpu.VMEM((size, BIG), bf16),
            pltpu.VMEM((size, 2 * BIG), f32),
            pltpu.VMEM((size, 2 * BIG), bf16),
            pltpu.VMEM((size, BIG), f32),
        ],
        compiler_params=params(56),
        cost_estimate=cost(2 * ch * 50e6, 2 * ch * nb * BLK * 8),
    )(tab, seq, a, kh, wave, back, gg)


def ssm_back(k, tab, seq, a, gm, kh, wave, back, gg, y, dg, da):
    nb, nseq, ch, cc, size, _, _, head, tables = ssm_specs(a.shape, seq)
    big = pl.BlockSpec((1, nb, cc, BLK), lambda i: (k, 0, i, 0))
    spec = pl.BlockSpec((1, LAGS, cc, 2 * BIG), lambda i: (k, 0, i, 0))
    out = pl.BlockSpec((1, nb, cc, BLK), lambda i: (0, 0, i, 0))
    out_spec = pl.BlockSpec((1, LAGS, cc, 2 * BIG), lambda i: (0, 0, i, 0))
    tables = [
        pl.BlockSpec((BIG, 2 * BIG), lambda i: (0, 0)),
        pl.BlockSpec((2 * BIG, BIG), lambda i: (0, 0)),
    ]
    return pl.pallas_call(
        partial(back_body, nb, nseq, cc, 64, k == 1),
        grid=(ch // cc,),
        in_specs=head + [big, big, spec] + tables + [big] * 4,
        out_specs=[out, out, out_spec, pl.BlockSpec((1, cc, 2 * BLK), lambda i: (0, i, 0))],
        out_shape=[jax.ShapeDtypeStruct((1,) + a.shape[1:], bf16)] * 2
        + [
            jax.ShapeDtypeStruct((1, LAGS, ch, 2 * BIG), f32),
            jax.ShapeDtypeStruct((1, ch, 2 * BLK), f32),
        ],
        scratch_shapes=[
            pltpu.VMEM((size, BIG), bf16),
            pltpu.VMEM((size, 2 * BIG), f32),
            pltpu.VMEM((size, 2 * BIG), f32),
            pltpu.VMEM((size, 2 * BIG), bf16),
            pltpu.VMEM((size, BIG), f32),
        ],
        compiler_params=params(60),
        cost_estimate=cost(ch * 80e6, ch * nb * BLK * 16),
    )(tab, seq, a, gm, kh, wave, back, gg, y, dg, da)


def stack_pair(refs):
    return jnp.concatenate(
        [jnp.concatenate([ref[k, 0], ref[k, 1]], axis=1) for ref in refs for k in range(ref.shape[0])], axis=0
    )


def mul_body(count, more, start_ref, w_ref, *refs):
    out = nn(w_ref[...], stack_pair(refs[:count]))
    o_ref = refs[-1]
    for h in range(2):
        part = out[:, h * BLK : (h + 1) * BLK]
        if more:
            part = part + refs[count][h].astype(f32)
        o_ref[h] = part.astype(o_ref.dtype)


def mul_rows(w, arrays, start, many, dtype=bf16, extra=None):
    width, deep = w.shape
    ch = arrays[0].shape[2]
    count = len(arrays)
    out = pl.BlockSpec((2, width, BLK), lambda i, at: (i, 0, 0))
    return pl.pallas_call(
        partial(mul_body, count, extra is not None),
        grid_spec=pltpu.PrefetchScalarGridSpec(
            num_scalar_prefetch=1,
            grid=(many // 2,),
            in_specs=[pl.BlockSpec((width, deep), lambda i, at: (0, 0))]
            + [pl.BlockSpec((x.shape[0], 2, ch, BLK), lambda i, at: (0, at[0] + i, 0, 0)) for x in arrays]
            + ([] if extra is None else [out]),
            out_specs=out,
        ),
        out_shape=jax.ShapeDtypeStruct((many, width, BLK), dtype),
        compiler_params=params(40),
        cost_estimate=cost(2 * many * BLK * width * deep, 2 * many * BLK * (2 * width + deep)),
    )(start // 2, w, *arrays, *([] if extra is None else [extra]))


def outer_body(ch, many, cuts, parts, at_ref, *refs):
    step = pl.program_id(0)
    xs, gs = refs[:parts], refs[parts : 2 * parts]
    gp_refs, gpg_refs, mix_ref = refs[2 * parts : 2 * parts + 2], refs[2 * parts + 2 : 2 * parts + 4], refs[2 * parts + 4]
    outs = refs[2 * parts + 5 : 2 * parts + 5 + cuts]
    acc_s, x_s, g_s = refs[-3:]

    def fill(at):
        for b in range(many):
            x_s[:, b * BLK : (b + 1) * BLK] = xs[at][b]
            g_s[:, b * BLK : (b + 1) * BLK] = gs[at][b]

    if parts == 1:
        fill(0)
    else:
        for at in range(parts):

            @pl.when(step == at)
            def _(at=at):
                fill(at)

    def part(ref, k):
        return jnp.concatenate([ref[k, b] for b in range(many)], axis=1)

    @pl.when(step == 0)
    def _():
        acc_s[...] = jnp.zeros_like(acc_s)

    split = 4 * ch
    left = jnp.concatenate([part(ref, 0) for ref in (*gp_refs, *gpg_refs)], axis=0)
    acc_s[:, :split] += nt(x_s[...], left)
    acc_s[:, split:] += nt(g_s[...], jnp.concatenate([part(mix_ref, 0), part(mix_ref, 1)], axis=0))

    @pl.when(step == pl.num_programs(0) - 1)
    def _():
        deep = acc_s.shape[0] // cuts
        for cut in range(cuts):
            start = pl.multiple_of(at_ref[pl.num_programs(0) + cut] * deep, 8)
            outs[cut][...] = acc_s[pl.ds(start, deep), :].astype(bf16)


def outer_sums(order, cuts, xs, gs, gp, gpg, mix):
    width = xs[0].shape[1]
    _, nb, ch, _ = mix.shape
    many = 8
    parts = len(xs)
    if parts == 1:
        rows = pl.BlockSpec((many, width, BLK), lambda i, at: (i, 0, 0))
    else:
        rows = pl.BlockSpec((many, width, BLK), lambda i, at: (0, 0, 0), pipeline_mode=pl.Buffered(1))
    chan = pl.BlockSpec((2, many, ch, BLK), lambda i, at: (0, at[i], 0, 0))
    one = pl.BlockSpec((1, many, ch, BLK), lambda i, at: (0, at[i], 0, 0))
    tok = nb * BLK
    return pl.pallas_call(
        partial(outer_body, ch, many, cuts, parts),
        grid_spec=pltpu.PrefetchScalarGridSpec(
            num_scalar_prefetch=1,
            grid=(nb // many,),
            in_specs=[rows] * (2 * parts) + [one] * 4 + [chan],
            out_specs=[pl.BlockSpec((width // cuts, 6 * ch), lambda i, at: (0, 0))] * cuts,
            scratch_shapes=[
                pltpu.VMEM((width, 6 * ch), f32),
                pltpu.VMEM((width, many * BLK), bf16),
                pltpu.VMEM((width, many * BLK), bf16),
            ],
        ),
        out_shape=[jax.ShapeDtypeStruct((width // cuts, 6 * ch), bf16)] * cuts,
        compiler_params=params(60),
        cost_estimate=cost(12 * tok * width * ch, tok * (4 * width + 12 * ch)),
    )(order, *xs, *gs, *gp, *gpg, mix)


def join_body(split, w_ref, head_ref, tail_ref, head_t_ref, tail_t_ref):
    head_ref[...] = w_ref[:, :split]
    tail_ref[...] = w_ref[:, split:]
    head_t_ref[...] = w_ref[:, :split].T
    tail_t_ref[...] = w_ref[:, split:].T


def split_weights(w, split):
    rows, wide = w.shape
    vmem = pl.BlockSpec(memory_space=pltpu.VMEM)
    return pl.pallas_call(
        partial(join_body, split),
        in_specs=[vmem],
        out_specs=[vmem] * 4,
        out_shape=[
            jax.ShapeDtypeStruct(shape, bf16)
            for shape in ((rows, split), (rows, wide - split), (split, rows), (wide - split, rows))
        ],
        compiler_params=params(48),
        cost_estimate=cost(0, 6 * rows * wide),
    )(w)


def meet_body(
    axes, rank_ref, x_ref, chan_ref, norm_ref, pack_ref, got_ref, call_ref, nall_ref, wall_ref, send_s, *sems
):
    xs_sem, xr_sem, cs_sem, cr_sem, ns_sem, nr_sem, ws_sem, wr_sem, own_sem = sems
    q, c, h, w = (lax.axis_index(name) for name in axes)
    rows = x_ref.shape[0]
    piece = rows // 8
    flat = ((2 * q + c) * 2 + h) * 2 + w

    def peer(bits):
        return (q ^ (bits // 8), c ^ (bits // 4 % 2), h ^ (bits // 2 % 2), w ^ (bits % 2))

    barrier = pltpu.get_barrier_semaphore()
    for bits in range(1, 32):
        pl.semaphore_signal(barrier, inc=1, device_id=peer(bits), device_id_type=pl.DeviceIdType.MESH)
    pl.semaphore_wait(barrier, 31)

    def remote(src, dst, send, recv, to):
        return pltpu.make_async_remote_copy(
            src_ref=src, dst_ref=dst, send_sem=send, recv_sem=recv, device_id=to, device_id_type=pl.DeviceIdType.MESH
        )

    deep = pack_ref.shape[0]

    def shard(at):
        return wall_ref.at[pl.ds(pl.multiple_of(at * deep, 16), deep)]

    def first_copy():
        return remote(pack_ref, shard(2 * q + c), ws_sem.at[0], wr_sem.at[c], (q, 1 - h, c, w))

    def second_copy():
        return remote(pack_ref, shard(2 * q + c), ws_sem.at[1], wr_sem.at[c], (q, 1 - h, 1 - c, w))

    def own_shard():
        return pltpu.make_async_copy(pack_ref, shard(2 * q + c), own_sem.at[2])

    def shard_came(at):
        return remote(pack_ref, shard(2 * q + at), ws_sem.at[0], wr_sem.at[at], peer(1))

    def pass_on(at, bits):
        spot_w = 3 * at + bits + 1
        return remote(shard(2 * q + at), shard(2 * q + at), ws_sem.at[spot_w], wr_sem.at[spot_w], (q ^ bits, c, h, w))

    first_copy().start()

    @pl.when(c != h)
    def _():
        own_shard().start()

    @pl.when(c == h)
    def _():
        second_copy().start()

    nall_ref[flat] = norm_ref[...]

    def norm_copy(bits):
        return remote(norm_ref, nall_ref.at[flat], ns_sem.at[bits], nr_sem.at[bits], peer(bits))

    for bits in range(1, 32):
        norm_copy(bits).start()

    pieces = [(kq, kh) for kh in (0, 1) for kq in (1, 2, 3, 0)]
    spot = lax.broadcasted_iota(jnp.int32, (piece, rows), 0)

    def row_copy(kq, kh):
        at = 2 * kq + kh
        return remote(
            send_s.at[at], got_ref.at[2 * q + c], xs_sem.at[at], xr_sem.at[2 * kq + c], (q ^ kq, 1 - h, h ^ kh, w)
        )

    def own_copy():
        return pltpu.make_async_copy(send_s.at[0], got_ref.at[2 * q + c], own_sem.at[0])

    for kq, kh in pieces:
        chunk = 2 * (q ^ kq) + (h ^ kh)
        pick = jnp.where(spot + chunk * piece == rank_ref[...], 1.0, 0.0).astype(bf16)
        send_s[2 * kq + kh] = nn(pick, x_ref[...]).astype(bf16)
        if (kq, kh) == (1, 1):
            for at in range(2):

                @pl.when((c != h) & (at == c))
                def _():
                    own_shard().wait()

                @pl.when(jnp.logical_not((c != h) & (at == c)))
                def _(at=at):
                    shard_came(at).wait_recv()

                for bits in range(1, 4):
                    pass_on(at, bits).start()
        if (kq, kh) == (0, 0):

            @pl.when(c != h)
            def _():
                own_copy().start()

            @pl.when(c == h)
            def _():
                row_copy(0, 0).start()

        else:
            row_copy(kq, kh).start()

    place = 2 * (1 - c) + w
    spot_c = 4 * c + 2 * h + w

    def chan_copy(at):
        to = (q ^ at, 1 - q // 2, h, q % 2) if at < 4 else (2 * c + w, 1 - q // 2, 1 - h, q % 2)
        return remote(chan_ref, call_ref.at[spot_c], cs_sem.at[at], cr_sem.at[spot_c], to)

    def own_chan():
        return pltpu.make_async_copy(chan_ref, call_ref.at[spot_c], own_sem.at[1])

    def chan_came(at):
        return remote(chan_ref, call_ref.at[at], cs_sem.at[0], cr_sem.at[at], peer(1))

    far_spot = 4 * (q // 2) + 2 * (1 - h) + q % 2

    def chan_pass(bits):
        return remote(
            call_ref.at[far_spot], call_ref.at[far_spot], cs_sem.at[4 + bits], cr_sem.at[far_spot], (q ^ bits, c, h, w)
        )

    for at in (4, 1, 2, 3, 0):
        if at:
            chan_copy(at).start()
        else:

            @pl.when(place == q)
            def _():
                own_chan().start()

            @pl.when(place != q)
            def _():
                chan_copy(0).start()

    for bits in range(1, 32):
        norm_copy(bits).wait()
    for at in range(8):

        @pl.when((c != h) & (at == c))
        def _():
            own_copy().wait()

        @pl.when(jnp.logical_not((c != h) & (at == c)))
        def _(at=at):
            remote(send_s.at[at], got_ref.at[at], xs_sem.at[at], xr_sem.at[at], peer(1)).wait_recv()

    chan_came(far_spot).wait_recv()
    for bits in range(1, 4):
        chan_pass(bits).start()
    for at in range(8):

        @pl.when((place == q) & (at == spot_c))
        def _():
            own_chan().wait()

        @pl.when(jnp.logical_not((place == q) & (at == spot_c)) & (at != far_spot))
        def _(at=at):
            chan_came(at).wait_recv()

    for bits in range(1, 4):
        chan_pass(bits).wait_send()
    for at in range(2):
        for bits in range(1, 4):
            pass_on(at, bits).wait()
    first_copy().wait_send()

    @pl.when(c == h)
    def _():
        second_copy().wait_send()

    for kq, kh in pieces:
        if (kq, kh) == (0, 0):

            @pl.when(c == h)
            def _():
                row_copy(0, 0).wait_send()

        else:
            row_copy(kq, kh).wait_send()
    for at in range(1, 5):
        chan_copy(at).wait_send()

    @pl.when(place != q)
    def _():
        chan_copy(0).wait_send()


def meet(axes, rank, x, chan, norm, pack):
    rows, width = x.shape
    vmem = pl.BlockSpec(memory_space=pltpu.VMEM)
    sem = pltpu.SemaphoreType.DMA
    return pl.pallas_call(
        partial(meet_body, axes),
        in_specs=[vmem] * 5,
        out_specs=[vmem] * 4,
        out_shape=[
            jax.ShapeDtypeStruct((8, rows // 8, width), bf16),
            jax.ShapeDtypeStruct((8,) + chan.shape, f32),
            jax.ShapeDtypeStruct((32,) + norm.shape, f32),
            jax.ShapeDtypeStruct((8 * pack.shape[0], pack.shape[1]), bf16),
        ],
        scratch_shapes=[pltpu.VMEM((8, rows // 8, width), bf16)]
        + [sem((8,)), sem((8,)), sem((8,)), sem((8,)), sem((32,)), sem((32,)), sem((8,)), sem((8,)), sem((3,))],
        compiler_params=pltpu.CompilerParams(collective_id=1, has_side_effects=True, vmem_limit_bytes=60 * MIB),
        cost_estimate=cost(2 * rows * rows * width, 100 * rows * width),
    )(rank.reshape(1, rows), x, chan, norm, pack)


def sequence_tables(lens, nb):
    nseq = lens.shape[0]
    blocks = (lens + BLK - 1) // BLK
    start = jnp.cumsum(blocks) - blocks
    bigs = (blocks + 1) // 2
    first_big = jnp.cumsum(bigs) - bigs
    h = jnp.arange((nb + nseq) // 2, dtype=jnp.int32)
    owner = (h[:, None] >= first_big[None, :]).astype(jnp.int32).sum(axis=1) - 1
    mine = owner[:, None] == jnp.arange(nseq, dtype=jnp.int32)[None, :]

    def at_owner(values):
        return jnp.sum(jnp.where(mine, values[None, :], 0), axis=1)

    rel = h - at_owner(first_big)
    first = jnp.minimum(at_owner(start) + 2 * rel, nb - 1)
    whole = (2 * rel + 1 < at_owner(blocks)).astype(jnp.int32)
    tab = jnp.stack([first, whole]).astype(jnp.int32)
    seq = jnp.stack(
        [jnp.append(first_big, jnp.sum(blocks)), jnp.append(bigs, jnp.sum(bigs))]
    ).astype(jnp.int32)
    return tab, seq


def live_rows(lens, rows):
    slot = (lens + BLK - 1) // BLK * BLK
    begin = jnp.cumsum(slot) - slot
    pos = jnp.arange(rows, dtype=jnp.int32)
    inside = (pos[:, None] >= begin[None, :]) & (pos[:, None] < (begin + lens)[None, :])
    return jnp.sum(inside.astype(f32), axis=1)


def after(values):
    return lax.optimization_barrier(values)


def rank_of(keys):
    return jnp.sum((keys[None, :] < keys[:, None]).astype(jnp.int32), axis=1)


class Line:
    def __init__(self, n_dp, n_t):
        self.n_dp, self.n_t = n_dp, n_t
        self.axes = {"dp": n_dp, "tensor": n_t}
        self.both = ("dp", "tensor")
        self.cuts = 1

    def place_of_group(self):
        return lax.axis_index("tensor")

    def regroup(self, x):
        return x

    def gather_first(self, x):
        return [lax.all_gather(x, "tensor", axis=0, tiled=True)]

    def gathered(self, x, early):
        return []

    def gather_last(self, x, got):
        return [(got[0], jnp.zeros((1,), jnp.int32))]

    def scatter_first(self, w, arrays, many):
        return [mul_rows(w, arrays, jnp.zeros((1,), jnp.int32), many * self.n_t)]

    def scatter_send(self, parts):
        return [lax.psum_scatter(parts[0], "tensor", scatter_dimension=0, tiled=True)]

    def scatter_own(self, w, arrays, many):
        return []

    def ungroup(self, x):
        return x

    def spread(self, x):
        return lax.all_to_all(x, "dp", split_axis=0, concat_axis=0, tiled=True)

    def order(self, pieces):
        return jnp.append(jnp.arange(pieces * self.n_t, dtype=jnp.int32), 0)

    def enter(self, rank, x, chan, norm, pack):
        (sent,) = permute_to(rank, [x])
        return (self.spread(sent),) + self.gather_channels(chan, norm) + (lax.all_gather(pack, "dp", axis=0, tiled=True),)

    def gather_channels(self, chan, norm):
        perm = [(f, (f % self.n_dp) * self.n_t + f // self.n_dp) for f in range(self.n_dp * self.n_t)]
        chan = lax.ppermute(chan, self.both, perm)
        norm = lax.all_gather(norm, self.both, axis=1, tiled=True)
        return lax.all_gather(chan[None], "dp", axis=0, tiled=True), norm

    def cut_order(self):
        return jnp.zeros((1,), jnp.int32)

    def grads_send(self, gw):
        return [lax.psum_scatter(gw[0], "dp", scatter_dimension=0, tiled=True)]

    def grads_last(self, parts):
        return parts[0].astype(f32)

    def scatter_channels(self, sums):
        return lax.psum_scatter(sums, "dp", scatter_dimension=0, tiled=True)

    def owner_channels(self, sums):
        perm = [((f % self.n_dp) * self.n_t + f // self.n_dp, f) for f in range(self.n_dp * self.n_t)]
        return lax.ppermute(sums, self.both, perm)

    def scatter_norm(self, sums):
        return lax.psum_scatter(sums, self.both, scatter_dimension=1, tiled=True)


class Pairs:
    def __init__(self, n_dp, n_t):
        self.quads = n_dp // 2
        self.axes = {"q": self.quads, "c": 2, "h": 2, "w": 2}
        self.both = ("q", "c", "h", "w")
        self.cuts = self.quads
        self.other = [(0, 1), (1, 0)]
        self.there = [(2 * c + h, 2 * (1 - h) + c) for c in range(2) for h in range(2)]
        self.back = [(b, a) for a, b in self.there]
        self.turned = [(2 * c + h, 2 * (1 - h) + 1 - c) for c in range(2) for h in range(2)]

    def flip(self, x, axis, bit=1):
        return lax.ppermute(x, axis, [(i, i ^ bit) for i in range(self.axes[axis])])

    def place_of_group(self):
        return 2 * (1 - lax.axis_index("c")) + lax.axis_index("w")

    def regroup(self, x):
        return lax.ppermute(x, ("c", "h"), self.there)

    def ungroup(self, x):
        return lax.ppermute(x, ("c", "h"), self.back)

    def spread(self, x):
        return lax.all_to_all(x, ("q", "c"), split_axis=0, concat_axis=0, tiled=True)

    def places(self):
        c, w = lax.axis_index("c"), lax.axis_index("w")
        return [2 * (1 - c) + w, 2 * c + w, 2 * (1 - c) + 1 - w, 2 * c + 1 - w]

    def starts(self, many):
        return [(place * many).astype(jnp.int32).reshape(1) for place in self.places()]

    def gather_first(self, x):
        return [self.flip(x, "c"), self.flip(x, "w")]

    def gathered(self, x, early):
        return list(zip([x] + early, self.starts(x.shape[0])))

    def gather_last(self, x, got):
        beside, near = got
        return list(zip([x, beside, near, self.flip(near, "c")], self.starts(x.shape[0])))

    def scatter_first(self, w, arrays, many):
        _, beside, near, far = self.starts(many)
        first = mul_rows(w, arrays, far, many)
        give = self.flip(first, "c")
        beside, first = after((beside, first))
        second = mul_rows(w, arrays, beside, many)
        second, give = after((second, give))
        return [second, mul_rows(w, arrays, near, many, extra=give)]

    def scatter_send(self, parts):
        return [self.flip(parts[0], "c"), self.flip(parts[1], "w")]

    def scatter_own(self, w, arrays, many):
        return [mul_rows(w, arrays, self.starts(many)[0], many, dtype=f32)]

    def order(self, pieces):
        place = jnp.stack(self.places())[:, None] * pieces + jnp.arange(pieces)[None, :]
        return jnp.concatenate([place.reshape(-1).astype(jnp.int32), self.cut_order()])

    def steps(self):
        bit = self.quads // 2
        while bit:
            yield "q", bit
            bit //= 2
        yield "h", 1

    def spot(self):
        return 2 * lax.axis_index("q") + lax.axis_index("h")

    def enter(self, rank, x, chan, norm, pack):
        small = norm.shape[1]
        norm = jnp.pad(norm, ((0, 5), (0, BLK - small)))
        got, chan, norm, weights = meet(self.both, rank, x, chan, norm, pack)
        norm = norm[:, :3, :small].transpose(1, 0, 2).reshape(3, -1)
        return got.reshape(x.shape), chan, norm, weights

    def grads_send(self, gw):
        return [gw[0]] + [self.flip(gw[bit], "q", bit) for bit in range(1, self.quads)]

    def grads_last(self, parts):
        total = parts[0].astype(f32)
        for part in parts[1:]:
            total = total + part.astype(f32)
        total = total.astype(bf16)
        half = total.shape[0] // 2
        h = lax.axis_index("h")
        first = jnp.where(h == 0, total[:half], total[half:])
        second = jnp.where(h == 0, total[half:], total[:half])
        return self.ungroup(first).astype(f32) + lax.ppermute(second, ("c", "h"), self.turned).astype(f32)

    def cut_order(self):
        return (lax.axis_index("q") ^ jnp.arange(self.quads)).astype(jnp.int32)

    def scatter_channels(self, sums):
        count = 2 * self.quads
        rows, wide = sums.shape[0] // count, sums.shape[1]
        sums = jnp.pad(sums, ((0, 0), (0, -wide % 8))).reshape(count, -1, BLK)
        sums = jnp.take(sums, jnp.arange(count) ^ self.spot(), axis=0)
        total = None
        for apart in range(count):
            perm = []
            for source in range(4 * count):
                q, c, h, w = source // 8, source // 4 % 2, source // 2 % 2, source % 2
                perm.append((source, count * (2 * (1 - c) + w) + ((2 * q + h) ^ apart)))
            part = lax.ppermute(sums[apart], self.both, perm)
            total = part if total is None else total + part
        return total.reshape(rows, -1)[:, :wide]

    def owner_channels(self, sums):
        return sums

    def scatter_norm(self, sums):
        count = 8 * self.quads
        part = sums.reshape(3, count, -1).transpose(1, 0, 2)
        wide = part.shape[2]
        part = jnp.pad(part, ((0, 0), (0, 5), (0, BLK - wide)))
        part = lax.all_to_all(part, self.both, split_axis=0, concat_axis=0, tiled=True)
        return jnp.sum(part, axis=0)[:3, :wide]


def local(
    net, wave, tokens, cotangent, source, target, lengths, ln_gain, ln_bias, w_fwd, b_fwd, w_bwd, b_bwd,
    w_gate, b_gate, w_out, b_out, log_dt, log_rate, ssm_b, ssm_c, ssm_d,
):
    rows, width = tokens.shape
    many = rows // BLK
    n_t = net.n_t
    group = rows * n_t
    nb = group // BLK
    ch = w_fwd.shape[1]
    back = (wave.T / BIG).astype(bf16)
    wave = wave.astype(bf16)

    def lanes(column):
        return jnp.broadcast_to(column[..., None], column.shape + (BLK,))

    def decays(log_dt, log_rate, ssm_b):
        rate = jnp.exp(log_rate)
        ld = -jnp.exp(log_dt)[..., None] * rate
        return rate, ld, (1.0 - jnp.exp(ld)) / rate * ssm_b

    rank = rank_of(target)
    sender = source // group
    place = rank_of(sender * rows + jnp.arange(rows, dtype=jnp.int32))
    pack = jnp.concatenate(
        [w_fwd, w_bwd, w_gate.reshape(-1, 2 * ch), w_out.transpose(2, 0, 1).reshape(-1, 2 * ch)], axis=1
    )
    table = net.regroup(jnp.concatenate([place, lengths[0]]))
    rate, ld, drive = decays(log_dt, log_rate, ssm_b)
    own = b_fwd.shape[0]
    small = jnp.concatenate([ssm_d, b_fwd[None], b_bwd[None], b_gate])
    chan = jnp.concatenate(
        [
            (ld * log2e).reshape(own, 2 * STATE),
            (ssm_c * drive).reshape(own, 2 * STATE),
            jnp.pad(small, ((0, -(2 * own + 6) % 8 + 0), (0, 2 * STATE - own))),
        ]
    )
    norm = jnp.stack([ln_gain, ln_bias, b_out])
    got_x, chan_all, norm_all, w_all = net.enter(rank, tokens, chan, norm, pack)
    got_x, chan_all, norm_all, w_all, table, cotangent = after((got_x, chan_all, norm_all, w_all, table, cotangent))

    place, lens = table[:rows], table[rows:]
    gain = lanes(norm_all[0])
    shift = lanes(norm_all[1])
    small = chan_all[:, 2 * own : 2 * own + 6, :own].transpose(1, 0, 2).reshape(6, ch)

    def pairs(at):
        both = chan_all[:, at : at + own].reshape(-1, 2, own // 2, 2 * STATE)
        return both.transpose(1, 0, 2, 3).reshape(2, ch // 2, 2 * STATE)

    ld_pairs = pairs(0)
    w_pairs = pairs(own)
    skip = lanes(small[0:2])
    live = live_rows(lens, group)
    live_own = lax.dynamic_slice_in_dim(live, net.place_of_group() * rows, rows, 0).reshape(many, 1, BLK)
    live = live.reshape(nb // 2, 1, BIG)
    tab, seq = sequence_tables(lens, nb)

    xt, xd = deal_x(place, got_x, gain, shift)
    xt, cotangent, ld_pairs, w_pairs, skip, w_all = after((xt, cotangent, ld_pairs, w_pairs, skip, w_all))
    x_got = net.gather_first(xt)
    (sent_g,) = permute_to(rank, [cotangent])
    got_g = net.spread(sent_g)
    kh = spectra(ld_pairs, w_pairs, skip, wave)
    w_in, w_back, w_in_t, w_back_t = split_weights(w_all, 4 * ch)
    bias_in = lanes(small[2:6].reshape(-1))
    bias_out = lanes(norm_all[2])
    early, got_g, kh, w_in_t, bias_in = after((x_got[:-1], got_g, kh, w_in_t, bias_in))
    got_g = net.regroup(got_g)
    kept = None
    for part, start in net.gathered(xt, early):
        kept = project(part, start, nb, live, w_in_t, bias_in, kept)
    kept, late = after((kept, x_got[-1]))
    xs = net.gather_last(xt, early + [late])
    for part, start in xs[len(early) + 1 if early else 0 :]:
        kept = project(part, start, nb, live, w_in_t, bias_in, kept)
    kept, got_g = after((kept, got_g))
    a, da, gg, dg = kept
    gt, gd, g_bias_out = deal_g(place, got_g, live_own)
    gt, a = after((gt, a))
    g_got = net.gather_first(gt)
    y, mix = ssm_scan(tab, seq, a, kh, wave, back, gg)
    g_got, y, mix = after((g_got, y, mix))
    gs = net.gather_last(gt, g_got)
    branch = net.scatter_first(w_back, [mix], many)
    gm = gate_grad(gs, nb, w_back_t)
    branch, gm = after((branch, gm))

    branch = net.scatter_send(branch)
    branch = net.scatter_own(w_back, [mix], many) + branch
    first = ssm_back(0, tab, seq, a, gm, kh, wave, back, gg, y, dg, da)
    branch, first, a = after((branch, first, a))
    sent_out = layer_rows(place, branch, xd, live_own, bias_out)
    sent_out, a = after((sent_out, a))
    sent_out = net.ungroup(sent_out)
    second = ssm_back(1, tab, seq, a, gm, kh, wave, back, gg, y, dg, da)
    sent_out, first, second = after((sent_out, first, second))
    gpg, gp, gh, bsum = zip(first, second)
    sent_out = net.spread(sent_out)
    back_list = [gp[0], gp[1], gpg[0], gpg[1]]
    g_normed = net.scatter_first(w_in, back_list, many)
    g_normed, back_list, mix = after((g_normed, back_list, mix))
    gp, gpg = back_list[:2], back_list[2:]
    g_normed = net.scatter_send(g_normed)
    g_normed = net.scatter_own(w_in, back_list, many) + g_normed
    gw = outer_sums(net.order(many // 8), net.cuts, [part for part, _ in xs], [part for part, _ in gs], gp, gpg, mix)
    g_normed, gw, gh, sent_out = after((g_normed, gw, gh, sent_out))
    sent_in, norm_sums = input_rows(place, g_normed, xd, gd, gain)
    sent_in, gh, gw, norm_sums, sent_out, bsum = after((sent_in, gh, gw, norm_sums, sent_out, bsum))
    sent_in = net.ungroup(sent_in)
    gw = net.grads_send(gw)
    s0, s1, g0 = [jnp.concatenate(part) for part in zip(*[moments(k, ld_pairs, gh[k], back) for k in range(2)])]
    layer_out = permute_from(rank, sent_out)

    s0 = s0.reshape(2, ch, STATE)
    s1 = s1.reshape(2, ch, STATE)
    bsum = jnp.concatenate(bsum)
    gb_gate = jnp.sum(bsum[:, :, :BLK], axis=2)
    gb_in = jnp.sum(bsum[:, :, BLK:], axis=2)
    sums = jnp.concatenate(
        [s0[0], s0[1], s1[0], s1[1], jnp.concatenate([g0[:, :, 0], gb_gate, gb_in], axis=0).T], axis=1
    )
    norm_sums = net.scatter_norm(jnp.sum(jnp.concatenate([norm_sums, g_bias_out[None]], axis=0), axis=2))
    sent_in, gw, sums, norm_sums, layer_out = after((sent_in, gw, sums, norm_sums, layer_out))
    in_grad = permute_from(rank, net.spread(sent_in))
    sums = net.owner_channels(net.scatter_channels(sums))
    gw = net.grads_last(gw)
    s0 = jnp.stack([sums[:, :STATE], sums[:, STATE : 2 * STATE]])
    s1 = jnp.stack([sums[:, 2 * STATE : 3 * STATE], sums[:, 3 * STATE : 4 * STATE]])
    tail = sums[:, 4 * STATE :].T
    step = jnp.exp(log_dt)[..., None]
    g_c = s0 * drive
    g_drive = s0 * ssm_c
    g_b = g_drive * (1.0 - jnp.exp(ld)) / rate
    g_ld = s1 * ssm_c * drive - g_drive * ssm_b / rate * jnp.exp(ld)
    g_rate = -g_drive * drive / rate - g_ld * step
    g_dt = jnp.sum(g_ld * ld, axis=2)
    return (
        layer_out,
        in_grad,
        norm_sums[0],
        norm_sums[1],
        gw[:, :ch],
        tail[4],
        gw[:, ch : 2 * ch],
        tail[5],
        gw[:, 2 * ch : 4 * ch].reshape(-1, 2, ch),
        tail[2:4],
        gw[:, 4 * ch :].T.reshape(2, ch, -1),
        norm_sums[2],
        g_dt,
        g_rate * rate,
        g_b,
        g_c,
        tail[0:2],
    )


def solution(mesh):
    n_dp, n_t = mesh.shape["dp"], mesh.shape["tensor"]
    if n_t == 4 and n_dp == 8:
        net = Pairs(n_dp, n_t)
        dp, tensor = ("q", "c"), ("h", "w")
    else:
        net = Line(n_dp, n_t)
        dp, tensor = ("dp",), ("tensor",)
    net.n_t = n_t
    mesh = jax.sharding.Mesh(mesh.devices.reshape(tuple(net.axes.values())), tuple(net.axes))
    both = P(dp + tensor)
    rows = P(dp + tensor, None)
    pair = P(None, dp + tensor)
    state = P(None, dp + tensor, None)
    proj = P(dp, tensor)
    gate = P(dp, None, tensor)
    out = P(None, tensor, dp)
    wave = wave_table()

    def run(*args):
        return local(net, jnp.asarray(wave), *args)

    return jax.shard_map(
        run,
        mesh=mesh,
        in_specs=(
            rows, rows, both, both, P(dp, None), both, both, proj, both, proj, both, gate, pair, out, both,
            pair, state, state, state, pair,
        ),
        out_specs=(
            rows, rows, both, both, proj, both, proj, both, gate, pair, out, both, pair, state, state, state, pair,
        ),
        check_vma=False,
    )
```

```python
from functools import partial

import jax
import jax.numpy as jnp
import numpy as np
from jax import lax
from jax.experimental import pallas as pl
from jax.experimental.pallas import tpu as pltpu
from jax.sharding import PartitionSpec as P

BLK = 128
BIG = 256
MOST = 2048
LAGS = MOST // BIG
STATE = 64
epsilon = 1e-05
log2e = 1.4426950408889634
f32 = jnp.float32
bf16 = jnp.bfloat16
MIB = 2**20


def nn(a, b):
    return lax.dot_general(a, b, (((1,), (0,)), ((), ())), preferred_element_type=f32)


def nt(a, b):
    return lax.dot_general(a, b, (((1,), (1,)), ((), ())), preferred_element_type=f32)


def params(limit):
    return pltpu.CompilerParams(vmem_limit_bytes=60 * MIB)


def cost(flops, moved, trans=0):
    scale = 0.05
    return pl.CostEstimate(
        flops=int(scale * flops), bytes_accessed=int(scale * moved), transcendentals=int(scale * trans)
    )


def halves(x):
    high = x.astype(bf16)
    return high, (x - high.astype(f32)).astype(bf16)


def wave_table():
    pos = np.arange(BIG)[:, None]
    freq = np.arange(BIG)[None, :]
    angle = 2 * np.pi * ((2 * freq + 1) * pos % (4 * BIG)) / (4 * BIG)
    return np.concatenate([np.cos(angle), np.sin(angle)], 1).astype(np.float32)


def chunk_of(channels, most):
    best = 16
    for size in range(16, most + 1, 16):
        if channels % size == 0:
            best = size
    return best


def permute_row_body(count, rank_ref, *refs):
    rows = rank_ref.shape[1]
    spot = lax.broadcasted_iota(jnp.int32, (rows, rows), 0)
    pick = jnp.where(spot == rank_ref[...], 1.0, 0.0).astype(bf16)
    for at in range(count):
        refs[count + at][...] = nn(pick, refs[at][...]).astype(bf16)


def permute_to(rank, arrays):
    rows, width = arrays[0].shape
    count = len(arrays)
    return pl.pallas_call(
        partial(permute_row_body, count),
        out_shape=[jax.ShapeDtypeStruct((rows, width), bf16)] * count,
        compiler_params=params(48),
        cost_estimate=cost(2 * count * rows * rows * width, 4 * count * rows * width),
    )(rank.reshape(1, rows), *arrays)


def permute_col_body(rank_ref, x_ref, o_ref):
    rows = x_ref.shape[0]
    spot = lax.broadcasted_iota(jnp.int32, (rows, rows), 1)
    pick = jnp.where(spot == rank_ref[...], 1.0, 0.0).astype(bf16)
    o_ref[...] = nn(pick, x_ref[...]).astype(bf16)


def permute_from(rank, x):
    rows, width = x.shape
    return pl.pallas_call(
        permute_col_body,
        out_shape=jax.ShapeDtypeStruct((rows, width), bf16),
        compiler_params=params(48),
        cost_estimate=cost(2 * rows * rows * width, 4 * rows * width),
    )(rank.reshape(rows, 1), x)


def pick_rows(place_ref, x_ref):
    spot = lax.broadcasted_iota(jnp.int32, (BLK, x_ref.shape[0]), 1)
    pick = jnp.where(spot == place_ref[...], 1.0, 0.0).astype(bf16)
    return nn(pick, x_ref[...]).T


def deal_x_body(place_ref, x_ref, gain_ref, shift_ref, xt_ref, xd_ref):
    x = pick_rows(place_ref, x_ref)
    xd_ref[0] = x.astype(bf16)
    centred = x - jnp.mean(x, axis=0, keepdims=True)
    inv_std = lax.rsqrt(jnp.mean(centred * centred, axis=0, keepdims=True) + epsilon)
    xt_ref[0] = (centred * inv_std * gain_ref[...] + shift_ref[...]).astype(bf16)


def deal_g_body(place_ref, g_ref, live_ref, gt_ref, gd_ref, bo_ref):
    g = pick_rows(place_ref, g_ref)
    gd_ref[0] = g.astype(bf16)
    g = g * live_ref[0]
    gt_ref[0] = g.astype(bf16)

    @pl.when(pl.program_id(0) == 0)
    def _():
        bo_ref[...] = jnp.zeros_like(bo_ref)

    bo_ref[...] += g


def deal_specs(rows, width):
    place = pl.BlockSpec((BLK, 1), lambda i: (i, 0))
    whole = pl.BlockSpec((rows, width), lambda i: (0, 0))
    wide = pl.BlockSpec((width, BLK), lambda i: (0, 0))
    out = pl.BlockSpec((1, width, BLK), lambda i: (i, 0, 0))
    return place, whole, wide, out


def deal_x(place, x, gain, shift):
    rows, width = x.shape
    blocks = rows // BLK
    spot, whole, wide, out = deal_specs(rows, width)
    return pl.pallas_call(
        deal_x_body,
        grid=(blocks,),
        in_specs=[spot, whole, wide, wide],
        out_specs=[out, out],
        out_shape=[jax.ShapeDtypeStruct((blocks, width, BLK), bf16)] * 2,
        compiler_params=params(40),
        cost_estimate=cost(2 * rows * rows * width, 6 * rows * width),
    )(place.reshape(rows, 1), x, gain, shift)


def deal_g(place, g, live):
    rows, width = g.shape
    blocks = rows // BLK
    spot, whole, wide, out = deal_specs(rows, width)
    return pl.pallas_call(
        deal_g_body,
        grid=(blocks,),
        in_specs=[spot, whole, pl.BlockSpec((1, 1, BLK), lambda i: (i, 0, 0))],
        out_specs=[out, out, wide],
        out_shape=[jax.ShapeDtypeStruct((blocks, width, BLK), bf16)] * 2
        + [jax.ShapeDtypeStruct((width, BLK), f32)],
        compiler_params=params(40),
        cost_estimate=cost(2 * rows * rows * width, 6 * rows * width),
    )(place.reshape(rows, 1), g, live)


def send_back(place_ref, out_s, o_ref):
    rows = out_s.shape[0]
    spot = lax.broadcasted_iota(jnp.int32, (rows, rows), 0)
    pick = jnp.where(spot == place_ref[...], 1.0, 0.0).astype(bf16)
    o_ref[...] = nn(pick, out_s[...]).astype(bf16)


def total(refs, at):
    value = refs[0][at].astype(f32)
    for ref in refs[1:]:
        value = value + ref[at].astype(f32)
    return value


def layer_body(place_ref, xd_ref, live_ref, bias_ref, *refs):
    o_ref, out_s = refs[-2:]
    for at in range(xd_ref.shape[0]):
        y = xd_ref[at].astype(f32) + live_ref[at] * (total(refs[:-2], at) + bias_ref[...])
        out_s[at * BLK : (at + 1) * BLK, :] = y.T.astype(bf16)
    send_back(place_ref, out_s, o_ref)


def layer_rows(place, parts, xd, live, bias):
    blocks, width, _ = xd.shape
    rows = blocks * BLK
    return pl.pallas_call(
        layer_body,
        out_shape=jax.ShapeDtypeStruct((rows, width), bf16),
        scratch_shapes=[pltpu.VMEM((rows, width), bf16)],
        compiler_params=params(48),
        cost_estimate=cost(2 * rows * rows * width, 6 * rows * width),
    )(place.reshape(1, rows), xd, live, bias, *parts)


def input_body(place_ref, xd_ref, gd_ref, gain_ref, *refs):
    o_ref, sums_ref, out_s = refs[-3:]
    g_gain = jnp.zeros(gain_ref.shape, f32)
    g_shift = jnp.zeros(gain_ref.shape, f32)
    for at in range(xd_ref.shape[0]):
        x = xd_ref[at].astype(f32)
        centred = x - jnp.mean(x, axis=0, keepdims=True)
        inv_std = lax.rsqrt(jnp.mean(centred * centred, axis=0, keepdims=True) + epsilon)
        x_hat = centred * inv_std
        g = total(refs[:-3], at)
        g_gain = g_gain + g * x_hat
        g_shift = g_shift + g
        hat = g * gain_ref[...]
        back = inv_std * (
            hat
            - jnp.mean(hat, axis=0, keepdims=True)
            - x_hat * jnp.mean(hat * x_hat, axis=0, keepdims=True)
        )
        out_s[at * BLK : (at + 1) * BLK, :] = (gd_ref[at].astype(f32) + back).T.astype(bf16)
    sums_ref[0] = g_gain
    sums_ref[1] = g_shift
    send_back(place_ref, out_s, o_ref)


def input_rows(place, parts, xd, gd, gain):
    blocks, width, _ = xd.shape
    rows = blocks * BLK
    return pl.pallas_call(
        input_body,
        out_shape=[
            jax.ShapeDtypeStruct((rows, width), bf16),
            jax.ShapeDtypeStruct((2, width, BLK), f32),
        ],
        scratch_shapes=[pltpu.VMEM((rows, width), bf16)],
        compiler_params=params(48),
        cost_estimate=cost(2 * rows * rows * width, 8 * rows * width),
    )(place.reshape(1, rows), xd, gd, gain, *parts)


def project_body(ch, many, start_ref, x_ref, live_ref, wt_ref, bias_ref, *refs):
    a_ref, da_ref, gg_ref, dg_ref = refs[-4:]
    x = jnp.concatenate([x_ref[0], x_ref[1]], axis=1)
    live = live_ref[0]
    root = 0.7978845608028654
    step = 64 if ch % 128 else 128

    def act(pre):
        square = pre * pre
        rise = 0.5 + 0.5 * jnp.tanh(pre * (root + (0.044715 * root) * square))
        value = pre * rise
        slope = rise + rise * (pre - value) * (2.0 * root + (6.0 * 0.044715 * root) * square)
        return value, slope

    def put(ref, k, at, value):
        value = value.astype(bf16)
        ref[k, 0, at, :] = value[:, :BLK]
        ref[k, 1, at, :] = value[:, BLK:]

    for k in range(2):
        for first, value_ref, slope_ref in ((k * ch, a_ref, da_ref), ((2 + k) * ch, gg_ref, dg_ref)):
            for at in range(0, ch, step):
                rows = pl.ds(first + at, step)
                bias = bias_ref[rows, :]
                pre = nn(wt_ref[rows, :], x) + jnp.concatenate([bias, bias], axis=1)
                value, slope = act(pre)
                if value_ref is a_ref:
                    value, slope = live * value, live * slope
                put(value_ref, k, pl.ds(at, step), value)
                put(slope_ref, k, pl.ds(at, step), slope)


def chained(body, grid, in_specs, out_specs, shapes, scratch, limit, estimate, start, operands, kept):
    kept = [] if kept is None else list(kept)
    specs = list(in_specs) + [pl.BlockSpec(memory_space=pl.ANY)] * len(kept)
    first = 1 + len(operands)
    return pl.pallas_call(
        body,
        grid_spec=pltpu.PrefetchScalarGridSpec(
            num_scalar_prefetch=1, grid=grid, in_specs=specs, out_specs=out_specs, scratch_shapes=scratch
        ),
        out_shape=shapes,
        input_output_aliases={first + at: at for at in range(len(kept))},
        compiler_params=params(limit),
        cost_estimate=estimate,
    )(start, *operands, *kept)


def project(xt, start, nb, live, wt, bias, kept):
    many, width, _ = xt.shape
    ch = wt.shape[0] // 4
    out = pl.BlockSpec((2, 2, ch, BLK), lambda i, at: (0, at[0] + i, 0, 0))
    tok = many * BLK
    return chained(
        partial(project_body, ch, many),
        (many // 2,),
        [
            pl.BlockSpec((2, width, BLK), lambda i, at: (i, 0, 0)),
            pl.BlockSpec((1, 1, BIG), lambda i, at: (at[0] + i, 0, 0)),
            pl.BlockSpec((4 * ch, width), lambda i, at: (0, 0)),
            pl.BlockSpec((4 * ch, BLK), lambda i, at: (0, 0)),
        ],
        [out] * 4,
        [jax.ShapeDtypeStruct((2, nb, ch, BLK), bf16)] * 4,
        [],
        48,
        cost(8 * tok * width * ch, 2 * tok * width + 16 * tok * ch, 4 * tok * ch),
        start // 2,
        [xt, live, wt, bias],
        kept,
    )


def gate_grad_body(ch, parts, at_ref, *refs):
    wt_ref, o_ref = refs[parts:]
    steps = pl.num_programs(0) // parts

    def work(g_ref):
        gm = nn(wt_ref[...], jnp.concatenate([g_ref[0], g_ref[1]], axis=1)).astype(bf16)
        for k in range(2):
            for h in range(2):
                o_ref[k, h] = gm[k * ch : (k + 1) * ch, h * BLK : (h + 1) * BLK]

    for part in range(parts):

        @pl.when(pl.program_id(0) // steps == part)
        def _(part=part):
            work(refs[part])


def gate_grad(gs, nb, wt):
    parts = len(gs)
    many, width, _ = gs[0][0].shape
    steps = many // 2
    ch = wt.shape[0] // 2
    tok = nb * BLK

    def rows(part):
        return pl.BlockSpec((2, width, BLK), lambda i, at: (jnp.clip(i - part * steps, 0, steps - 1), 0, 0))

    order = jnp.concatenate([start // 2 for _, start in gs]).astype(jnp.int32)
    return pl.pallas_call(
        partial(gate_grad_body, ch, parts),
        grid_spec=pltpu.PrefetchScalarGridSpec(
            num_scalar_prefetch=1,
            grid=(parts * steps,),
            in_specs=[rows(part) for part in range(parts)] + [pl.BlockSpec((2 * ch, width), lambda i, at: (0, 0))],
            out_specs=pl.BlockSpec((2, 2, ch, BLK), lambda i, at: (0, at[i // steps] + i % steps, 0, 0)),
        ),
        out_shape=jax.ShapeDtypeStruct((2, nb, ch, BLK), bf16),
        compiler_params=params(40),
        cost_estimate=cost(4 * tok * width * ch, 2 * tok * width + 4 * tok * ch),
    )(order, *[part for part, _ in gs], wt)


def spectra_body(cc, ld_ref, w_ref, d_ref, wave_ref, kh_ref, k_s):
    t = lax.broadcasted_iota(jnp.int32, (BLK, BLK), 0).astype(f32)
    block = lax.broadcasted_iota(jnp.int32, (2 * LAGS, BLK), 0).astype(f32) * float(BLK)
    low = lax.broadcasted_iota(jnp.int32, (2 * LAGS, BLK), 1) < STATE
    count = 2 * LAGS

    def one(p, carry):
        ld = ld_ref[0, pl.ds(p, 1), :]
        decay = jnp.exp2(t * ld)
        scale = w_ref[0, pl.ds(p, 1), :] * jnp.exp2(block * ld)
        lhs = jnp.concatenate([jnp.where(low, scale, 0.0), jnp.where(low, 0.0, scale)], axis=0)
        lhs_high, lhs_low = halves(lhs)
        k = nt(jnp.concatenate([lhs_high, lhs_low], axis=0), decay.astype(bf16))
        k = k[0 : 2 * count] + k[2 * count : 4 * count]
        k_s[pl.ds(2 * p, count, stride=cc), :] = k[0:count]
        k_s[pl.ds(2 * p + 1, count, stride=cc), :] = k[count : 2 * count]
        return carry

    lax.fori_loop(0, cc // 2, one, 0, unroll=16)
    sign = jnp.where(lax.broadcasted_iota(jnp.int32, (cc, BIG), 1) % 2 == 0, 1.0, -1.0)
    before = None
    for big in range(LAGS):
        rows = jnp.concatenate(
            [k_s[pl.ds(2 * big * cc, cc), :], k_s[pl.ds((2 * big + 1) * cc, cc), :]], axis=1
        )
        high, rest = halves(rows)
        x = nn(high, wave_ref[...]) + nn(rest, wave_ref[...])
        xc, xs = x[:, :BIG], x[:, BIG:]
        if big == 0:
            kh_ref[0, 0, :, :BIG] = xc + d_ref[0][:, 0:1]
            kh_ref[0, 0, :, BIG:] = xs
        else:
            kh_ref[0, big, :, :BIG] = xc + sign * before[1]
            kh_ref[0, big, :, BIG:] = xs - sign * before[0]
        before = (xc, xs)


def spectra(ld, w, d, wave):
    ch = 2 * ld.shape[1]
    cc = chunk_of(ch, 128)
    return pl.pallas_call(
        partial(spectra_body, cc),
        grid=(2, ch // cc),
        in_specs=[pl.BlockSpec((1, cc // 2, BLK), lambda k, i: (k, i, 0))] * 2
        + [
            pl.BlockSpec((1, cc, BLK), lambda k, i: (k, i, 0)),
            pl.BlockSpec((BIG, 2 * BIG), lambda k, i: (0, 0)),
        ],
        out_specs=pl.BlockSpec((1, LAGS, cc, 2 * BIG), lambda k, i: (k, 0, i, 0)),
        out_shape=jax.ShapeDtypeStruct((2, LAGS, ch, 2 * BIG), f32),
        scratch_shapes=[pltpu.VMEM((2 * LAGS * cc, BLK), f32)],
        compiler_params=params(40),
        cost_estimate=cost(2 * ch * 40e6, 2 * ch * LAGS * 2 * BIG * 4),
    )(ld, w, d, wave)


def moments_body(cc, ld_ref, gh_ref, back_ref, s0_ref, s1_ref, g0_ref, g_s):
    sign = jnp.where(lax.broadcasted_iota(jnp.int32, (cc, BIG), 1) % 2 == 0, 1.0, -1.0)
    count = 2 * LAGS
    for big in range(LAGS):
        c = gh_ref[0, big, :, :BIG]
        s = gh_ref[0, big, :, BIG:]
        if big < LAGS - 1:
            c, s = c - sign * gh_ref[0, big + 1, :, BIG:], s + sign * gh_ref[0, big + 1, :, :BIG]
        high, rest = halves(jnp.concatenate([c, s], axis=1))
        g = nn(high, back_ref[...]) + nn(rest, back_ref[...])
        g_s[pl.ds(2 * big * cc, cc), :] = g[:, :BLK]
        g_s[pl.ds((2 * big + 1) * cc, cc), :] = g[:, BLK:]
        if big == 0:
            g0_ref[0] = g[:, :BLK]
    t = lax.broadcasted_iota(jnp.int32, (BLK, BLK), 0).astype(f32)
    lane = lax.broadcasted_iota(jnp.int32, (count, BLK), 1)
    lag = lane.astype(f32)
    block = lax.broadcasted_iota(jnp.int32, (count, BLK), 0).astype(f32) * float(BLK)
    low = lane < STATE

    def one(p, carry):
        ld = ld_ref[0, pl.ds(p, 1), :]
        decay = jnp.exp2(t * ld).astype(bf16)
        far = jnp.exp2(block * ld)
        ga = g_s[pl.ds(2 * p, count, stride=cc), :]
        gb = g_s[pl.ds(2 * p + 1, count, stride=cc), :]
        high, rest = halves(jnp.concatenate([ga, gb, ga * lag, gb * lag], axis=0))
        m = nn(jnp.concatenate([high, rest], axis=0), decay)
        m = m[0 : 4 * count] + m[4 * count : 8 * count]
        m0 = jnp.where(low, m[0:count], m[count : 2 * count])
        m1 = jnp.where(low, m[2 * count : 3 * count], m[3 * count : 4 * count]) + block * m0
        s0_ref[0, pl.ds(p, 1), :] = jnp.sum(far * m0, axis=0, keepdims=True)
        s1_ref[0, pl.ds(p, 1), :] = jnp.sum(far * m1, axis=0, keepdims=True)
        return carry

    lax.fori_loop(0, cc // 2, one, 0, unroll=16)


def moments(k, ld, gh, back):
    ch = gh.shape[2]
    cc = chunk_of(ch, 128)
    row = pl.BlockSpec((1, cc // 2, BLK), lambda i: (0, i, 0))
    return pl.pallas_call(
        partial(moments_body, cc),
        grid=(ch // cc,),
        in_specs=[
            pl.BlockSpec((1, cc // 2, BLK), lambda i: (k, i, 0)),
            pl.BlockSpec((1, LAGS, cc, 2 * BIG), lambda i: (0, 0, i, 0)),
            pl.BlockSpec((2 * BIG, BIG), lambda i: (0, 0)),
        ],
        out_specs=[row, row, pl.BlockSpec((1, cc, BLK), lambda i: (0, i, 0))],
        out_shape=[jax.ShapeDtypeStruct((1, ch // 2, BLK), f32)] * 2
        + [jax.ShapeDtypeStruct((1, ch, BLK), f32)],
        scratch_shapes=[pltpu.VMEM((2 * LAGS * cc, BLK), f32)],
        compiler_params=params(40),
        cost_estimate=cost(ch * 40e6, ch * LAGS * 2 * BIG * 4),
    )(ld, gh, back)


def load_pieces(nb, pieces, cc, tab_ref, block, in_s, wave_ref, dst):
    for h in range(pieces):
        first = tab_ref[0, h]
        whole = tab_ref[1, h].astype(f32)
        in_s[pl.ds(h * cc, cc), 0:BLK] = block(first).astype(bf16)
        in_s[pl.ds(h * cc, cc), BLK:BIG] = (block(jnp.minimum(first + 1, nb - 1)) * whole).astype(bf16)
    for h in range(pieces):
        at = pl.ds(h * cc, cc)
        dst[at, :] = nn(in_s[at, :], wave_ref[...])


def over_pieces(nseq, cc, rg, seq_ref, piece):
    def group(r, carry):
        off = pl.multiple_of(r * rg, rg)
        for s in range(nseq):
            base = seq_ref[0, s]
            count = seq_ref[1, s]

            def outer(i, carry):
                piece(i, count, base, off)
                return carry

            lax.fori_loop(0, count, outer, 0)
        return carry

    lax.fori_loop(0, cc // rg, group, 0)


def scan_body(
    nb, nseq, cc, rg, tab_ref, seq_ref, a_ref, kh_ref, wave_ref, back_ref, gg_ref, y_ref, mix_ref, in_s, ah_s, yh_s, y_s
):
    pieces = (nb + nseq) // 2
    load_pieces(nb, pieces, cc, tab_ref, lambda b: a_ref[0, b].astype(f32), in_s, wave_ref, ah_s)
    zero = jnp.zeros((rg, BIG), f32)

    def products(flip):
        def piece(i, count, base, off):
            def inner(j, acc):
                yc, ys = acc
                other = (base + i + j) if flip else (base + i - j)
                m = pl.ds(pl.multiple_of(other * cc + off, rg), rg)
                rows = pl.ds(off, rg)
                ac = ah_s[m, :BIG]
                as_ = ah_s[m, BIG:]
                kc = kh_ref[0, j, rows, :BIG]
                ks = kh_ref[0, j, rows, BIG:]
                if flip:
                    return (yc + kc * ac + ks * as_, ys + kc * as_ - ks * ac)
                return (yc + kc * ac - ks * as_, ys + kc * as_ + ks * ac)

            yc, ys = lax.fori_loop(0, (count - i) if flip else (i + 1), inner, (zero, zero))
            at = pl.ds(pl.multiple_of((base + i) * cc + off, rg), rg)
            yh_s[at, :BIG] = yc.astype(bf16)
            yh_s[at, BIG:] = ys.astype(bf16)

        over_pieces(nseq, cc, rg, seq_ref, piece)

    @pl.when(pl.program_id(0) == 0)
    def _():
        products(False)

    @pl.when(pl.program_id(0) == 1)
    def _():
        products(True)

    for h in range(pieces):
        at = pl.ds(h * cc, cc)
        y_s[at, :] = nn(yh_s[at, :], back_ref[...])

    def one(b, y):
        y_ref[0, b] = y.astype(bf16)
        mix_ref[0, b] = (y * gg_ref[0, b].astype(f32)).astype(bf16)

    def last(h, carry):
        b = tab_ref[0, h]
        at = pl.ds(pl.multiple_of(h * cc, cc), cc)
        one(b, y_s[at, 0:BLK])

        @pl.when(tab_ref[1, h] == 1)
        def _():
            one(b + 1, y_s[at, BLK:])

        return carry

    lax.fori_loop(0, seq_ref[1, nseq], last, 0)
    nothing = jnp.zeros((cc, BLK), bf16)

    def fill(b, carry):
        y_ref[0, b] = nothing
        mix_ref[0, b] = nothing
        return carry

    lax.fori_loop(seq_ref[0, nseq], nb, fill, 0)


def back_body(
    nb, nseq, cc, rg, flip, tab_ref, seq_ref, a_ref, gm_ref, kh_ref, wave_ref, back_ref, gg_ref, y_ref, dg_ref, da_ref,
    gpg_ref, gp_ref, gh_ref, bs_ref, in_s, ah_s, gh_s, xh_s, x_s,
):
    pieces = (nb + nseq) // 2
    load_pieces(nb, pieces, cc, tab_ref, lambda b: a_ref[0, b].astype(f32), in_s, wave_ref, ah_s)
    load_pieces(
        nb, pieces, cc, tab_ref, lambda b: gm_ref[0, b].astype(f32) * gg_ref[0, b].astype(f32), in_s, wave_ref, gh_s
    )
    gh_ref[...] = jnp.zeros_like(gh_ref)
    zero = jnp.zeros((rg, BIG), f32)

    def piece(i, count, base, off):
        at = pl.ds(pl.multiple_of((base + i) * cc + off, rg), rg)
        ac = ah_s[at, :BIG]
        as_ = ah_s[at, BIG:]

        def inner(j, acc):
            xc, xs = acc
            other = (base + i - j) if flip else (base + i + j)
            m = pl.ds(pl.multiple_of(other * cc + off, rg), rg)
            rows = pl.ds(off, rg)
            gc = gh_s[m, :BIG]
            gs = gh_s[m, BIG:]
            kc = kh_ref[0, j, rows, :BIG]
            ks = kh_ref[0, j, rows, BIG:]
            gh_ref[0, j, rows, :BIG] += ac * gc + as_ * gs
            if flip:
                gh_ref[0, j, rows, BIG:] += gc * as_ - gs * ac
                return (xc + kc * gc - ks * gs, xs + kc * gs + ks * gc)
            gh_ref[0, j, rows, BIG:] += ac * gs - as_ * gc
            return (xc + kc * gc + ks * gs, xs + kc * gs - ks * gc)

        xc, xs = lax.fori_loop(0, (i + 1) if flip else (count - i), inner, (zero, zero))
        xh_s[at, :BIG] = xc.astype(bf16)
        xh_s[at, BIG:] = xs.astype(bf16)

    over_pieces(nseq, cc, rg, seq_ref, piece)

    for h in range(pieces):
        at = pl.ds(h * cc, cc)
        x_s[at, :] = nn(xh_s[at, :], back_ref[...])

    none = jnp.zeros((cc, BLK), f32)

    def one(b, gx, carry):
        s0, s1 = carry
        gpg = (y_ref[0, b].astype(f32) * gm_ref[0, b].astype(f32) * dg_ref[0, b].astype(f32)).astype(bf16)
        gpg_ref[0, b] = gpg
        gp = (gx * da_ref[0, b].astype(f32)).astype(bf16)
        gp_ref[0, b] = gp
        return (s0 + gpg.astype(f32), s1 + gp.astype(f32))

    def last(h, carry):
        b = tab_ref[0, h]
        at = pl.ds(pl.multiple_of(h * cc, cc), cc)
        carry = one(b, x_s[at, 0:BLK], carry)

        def more(kept):
            return one(b + 1, x_s[at, BLK:], kept)

        return lax.cond(tab_ref[1, h] == 1, more, lambda kept: kept, carry)

    s0, s1 = lax.fori_loop(0, seq_ref[1, nseq], last, (none, none))
    bs_ref[0, :, 0:BLK] = s0
    bs_ref[0, :, BLK:] = s1
    nothing = jnp.zeros((cc, BLK), bf16)

    def fill(b, carry):
        gpg_ref[0, b] = nothing
        gp_ref[0, b] = nothing
        return carry

    lax.fori_loop(seq_ref[0, nseq], nb, fill, 0)


def ssm_specs(shape, seq):
    _, nb, ch, _ = shape
    nseq = seq.shape[1] - 1
    pieces = (nb + nseq) // 2
    cc = chunk_of(ch, 128 if nb <= 32 else 64)
    big = pl.BlockSpec((1, nb, cc, BLK), lambda k, i: (k, 0, i, 0))
    spec = pl.BlockSpec((1, LAGS, cc, 2 * BIG), lambda k, i: (k, 0, i, 0))
    smem = pl.BlockSpec(memory_space=pltpu.SMEM)
    head = [smem, smem]
    tables = [pl.BlockSpec((BIG, 2 * BIG), lambda k, i: (0, 0)), pl.BlockSpec((2 * BIG, BIG), lambda k, i: (0, 0))]
    return nb, nseq, ch, cc, pieces * cc, big, spec, head, tables


def ssm_scan(tab, seq, a, kh, wave, back, gg):
    nb, nseq, ch, cc, size, big, spec, head, tables = ssm_specs(a.shape, seq)
    return pl.pallas_call(
        partial(scan_body, nb, nseq, cc, 32),
        grid=(2, ch // cc),
        in_specs=head + [big, spec] + tables + [big],
        out_specs=[big, big],
        out_shape=[jax.ShapeDtypeStruct(a.shape, bf16)] * 2,
        scratch_shapes=[
            pltpu.VMEM((size, BIG), bf16),
            pltpu.VMEM((size, 2 * BIG), f32),
            pltpu.VMEM((size, 2 * BIG), bf16),
            pltpu.VMEM((size, BIG), f32),
        ],
        compiler_params=params(56),
        cost_estimate=cost(2 * ch * 50e6, 2 * ch * nb * BLK * 8),
    )(tab, seq, a, kh, wave, back, gg)


def ssm_back(k, tab, seq, a, gm, kh, wave, back, gg, y, dg, da):
    nb, nseq, ch, cc, size, _, _, head, tables = ssm_specs(a.shape, seq)
    big = pl.BlockSpec((1, nb, cc, BLK), lambda i: (k, 0, i, 0))
    spec = pl.BlockSpec((1, LAGS, cc, 2 * BIG), lambda i: (k, 0, i, 0))
    out = pl.BlockSpec((1, nb, cc, BLK), lambda i: (0, 0, i, 0))
    out_spec = pl.BlockSpec((1, LAGS, cc, 2 * BIG), lambda i: (0, 0, i, 0))
    tables = [
        pl.BlockSpec((BIG, 2 * BIG), lambda i: (0, 0)),
        pl.BlockSpec((2 * BIG, BIG), lambda i: (0, 0)),
    ]
    return pl.pallas_call(
        partial(back_body, nb, nseq, cc, 64, k == 1),
        grid=(ch // cc,),
        in_specs=head + [big, big, spec] + tables + [big] * 4,
        out_specs=[out, out, out_spec, pl.BlockSpec((1, cc, 2 * BLK), lambda i: (0, i, 0))],
        out_shape=[jax.ShapeDtypeStruct((1,) + a.shape[1:], bf16)] * 2
        + [
            jax.ShapeDtypeStruct((1, LAGS, ch, 2 * BIG), f32),
            jax.ShapeDtypeStruct((1, ch, 2 * BLK), f32),
        ],
        scratch_shapes=[
            pltpu.VMEM((size, BIG), bf16),
            pltpu.VMEM((size, 2 * BIG), f32),
            pltpu.VMEM((size, 2 * BIG), f32),
            pltpu.VMEM((size, 2 * BIG), bf16),
            pltpu.VMEM((size, BIG), f32),
        ],
        compiler_params=params(60),
        cost_estimate=cost(ch * 80e6, ch * nb * BLK * 16),
    )(tab, seq, a, gm, kh, wave, back, gg, y, dg, da)


def stack_pair(refs):
    return jnp.concatenate(
        [jnp.concatenate([ref[k, 0], ref[k, 1]], axis=1) for ref in refs for k in range(ref.shape[0])], axis=0
    )


def mul_body(count, more, start_ref, w_ref, *refs):
    out = nn(w_ref[...], stack_pair(refs[:count]))
    o_ref = refs[-1]
    for h in range(2):
        part = out[:, h * BLK : (h + 1) * BLK]
        if more:
            part = part + refs[count][h].astype(f32)
        o_ref[h] = part.astype(o_ref.dtype)


def mul_rows(w, arrays, start, many, dtype=bf16, extra=None):
    width, deep = w.shape
    ch = arrays[0].shape[2]
    count = len(arrays)
    out = pl.BlockSpec((2, width, BLK), lambda i, at: (i, 0, 0))
    return pl.pallas_call(
        partial(mul_body, count, extra is not None),
        grid_spec=pltpu.PrefetchScalarGridSpec(
            num_scalar_prefetch=1,
            grid=(many // 2,),
            in_specs=[pl.BlockSpec((width, deep), lambda i, at: (0, 0))]
            + [pl.BlockSpec((x.shape[0], 2, ch, BLK), lambda i, at: (0, at[0] + i, 0, 0)) for x in arrays]
            + ([] if extra is None else [out]),
            out_specs=out,
        ),
        out_shape=jax.ShapeDtypeStruct((many, width, BLK), dtype),
        compiler_params=params(40),
        cost_estimate=cost(2 * many * BLK * width * deep, 2 * many * BLK * (2 * width + deep)),
    )(start // 2, w, *arrays, *([] if extra is None else [extra]))


def outer_body(ch, many, cuts, parts, at_ref, *refs):
    step = pl.program_id(0)
    xs, gs = refs[:parts], refs[parts : 2 * parts]
    gp_refs, gpg_refs, mix_ref = refs[2 * parts : 2 * parts + 2], refs[2 * parts + 2 : 2 * parts + 4], refs[2 * parts + 4]
    outs = refs[2 * parts + 5 : 2 * parts + 5 + cuts]
    acc_s, x_s, g_s = refs[-3:]

    def fill(at):
        for b in range(many):
            x_s[:, b * BLK : (b + 1) * BLK] = xs[at][b]
            g_s[:, b * BLK : (b + 1) * BLK] = gs[at][b]

    if parts == 1:
        fill(0)
    else:
        for at in range(parts):

            @pl.when(step == at)
            def _(at=at):
                fill(at)

    def part(ref, k):
        return jnp.concatenate([ref[k, b] for b in range(many)], axis=1)

    @pl.when(step == 0)
    def _():
        acc_s[...] = jnp.zeros_like(acc_s)

    split = 4 * ch
    left = jnp.concatenate([part(ref, 0) for ref in (*gp_refs, *gpg_refs)], axis=0)
    acc_s[:, :split] += nt(x_s[...], left)
    acc_s[:, split:] += nt(g_s[...], jnp.concatenate([part(mix_ref, 0), part(mix_ref, 1)], axis=0))

    @pl.when(step == pl.num_programs(0) - 1)
    def _():
        deep = acc_s.shape[0] // cuts
        for cut in range(cuts):
            start = pl.multiple_of(at_ref[pl.num_programs(0) + cut] * deep, 8)
            outs[cut][...] = acc_s[pl.ds(start, deep), :].astype(bf16)


def outer_sums(order, cuts, xs, gs, gp, gpg, mix):
    width = xs[0].shape[1]
    _, nb, ch, _ = mix.shape
    many = 8
    parts = len(xs)
    if parts == 1:
        rows = pl.BlockSpec((many, width, BLK), lambda i, at: (i, 0, 0))
    else:
        rows = pl.BlockSpec((many, width, BLK), lambda i, at: (0, 0, 0), pipeline_mode=pl.Buffered(1))
    chan = pl.BlockSpec((2, many, ch, BLK), lambda i, at: (0, at[i], 0, 0))
    one = pl.BlockSpec((1, many, ch, BLK), lambda i, at: (0, at[i], 0, 0))
    tok = nb * BLK
    return pl.pallas_call(
        partial(outer_body, ch, many, cuts, parts),
        grid_spec=pltpu.PrefetchScalarGridSpec(
            num_scalar_prefetch=1,
            grid=(nb // many,),
            in_specs=[rows] * (2 * parts) + [one] * 4 + [chan],
            out_specs=[pl.BlockSpec((width // cuts, 6 * ch), lambda i, at: (0, 0))] * cuts,
            scratch_shapes=[
                pltpu.VMEM((width, 6 * ch), f32),
                pltpu.VMEM((width, many * BLK), bf16),
                pltpu.VMEM((width, many * BLK), bf16),
            ],
        ),
        out_shape=[jax.ShapeDtypeStruct((width // cuts, 6 * ch), bf16)] * cuts,
        compiler_params=params(60),
        cost_estimate=cost(12 * tok * width * ch, tok * (4 * width + 12 * ch)),
    )(order, *xs, *gs, *gp, *gpg, mix)


def join_body(split, w_ref, head_ref, tail_ref, head_t_ref, tail_t_ref):
    head_ref[...] = w_ref[:, :split]
    tail_ref[...] = w_ref[:, split:]
    head_t_ref[...] = w_ref[:, :split].T
    tail_t_ref[...] = w_ref[:, split:].T


def split_weights(w, split):
    rows, wide = w.shape
    vmem = pl.BlockSpec(memory_space=pltpu.VMEM)
    return pl.pallas_call(
        partial(join_body, split),
        in_specs=[vmem],
        out_specs=[vmem] * 4,
        out_shape=[
            jax.ShapeDtypeStruct(shape, bf16)
            for shape in ((rows, split), (rows, wide - split), (split, rows), (wide - split, rows))
        ],
        compiler_params=params(48),
        cost_estimate=cost(0, 6 * rows * wide),
    )(w)


def meet_body(
    axes, rank_ref, x_ref, g_ref, chan_ref, norm_ref, pack_ref, got_ref, gotg_ref, call_ref, nall_ref, wall_ref,
    send_s, sendg_s, *sems
):
    xs_sem, xr_sem, gs_sem, gr_sem, cs_sem, cr_sem, ns_sem, nr_sem, ws_sem, wr_sem, own_sem = sems
    q, c, h, w = (lax.axis_index(name) for name in axes)
    rows = x_ref.shape[0]
    piece = rows // 8
    flat = ((2 * q + c) * 2 + h) * 2 + w

    def peer(bits):
        return (q ^ (bits // 8), c ^ (bits // 4 % 2), h ^ (bits // 2 % 2), w ^ (bits % 2))

    barrier = pltpu.get_barrier_semaphore()
    for bits in range(1, 32):
        pl.semaphore_signal(barrier, inc=1, device_id=peer(bits), device_id_type=pl.DeviceIdType.MESH)
    pl.semaphore_wait(barrier, 31)

    def remote(src, dst, send, recv, to):
        return pltpu.make_async_remote_copy(
            src_ref=src, dst_ref=dst, send_sem=send, recv_sem=recv, device_id=to, device_id_type=pl.DeviceIdType.MESH
        )

    deep = pack_ref.shape[0]

    def shard(at):
        return wall_ref.at[pl.ds(pl.multiple_of(at * deep, 16), deep)]

    def first_copy():
        return remote(pack_ref, shard(2 * q + c), ws_sem.at[0], wr_sem.at[c], (q, 1 - h, c, w))

    def second_copy():
        return remote(pack_ref, shard(2 * q + c), ws_sem.at[1], wr_sem.at[c], (q, 1 - h, 1 - c, w))

    def own_shard():
        return pltpu.make_async_copy(pack_ref, shard(2 * q + c), own_sem.at[2])

    def shard_came(at):
        return remote(pack_ref, shard(2 * q + at), ws_sem.at[0], wr_sem.at[at], peer(1))

    def pass_on(at, bits):
        spot_w = 3 * at + bits + 1
        return remote(shard(2 * q + at), shard(2 * q + at), ws_sem.at[spot_w], wr_sem.at[spot_w], (q ^ bits, c, h, w))

    first_copy().start()

    @pl.when(c != h)
    def _():
        own_shard().start()

    @pl.when(c == h)
    def _():
        second_copy().start()

    nall_ref[flat] = norm_ref[...]

    def norm_copy(bits):
        return remote(norm_ref, nall_ref.at[flat], ns_sem.at[bits], nr_sem.at[bits], peer(bits))

    for bits in range(1, 32):
        norm_copy(bits).start()

    pieces = [(kq, kh) for kh in (0, 1) for kq in (1, 2, 3, 0)]
    spot = lax.broadcasted_iota(jnp.int32, (piece, rows), 0)

    x_side = (send_s, got_ref, xs_sem, xr_sem, 0)
    g_side = (sendg_s, gotg_ref, gs_sem, gr_sem, 3)

    def row_copy(side, kq, kh):
        held, got, send, recv, _ = side
        at = 2 * kq + kh
        return remote(held.at[at], got.at[2 * q + c], send.at[at], recv.at[2 * kq + c], (q ^ kq, 1 - h, h ^ kh, w))

    def own_copy(side):
        held, got, _, _, at = side
        return pltpu.make_async_copy(held.at[0], got.at[2 * q + c], own_sem.at[at])

    def send_rows(side, kq, kh):
        if (kq, kh) == (0, 0):

            @pl.when(c != h)
            def _():
                own_copy(side).start()

            @pl.when(c == h)
            def _():
                row_copy(side, 0, 0).start()

        else:
            row_copy(side, kq, kh).start()

    for kq, kh in pieces:
        chunk = 2 * (q ^ kq) + (h ^ kh)
        pick = jnp.where(spot + chunk * piece == rank_ref[...], 1.0, 0.0).astype(bf16)
        send_s[2 * kq + kh] = nn(pick, x_ref[...]).astype(bf16)
        sendg_s[2 * kq + kh] = nn(pick, g_ref[...]).astype(bf16)
        if (kq, kh) == (1, 1):
            for at in range(2):

                @pl.when((c != h) & (at == c))
                def _():
                    own_shard().wait()

                @pl.when(jnp.logical_not((c != h) & (at == c)))
                def _(at=at):
                    shard_came(at).wait_recv()

                for bits in range(1, 4):
                    pass_on(at, bits).start()
        send_rows(x_side, kq, kh)

    place = 2 * (1 - c) + w
    spot_c = 4 * c + 2 * h + w

    def chan_copy(at):
        to = (q ^ at, 1 - q // 2, h, q % 2) if at < 4 else (2 * c + w, 1 - q // 2, 1 - h, q % 2)
        return remote(chan_ref, call_ref.at[spot_c], cs_sem.at[at], cr_sem.at[spot_c], to)

    def own_chan():
        return pltpu.make_async_copy(chan_ref, call_ref.at[spot_c], own_sem.at[1])

    def chan_came(at):
        return remote(chan_ref, call_ref.at[at], cs_sem.at[0], cr_sem.at[at], peer(1))

    far_spot = 4 * (q // 2) + 2 * (1 - h) + q % 2

    def chan_pass(bits):
        return remote(
            call_ref.at[far_spot], call_ref.at[far_spot], cs_sem.at[4 + bits], cr_sem.at[far_spot], (q ^ bits, c, h, w)
        )

    for at in (4, 1, 2, 3, 0):
        if at:
            chan_copy(at).start()
        else:

            @pl.when(place == q)
            def _():
                own_chan().start()

            @pl.when(place != q)
            def _():
                chan_copy(0).start()

    for kq, kh in pieces[4:] + pieces[:4]:
        send_rows(g_side, kq, kh)

    for bits in range(1, 32):
        norm_copy(bits).wait()
    chan_came(far_spot).wait_recv()
    for bits in range(1, 4):
        chan_pass(bits).start()
    for at in range(8):

        @pl.when((place == q) & (at == spot_c))
        def _():
            own_chan().wait()

        @pl.when(jnp.logical_not((place == q) & (at == spot_c)) & (at != far_spot))
        def _(at=at):
            chan_came(at).wait_recv()

    for bits in range(1, 4):
        chan_pass(bits).wait_send()
    for at in range(2):
        for bits in range(1, 4):
            pass_on(at, bits).wait()
    first_copy().wait_send()

    @pl.when(c == h)
    def _():
        second_copy().wait_send()

    for side in (x_side, g_side):
        held, got, send, recv, _ = side
        for at in range(8):

            @pl.when((c != h) & (at == c))
            def _(side=side):
                own_copy(side).wait()

            @pl.when(jnp.logical_not((c != h) & (at == c)))
            def _(at=at, held=held, got=got, send=send, recv=recv):
                remote(held.at[at], got.at[at], send.at[at], recv.at[at], peer(1)).wait_recv()

        for kq, kh in pieces:
            if (kq, kh) == (0, 0):

                @pl.when(c == h)
                def _(side=side):
                    row_copy(side, 0, 0).wait_send()

            else:
                row_copy(side, kq, kh).wait_send()
    for at in range(1, 5):
        chan_copy(at).wait_send()

    @pl.when(place != q)
    def _():
        chan_copy(0).wait_send()


def meet(axes, rank, x, g, chan, norm, pack):
    rows, width = x.shape
    vmem = pl.BlockSpec(memory_space=pltpu.VMEM)
    sem = pltpu.SemaphoreType.DMA
    return pl.pallas_call(
        partial(meet_body, axes),
        in_specs=[vmem] * 6,
        out_specs=[vmem] * 5,
        out_shape=[
            jax.ShapeDtypeStruct((8, rows // 8, width), bf16),
            jax.ShapeDtypeStruct((8, rows // 8, width), bf16),
            jax.ShapeDtypeStruct((8,) + chan.shape, f32),
            jax.ShapeDtypeStruct((32,) + norm.shape, f32),
            jax.ShapeDtypeStruct((8 * pack.shape[0], pack.shape[1]), bf16),
        ],
        scratch_shapes=[pltpu.VMEM((8, rows // 8, width), bf16)] * 2
        + [sem((8,)), sem((8,)), sem((8,)), sem((8,)), sem((8,)), sem((8,)), sem((32,)), sem((32,)), sem((8,)), sem((8,)), sem((4,))],
        compiler_params=pltpu.CompilerParams(collective_id=1, has_side_effects=True, vmem_limit_bytes=60 * MIB),
        cost_estimate=cost(2 * rows * rows * width, 100 * rows * width),
    )(rank.reshape(1, rows), x, g, chan, norm, pack)


def sequence_tables(lens, nb):
    nseq = lens.shape[0]
    blocks = (lens + BLK - 1) // BLK
    start = jnp.cumsum(blocks) - blocks
    bigs = (blocks + 1) // 2
    first_big = jnp.cumsum(bigs) - bigs
    h = jnp.arange((nb + nseq) // 2, dtype=jnp.int32)
    owner = (h[:, None] >= first_big[None, :]).astype(jnp.int32).sum(axis=1) - 1
    mine = owner[:, None] == jnp.arange(nseq, dtype=jnp.int32)[None, :]

    def at_owner(values):
        return jnp.sum(jnp.where(mine, values[None, :], 0), axis=1)

    rel = h - at_owner(first_big)
    first = jnp.minimum(at_owner(start) + 2 * rel, nb - 1)
    whole = (2 * rel + 1 < at_owner(blocks)).astype(jnp.int32)
    tab = jnp.stack([first, whole]).astype(jnp.int32)
    seq = jnp.stack(
        [jnp.append(first_big, jnp.sum(blocks)), jnp.append(bigs, jnp.sum(bigs))]
    ).astype(jnp.int32)
    return tab, seq


def live_rows(lens, rows):
    slot = (lens + BLK - 1) // BLK * BLK
    begin = jnp.cumsum(slot) - slot
    pos = jnp.arange(rows, dtype=jnp.int32)
    inside = (pos[:, None] >= begin[None, :]) & (pos[:, None] < (begin + lens)[None, :])
    return jnp.sum(inside.astype(f32), axis=1)


def after(values):
    return lax.optimization_barrier(values)


def rank_of(keys):
    return jnp.sum((keys[None, :] < keys[:, None]).astype(jnp.int32), axis=1)


class Line:
    def __init__(self, n_dp, n_t):
        self.n_dp, self.n_t = n_dp, n_t
        self.axes = {"dp": n_dp, "tensor": n_t}
        self.both = ("dp", "tensor")
        self.cuts = 1

    def place_of_group(self):
        return lax.axis_index("tensor")

    def regroup(self, x):
        return x

    def gather_first(self, x):
        return [lax.all_gather(x, "tensor", axis=0, tiled=True)]

    def gathered(self, x, early):
        return []

    def gather_last(self, x, got):
        return [(got[0], jnp.zeros((1,), jnp.int32))]

    def scatter_first(self, w, arrays, many):
        return [mul_rows(w, arrays, jnp.zeros((1,), jnp.int32), many * self.n_t)]

    def scatter_send(self, parts):
        return [lax.psum_scatter(parts[0], "tensor", scatter_dimension=0, tiled=True)]

    def scatter_own(self, w, arrays, many):
        return []

    def ungroup(self, x):
        return x

    def spread(self, x):
        return lax.all_to_all(x, "dp", split_axis=0, concat_axis=0, tiled=True)

    def order(self, pieces):
        return jnp.append(jnp.arange(pieces * self.n_t, dtype=jnp.int32), 0)

    def enter(self, rank, x, g, chan, norm, pack):
        sent_x, sent_g = permute_to(rank, [x, g])
        return (self.spread(sent_x), self.spread(sent_g)) + self.gather_channels(chan, norm) + (lax.all_gather(pack, "dp", axis=0, tiled=True),)

    def gather_channels(self, chan, norm):
        perm = [(f, (f % self.n_dp) * self.n_t + f // self.n_dp) for f in range(self.n_dp * self.n_t)]
        chan = lax.ppermute(chan, self.both, perm)
        norm = lax.all_gather(norm, self.both, axis=1, tiled=True)
        return lax.all_gather(chan[None], "dp", axis=0, tiled=True), norm

    def cut_order(self):
        return jnp.zeros((1,), jnp.int32)

    def grads_send(self, gw):
        return [lax.psum_scatter(gw[0], "dp", scatter_dimension=0, tiled=True)]

    def grads_last(self, parts):
        return parts[0], lambda part: part.astype(f32)

    def scatter_small(self, sums, norm):
        sums = lax.psum_scatter(sums, "dp", scatter_dimension=0, tiled=True)
        norm = lax.psum_scatter(norm, self.both, scatter_dimension=1, tiled=True)
        perm = [((f % self.n_dp) * self.n_t + f // self.n_dp, f) for f in range(self.n_dp * self.n_t)]
        return (sums, norm), lambda part: (lax.ppermute(part[0], self.both, perm), part[1])


class Pairs:
    def __init__(self, n_dp, n_t):
        self.quads = n_dp // 2
        self.axes = {"q": self.quads, "c": 2, "h": 2, "w": 2}
        self.both = ("q", "c", "h", "w")
        self.cuts = self.quads
        self.other = [(0, 1), (1, 0)]
        self.there = [(2 * c + h, 2 * (1 - h) + c) for c in range(2) for h in range(2)]
        self.back = [(b, a) for a, b in self.there]
        self.turned = [(2 * c + h, 2 * (1 - h) + 1 - c) for c in range(2) for h in range(2)]

    def flip(self, x, axis, bit=1):
        return lax.ppermute(x, axis, [(i, i ^ bit) for i in range(self.axes[axis])])

    def place_of_group(self):
        return 2 * (1 - lax.axis_index("c")) + lax.axis_index("w")

    def regroup(self, x):
        return lax.ppermute(x, ("c", "h"), self.there)

    def ungroup(self, x):
        return lax.ppermute(x, ("c", "h"), self.back)

    def spread(self, x):
        return lax.all_to_all(x, ("q", "c"), split_axis=0, concat_axis=0, tiled=True)

    def places(self):
        c, w = lax.axis_index("c"), lax.axis_index("w")
        return [2 * (1 - c) + w, 2 * c + w, 2 * (1 - c) + 1 - w, 2 * c + 1 - w]

    def starts(self, many):
        return [(place * many).astype(jnp.int32).reshape(1) for place in self.places()]

    def gather_first(self, x):
        return [self.flip(x, "c"), self.flip(x, "w")]

    def gathered(self, x, early):
        return list(zip([x] + early, self.starts(x.shape[0])))

    def gather_last(self, x, got):
        beside, near = got
        return list(zip([x, beside, near, self.flip(near, "c")], self.starts(x.shape[0])))

    def scatter_first(self, w, arrays, many):
        _, beside, near, far = self.starts(many)
        first = mul_rows(w, arrays, far, many)
        give = self.flip(first, "c")
        beside, first = after((beside, first))
        second = mul_rows(w, arrays, beside, many)
        second, give = after((second, give))
        return [second, mul_rows(w, arrays, near, many, extra=give)]

    def scatter_send(self, parts):
        return [self.flip(parts[0], "c"), self.flip(parts[1], "w")]

    def scatter_own(self, w, arrays, many):
        return [mul_rows(w, arrays, self.starts(many)[0], many, dtype=f32)]

    def order(self, pieces):
        place = jnp.stack(self.places())[:, None] * pieces + jnp.arange(pieces)[None, :]
        return jnp.concatenate([place.reshape(-1).astype(jnp.int32), self.cut_order()])

    def steps(self):
        bit = self.quads // 2
        while bit:
            yield "q", bit
            bit //= 2
        yield "h", 1

    def spot(self):
        return 2 * lax.axis_index("q") + lax.axis_index("h")

    def enter(self, rank, x, g, chan, norm, pack):
        small = norm.shape[1]
        norm = jnp.pad(norm, ((0, 5), (0, BLK - small)))
        got, got_g, chan, norm, weights = meet(self.both, rank, x, g, chan, norm, pack)
        norm = norm[:, :3, :small].transpose(1, 0, 2).reshape(3, -1)
        return got.reshape(x.shape), got_g.reshape(x.shape), chan, norm, weights

    def grads_send(self, gw):
        return [gw[0]] + [self.flip(gw[bit], "q", bit) for bit in range(1, self.quads)]

    def grads_last(self, parts):
        total = parts[0].astype(f32)
        for part in parts[1:]:
            total = total + part.astype(f32)
        total = total.astype(bf16)
        half = total.shape[0] // 2
        h = lax.axis_index("h")
        first = jnp.where(h == 0, total[:half], total[half:])
        second = jnp.where(h == 0, total[half:], total[:half])

        def finish(parts):
            return self.ungroup(parts[0]).astype(f32) + lax.ppermute(parts[1], ("c", "h"), self.turned).astype(f32)

        return (first, second), finish

    def cut_order(self):
        return (lax.axis_index("q") ^ jnp.arange(self.quads)).astype(jnp.int32)

    def scatter_small(self, sums, norm):
        count = 2 * self.quads
        rows, wide = sums.shape[0] // count, sums.shape[1]
        norm = norm.reshape(3, 4 * count, -1).transpose(1, 0, 2)
        small = norm.shape[2]
        norm = jnp.pad(norm, ((0, 0), (0, 5), (0, BLK - small)))
        norm = lax.all_to_all(norm, self.both, split_axis=0, concat_axis=0, tiled=True)
        flat = jnp.pad(sums, ((0, 0), (0, -wide % 8))).reshape(count, -1, BLK)
        near = jnp.arange(self.quads) ^ lax.axis_index("q")
        h = lax.axis_index("h")
        keep, give = jnp.take(flat, 2 * near + h, axis=0), jnp.take(flat, 2 * near + 1 - h, axis=0)

        def finish(parts):
            keep, give, norm = parts
            part = keep + self.flip(give, "h")
            total = None
            for apart in range(self.quads):
                perm = []
                for source in range(4 * count):
                    q, c, h, w = source // 8, source // 4 % 2, source // 2 % 2, source % 2
                    perm.append((source, count * (2 * (1 - c) + w) + 2 * (q ^ apart) + h))
                got = lax.ppermute(part[apart], self.both, perm)
                total = got if total is None else total + got
            return total.reshape(rows, -1)[:, :wide], jnp.sum(norm, axis=0)[:3, :small]

        return (keep, give, norm), finish


def local(
    net, wave, tokens, cotangent, source, target, lengths, ln_gain, ln_bias, w_fwd, b_fwd, w_bwd, b_bwd,
    w_gate, b_gate, w_out, b_out, log_dt, log_rate, ssm_b, ssm_c, ssm_d,
):
    rows, width = tokens.shape
    many = rows // BLK
    n_t = net.n_t
    group = rows * n_t
    nb = group // BLK
    ch = w_fwd.shape[1]
    back = (wave.T / BIG).astype(bf16)
    wave = wave.astype(bf16)

    def lanes(column):
        return jnp.broadcast_to(column[..., None], column.shape + (BLK,))

    def decays(log_dt, log_rate, ssm_b):
        rate = jnp.exp(log_rate)
        ld = -jnp.exp(log_dt)[..., None] * rate
        return rate, ld, (1.0 - jnp.exp(ld)) / rate * ssm_b

    rank = rank_of(target)
    sender = source // group
    place = rank_of(sender * rows + jnp.arange(rows, dtype=jnp.int32))
    pack = jnp.concatenate(
        [w_fwd, w_bwd, w_gate.reshape(-1, 2 * ch), w_out.transpose(2, 0, 1).reshape(-1, 2 * ch)], axis=1
    )
    table = net.regroup(jnp.concatenate([place, lengths[0]]))
    rate, ld, drive = decays(log_dt, log_rate, ssm_b)
    own = b_fwd.shape[0]
    small = jnp.concatenate([ssm_d, b_fwd[None], b_bwd[None], b_gate])
    chan = jnp.concatenate(
        [
            (ld * log2e).reshape(own, 2 * STATE),
            (ssm_c * drive).reshape(own, 2 * STATE),
            jnp.pad(small, ((0, -(2 * own + 6) % 8 + 0), (0, 2 * STATE - own))),
        ]
    )
    norm = jnp.stack([ln_gain, ln_bias, b_out])
    got_x, got_g, chan_all, norm_all, w_all = net.enter(rank, tokens, cotangent, chan, norm, pack)
    got_x, got_g, chan_all, norm_all, w_all, table = after((got_x, got_g, chan_all, norm_all, w_all, table))

    place, lens = table[:rows], table[rows:]
    gain = lanes(norm_all[0])
    shift = lanes(norm_all[1])
    small = chan_all[:, 2 * own : 2 * own + 6, :own].transpose(1, 0, 2).reshape(6, ch)

    def pairs(at):
        both = chan_all[:, at : at + own].reshape(-1, 2, own // 2, 2 * STATE)
        return both.transpose(1, 0, 2, 3).reshape(2, ch // 2, 2 * STATE)

    ld_pairs = pairs(0)
    w_pairs = pairs(own)
    skip = lanes(small[0:2])
    live = live_rows(lens, group)
    live_own = lax.dynamic_slice_in_dim(live, net.place_of_group() * rows, rows, 0).reshape(many, 1, BLK)
    live = live.reshape(nb // 2, 1, BIG)
    tab, seq = sequence_tables(lens, nb)

    xt, xd = deal_x(place, got_x, gain, shift)
    xt, ld_pairs, w_pairs, skip, w_all = after((xt, ld_pairs, w_pairs, skip, w_all))
    x_got = net.gather_first(xt)
    kh = spectra(ld_pairs, w_pairs, skip, wave)
    w_in, w_back, w_in_t, w_back_t = split_weights(w_all, 4 * ch)
    bias_in = lanes(small[2:6].reshape(-1))
    bias_out = lanes(norm_all[2])
    gt, gd, g_bias_out = deal_g(place, got_g, live_own)
    early, kh, w_in_t, bias_in, gt = after((x_got[:-1], kh, w_in_t, bias_in, gt))
    kept = None
    for part, start in net.gathered(xt, early):
        kept = project(part, start, nb, live, w_in_t, bias_in, kept)
    kept, late, gt = after((kept, x_got[-1], gt))
    g_got = net.gather_first(gt)
    xs = net.gather_last(xt, early + [late])
    for part, start in xs[len(early) + 1 if early else 0 :]:
        kept = project(part, start, nb, live, w_in_t, bias_in, kept)
    a, da, gg, dg = kept
    y, mix = ssm_scan(tab, seq, a, kh, wave, back, gg)
    g_got, y, mix = after((g_got, y, mix))
    gs = net.gather_last(gt, g_got)
    branch = net.scatter_first(w_back, [mix], many)
    gm = gate_grad(gs, nb, w_back_t)
    branch, gm = after((branch, gm))

    branch = net.scatter_send(branch)
    branch = net.scatter_own(w_back, [mix], many) + branch
    first = ssm_back(0, tab, seq, a, gm, kh, wave, back, gg, y, dg, da)
    branch, first, a = after((branch, first, a))
    sent_out = layer_rows(place, branch, xd, live_own, bias_out)
    sent_out, a = after((sent_out, a))
    sent_out = net.ungroup(sent_out)
    second = ssm_back(1, tab, seq, a, gm, kh, wave, back, gg, y, dg, da)
    sent_out, first, second = after((sent_out, first, second))
    gpg, gp, gh, bsum = zip(first, second)
    sent_out = net.spread(sent_out)
    back_list = [gp[0], gp[1], gpg[0], gpg[1]]
    g_normed = net.scatter_first(w_in, back_list, many)
    g_normed, back_list, mix = after((g_normed, back_list, mix))
    gp, gpg = back_list[:2], back_list[2:]
    g_normed = net.scatter_send(g_normed)
    g_normed = net.scatter_own(w_in, back_list, many) + g_normed
    gw = outer_sums(net.order(many // 8), net.cuts, [part for part, _ in xs], [part for part, _ in gs], gp, gpg, mix)
    g_normed, gw, gh, sent_out = after((g_normed, gw, gh, sent_out))
    sent_in, norm_sums = input_rows(place, g_normed, xd, gd, gain)
    sent_in, gh, gw, norm_sums, sent_out, bsum = after((sent_in, gh, gw, norm_sums, sent_out, bsum))
    sent_in = net.ungroup(sent_in)
    gw = net.grads_send(gw)
    s0, s1, g0 = [jnp.concatenate(part) for part in zip(*[moments(k, ld_pairs, gh[k], back) for k in range(2)])]
    layer_out = permute_from(rank, sent_out)

    s0 = s0.reshape(2, ch, STATE)
    s1 = s1.reshape(2, ch, STATE)
    bsum = jnp.concatenate(bsum)
    gb_gate = jnp.sum(bsum[:, :, :BLK], axis=2)
    gb_in = jnp.sum(bsum[:, :, BLK:], axis=2)
    sums = jnp.concatenate(
        [s0[0], s0[1], s1[0], s1[1], jnp.concatenate([g0[:, :, 0], gb_gate, gb_in], axis=0).T], axis=1
    )
    norm_sums = jnp.sum(jnp.concatenate([norm_sums, g_bias_out[None]], axis=0), axis=2)
    part, finish = net.scatter_small(sums, norm_sums)
    gw, gw_finish = net.grads_last(gw)
    sent_in, gw, part, layer_out = after((sent_in, gw, part, layer_out))
    in_grad = permute_from(rank, net.spread(sent_in))
    gw = gw_finish(gw)
    sums, norm_sums = finish(part)
    s0 = jnp.stack([sums[:, :STATE], sums[:, STATE : 2 * STATE]])
    s1 = jnp.stack([sums[:, 2 * STATE : 3 * STATE], sums[:, 3 * STATE : 4 * STATE]])
    tail = sums[:, 4 * STATE :].T
    step = jnp.exp(log_dt)[..., None]
    g_c = s0 * drive
    g_drive = s0 * ssm_c
    g_b = g_drive * (1.0 - jnp.exp(ld)) / rate
    g_ld = s1 * ssm_c * drive - g_drive * ssm_b / rate * jnp.exp(ld)
    g_rate = -g_drive * drive / rate - g_ld * step
    g_dt = jnp.sum(g_ld * ld, axis=2)
    return (
        layer_out,
        in_grad,
        norm_sums[0],
        norm_sums[1],
        gw[:, :ch],
        tail[4],
        gw[:, ch : 2 * ch],
        tail[5],
        gw[:, 2 * ch : 4 * ch].reshape(-1, 2, ch),
        tail[2:4],
        gw[:, 4 * ch :].T.reshape(2, ch, -1),
        norm_sums[2],
        g_dt,
        g_rate * rate,
        g_b,
        g_c,
        tail[0:2],
    )


def solution(mesh):
    n_dp, n_t = mesh.shape["dp"], mesh.shape["tensor"]
    if n_t == 4 and n_dp == 8:
        net = Pairs(n_dp, n_t)
        dp, tensor = ("q", "c"), ("h", "w")
    else:
        net = Line(n_dp, n_t)
        dp, tensor = ("dp",), ("tensor",)
    net.n_t = n_t
    mesh = jax.sharding.Mesh(mesh.devices.reshape(tuple(net.axes.values())), tuple(net.axes))
    both = P(dp + tensor)
    rows = P(dp + tensor, None)
    pair = P(None, dp + tensor)
    state = P(None, dp + tensor, None)
    proj = P(dp, tensor)
    gate = P(dp, None, tensor)
    out = P(None, tensor, dp)
    wave = wave_table()

    def run(*args):
        return local(net, jnp.asarray(wave), *args)

    return jax.shard_map(
        run,
        mesh=mesh,
        in_specs=(
            rows, rows, both, both, P(dp, None), both, both, proj, both, proj, both, gate, pair, out, both,
            pair, state, state, state, pair,
        ),
        out_specs=(
            rows, rows, both, both, proj, both, proj, both, gate, pair, out, both, pair, state, state, state, pair,
        ),
        check_vma=False,
    )
```

```python
from functools import partial

import jax
import jax.numpy as jnp
import numpy as np
from jax import lax
from jax.experimental import pallas as pl
from jax.experimental.pallas import tpu as pltpu
from jax.sharding import PartitionSpec as P

BLK = 128
BIG = 256
MOST = 2048
LAGS = MOST // BIG
STATE = 64
epsilon = 1e-05
log2e = 1.4426950408889634
f32 = jnp.float32
bf16 = jnp.bfloat16
MIB = 2**20


def nn(a, b):
    return lax.dot_general(a, b, (((1,), (0,)), ((), ())), preferred_element_type=f32)


def nt(a, b):
    return lax.dot_general(a, b, (((1,), (1,)), ((), ())), preferred_element_type=f32)


def params(limit):
    return pltpu.CompilerParams(vmem_limit_bytes=60 * MIB)


def cost(flops, moved, trans=0):
    scale = 0.05
    return pl.CostEstimate(
        flops=int(scale * flops), bytes_accessed=int(scale * moved), transcendentals=int(scale * trans)
    )


def halves(x):
    high = x.astype(bf16)
    return high, (x - high.astype(f32)).astype(bf16)


def wave_table():
    pos = np.arange(BIG)[:, None]
    freq = np.arange(BIG)[None, :]
    angle = 2 * np.pi * ((2 * freq + 1) * pos % (4 * BIG)) / (4 * BIG)
    return np.concatenate([np.cos(angle), np.sin(angle)], 1).astype(np.float32)


def chunk_of(channels, most):
    best = 16
    for size in range(16, most + 1, 16):
        if channels % size == 0:
            best = size
    return best


def permute_row_body(count, rank_ref, *refs):
    rows = rank_ref.shape[1]
    spot = lax.broadcasted_iota(jnp.int32, (rows, rows), 0)
    pick = jnp.where(spot == rank_ref[...], 1.0, 0.0).astype(bf16)
    for at in range(count):
        refs[count + at][...] = nn(pick, refs[at][...]).astype(bf16)


def permute_to(rank, arrays):
    rows, width = arrays[0].shape
    count = len(arrays)
    return pl.pallas_call(
        partial(permute_row_body, count),
        out_shape=[jax.ShapeDtypeStruct((rows, width), bf16)] * count,
        compiler_params=params(48),
        cost_estimate=cost(2 * count * rows * rows * width, 4 * count * rows * width),
    )(rank.reshape(1, rows), *arrays)


def permute_col_body(rank_ref, x_ref, o_ref):
    rows = x_ref.shape[0]
    spot = lax.broadcasted_iota(jnp.int32, (rows, rows), 1)
    pick = jnp.where(spot == rank_ref[...], 1.0, 0.0).astype(bf16)
    o_ref[...] = nn(pick, x_ref[...]).astype(bf16)


def permute_from(rank, x):
    rows, width = x.shape
    return pl.pallas_call(
        permute_col_body,
        out_shape=jax.ShapeDtypeStruct((rows, width), bf16),
        compiler_params=params(48),
        cost_estimate=cost(2 * rows * rows * width, 4 * rows * width),
    )(rank.reshape(rows, 1), x)


def pick_rows(place_ref, x_ref):
    spot = lax.broadcasted_iota(jnp.int32, (BLK, x_ref.shape[0]), 1)
    pick = jnp.where(spot == place_ref[...], 1.0, 0.0).astype(bf16)
    return nn(pick, x_ref[...]).T


def deal_x_body(place_ref, x_ref, gain_ref, shift_ref, xt_ref, xd_ref):
    x = pick_rows(place_ref, x_ref)
    xd_ref[0] = x.astype(bf16)
    centred = x - jnp.mean(x, axis=0, keepdims=True)
    inv_std = lax.rsqrt(jnp.mean(centred * centred, axis=0, keepdims=True) + epsilon)
    xt_ref[0] = (centred * inv_std * gain_ref[...] + shift_ref[...]).astype(bf16)


def deal_g_body(place_ref, g_ref, live_ref, gt_ref, gd_ref, bo_ref):
    g = pick_rows(place_ref, g_ref)
    gd_ref[0] = g.astype(bf16)
    g = g * live_ref[0]
    gt_ref[0] = g.astype(bf16)

    @pl.when(pl.program_id(0) == 0)
    def _():
        bo_ref[...] = jnp.zeros_like(bo_ref)

    bo_ref[...] += g


def deal_specs(rows, width):
    place = pl.BlockSpec((BLK, 1), lambda i: (i, 0))
    whole = pl.BlockSpec((rows, width), lambda i: (0, 0))
    wide = pl.BlockSpec((width, BLK), lambda i: (0, 0))
    out = pl.BlockSpec((1, width, BLK), lambda i: (i, 0, 0))
    return place, whole, wide, out


def deal_x(place, x, gain, shift):
    rows, width = x.shape
    blocks = rows // BLK
    spot, whole, wide, out = deal_specs(rows, width)
    return pl.pallas_call(
        deal_x_body,
        grid=(blocks,),
        in_specs=[spot, whole, wide, wide],
        out_specs=[out, out],
        out_shape=[jax.ShapeDtypeStruct((blocks, width, BLK), bf16)] * 2,
        compiler_params=params(40),
        cost_estimate=cost(2 * rows * rows * width, 6 * rows * width),
    )(place.reshape(rows, 1), x, gain, shift)


def deal_g(place, g, live):
    rows, width = g.shape
    blocks = rows // BLK
    spot, whole, wide, out = deal_specs(rows, width)
    return pl.pallas_call(
        deal_g_body,
        grid=(blocks,),
        in_specs=[spot, whole, pl.BlockSpec((1, 1, BLK), lambda i: (i, 0, 0))],
        out_specs=[out, out, wide],
        out_shape=[jax.ShapeDtypeStruct((blocks, width, BLK), bf16)] * 2
        + [jax.ShapeDtypeStruct((width, BLK), f32)],
        compiler_params=params(40),
        cost_estimate=cost(2 * rows * rows * width, 6 * rows * width),
    )(place.reshape(rows, 1), g, live)


def send_back(place_ref, out_s, o_ref):
    rows = out_s.shape[0]
    spot = lax.broadcasted_iota(jnp.int32, (rows, rows), 0)
    pick = jnp.where(spot == place_ref[...], 1.0, 0.0).astype(bf16)
    o_ref[...] = nn(pick, out_s[...]).astype(bf16)


def total(refs, at):
    value = refs[0][at].astype(f32)
    for ref in refs[1:]:
        value = value + ref[at].astype(f32)
    return value


def layer_body(place_ref, xd_ref, live_ref, bias_ref, *refs):
    o_ref, out_s = refs[-2:]
    for at in range(xd_ref.shape[0]):
        y = xd_ref[at].astype(f32) + live_ref[at] * (total(refs[:-2], at) + bias_ref[...])
        out_s[at * BLK : (at + 1) * BLK, :] = y.T.astype(bf16)
    send_back(place_ref, out_s, o_ref)


def layer_rows(place, parts, xd, live, bias):
    blocks, width, _ = xd.shape
    rows = blocks * BLK
    return pl.pallas_call(
        layer_body,
        out_shape=jax.ShapeDtypeStruct((rows, width), bf16),
        scratch_shapes=[pltpu.VMEM((rows, width), bf16)],
        compiler_params=params(48),
        cost_estimate=cost(2 * rows * rows * width, 6 * rows * width),
    )(place.reshape(1, rows), xd, live, bias, *parts)


def input_body(place_ref, xd_ref, gd_ref, gain_ref, *refs):
    o_ref, sums_ref, out_s = refs[-3:]
    g_gain = jnp.zeros(gain_ref.shape, f32)
    g_shift = jnp.zeros(gain_ref.shape, f32)
    for at in range(xd_ref.shape[0]):
        x = xd_ref[at].astype(f32)
        centred = x - jnp.mean(x, axis=0, keepdims=True)
        inv_std = lax.rsqrt(jnp.mean(centred * centred, axis=0, keepdims=True) + epsilon)
        x_hat = centred * inv_std
        g = total(refs[:-3], at)
        g_gain = g_gain + g * x_hat
        g_shift = g_shift + g
        hat = g * gain_ref[...]
        back = inv_std * (
            hat
            - jnp.mean(hat, axis=0, keepdims=True)
            - x_hat * jnp.mean(hat * x_hat, axis=0, keepdims=True)
        )
        out_s[at * BLK : (at + 1) * BLK, :] = (gd_ref[at].astype(f32) + back).T.astype(bf16)
    sums_ref[0] = g_gain
    sums_ref[1] = g_shift
    send_back(place_ref, out_s, o_ref)


def input_rows(place, parts, xd, gd, gain):
    blocks, width, _ = xd.shape
    rows = blocks * BLK
    return pl.pallas_call(
        input_body,
        out_shape=[
            jax.ShapeDtypeStruct((rows, width), bf16),
            jax.ShapeDtypeStruct((2, width, BLK), f32),
        ],
        scratch_shapes=[pltpu.VMEM((rows, width), bf16)],
        compiler_params=params(48),
        cost_estimate=cost(2 * rows * rows * width, 8 * rows * width),
    )(place.reshape(1, rows), xd, gd, gain, *parts)


def project_body(ch, many, start_ref, x_ref, live_ref, wt_ref, bias_ref, *refs):
    a_ref, da_ref, gg_ref, dg_ref = refs[-4:]
    x = jnp.concatenate([x_ref[0], x_ref[1]], axis=1)
    live = live_ref[0]
    root = 0.7978845608028654
    step = 64 if ch % 128 else 128

    def act(pre):
        square = pre * pre
        rise = 0.5 + 0.5 * jnp.tanh(pre * (root + (0.044715 * root) * square))
        value = pre * rise
        slope = rise + rise * (pre - value) * (2.0 * root + (6.0 * 0.044715 * root) * square)
        return value, slope

    def put(ref, k, at, value):
        value = value.astype(bf16)
        ref[k, 0, at, :] = value[:, :BLK]
        ref[k, 1, at, :] = value[:, BLK:]

    for k in range(2):
        for first, value_ref, slope_ref in ((k * ch, a_ref, da_ref), ((2 + k) * ch, gg_ref, dg_ref)):
            for at in range(0, ch, step):
                rows = pl.ds(first + at, step)
                bias = bias_ref[rows, :]
                pre = nn(wt_ref[rows, :], x) + jnp.concatenate([bias, bias], axis=1)
                value, slope = act(pre)
                if value_ref is a_ref:
                    value, slope = live * value, live * slope
                put(value_ref, k, pl.ds(at, step), value)
                put(slope_ref, k, pl.ds(at, step), slope)


def chained(body, grid, in_specs, out_specs, shapes, scratch, limit, estimate, start, operands, kept):
    kept = [] if kept is None else list(kept)
    specs = list(in_specs) + [pl.BlockSpec(memory_space=pl.ANY)] * len(kept)
    first = 1 + len(operands)
    return pl.pallas_call(
        body,
        grid_spec=pltpu.PrefetchScalarGridSpec(
            num_scalar_prefetch=1, grid=grid, in_specs=specs, out_specs=out_specs, scratch_shapes=scratch
        ),
        out_shape=shapes,
        input_output_aliases={first + at: at for at in range(len(kept))},
        compiler_params=params(limit),
        cost_estimate=estimate,
    )(start, *operands, *kept)


def project(xt, start, nb, live, wt, bias, kept):
    many, width, _ = xt.shape
    ch = wt.shape[0] // 4
    out = pl.BlockSpec((2, 2, ch, BLK), lambda i, at: (0, at[0] + i, 0, 0))
    tok = many * BLK
    return chained(
        partial(project_body, ch, many),
        (many // 2,),
        [
            pl.BlockSpec((2, width, BLK), lambda i, at: (i, 0, 0)),
            pl.BlockSpec((1, 1, BIG), lambda i, at: (at[0] + i, 0, 0)),
            pl.BlockSpec((4 * ch, width), lambda i, at: (0, 0)),
            pl.BlockSpec((4 * ch, BLK), lambda i, at: (0, 0)),
        ],
        [out] * 4,
        [jax.ShapeDtypeStruct((2, nb, ch, BLK), bf16)] * 4,
        [],
        48,
        cost(8 * tok * width * ch, 2 * tok * width + 16 * tok * ch, 4 * tok * ch),
        start // 2,
        [xt, live, wt, bias],
        kept,
    )


def gate_grad_body(ch, parts, at_ref, *refs):
    wt_ref, o_ref = refs[parts:]
    steps = pl.num_programs(0) // parts

    def work(g_ref):
        gm = nn(wt_ref[...], jnp.concatenate([g_ref[0], g_ref[1]], axis=1)).astype(bf16)
        for k in range(2):
            for h in range(2):
                o_ref[k, h] = gm[k * ch : (k + 1) * ch, h * BLK : (h + 1) * BLK]

    for part in range(parts):

        @pl.when(pl.program_id(0) // steps == part)
        def _(part=part):
            work(refs[part])


def gate_grad(gs, nb, wt):
    parts = len(gs)
    many, width, _ = gs[0][0].shape
    steps = many // 2
    ch = wt.shape[0] // 2
    tok = nb * BLK

    def rows(part):
        return pl.BlockSpec((2, width, BLK), lambda i, at: (jnp.clip(i - part * steps, 0, steps - 1), 0, 0))

    order = jnp.concatenate([start // 2 for _, start in gs]).astype(jnp.int32)
    return pl.pallas_call(
        partial(gate_grad_body, ch, parts),
        grid_spec=pltpu.PrefetchScalarGridSpec(
            num_scalar_prefetch=1,
            grid=(parts * steps,),
            in_specs=[rows(part) for part in range(parts)] + [pl.BlockSpec((2 * ch, width), lambda i, at: (0, 0))],
            out_specs=pl.BlockSpec((2, 2, ch, BLK), lambda i, at: (0, at[i // steps] + i % steps, 0, 0)),
        ),
        out_shape=jax.ShapeDtypeStruct((2, nb, ch, BLK), bf16),
        compiler_params=params(40),
        cost_estimate=cost(4 * tok * width * ch, 2 * tok * width + 4 * tok * ch),
    )(order, *[part for part, _ in gs], wt)


def spectra_body(cc, ld_ref, w_ref, d_ref, wave_ref, kh_ref, k_s):
    t = lax.broadcasted_iota(jnp.int32, (BLK, BLK), 0).astype(f32)
    block = lax.broadcasted_iota(jnp.int32, (2 * LAGS, BLK), 0).astype(f32) * float(BLK)
    low = lax.broadcasted_iota(jnp.int32, (2 * LAGS, BLK), 1) < STATE
    count = 2 * LAGS

    def one(p, carry):
        ld = ld_ref[0, pl.ds(p, 1), :]
        decay = jnp.exp2(t * ld)
        scale = w_ref[0, pl.ds(p, 1), :] * jnp.exp2(block * ld)
        lhs = jnp.concatenate([jnp.where(low, scale, 0.0), jnp.where(low, 0.0, scale)], axis=0)
        lhs_high, lhs_low = halves(lhs)
        k = nt(jnp.concatenate([lhs_high, lhs_low], axis=0), decay.astype(bf16))
        k = k[0 : 2 * count] + k[2 * count : 4 * count]
        k_s[pl.ds(2 * p, count, stride=cc), :] = k[0:count]
        k_s[pl.ds(2 * p + 1, count, stride=cc), :] = k[count : 2 * count]
        return carry

    lax.fori_loop(0, cc // 2, one, 0, unroll=16)
    sign = jnp.where(lax.broadcasted_iota(jnp.int32, (cc, BIG), 1) % 2 == 0, 1.0, -1.0)
    before = None
    for big in range(LAGS):
        rows = jnp.concatenate(
            [k_s[pl.ds(2 * big * cc, cc), :], k_s[pl.ds((2 * big + 1) * cc, cc), :]], axis=1
        )
        high, rest = halves(rows)
        x = nn(high, wave_ref[...]) + nn(rest, wave_ref[...])
        xc, xs = x[:, :BIG], x[:, BIG:]
        if big == 0:
            kh_ref[0, 0, :, :BIG] = xc + d_ref[0][:, 0:1]
            kh_ref[0, 0, :, BIG:] = xs
        else:
            kh_ref[0, big, :, :BIG] = xc + sign * before[1]
            kh_ref[0, big, :, BIG:] = xs - sign * before[0]
        before = (xc, xs)


def spectra(ld, w, d, wave):
    ch = 2 * ld.shape[1]
    cc = chunk_of(ch, 128)
    return pl.pallas_call(
        partial(spectra_body, cc),
        grid=(2, ch // cc),
        in_specs=[pl.BlockSpec((1, cc // 2, BLK), lambda k, i: (k, i, 0))] * 2
        + [
            pl.BlockSpec((1, cc, BLK), lambda k, i: (k, i, 0)),
            pl.BlockSpec((BIG, 2 * BIG), lambda k, i: (0, 0)),
        ],
        out_specs=pl.BlockSpec((1, LAGS, cc, 2 * BIG), lambda k, i: (k, 0, i, 0)),
        out_shape=jax.ShapeDtypeStruct((2, LAGS, ch, 2 * BIG), f32),
        scratch_shapes=[pltpu.VMEM((2 * LAGS * cc, BLK), f32)],
        compiler_params=params(40),
        cost_estimate=cost(2 * ch * 40e6, 2 * ch * LAGS * 2 * BIG * 4),
    )(ld, w, d, wave)


def moments_body(cc, ld_ref, gh_ref, back_ref, s0_ref, s1_ref, g0_ref, g_s):
    sign = jnp.where(lax.broadcasted_iota(jnp.int32, (cc, BIG), 1) % 2 == 0, 1.0, -1.0)
    count = 2 * LAGS
    for big in range(LAGS):
        c = gh_ref[0, big, :, :BIG]
        s = gh_ref[0, big, :, BIG:]
        if big < LAGS - 1:
            c, s = c - sign * gh_ref[0, big + 1, :, BIG:], s + sign * gh_ref[0, big + 1, :, :BIG]
        high, rest = halves(jnp.concatenate([c, s], axis=1))
        g = nn(high, back_ref[...]) + nn(rest, back_ref[...])
        g_s[pl.ds(2 * big * cc, cc), :] = g[:, :BLK]
        g_s[pl.ds((2 * big + 1) * cc, cc), :] = g[:, BLK:]
        if big == 0:
            g0_ref[0] = g[:, :BLK]
    t = lax.broadcasted_iota(jnp.int32, (BLK, BLK), 0).astype(f32)
    lane = lax.broadcasted_iota(jnp.int32, (count, BLK), 1)
    lag = lane.astype(f32)
    block = lax.broadcasted_iota(jnp.int32, (count, BLK), 0).astype(f32) * float(BLK)
    low = lane < STATE

    def one(p, carry):
        ld = ld_ref[0, pl.ds(p, 1), :]
        decay = jnp.exp2(t * ld).astype(bf16)
        far = jnp.exp2(block * ld)
        ga = g_s[pl.ds(2 * p, count, stride=cc), :]
        gb = g_s[pl.ds(2 * p + 1, count, stride=cc), :]
        high, rest = halves(jnp.concatenate([ga, gb, ga * lag, gb * lag], axis=0))
        m = nn(jnp.concatenate([high, rest], axis=0), decay)
        m = m[0 : 4 * count] + m[4 * count : 8 * count]
        m0 = jnp.where(low, m[0:count], m[count : 2 * count])
        m1 = jnp.where(low, m[2 * count : 3 * count], m[3 * count : 4 * count]) + block * m0
        s0_ref[0, pl.ds(p, 1), :] = jnp.sum(far * m0, axis=0, keepdims=True)
        s1_ref[0, pl.ds(p, 1), :] = jnp.sum(far * m1, axis=0, keepdims=True)
        return carry

    lax.fori_loop(0, cc // 2, one, 0, unroll=16)


def moments(k, ld, gh, back):
    ch = gh.shape[2]
    cc = chunk_of(ch, 128)
    row = pl.BlockSpec((1, cc // 2, BLK), lambda i: (0, i, 0))
    return pl.pallas_call(
        partial(moments_body, cc),
        grid=(ch // cc,),
        in_specs=[
            pl.BlockSpec((1, cc // 2, BLK), lambda i: (k, i, 0)),
            pl.BlockSpec((1, LAGS, cc, 2 * BIG), lambda i: (0, 0, i, 0)),
            pl.BlockSpec((2 * BIG, BIG), lambda i: (0, 0)),
        ],
        out_specs=[row, row, pl.BlockSpec((1, cc, BLK), lambda i: (0, i, 0))],
        out_shape=[jax.ShapeDtypeStruct((1, ch // 2, BLK), f32)] * 2
        + [jax.ShapeDtypeStruct((1, ch, BLK), f32)],
        scratch_shapes=[pltpu.VMEM((2 * LAGS * cc, BLK), f32)],
        compiler_params=params(40),
        cost_estimate=cost(ch * 40e6, ch * LAGS * 2 * BIG * 4),
    )(ld, gh, back)


def load_pieces(nb, pieces, cc, tab_ref, block, in_s, wave_ref, dst):
    for h in range(pieces):
        first = tab_ref[0, h]
        whole = tab_ref[1, h].astype(f32)
        in_s[pl.ds(h * cc, cc), 0:BLK] = block(first).astype(bf16)
        in_s[pl.ds(h * cc, cc), BLK:BIG] = (block(jnp.minimum(first + 1, nb - 1)) * whole).astype(bf16)
    for h in range(pieces):
        at = pl.ds(h * cc, cc)
        dst[at, :] = nn(in_s[at, :], wave_ref[...])


def over_pieces(nseq, cc, rg, seq_ref, piece):
    def group(r, carry):
        off = pl.multiple_of(r * rg, rg)
        for s in range(nseq):
            base = seq_ref[0, s]
            count = seq_ref[1, s]

            def outer(i, carry):
                piece(i, count, base, off)
                return carry

            lax.fori_loop(0, count, outer, 0)
        return carry

    lax.fori_loop(0, cc // rg, group, 0)


def scan_body(
    nb, nseq, cc, rg, tab_ref, seq_ref, a_ref, kh_ref, wave_ref, back_ref, gg_ref, y_ref, mix_ref, in_s, ah_s, yh_s, y_s
):
    pieces = (nb + nseq) // 2
    load_pieces(nb, pieces, cc, tab_ref, lambda b: a_ref[0, b].astype(f32), in_s, wave_ref, ah_s)
    zero = jnp.zeros((rg, BIG), f32)

    def products(flip):
        def piece(i, count, base, off):
            def inner(j, acc):
                yc, ys = acc
                other = (base + i + j) if flip else (base + i - j)
                m = pl.ds(pl.multiple_of(other * cc + off, rg), rg)
                rows = pl.ds(off, rg)
                ac = ah_s[m, :BIG]
                as_ = ah_s[m, BIG:]
                kc = kh_ref[0, j, rows, :BIG]
                ks = kh_ref[0, j, rows, BIG:]
                if flip:
                    return (yc + kc * ac + ks * as_, ys + kc * as_ - ks * ac)
                return (yc + kc * ac - ks * as_, ys + kc * as_ + ks * ac)

            yc, ys = lax.fori_loop(0, (count - i) if flip else (i + 1), inner, (zero, zero))
            at = pl.ds(pl.multiple_of((base + i) * cc + off, rg), rg)
            yh_s[at, :BIG] = yc.astype(bf16)
            yh_s[at, BIG:] = ys.astype(bf16)

        over_pieces(nseq, cc, rg, seq_ref, piece)

    @pl.when(pl.program_id(0) == 0)
    def _():
        products(False)

    @pl.when(pl.program_id(0) == 1)
    def _():
        products(True)

    for h in range(pieces):
        at = pl.ds(h * cc, cc)
        y_s[at, :] = nn(yh_s[at, :], back_ref[...])

    def one(b, y):
        y_ref[0, b] = y.astype(bf16)
        mix_ref[0, b] = (y * gg_ref[0, b].astype(f32)).astype(bf16)

    def last(h, carry):
        b = tab_ref[0, h]
        at = pl.ds(pl.multiple_of(h * cc, cc), cc)
        one(b, y_s[at, 0:BLK])

        @pl.when(tab_ref[1, h] == 1)
        def _():
            one(b + 1, y_s[at, BLK:])

        return carry

    lax.fori_loop(0, seq_ref[1, nseq], last, 0)
    nothing = jnp.zeros((cc, BLK), bf16)

    def fill(b, carry):
        y_ref[0, b] = nothing
        mix_ref[0, b] = nothing
        return carry

    lax.fori_loop(seq_ref[0, nseq], nb, fill, 0)


def back_body(
    nb, nseq, cc, rg, flip, tab_ref, seq_ref, a_ref, gm_ref, kh_ref, wave_ref, back_ref, gg_ref, y_ref, dg_ref, da_ref,
    gpg_ref, gp_ref, gh_ref, bs_ref, in_s, ah_s, gh_s, xh_s, x_s,
):
    pieces = (nb + nseq) // 2
    load_pieces(nb, pieces, cc, tab_ref, lambda b: a_ref[0, b].astype(f32), in_s, wave_ref, ah_s)
    load_pieces(
        nb, pieces, cc, tab_ref, lambda b: gm_ref[0, b].astype(f32) * gg_ref[0, b].astype(f32), in_s, wave_ref, gh_s
    )
    gh_ref[...] = jnp.zeros_like(gh_ref)
    zero = jnp.zeros((rg, BIG), f32)

    def piece(i, count, base, off):
        at = pl.ds(pl.multiple_of((base + i) * cc + off, rg), rg)
        ac = ah_s[at, :BIG]
        as_ = ah_s[at, BIG:]

        def inner(j, acc):
            xc, xs = acc
            other = (base + i - j) if flip else (base + i + j)
            m = pl.ds(pl.multiple_of(other * cc + off, rg), rg)
            rows = pl.ds(off, rg)
            gc = gh_s[m, :BIG]
            gs = gh_s[m, BIG:]
            kc = kh_ref[0, j, rows, :BIG]
            ks = kh_ref[0, j, rows, BIG:]
            gh_ref[0, j, rows, :BIG] += ac * gc + as_ * gs
            if flip:
                gh_ref[0, j, rows, BIG:] += gc * as_ - gs * ac
                return (xc + kc * gc - ks * gs, xs + kc * gs + ks * gc)
            gh_ref[0, j, rows, BIG:] += ac * gs - as_ * gc
            return (xc + kc * gc + ks * gs, xs + kc * gs - ks * gc)

        xc, xs = lax.fori_loop(0, (i + 1) if flip else (count - i), inner, (zero, zero))
        xh_s[at, :BIG] = xc.astype(bf16)
        xh_s[at, BIG:] = xs.astype(bf16)

    over_pieces(nseq, cc, rg, seq_ref, piece)

    for h in range(pieces):
        at = pl.ds(h * cc, cc)
        x_s[at, :] = nn(xh_s[at, :], back_ref[...])

    none = jnp.zeros((cc, BLK), f32)

    def one(b, gx, carry):
        s0, s1 = carry
        gpg = (y_ref[0, b].astype(f32) * gm_ref[0, b].astype(f32) * dg_ref[0, b].astype(f32)).astype(bf16)
        gpg_ref[0, b] = gpg
        gp = (gx * da_ref[0, b].astype(f32)).astype(bf16)
        gp_ref[0, b] = gp
        return (s0 + gpg.astype(f32), s1 + gp.astype(f32))

    def last(h, carry):
        b = tab_ref[0, h]
        at = pl.ds(pl.multiple_of(h * cc, cc), cc)
        carry = one(b, x_s[at, 0:BLK], carry)

        def more(kept):
            return one(b + 1, x_s[at, BLK:], kept)

        return lax.cond(tab_ref[1, h] == 1, more, lambda kept: kept, carry)

    s0, s1 = lax.fori_loop(0, seq_ref[1, nseq], last, (none, none))
    bs_ref[0, :, 0:BLK] = s0
    bs_ref[0, :, BLK:] = s1
    nothing = jnp.zeros((cc, BLK), bf16)

    def fill(b, carry):
        gpg_ref[0, b] = nothing
        gp_ref[0, b] = nothing
        return carry

    lax.fori_loop(seq_ref[0, nseq], nb, fill, 0)


def ssm_specs(shape, seq):
    _, nb, ch, _ = shape
    nseq = seq.shape[1] - 1
    pieces = (nb + nseq) // 2
    cc = chunk_of(ch, 128 if nb <= 32 else 64)
    big = pl.BlockSpec((1, nb, cc, BLK), lambda k, i: (k, 0, i, 0))
    spec = pl.BlockSpec((1, LAGS, cc, 2 * BIG), lambda k, i: (k, 0, i, 0))
    smem = pl.BlockSpec(memory_space=pltpu.SMEM)
    head = [smem, smem]
    tables = [pl.BlockSpec((BIG, 2 * BIG), lambda k, i: (0, 0)), pl.BlockSpec((2 * BIG, BIG), lambda k, i: (0, 0))]
    return nb, nseq, ch, cc, pieces * cc, big, spec, head, tables


def ssm_scan(tab, seq, a, kh, wave, back, gg):
    nb, nseq, ch, cc, size, big, spec, head, tables = ssm_specs(a.shape, seq)
    return pl.pallas_call(
        partial(scan_body, nb, nseq, cc, 32),
        grid=(2, ch // cc),
        in_specs=head + [big, spec] + tables + [big],
        out_specs=[big, big],
        out_shape=[jax.ShapeDtypeStruct(a.shape, bf16)] * 2,
        scratch_shapes=[
            pltpu.VMEM((size, BIG), bf16),
            pltpu.VMEM((size, 2 * BIG), f32),
            pltpu.VMEM((size, 2 * BIG), bf16),
            pltpu.VMEM((size, BIG), f32),
        ],
        compiler_params=params(56),
        cost_estimate=cost(2 * ch * 50e6, 2 * ch * nb * BLK * 8),
    )(tab, seq, a, kh, wave, back, gg)


def ssm_back(k, tab, seq, a, gm, kh, wave, back, gg, y, dg, da):
    nb, nseq, ch, cc, size, _, _, head, tables = ssm_specs(a.shape, seq)
    big = pl.BlockSpec((1, nb, cc, BLK), lambda i: (k, 0, i, 0))
    spec = pl.BlockSpec((1, LAGS, cc, 2 * BIG), lambda i: (k, 0, i, 0))
    out = pl.BlockSpec((1, nb, cc, BLK), lambda i: (0, 0, i, 0))
    out_spec = pl.BlockSpec((1, LAGS, cc, 2 * BIG), lambda i: (0, 0, i, 0))
    tables = [
        pl.BlockSpec((BIG, 2 * BIG), lambda i: (0, 0)),
        pl.BlockSpec((2 * BIG, BIG), lambda i: (0, 0)),
    ]
    return pl.pallas_call(
        partial(back_body, nb, nseq, cc, 64, k == 1),
        grid=(ch // cc,),
        in_specs=head + [big, big, spec] + tables + [big] * 4,
        out_specs=[out, out, out_spec, pl.BlockSpec((1, cc, 2 * BLK), lambda i: (0, i, 0))],
        out_shape=[jax.ShapeDtypeStruct((1,) + a.shape[1:], bf16)] * 2
        + [
            jax.ShapeDtypeStruct((1, LAGS, ch, 2 * BIG), f32),
            jax.ShapeDtypeStruct((1, ch, 2 * BLK), f32),
        ],
        scratch_shapes=[
            pltpu.VMEM((size, BIG), bf16),
            pltpu.VMEM((size, 2 * BIG), f32),
            pltpu.VMEM((size, 2 * BIG), f32),
            pltpu.VMEM((size, 2 * BIG), bf16),
            pltpu.VMEM((size, BIG), f32),
        ],
        compiler_params=params(60),
        cost_estimate=cost(ch * 80e6, ch * nb * BLK * 16),
    )(tab, seq, a, gm, kh, wave, back, gg, y, dg, da)


def stack_pair(refs):
    return jnp.concatenate(
        [jnp.concatenate([ref[k, 0], ref[k, 1]], axis=1) for ref in refs for k in range(ref.shape[0])], axis=0
    )


def mul_body(count, more, start_ref, w_ref, *refs):
    out = nn(w_ref[...], stack_pair(refs[:count]))
    o_ref = refs[-1]
    for h in range(2):
        part = out[:, h * BLK : (h + 1) * BLK]
        if more:
            part = part + refs[count][h].astype(f32)
        o_ref[h] = part.astype(o_ref.dtype)


def mul_rows(w, arrays, start, many, dtype=bf16, extra=None):
    width, deep = w.shape
    ch = arrays[0].shape[2]
    count = len(arrays)
    out = pl.BlockSpec((2, width, BLK), lambda i, at: (i, 0, 0))
    return pl.pallas_call(
        partial(mul_body, count, extra is not None),
        grid_spec=pltpu.PrefetchScalarGridSpec(
            num_scalar_prefetch=1,
            grid=(many // 2,),
            in_specs=[pl.BlockSpec((width, deep), lambda i, at: (0, 0))]
            + [pl.BlockSpec((x.shape[0], 2, ch, BLK), lambda i, at: (0, at[0] + i, 0, 0)) for x in arrays]
            + ([] if extra is None else [out]),
            out_specs=out,
        ),
        out_shape=jax.ShapeDtypeStruct((many, width, BLK), dtype),
        compiler_params=params(40),
        cost_estimate=cost(2 * many * BLK * width * deep, 2 * many * BLK * (2 * width + deep)),
    )(start // 2, w, *arrays, *([] if extra is None else [extra]))


def outer_body(ch, many, cuts, parts, at_ref, *refs):
    step = pl.program_id(0)
    xs, gs = refs[:parts], refs[parts : 2 * parts]
    gp_refs, gpg_refs, mix_ref = refs[2 * parts : 2 * parts + 2], refs[2 * parts + 2 : 2 * parts + 4], refs[2 * parts + 4]
    outs = refs[2 * parts + 5 : 2 * parts + 5 + cuts]
    acc_s, x_s, g_s = refs[-3:]

    def fill(at):
        for b in range(many):
            x_s[:, b * BLK : (b + 1) * BLK] = xs[at][b]
            g_s[:, b * BLK : (b + 1) * BLK] = gs[at][b]

    if parts == 1:
        fill(0)
    else:
        for at in range(parts):

            @pl.when(step == at)
            def _(at=at):
                fill(at)

    def part(ref, k):
        return jnp.concatenate([ref[k, b] for b in range(many)], axis=1)

    @pl.when(step == 0)
    def _():
        acc_s[...] = jnp.zeros_like(acc_s)

    split = 4 * ch
    left = jnp.concatenate([part(ref, 0) for ref in (*gp_refs, *gpg_refs)], axis=0)
    acc_s[:, :split] += nt(x_s[...], left)
    acc_s[:, split:] += nt(g_s[...], jnp.concatenate([part(mix_ref, 0), part(mix_ref, 1)], axis=0))

    @pl.when(step == pl.num_programs(0) - 1)
    def _():
        deep = acc_s.shape[0] // cuts
        for cut in range(cuts):
            start = pl.multiple_of(at_ref[pl.num_programs(0) + cut] * deep, 8)
            outs[cut][...] = acc_s[pl.ds(start, deep), :].astype(bf16)


def outer_sums(order, cuts, xs, gs, gp, gpg, mix):
    width = xs[0].shape[1]
    _, nb, ch, _ = mix.shape
    many = 8
    parts = len(xs)
    if parts == 1:
        rows = pl.BlockSpec((many, width, BLK), lambda i, at: (i, 0, 0))
    else:
        rows = pl.BlockSpec((many, width, BLK), lambda i, at: (0, 0, 0), pipeline_mode=pl.Buffered(1))
    chan = pl.BlockSpec((2, many, ch, BLK), lambda i, at: (0, at[i], 0, 0))
    one = pl.BlockSpec((1, many, ch, BLK), lambda i, at: (0, at[i], 0, 0))
    tok = nb * BLK
    return pl.pallas_call(
        partial(outer_body, ch, many, cuts, parts),
        grid_spec=pltpu.PrefetchScalarGridSpec(
            num_scalar_prefetch=1,
            grid=(nb // many,),
            in_specs=[rows] * (2 * parts) + [one] * 4 + [chan],
            out_specs=[pl.BlockSpec((width // cuts, 6 * ch), lambda i, at: (0, 0))] * cuts,
            scratch_shapes=[
                pltpu.VMEM((width, 6 * ch), f32),
                pltpu.VMEM((width, many * BLK), bf16),
                pltpu.VMEM((width, many * BLK), bf16),
            ],
        ),
        out_shape=[jax.ShapeDtypeStruct((width // cuts, 6 * ch), bf16)] * cuts,
        compiler_params=params(60),
        cost_estimate=cost(12 * tok * width * ch, tok * (4 * width + 12 * ch)),
    )(order, *xs, *gs, *gp, *gpg, mix)


def join_body(parts, split, at_ref, *refs):
    head_ref, tail_ref, head_t_ref, tail_t_ref = refs[parts:]
    deep = refs[0].shape[0]
    for at in range(parts):
        rows = pl.ds(pl.multiple_of(at_ref[at] * deep, 16), deep)
        head_ref[rows, :] = refs[at][:, :split]
        tail_ref[rows, :] = refs[at][:, split:]
    head_t_ref[...] = head_ref[...].T
    tail_t_ref[...] = tail_ref[...].T


def join_weights(order, parts, split):
    count = len(parts)
    deep, wide = parts[0].shape
    rows = deep * count
    vmem = pl.BlockSpec(memory_space=pltpu.VMEM)
    return pl.pallas_call(
        partial(join_body, count, split),
        in_specs=[pl.BlockSpec(memory_space=pltpu.SMEM)] + [vmem] * count,
        out_specs=[vmem] * 4,
        out_shape=[
            jax.ShapeDtypeStruct(shape, bf16)
            for shape in ((rows, split), (rows, wide - split), (split, rows), (wide - split, rows))
        ],
        compiler_params=params(48),
        cost_estimate=cost(0, 6 * rows * wide),
    )(order, *parts)


def meet_body(axes, rank_ref, x_ref, chan_ref, norm_ref, got_ref, call_ref, nall_ref, send_s, *sems):
    xs_sem, xr_sem, cs_sem, cr_sem, ns_sem, nr_sem, own_sem = sems
    q, c, h, w = (lax.axis_index(name) for name in axes)
    rows = x_ref.shape[0]
    piece = rows // 8
    flat = ((2 * q + c) * 2 + h) * 2 + w

    def peer(bits):
        return (q ^ (bits // 8), c ^ (bits // 4 % 2), h ^ (bits // 2 % 2), w ^ (bits % 2))

    barrier = pltpu.get_barrier_semaphore()
    for bits in range(1, 32):
        pl.semaphore_signal(barrier, inc=1, device_id=peer(bits), device_id_type=pl.DeviceIdType.MESH)
    pl.semaphore_wait(barrier, 31)

    def remote(src, dst, send, recv, to):
        return pltpu.make_async_remote_copy(
            src_ref=src, dst_ref=dst, send_sem=send, recv_sem=recv, device_id=to, device_id_type=pl.DeviceIdType.MESH
        )

    nall_ref[flat] = norm_ref[...]

    def norm_copy(bits):
        return remote(norm_ref, nall_ref.at[flat], ns_sem.at[bits], nr_sem.at[bits], peer(bits))

    for bits in range(1, 32):
        norm_copy(bits).start()

    place = 2 * (1 - c) + w
    spot_c = 4 * c + 2 * h + w

    def chan_copy(at):
        to = (q ^ at, 1 - q // 2, h, q % 2) if at < 4 else (2 * c + w, 1 - q // 2, 1 - h, q % 2)
        return remote(chan_ref, call_ref.at[spot_c], cs_sem.at[at], cr_sem.at[spot_c], to)

    def own_chan():
        return pltpu.make_async_copy(chan_ref, call_ref.at[spot_c], own_sem.at[1])

    def chan_came(at):
        return remote(chan_ref, call_ref.at[at], cs_sem.at[0], cr_sem.at[at], peer(1))

    far_spot = 4 * (q // 2) + 2 * (1 - h) + q % 2

    def chan_pass(bits):
        return remote(
            call_ref.at[far_spot], call_ref.at[far_spot], cs_sem.at[4 + bits], cr_sem.at[far_spot], (q ^ bits, c, h, w)
        )

    for at in (4, 1, 2, 3, 0):
        if at:
            chan_copy(at).start()
        else:

            @pl.when(place == q)
            def _():
                own_chan().start()

            @pl.when(place != q)
            def _():
                chan_copy(0).start()

    pieces = [(kq, kh) for kh in (1, 0) for kq in (1, 2, 3, 0)]
    spot = lax.broadcasted_iota(jnp.int32, (piece, rows), 0)

    def row_copy(kq, kh):
        at = 2 * kq + kh
        return remote(
            send_s.at[at], got_ref.at[2 * q + c], xs_sem.at[at], xr_sem.at[2 * kq + c], (q ^ kq, 1 - h, h ^ kh, w)
        )

    def own_copy():
        return pltpu.make_async_copy(send_s.at[0], got_ref.at[2 * q + c], own_sem.at[0])

    for kq, kh in pieces:
        chunk = 2 * (q ^ kq) + (h ^ kh)
        pick = jnp.where(spot + chunk * piece == rank_ref[...], 1.0, 0.0).astype(bf16)
        send_s[2 * kq + kh] = nn(pick, x_ref[...]).astype(bf16)
        if (kq, kh) == (0, 0):

            @pl.when(c != h)
            def _():
                own_copy().start()

            @pl.when(c == h)
            def _():
                row_copy(0, 0).start()

        else:
            row_copy(kq, kh).start()

    for bits in range(1, 32):
        norm_copy(bits).wait()
    for at in range(8):

        @pl.when((c != h) & (at == c))
        def _():
            own_copy().wait()

        @pl.when(jnp.logical_not((c != h) & (at == c)))
        def _(at=at):
            remote(send_s.at[at], got_ref.at[at], xs_sem.at[at], xr_sem.at[at], peer(1)).wait_recv()

    chan_came(far_spot).wait_recv()
    for bits in range(1, 4):
        chan_pass(bits).start()
    for at in range(8):

        @pl.when((place == q) & (at == spot_c))
        def _():
            own_chan().wait()

        @pl.when(jnp.logical_not((place == q) & (at == spot_c)) & (at != far_spot))
        def _(at=at):
            chan_came(at).wait_recv()

    for bits in range(1, 4):
        chan_pass(bits).wait_send()
    for kq, kh in pieces:
        if (kq, kh) == (0, 0):

            @pl.when(c == h)
            def _():
                row_copy(0, 0).wait_send()

        else:
            row_copy(kq, kh).wait_send()
    for at in range(1, 5):
        chan_copy(at).wait_send()

    @pl.when(place != q)
    def _():
        chan_copy(0).wait_send()


def meet(axes, rank, x, chan, norm):
    rows, width = x.shape
    vmem = pl.BlockSpec(memory_space=pltpu.VMEM)
    sem = pltpu.SemaphoreType.DMA
    return pl.pallas_call(
        partial(meet_body, axes),
        in_specs=[vmem] * 4,
        out_specs=[vmem] * 3,
        out_shape=[
            jax.ShapeDtypeStruct((8, rows // 8, width), bf16),
            jax.ShapeDtypeStruct((8,) + chan.shape, f32),
            jax.ShapeDtypeStruct((32,) + norm.shape, f32),
        ],
        scratch_shapes=[pltpu.VMEM((8, rows // 8, width), bf16)]
        + [sem((8,)), sem((8,)), sem((8,)), sem((8,)), sem((32,)), sem((32,)), sem((2,))],
        compiler_params=pltpu.CompilerParams(collective_id=1, has_side_effects=True, vmem_limit_bytes=60 * MIB),
        cost_estimate=cost(2 * rows * rows * width, 100 * rows * width),
    )(rank.reshape(1, rows), x, chan, norm)


def sequence_tables(lens, nb):
    nseq = lens.shape[0]
    blocks = (lens + BLK - 1) // BLK
    start = jnp.cumsum(blocks) - blocks
    bigs = (blocks + 1) // 2
    first_big = jnp.cumsum(bigs) - bigs
    h = jnp.arange((nb + nseq) // 2, dtype=jnp.int32)
    owner = (h[:, None] >= first_big[None, :]).astype(jnp.int32).sum(axis=1) - 1
    mine = owner[:, None] == jnp.arange(nseq, dtype=jnp.int32)[None, :]

    def at_owner(values):
        return jnp.sum(jnp.where(mine, values[None, :], 0), axis=1)

    rel = h - at_owner(first_big)
    first = jnp.minimum(at_owner(start) + 2 * rel, nb - 1)
    whole = (2 * rel + 1 < at_owner(blocks)).astype(jnp.int32)
    tab = jnp.stack([first, whole]).astype(jnp.int32)
    seq = jnp.stack(
        [jnp.append(first_big, jnp.sum(blocks)), jnp.append(bigs, jnp.sum(bigs))]
    ).astype(jnp.int32)
    return tab, seq


def live_rows(lens, rows):
    slot = (lens + BLK - 1) // BLK * BLK
    begin = jnp.cumsum(slot) - slot
    pos = jnp.arange(rows, dtype=jnp.int32)
    inside = (pos[:, None] >= begin[None, :]) & (pos[:, None] < (begin + lens)[None, :])
    return jnp.sum(inside.astype(f32), axis=1)


def after(values):
    return lax.optimization_barrier(values)


def rank_of(keys):
    return jnp.sum((keys[None, :] < keys[:, None]).astype(jnp.int32), axis=1)


class Line:
    def __init__(self, n_dp, n_t):
        self.n_dp, self.n_t = n_dp, n_t
        self.axes = {"dp": n_dp, "tensor": n_t}
        self.both = ("dp", "tensor")
        self.cuts = 1

    def place_of_group(self):
        return lax.axis_index("tensor")

    def gather_first(self, x):
        return [lax.all_gather(x, "tensor", axis=0, tiled=True)]

    def gathered(self, x, early):
        return []

    def gather_last(self, x, got):
        return [(got[0], jnp.zeros((1,), jnp.int32))]

    def scatter_first(self, w, arrays, many):
        return [mul_rows(w, arrays, jnp.zeros((1,), jnp.int32), many * self.n_t)]

    def scatter_send(self, parts):
        return [lax.psum_scatter(parts[0], "tensor", scatter_dimension=0, tiled=True)]

    def scatter_own(self, w, arrays, many):
        return []

    def regroup(self, x):
        return x

    def ungroup(self, x):
        return x

    def spread(self, x):
        return lax.all_to_all(x, "dp", split_axis=0, concat_axis=0, tiled=True)

    def order(self, pieces):
        return jnp.append(jnp.arange(pieces * self.n_t, dtype=jnp.int32), 0)

    def enter(self, rank, x, chan, norm):
        (sent,) = permute_to(rank, [x])
        return (self.spread(sent),) + self.gather_channels(chan, norm)

    def weights_first(self, pack):
        return [pack]

    def weights_send(self, packs):
        return [lax.all_gather(packs[0], "dp", axis=0, tiled=True)]

    def gather_channels(self, chan, norm):
        perm = [(f, (f % self.n_dp) * self.n_t + f // self.n_dp) for f in range(self.n_dp * self.n_t)]
        chan = lax.ppermute(chan, self.both, perm)
        norm = lax.all_gather(norm, self.both, axis=1, tiled=True)
        return lax.all_gather(chan[None], "dp", axis=0, tiled=True), norm

    def cut_order(self):
        return jnp.zeros((1,), jnp.int32)

    def grads_send(self, gw):
        return [lax.psum_scatter(gw[0], "dp", scatter_dimension=0, tiled=True)]

    def grads_last(self, parts):
        return parts[0], lambda part: part.astype(f32)

    def scatter_small(self, sums, norm):
        sums = lax.psum_scatter(sums, "dp", scatter_dimension=0, tiled=True)
        norm = lax.psum_scatter(norm, self.both, scatter_dimension=1, tiled=True)
        perm = [((f % self.n_dp) * self.n_t + f // self.n_dp, f) for f in range(self.n_dp * self.n_t)]
        return (sums, norm), lambda part: (lax.ppermute(part[0], self.both, perm), part[1])


class Pairs:
    def __init__(self, n_dp, n_t):
        self.quads = n_dp // 2
        self.axes = {"q": self.quads, "c": 2, "h": 2, "w": 2}
        self.both = ("q", "c", "h", "w")
        self.cuts = self.quads
        self.other = [(0, 1), (1, 0)]
        self.there = [(2 * c + h, 2 * (1 - h) + c) for c in range(2) for h in range(2)]
        self.back = [(b, a) for a, b in self.there]
        self.turned = [(2 * c + h, 2 * (1 - h) + 1 - c) for c in range(2) for h in range(2)]

    def flip(self, x, axis, bit=1):
        return lax.ppermute(x, axis, [(i, i ^ bit) for i in range(self.axes[axis])])

    def place_of_group(self):
        return 2 * (1 - lax.axis_index("c")) + lax.axis_index("w")

    def regroup(self, x):
        return lax.ppermute(x, ("c", "h"), self.there)

    def ungroup(self, x):
        return lax.ppermute(x, ("c", "h"), self.back)

    def spread(self, x):
        return lax.all_to_all(x, ("q", "c"), split_axis=0, concat_axis=0, tiled=True)

    def places(self):
        c, w = lax.axis_index("c"), lax.axis_index("w")
        return [2 * (1 - c) + w, 2 * c + w, 2 * (1 - c) + 1 - w, 2 * c + 1 - w]

    def starts(self, many):
        return [(place * many).astype(jnp.int32).reshape(1) for place in self.places()]

    def gather_first(self, x):
        return [self.flip(x, "c"), self.flip(x, "w")]

    def gathered(self, x, early):
        return list(zip([x] + early, self.starts(x.shape[0])))

    def gather_last(self, x, got):
        beside, near = got
        return list(zip([x, beside, near, self.flip(near, "c")], self.starts(x.shape[0])))

    def scatter_first(self, w, arrays, many):
        _, beside, near, far = self.starts(many)
        first = mul_rows(w, arrays, far, many)
        give = self.flip(first, "c")
        beside, first = after((beside, first))
        second = mul_rows(w, arrays, beside, many)
        second, give = after((second, give))
        return [second, mul_rows(w, arrays, near, many, extra=give)]

    def scatter_send(self, parts):
        return [self.flip(parts[0], "c"), self.flip(parts[1], "w")]

    def scatter_own(self, w, arrays, many):
        return [mul_rows(w, arrays, self.starts(many)[0], many, dtype=f32)]

    def order(self, pieces):
        place = jnp.stack(self.places())[:, None] * pieces + jnp.arange(pieces)[None, :]
        return jnp.concatenate([place.reshape(-1).astype(jnp.int32), self.cut_order()])

    def steps(self):
        bit = self.quads // 2
        while bit:
            yield "q", bit
            bit //= 2
        yield "h", 1

    def spot(self):
        return 2 * lax.axis_index("q") + lax.axis_index("h")

    def enter(self, rank, x, chan, norm):
        small = norm.shape[1]
        norm = jnp.pad(norm, ((0, 5), (0, BLK - small)))
        got, chan, norm = meet(self.both, rank, x, chan, norm)
        norm = norm[:, :3, :small].transpose(1, 0, 2).reshape(3, -1)
        return got.reshape(x.shape), chan, norm

    def weights_first(self, pack):
        return [self.regroup(pack), lax.ppermute(pack, ("c", "h"), self.turned)]

    def weights_send(self, packs):
        h = lax.axis_index("h")
        first, second = packs
        pair = jnp.concatenate([jnp.where(h == 0, first, second), jnp.where(h == 0, second, first)], axis=0)
        return [pair] + [self.flip(pair, "q", bit) for bit in range(1, self.quads)]

    def grads_send(self, gw):
        return [gw[0]] + [self.flip(gw[bit], "q", bit) for bit in range(1, self.quads)]

    def grads_last(self, parts):
        total = parts[0].astype(f32)
        for part in parts[1:]:
            total = total + part.astype(f32)
        total = total.astype(bf16)
        half = total.shape[0] // 2
        h = lax.axis_index("h")
        first = jnp.where(h == 0, total[:half], total[half:])
        second = jnp.where(h == 0, total[half:], total[:half])

        def finish(parts):
            return self.ungroup(parts[0]).astype(f32) + lax.ppermute(parts[1], ("c", "h"), self.turned).astype(f32)

        return (first, second), finish

    def cut_order(self):
        return (lax.axis_index("q") ^ jnp.arange(self.quads)).astype(jnp.int32)

    def scatter_small(self, sums, norm):
        count = 2 * self.quads
        rows, wide = sums.shape[0] // count, sums.shape[1]
        norm = norm.reshape(3, 4 * count, -1).transpose(1, 0, 2)
        small = norm.shape[2]
        norm = jnp.pad(norm, ((0, 0), (0, 5), (0, BLK - small)))
        norm = lax.all_to_all(norm, self.both, split_axis=0, concat_axis=0, tiled=True)
        flat = jnp.pad(sums, ((0, 0), (0, -wide % 8))).reshape(count, -1, BLK)
        near = jnp.arange(self.quads) ^ lax.axis_index("q")
        h = lax.axis_index("h")
        keep, give = jnp.take(flat, 2 * near + h, axis=0), jnp.take(flat, 2 * near + 1 - h, axis=0)

        def finish(parts):
            keep, give, norm = parts
            part = keep + self.flip(give, "h")
            total = None
            for apart in range(self.quads):
                perm = []
                for source in range(4 * count):
                    q, c, h, w = source // 8, source // 4 % 2, source // 2 % 2, source % 2
                    perm.append((source, count * (2 * (1 - c) + w) + 2 * (q ^ apart) + h))
                got = lax.ppermute(part[apart], self.both, perm)
                total = got if total is None else total + got
            return total.reshape(rows, -1)[:, :wide], jnp.sum(norm, axis=0)[:3, :small]

        return (keep, give, norm), finish


def local(
    net, wave, tokens, cotangent, source, target, lengths, ln_gain, ln_bias, w_fwd, b_fwd, w_bwd, b_bwd,
    w_gate, b_gate, w_out, b_out, log_dt, log_rate, ssm_b, ssm_c, ssm_d,
):
    rows, width = tokens.shape
    many = rows // BLK
    n_t = net.n_t
    group = rows * n_t
    nb = group // BLK
    ch = w_fwd.shape[1]
    back = (wave.T / BIG).astype(bf16)
    wave = wave.astype(bf16)

    def lanes(column):
        return jnp.broadcast_to(column[..., None], column.shape + (BLK,))

    def decays(log_dt, log_rate, ssm_b):
        rate = jnp.exp(log_rate)
        ld = -jnp.exp(log_dt)[..., None] * rate
        return rate, ld, (1.0 - jnp.exp(ld)) / rate * ssm_b

    rank = rank_of(target)
    sender = source // group
    place = rank_of(sender * rows + jnp.arange(rows, dtype=jnp.int32))
    pack = jnp.concatenate(
        [w_fwd, w_bwd, w_gate.reshape(-1, 2 * ch), w_out.transpose(2, 0, 1).reshape(-1, 2 * ch)], axis=1
    )
    table = net.regroup(jnp.concatenate([place, lengths[0]]))
    rate, ld, drive = decays(log_dt, log_rate, ssm_b)
    own = b_fwd.shape[0]
    small = jnp.concatenate([ssm_d, b_fwd[None], b_bwd[None], b_gate])
    chan = jnp.concatenate(
        [
            (ld * log2e).reshape(own, 2 * STATE),
            (ssm_c * drive).reshape(own, 2 * STATE),
            jnp.pad(small, ((0, -(2 * own + 6) % 8 + 0), (0, 2 * STATE - own))),
        ]
    )
    norm = jnp.stack([ln_gain, ln_bias, b_out])
    (sent_g,) = permute_to(rank, [cotangent])
    sent_g, tokens = after((sent_g, tokens))
    got_g = net.spread(sent_g)
    got_x, chan_all, norm_all = net.enter(rank, tokens, chan, norm)
    got_x, got_g, chan_all, norm_all, pack, table = after((got_x, got_g, chan_all, norm_all, pack, table))
    packs = net.weights_first(pack)

    place, lens = table[:rows], table[rows:]
    gain = lanes(norm_all[0])
    shift = lanes(norm_all[1])
    small = chan_all[:, 2 * own : 2 * own + 6, :own].transpose(1, 0, 2).reshape(6, ch)

    def pairs(at):
        both = chan_all[:, at : at + own].reshape(-1, 2, own // 2, 2 * STATE)
        return both.transpose(1, 0, 2, 3).reshape(2, ch // 2, 2 * STATE)

    ld_pairs = pairs(0)
    w_pairs = pairs(own)
    skip = lanes(small[0:2])
    live = live_rows(lens, group)
    live_own = lax.dynamic_slice_in_dim(live, net.place_of_group() * rows, rows, 0).reshape(many, 1, BLK)
    live = live.reshape(nb // 2, 1, BIG)
    tab, seq = sequence_tables(lens, nb)

    xt, xd = deal_x(place, got_x, gain, shift)
    x_got = net.gather_first(xt)
    _, ld_pairs, w_pairs, skip, packs = after((xt, ld_pairs, w_pairs, skip, packs))
    w_parts = net.weights_send(packs)
    kh = spectra(ld_pairs, w_pairs, skip, wave)
    w_parts, x_got, kh, norm_all, small, got_g = after((w_parts, x_got, kh, norm_all, small, got_g))
    bias_in = lanes(small[2:6].reshape(-1))
    bias_out = lanes(norm_all[2])
    got_g = net.regroup(got_g)
    w_in, w_back, w_in_t, w_back_t = join_weights(net.cut_order(), w_parts, 4 * ch)
    xs = net.gather_last(xt, x_got)
    kept = None
    for part, start in xs:
        kept = project(part, start, nb, live, w_in_t, bias_in, kept)
    kept, got_g = after((kept, got_g))
    a, da, gg, dg = kept
    gt, gd, g_bias_out = deal_g(place, got_g, live_own)
    gt, a = after((gt, a))
    g_got = net.gather_first(gt)
    y, mix = ssm_scan(tab, seq, a, kh, wave, back, gg)
    g_got, y, mix = after((g_got, y, mix))
    gs = net.gather_last(gt, g_got)
    branch = net.scatter_first(w_back, [mix], many)
    gm = gate_grad(gs, nb, w_back_t)
    branch, gm = after((branch, gm))

    branch = net.scatter_send(branch)
    branch = net.scatter_own(w_back, [mix], many) + branch
    first = ssm_back(0, tab, seq, a, gm, kh, wave, back, gg, y, dg, da)
    branch, first, a = after((branch, first, a))
    sent_out = layer_rows(place, branch, xd, live_own, bias_out)
    sent_out, a = after((sent_out, a))
    sent_out = net.ungroup(sent_out)
    second = ssm_back(1, tab, seq, a, gm, kh, wave, back, gg, y, dg, da)
    sent_out, first, second = after((sent_out, first, second))
    gpg, gp, gh, bsum = zip(first, second)
    sent_out = net.spread(sent_out)
    back_list = [gp[0], gp[1], gpg[0], gpg[1]]
    g_normed = net.scatter_first(w_in, back_list, many)
    g_normed, back_list, mix = after((g_normed, back_list, mix))
    gp, gpg = back_list[:2], back_list[2:]
    g_normed = net.scatter_send(g_normed)
    g_normed = net.scatter_own(w_in, back_list, many) + g_normed
    gw = outer_sums(net.order(many // 8), net.cuts, [part for part, _ in xs], [part for part, _ in gs], gp, gpg, mix)
    g_normed, gw, gh, sent_out = after((g_normed, gw, gh, sent_out))
    sent_in, norm_sums = input_rows(place, g_normed, xd, gd, gain)
    sent_in, gh, gw, norm_sums, sent_out, bsum = after((sent_in, gh, gw, norm_sums, sent_out, bsum))
    sent_in = net.ungroup(sent_in)
    gw = net.grads_send(gw)
    s0, s1, g0 = [jnp.concatenate(part) for part in zip(*[moments(k, ld_pairs, gh[k], back) for k in range(2)])]
    layer_out = permute_from(rank, sent_out)

    s0 = s0.reshape(2, ch, STATE)
    s1 = s1.reshape(2, ch, STATE)
    bsum = jnp.concatenate(bsum)
    gb_gate = jnp.sum(bsum[:, :, :BLK], axis=2)
    gb_in = jnp.sum(bsum[:, :, BLK:], axis=2)
    sums = jnp.concatenate(
        [s0[0], s0[1], s1[0], s1[1], jnp.concatenate([g0[:, :, 0], gb_gate, gb_in], axis=0).T], axis=1
    )
    norm_sums = jnp.sum(jnp.concatenate([norm_sums, g_bias_out[None]], axis=0), axis=2)
    part, finish = net.scatter_small(sums, norm_sums)
    gw, gw_finish = net.grads_last(gw)
    sent_in, gw, part, layer_out = after((sent_in, gw, part, layer_out))
    in_grad = permute_from(rank, net.spread(sent_in))
    gw = gw_finish(gw)
    sums, norm_sums = finish(part)
    s0 = jnp.stack([sums[:, :STATE], sums[:, STATE : 2 * STATE]])
    s1 = jnp.stack([sums[:, 2 * STATE : 3 * STATE], sums[:, 3 * STATE : 4 * STATE]])
    tail = sums[:, 4 * STATE :].T
    step = jnp.exp(log_dt)[..., None]
    g_c = s0 * drive
    g_drive = s0 * ssm_c
    g_b = g_drive * (1.0 - jnp.exp(ld)) / rate
    g_ld = s1 * ssm_c * drive - g_drive * ssm_b / rate * jnp.exp(ld)
    g_rate = -g_drive * drive / rate - g_ld * step
    g_dt = jnp.sum(g_ld * ld, axis=2)
    return (
        layer_out,
        in_grad,
        norm_sums[0],
        norm_sums[1],
        gw[:, :ch],
        tail[4],
        gw[:, ch : 2 * ch],
        tail[5],
        gw[:, 2 * ch : 4 * ch].reshape(-1, 2, ch),
        tail[2:4],
        gw[:, 4 * ch :].T.reshape(2, ch, -1),
        norm_sums[2],
        g_dt,
        g_rate * rate,
        g_b,
        g_c,
        tail[0:2],
    )


def solution(mesh):
    n_dp, n_t = mesh.shape["dp"], mesh.shape["tensor"]
    if n_t == 4 and n_dp == 8:
        net = Pairs(n_dp, n_t)
        dp, tensor = ("q", "c"), ("h", "w")
    else:
        net = Line(n_dp, n_t)
        dp, tensor = ("dp",), ("tensor",)
    net.n_t = n_t
    mesh = jax.sharding.Mesh(mesh.devices.reshape(tuple(net.axes.values())), tuple(net.axes))
    both = P(dp + tensor)
    rows = P(dp + tensor, None)
    pair = P(None, dp + tensor)
    state = P(None, dp + tensor, None)
    proj = P(dp, tensor)
    gate = P(dp, None, tensor)
    out = P(None, tensor, dp)
    wave = wave_table()

    def run(*args):
        return local(net, jnp.asarray(wave), *args)

    return jax.shard_map(
        run,
        mesh=mesh,
        in_specs=(
            rows, rows, both, both, P(dp, None), both, both, proj, both, proj, both, gate, pair, out, both,
            pair, state, state, state, pair,
        ),
        out_specs=(
            rows, rows, both, both, proj, both, proj, both, gate, pair, out, both, pair, state, state, state, pair,
        ),
        check_vma=False,
    )
```

```python
from functools import partial

import jax
import jax.numpy as jnp
import numpy as np
from jax import lax
from jax.experimental import pallas as pl
from jax.experimental.pallas import tpu as pltpu
from jax.sharding import PartitionSpec as P

BLK = 128
BIG = 256
MOST = 2048
LAGS = MOST // BIG
STATE = 64
epsilon = 1e-05
log2e = 1.4426950408889634
f32 = jnp.float32
bf16 = jnp.bfloat16
MIB = 2**20


def nn(a, b):
    return lax.dot_general(a, b, (((1,), (0,)), ((), ())), preferred_element_type=f32)


def nt(a, b):
    return lax.dot_general(a, b, (((1,), (1,)), ((), ())), preferred_element_type=f32)


def params(limit):
    return pltpu.CompilerParams(vmem_limit_bytes=60 * MIB)


def cost(flops, moved, trans=0):
    scale = 0.05
    return pl.CostEstimate(
        flops=int(scale * flops), bytes_accessed=int(scale * moved), transcendentals=int(scale * trans)
    )


def halves(x):
    high = x.astype(bf16)
    return high, (x - high.astype(f32)).astype(bf16)


def wave_table():
    pos = np.arange(BIG)[:, None]
    freq = np.arange(BIG)[None, :]
    angle = 2 * np.pi * ((2 * freq + 1) * pos % (4 * BIG)) / (4 * BIG)
    return np.concatenate([np.cos(angle), np.sin(angle)], 1).astype(np.float32)


def chunk_of(channels, most):
    best = 16
    for size in range(16, most + 1, 16):
        if channels % size == 0:
            best = size
    return best


def permute_row_body(count, rank_ref, *refs):
    rows = rank_ref.shape[1]
    spot = lax.broadcasted_iota(jnp.int32, (rows, rows), 0)
    pick = jnp.where(spot == rank_ref[...], 1.0, 0.0).astype(bf16)
    for at in range(count):
        refs[count + at][...] = nn(pick, refs[at][...]).astype(bf16)


def permute_to(rank, arrays):
    rows, width = arrays[0].shape
    count = len(arrays)
    return pl.pallas_call(
        partial(permute_row_body, count),
        out_shape=[jax.ShapeDtypeStruct((rows, width), bf16)] * count,
        compiler_params=params(48),
        cost_estimate=cost(2 * count * rows * rows * width, 4 * count * rows * width),
    )(rank.reshape(1, rows), *arrays)


def permute_col_body(rank_ref, x_ref, o_ref):
    rows = x_ref.shape[0]
    spot = lax.broadcasted_iota(jnp.int32, (rows, rows), 1)
    pick = jnp.where(spot == rank_ref[...], 1.0, 0.0).astype(bf16)
    o_ref[...] = nn(pick, x_ref[...]).astype(bf16)


def permute_from(rank, x):
    rows, width = x.shape
    return pl.pallas_call(
        permute_col_body,
        out_shape=jax.ShapeDtypeStruct((rows, width), bf16),
        compiler_params=params(48),
        cost_estimate=cost(2 * rows * rows * width, 4 * rows * width),
    )(rank.reshape(rows, 1), x)


def pick_rows(place_ref, x_ref):
    spot = lax.broadcasted_iota(jnp.int32, (BLK, x_ref.shape[0]), 1)
    pick = jnp.where(spot == place_ref[...], 1.0, 0.0).astype(bf16)
    return nn(pick, x_ref[...]).T


def deal_x_body(place_ref, x_ref, gain_ref, shift_ref, xt_ref, xd_ref):
    x = pick_rows(place_ref, x_ref)
    xd_ref[0] = x.astype(bf16)
    centred = x - jnp.mean(x, axis=0, keepdims=True)
    inv_std = lax.rsqrt(jnp.mean(centred * centred, axis=0, keepdims=True) + epsilon)
    xt_ref[0] = (centred * inv_std * gain_ref[...] + shift_ref[...]).astype(bf16)


def deal_g_body(place_ref, g_ref, live_ref, gt_ref, gd_ref, bo_ref):
    g = pick_rows(place_ref, g_ref)
    gd_ref[0] = g.astype(bf16)
    g = g * live_ref[0]
    gt_ref[0] = g.astype(bf16)

    @pl.when(pl.program_id(0) == 0)
    def _():
        bo_ref[...] = jnp.zeros_like(bo_ref)

    bo_ref[...] += g


def deal_specs(rows, width):
    place = pl.BlockSpec((BLK, 1), lambda i: (i, 0))
    whole = pl.BlockSpec((rows, width), lambda i: (0, 0))
    wide = pl.BlockSpec((width, BLK), lambda i: (0, 0))
    out = pl.BlockSpec((1, width, BLK), lambda i: (i, 0, 0))
    return place, whole, wide, out


def deal_x(place, x, gain, shift):
    rows, width = x.shape
    blocks = rows // BLK
    spot, whole, wide, out = deal_specs(rows, width)
    return pl.pallas_call(
        deal_x_body,
        grid=(blocks,),
        in_specs=[spot, whole, wide, wide],
        out_specs=[out, out],
        out_shape=[jax.ShapeDtypeStruct((blocks, width, BLK), bf16)] * 2,
        compiler_params=params(40),
        cost_estimate=cost(2 * rows * rows * width, 6 * rows * width),
    )(place.reshape(rows, 1), x, gain, shift)


def deal_g(place, g, live):
    rows, width = g.shape
    blocks = rows // BLK
    spot, whole, wide, out = deal_specs(rows, width)
    return pl.pallas_call(
        deal_g_body,
        grid=(blocks,),
        in_specs=[spot, whole, pl.BlockSpec((1, 1, BLK), lambda i: (i, 0, 0))],
        out_specs=[out, out, wide],
        out_shape=[jax.ShapeDtypeStruct((blocks, width, BLK), bf16)] * 2
        + [jax.ShapeDtypeStruct((width, BLK), f32)],
        compiler_params=params(40),
        cost_estimate=cost(2 * rows * rows * width, 6 * rows * width),
    )(place.reshape(rows, 1), g, live)


def send_back(place_ref, out_s, o_ref):
    rows = out_s.shape[0]
    spot = lax.broadcasted_iota(jnp.int32, (rows, rows), 0)
    pick = jnp.where(spot == place_ref[...], 1.0, 0.0).astype(bf16)
    o_ref[...] = nn(pick, out_s[...]).astype(bf16)


def total(refs, at):
    value = refs[0][at].astype(f32)
    for ref in refs[1:]:
        value = value + ref[at].astype(f32)
    return value


def layer_body(place_ref, xd_ref, live_ref, bias_ref, *refs):
    o_ref, out_s = refs[-2:]
    for at in range(xd_ref.shape[0]):
        y = xd_ref[at].astype(f32) + live_ref[at] * (total(refs[:-2], at) + bias_ref[...])
        out_s[at * BLK : (at + 1) * BLK, :] = y.T.astype(bf16)
    send_back(place_ref, out_s, o_ref)


def layer_rows(place, parts, xd, live, bias):
    blocks, width, _ = xd.shape
    rows = blocks * BLK
    return pl.pallas_call(
        layer_body,
        out_shape=jax.ShapeDtypeStruct((rows, width), bf16),
        scratch_shapes=[pltpu.VMEM((rows, width), bf16)],
        compiler_params=params(48),
        cost_estimate=cost(2 * rows * rows * width, 6 * rows * width),
    )(place.reshape(1, rows), xd, live, bias, *parts)


def input_body(place_ref, xd_ref, gd_ref, gain_ref, *refs):
    o_ref, sums_ref, out_s = refs[-3:]
    g_gain = jnp.zeros(gain_ref.shape, f32)
    g_shift = jnp.zeros(gain_ref.shape, f32)
    for at in range(xd_ref.shape[0]):
        x = xd_ref[at].astype(f32)
        centred = x - jnp.mean(x, axis=0, keepdims=True)
        inv_std = lax.rsqrt(jnp.mean(centred * centred, axis=0, keepdims=True) + epsilon)
        x_hat = centred * inv_std
        g = total(refs[:-3], at)
        g_gain = g_gain + g * x_hat
        g_shift = g_shift + g
        hat = g * gain_ref[...]
        back = inv_std * (
            hat
            - jnp.mean(hat, axis=0, keepdims=True)
            - x_hat * jnp.mean(hat * x_hat, axis=0, keepdims=True)
        )
        out_s[at * BLK : (at + 1) * BLK, :] = (gd_ref[at].astype(f32) + back).T.astype(bf16)
    sums_ref[0] = g_gain
    sums_ref[1] = g_shift
    send_back(place_ref, out_s, o_ref)


def input_rows(place, parts, xd, gd, gain):
    blocks, width, _ = xd.shape
    rows = blocks * BLK
    return pl.pallas_call(
        input_body,
        out_shape=[
            jax.ShapeDtypeStruct((rows, width), bf16),
            jax.ShapeDtypeStruct((2, width, BLK), f32),
        ],
        scratch_shapes=[pltpu.VMEM((rows, width), bf16)],
        compiler_params=params(48),
        cost_estimate=cost(2 * rows * rows * width, 8 * rows * width),
    )(place.reshape(1, rows), xd, gd, gain, *parts)


def project_body(ch, many, start_ref, x_ref, live_ref, wt_ref, bias_ref, *refs):
    a_ref, da_ref, gg_ref, dg_ref = refs[-4:]
    x = jnp.concatenate([x_ref[0], x_ref[1]], axis=1)
    live = live_ref[0]
    root = 0.7978845608028654
    step = 64 if ch % 128 else 128

    def act(pre):
        square = pre * pre
        rise = 0.5 + 0.5 * jnp.tanh(pre * (root + (0.044715 * root) * square))
        value = pre * rise
        slope = rise + rise * (pre - value) * (2.0 * root + (6.0 * 0.044715 * root) * square)
        return value, slope

    def put(ref, k, at, value):
        value = value.astype(bf16)
        ref[k, 0, at, :] = value[:, :BLK]
        ref[k, 1, at, :] = value[:, BLK:]

    for k in range(2):
        for first, value_ref, slope_ref in ((k * ch, a_ref, da_ref), ((2 + k) * ch, gg_ref, dg_ref)):
            for at in range(0, ch, step):
                rows = pl.ds(first + at, step)
                bias = bias_ref[rows, :]
                pre = nn(wt_ref[rows, :], x) + jnp.concatenate([bias, bias], axis=1)
                value, slope = act(pre)
                if value_ref is a_ref:
                    value, slope = live * value, live * slope
                put(value_ref, k, pl.ds(at, step), value)
                put(slope_ref, k, pl.ds(at, step), slope)


def chained(body, grid, in_specs, out_specs, shapes, scratch, limit, estimate, start, operands, kept):
    kept = [] if kept is None else list(kept)
    specs = list(in_specs) + [pl.BlockSpec(memory_space=pl.ANY)] * len(kept)
    first = 1 + len(operands)
    return pl.pallas_call(
        body,
        grid_spec=pltpu.PrefetchScalarGridSpec(
            num_scalar_prefetch=1, grid=grid, in_specs=specs, out_specs=out_specs, scratch_shapes=scratch
        ),
        out_shape=shapes,
        input_output_aliases={first + at: at for at in range(len(kept))},
        compiler_params=params(limit),
        cost_estimate=estimate,
    )(start, *operands, *kept)


def project(xt, start, nb, live, wt, bias, kept):
    many, width, _ = xt.shape
    ch = wt.shape[0] // 4
    out = pl.BlockSpec((2, 2, ch, BLK), lambda i, at: (0, at[0] + i, 0, 0))
    tok = many * BLK
    return chained(
        partial(project_body, ch, many),
        (many // 2,),
        [
            pl.BlockSpec((2, width, BLK), lambda i, at: (i, 0, 0)),
            pl.BlockSpec((1, 1, BIG), lambda i, at: (at[0] + i, 0, 0)),
            pl.BlockSpec((4 * ch, width), lambda i, at: (0, 0)),
            pl.BlockSpec((4 * ch, BLK), lambda i, at: (0, 0)),
        ],
        [out] * 4,
        [jax.ShapeDtypeStruct((2, nb, ch, BLK), bf16)] * 4,
        [],
        48,
        cost(8 * tok * width * ch, 2 * tok * width + 16 * tok * ch, 4 * tok * ch),
        start // 2,
        [xt, live, wt, bias],
        kept,
    )


def gate_grad_body(ch, parts, at_ref, *refs):
    wt_ref, o_ref, g_s = refs[parts:]
    steps = pl.num_programs(0) // parts
    many = refs[0].shape[0]

    for part in range(parts):

        @pl.when(pl.program_id(0) // steps == part)
        def _(part=part):
            for h in range(many):
                g_s[:, h * BLK : (h + 1) * BLK] = refs[part][h]

    for k in range(2):
        gm = nn(wt_ref[k * ch : (k + 1) * ch, :], g_s[...]).astype(bf16)
        for h in range(many):
            o_ref[k, h] = gm[:, h * BLK : (h + 1) * BLK]


def gate_grad(gs, nb, wt):
    parts = len(gs)
    rows_in, width, _ = gs[0][0].shape
    many = 4
    steps = rows_in // many
    ch = wt.shape[0] // 2
    tok = nb * BLK

    def rows(part):
        return pl.BlockSpec((many, width, BLK), lambda i, at: (jnp.clip(i - part * steps, 0, steps - 1), 0, 0))

    order = jnp.concatenate([start // many for _, start in gs]).astype(jnp.int32)
    return pl.pallas_call(
        partial(gate_grad_body, ch, parts),
        grid_spec=pltpu.PrefetchScalarGridSpec(
            num_scalar_prefetch=1,
            grid=(parts * steps,),
            in_specs=[rows(part) for part in range(parts)] + [pl.BlockSpec((2 * ch, width), lambda i, at: (0, 0))],
            out_specs=pl.BlockSpec((2, many, ch, BLK), lambda i, at: (0, at[i // steps] + i % steps, 0, 0)),
            scratch_shapes=[pltpu.VMEM((width, many * BLK), bf16)],
        ),
        out_shape=jax.ShapeDtypeStruct((2, nb, ch, BLK), bf16),
        compiler_params=params(40),
        cost_estimate=cost(4 * tok * width * ch, 2 * tok * width + 4 * tok * ch),
    )(order, *[part for part, _ in gs], wt)


def spectra_body(cc, ld_ref, w_ref, d_ref, wave_ref, kh_ref, k_s):
    t = lax.broadcasted_iota(jnp.int32, (BLK, BLK), 0).astype(f32)
    block = lax.broadcasted_iota(jnp.int32, (2 * LAGS, BLK), 0).astype(f32) * float(BLK)
    low = lax.broadcasted_iota(jnp.int32, (2 * LAGS, BLK), 1) < STATE
    count = 2 * LAGS

    def one(p, carry):
        ld = ld_ref[0, pl.ds(p, 1), :]
        decay = jnp.exp2(t * ld)
        scale = w_ref[0, pl.ds(p, 1), :] * jnp.exp2(block * ld)
        lhs = jnp.concatenate([jnp.where(low, scale, 0.0), jnp.where(low, 0.0, scale)], axis=0)
        lhs_high, lhs_low = halves(lhs)
        k = nt(jnp.concatenate([lhs_high, lhs_low], axis=0), decay.astype(bf16))
        k = k[0 : 2 * count] + k[2 * count : 4 * count]
        k_s[pl.ds(2 * p, count, stride=cc), :] = k[0:count]
        k_s[pl.ds(2 * p + 1, count, stride=cc), :] = k[count : 2 * count]
        return carry

    lax.fori_loop(0, cc // 2, one, 0, unroll=16)
    sign = jnp.where(lax.broadcasted_iota(jnp.int32, (cc, BIG), 1) % 2 == 0, 1.0, -1.0)
    before = None
    for big in range(LAGS):
        rows = jnp.concatenate(
            [k_s[pl.ds(2 * big * cc, cc), :], k_s[pl.ds((2 * big + 1) * cc, cc), :]], axis=1
        )
        high, rest = halves(rows)
        x = nn(high, wave_ref[...]) + nn(rest, wave_ref[...])
        xc, xs = x[:, :BIG], x[:, BIG:]
        if big == 0:
            kh_ref[0, 0, :, :BIG] = xc + d_ref[0][:, 0:1]
            kh_ref[0, 0, :, BIG:] = xs
        else:
            kh_ref[0, big, :, :BIG] = xc + sign * before[1]
            kh_ref[0, big, :, BIG:] = xs - sign * before[0]
        before = (xc, xs)


def spectra(ld, w, d, wave):
    ch = 2 * ld.shape[1]
    cc = chunk_of(ch, 128)
    return pl.pallas_call(
        partial(spectra_body, cc),
        grid=(2, ch // cc),
        in_specs=[pl.BlockSpec((1, cc // 2, BLK), lambda k, i: (k, i, 0))] * 2
        + [
            pl.BlockSpec((1, cc, BLK), lambda k, i: (k, i, 0)),
            pl.BlockSpec((BIG, 2 * BIG), lambda k, i: (0, 0)),
        ],
        out_specs=pl.BlockSpec((1, LAGS, cc, 2 * BIG), lambda k, i: (k, 0, i, 0)),
        out_shape=jax.ShapeDtypeStruct((2, LAGS, ch, 2 * BIG), f32),
        scratch_shapes=[pltpu.VMEM((2 * LAGS * cc, BLK), f32)],
        compiler_params=params(40),
        cost_estimate=cost(2 * ch * 40e6, 2 * ch * LAGS * 2 * BIG * 4),
    )(ld, w, d, wave)


def moments_body(cc, ld_ref, gh_ref, back_ref, s0_ref, s1_ref, g0_ref, g_s):
    sign = jnp.where(lax.broadcasted_iota(jnp.int32, (cc, BIG), 1) % 2 == 0, 1.0, -1.0)
    count = 2 * LAGS
    for big in range(LAGS):
        c = gh_ref[0, big, :, :BIG]
        s = gh_ref[0, big, :, BIG:]
        if big < LAGS - 1:
            c, s = c - sign * gh_ref[0, big + 1, :, BIG:], s + sign * gh_ref[0, big + 1, :, :BIG]
        high, rest = halves(jnp.concatenate([c, s], axis=1))
        g = nn(high, back_ref[...]) + nn(rest, back_ref[...])
        g_s[pl.ds(2 * big * cc, cc), :] = g[:, :BLK]
        g_s[pl.ds((2 * big + 1) * cc, cc), :] = g[:, BLK:]
        if big == 0:
            g0_ref[0] = g[:, :BLK]
    t = lax.broadcasted_iota(jnp.int32, (BLK, BLK), 0).astype(f32)
    lane = lax.broadcasted_iota(jnp.int32, (count, BLK), 1)
    lag = lane.astype(f32)
    block = lax.broadcasted_iota(jnp.int32, (count, BLK), 0).astype(f32) * float(BLK)
    low = lane < STATE

    def one(p, carry):
        ld = ld_ref[0, pl.ds(p, 1), :]
        decay = jnp.exp2(t * ld).astype(bf16)
        far = jnp.exp2(block * ld)
        ga = g_s[pl.ds(2 * p, count, stride=cc), :]
        gb = g_s[pl.ds(2 * p + 1, count, stride=cc), :]
        high, rest = halves(jnp.concatenate([ga, gb, ga * lag, gb * lag], axis=0))
        m = nn(jnp.concatenate([high, rest], axis=0), decay)
        m = m[0 : 4 * count] + m[4 * count : 8 * count]
        m0 = jnp.where(low, m[0:count], m[count : 2 * count])
        m1 = jnp.where(low, m[2 * count : 3 * count], m[3 * count : 4 * count]) + block * m0
        s0_ref[0, pl.ds(p, 1), :] = jnp.sum(far * m0, axis=0, keepdims=True)
        s1_ref[0, pl.ds(p, 1), :] = jnp.sum(far * m1, axis=0, keepdims=True)
        return carry

    lax.fori_loop(0, cc // 2, one, 0, unroll=16)


def moments(k, ld, gh, back):
    ch = gh.shape[2]
    cc = chunk_of(ch, 128)
    row = pl.BlockSpec((1, cc // 2, BLK), lambda i: (0, i, 0))
    return pl.pallas_call(
        partial(moments_body, cc),
        grid=(ch // cc,),
        in_specs=[
            pl.BlockSpec((1, cc // 2, BLK), lambda i: (k, i, 0)),
            pl.BlockSpec((1, LAGS, cc, 2 * BIG), lambda i: (0, 0, i, 0)),
            pl.BlockSpec((2 * BIG, BIG), lambda i: (0, 0)),
        ],
        out_specs=[row, row, pl.BlockSpec((1, cc, BLK), lambda i: (0, i, 0))],
        out_shape=[jax.ShapeDtypeStruct((1, ch // 2, BLK), f32)] * 2
        + [jax.ShapeDtypeStruct((1, ch, BLK), f32)],
        scratch_shapes=[pltpu.VMEM((2 * LAGS * cc, BLK), f32)],
        compiler_params=params(40),
        cost_estimate=cost(ch * 40e6, ch * LAGS * 2 * BIG * 4),
    )(ld, gh, back)


def load_pieces(nb, pieces, cc, tab_ref, block, in_s, wave_ref, dst):
    for h in range(pieces):
        first = tab_ref[0, h]
        whole = tab_ref[1, h].astype(f32)
        in_s[pl.ds(h * cc, cc), 0:BLK] = block(first).astype(bf16)
        in_s[pl.ds(h * cc, cc), BLK:BIG] = (block(jnp.minimum(first + 1, nb - 1)) * whole).astype(bf16)
    for h in range(pieces):
        at = pl.ds(h * cc, cc)
        dst[at, :] = nn(in_s[at, :], wave_ref[...])


def over_pieces(nseq, cc, rg, seq_ref, piece):
    def group(r, carry):
        off = pl.multiple_of(r * rg, rg)
        for s in range(nseq):
            base = seq_ref[0, s]
            count = seq_ref[1, s]

            def outer(i, carry):
                piece(i, count, base, off)
                return carry

            lax.fori_loop(0, count, outer, 0)
        return carry

    lax.fori_loop(0, cc // rg, group, 0)


def scan_body(
    nb, nseq, cc, rg, tab_ref, seq_ref, a_ref, kh_ref, wave_ref, back_ref, gg_ref, y_ref, mix_ref, in_s, ah_s, yh_s, y_s
):
    pieces = (nb + nseq) // 2
    load_pieces(nb, pieces, cc, tab_ref, lambda b: a_ref[0, b].astype(f32), in_s, wave_ref, ah_s)
    zero = jnp.zeros((rg, BIG), f32)

    def products(flip):
        def piece(i, count, base, off):
            def inner(j, acc):
                yc, ys = acc
                other = (base + i + j) if flip else (base + i - j)
                m = pl.ds(pl.multiple_of(other * cc + off, rg), rg)
                rows = pl.ds(off, rg)
                ac = ah_s[m, :BIG]
                as_ = ah_s[m, BIG:]
                kc = kh_ref[0, j, rows, :BIG]
                ks = kh_ref[0, j, rows, BIG:]
                if flip:
                    return (yc + kc * ac + ks * as_, ys + kc * as_ - ks * ac)
                return (yc + kc * ac - ks * as_, ys + kc * as_ + ks * ac)

            yc, ys = lax.fori_loop(0, (count - i) if flip else (i + 1), inner, (zero, zero))
            at = pl.ds(pl.multiple_of((base + i) * cc + off, rg), rg)
            yh_s[at, :BIG] = yc.astype(bf16)
            yh_s[at, BIG:] = ys.astype(bf16)

        over_pieces(nseq, cc, rg, seq_ref, piece)

    @pl.when(pl.program_id(0) == 0)
    def _():
        products(False)

    @pl.when(pl.program_id(0) == 1)
    def _():
        products(True)

    for h in range(pieces):
        at = pl.ds(h * cc, cc)
        y_s[at, :] = nn(yh_s[at, :], back_ref[...])

    def one(b, y):
        y_ref[0, b] = y.astype(bf16)
        mix_ref[0, b] = (y * gg_ref[0, b].astype(f32)).astype(bf16)

    def last(h, carry):
        b = tab_ref[0, h]
        at = pl.ds(pl.multiple_of(h * cc, cc), cc)
        one(b, y_s[at, 0:BLK])

        @pl.when(tab_ref[1, h] == 1)
        def _():
            one(b + 1, y_s[at, BLK:])

        return carry

    lax.fori_loop(0, seq_ref[1, nseq], last, 0)
    nothing = jnp.zeros((cc, BLK), bf16)

    def fill(b, carry):
        y_ref[0, b] = nothing
        mix_ref[0, b] = nothing
        return carry

    lax.fori_loop(seq_ref[0, nseq], nb, fill, 0)


def back_body(
    nb, nseq, cc, rg, flip, tab_ref, seq_ref, a_ref, gm_ref, kh_ref, wave_ref, back_ref, gg_ref, y_ref, dg_ref, da_ref,
    gpg_ref, gp_ref, gh_ref, bs_ref, in_s, ah_s, gh_s, xh_s, x_s,
):
    pieces = (nb + nseq) // 2
    load_pieces(nb, pieces, cc, tab_ref, lambda b: a_ref[0, b].astype(f32), in_s, wave_ref, ah_s)
    load_pieces(
        nb, pieces, cc, tab_ref, lambda b: gm_ref[0, b].astype(f32) * gg_ref[0, b].astype(f32), in_s, wave_ref, gh_s
    )
    gh_ref[...] = jnp.zeros_like(gh_ref)
    zero = jnp.zeros((rg, BIG), f32)

    def piece(i, count, base, off):
        at = pl.ds(pl.multiple_of((base + i) * cc + off, rg), rg)
        ac = ah_s[at, :BIG]
        as_ = ah_s[at, BIG:]

        def inner(j, acc):
            xc, xs = acc
            other = (base + i - j) if flip else (base + i + j)
            m = pl.ds(pl.multiple_of(other * cc + off, rg), rg)
            rows = pl.ds(off, rg)
            gc = gh_s[m, :BIG]
            gs = gh_s[m, BIG:]
            kc = kh_ref[0, j, rows, :BIG]
            ks = kh_ref[0, j, rows, BIG:]
            gh_ref[0, j, rows, :BIG] += ac * gc + as_ * gs
            if flip:
                gh_ref[0, j, rows, BIG:] += gc * as_ - gs * ac
                return (xc + kc * gc - ks * gs, xs + kc * gs + ks * gc)
            gh_ref[0, j, rows, BIG:] += ac * gs - as_ * gc
            return (xc + kc * gc + ks * gs, xs + kc * gs - ks * gc)

        xc, xs = lax.fori_loop(0, (i + 1) if flip else (count - i), inner, (zero, zero))
        xh_s[at, :BIG] = xc.astype(bf16)
        xh_s[at, BIG:] = xs.astype(bf16)

    over_pieces(nseq, cc, rg, seq_ref, piece)

    for h in range(pieces):
        at = pl.ds(h * cc, cc)
        x_s[at, :] = nn(xh_s[at, :], back_ref[...])

    none = jnp.zeros((cc, BLK), f32)

    def one(b, gx, carry):
        s0, s1 = carry
        gpg = (y_ref[0, b].astype(f32) * gm_ref[0, b].astype(f32) * dg_ref[0, b].astype(f32)).astype(bf16)
        gpg_ref[0, b] = gpg
        gp = (gx * da_ref[0, b].astype(f32)).astype(bf16)
        gp_ref[0, b] = gp
        return (s0 + gpg.astype(f32), s1 + gp.astype(f32))

    def last(h, carry):
        b = tab_ref[0, h]
        at = pl.ds(pl.multiple_of(h * cc, cc), cc)
        carry = one(b, x_s[at, 0:BLK], carry)

        def more(kept):
            return one(b + 1, x_s[at, BLK:], kept)

        return lax.cond(tab_ref[1, h] == 1, more, lambda kept: kept, carry)

    s0, s1 = lax.fori_loop(0, seq_ref[1, nseq], last, (none, none))
    bs_ref[0, :, 0:BLK] = s0
    bs_ref[0, :, BLK:] = s1
    nothing = jnp.zeros((cc, BLK), bf16)

    def fill(b, carry):
        gpg_ref[0, b] = nothing
        gp_ref[0, b] = nothing
        return carry

    lax.fori_loop(seq_ref[0, nseq], nb, fill, 0)


def ssm_specs(shape, seq):
    _, nb, ch, _ = shape
    nseq = seq.shape[1] - 1
    pieces = (nb + nseq) // 2
    cc = chunk_of(ch, 128 if nb <= 32 else 64)
    big = pl.BlockSpec((1, nb, cc, BLK), lambda k, i: (k, 0, i, 0))
    spec = pl.BlockSpec((1, LAGS, cc, 2 * BIG), lambda k, i: (k, 0, i, 0))
    smem = pl.BlockSpec(memory_space=pltpu.SMEM)
    head = [smem, smem]
    tables = [pl.BlockSpec((BIG, 2 * BIG), lambda k, i: (0, 0)), pl.BlockSpec((2 * BIG, BIG), lambda k, i: (0, 0))]
    return nb, nseq, ch, cc, pieces * cc, big, spec, head, tables


def ssm_scan(tab, seq, a, kh, wave, back, gg):
    nb, nseq, ch, cc, size, big, spec, head, tables = ssm_specs(a.shape, seq)
    return pl.pallas_call(
        partial(scan_body, nb, nseq, cc, 32),
        grid=(2, ch // cc),
        in_specs=head + [big, spec] + tables + [big],
        out_specs=[big, big],
        out_shape=[jax.ShapeDtypeStruct(a.shape, bf16)] * 2,
        scratch_shapes=[
            pltpu.VMEM((size, BIG), bf16),
            pltpu.VMEM((size, 2 * BIG), f32),
            pltpu.VMEM((size, 2 * BIG), bf16),
            pltpu.VMEM((size, BIG), f32),
        ],
        compiler_params=params(56),
        cost_estimate=cost(2 * ch * 50e6, 2 * ch * nb * BLK * 8),
    )(tab, seq, a, kh, wave, back, gg)


def ssm_back(k, tab, seq, a, gm, kh, wave, back, gg, y, dg, da):
    nb, nseq, ch, cc, size, _, _, head, tables = ssm_specs(a.shape, seq)
    big = pl.BlockSpec((1, nb, cc, BLK), lambda i: (k, 0, i, 0))
    spec = pl.BlockSpec((1, LAGS, cc, 2 * BIG), lambda i: (k, 0, i, 0))
    out = pl.BlockSpec((1, nb, cc, BLK), lambda i: (0, 0, i, 0))
    out_spec = pl.BlockSpec((1, LAGS, cc, 2 * BIG), lambda i: (0, 0, i, 0))
    tables = [
        pl.BlockSpec((BIG, 2 * BIG), lambda i: (0, 0)),
        pl.BlockSpec((2 * BIG, BIG), lambda i: (0, 0)),
    ]
    return pl.pallas_call(
        partial(back_body, nb, nseq, cc, 64, k == 1),
        grid=(ch // cc,),
        in_specs=head + [big, big, spec] + tables + [big] * 4,
        out_specs=[out, out, out_spec, pl.BlockSpec((1, cc, 2 * BLK), lambda i: (0, i, 0))],
        out_shape=[jax.ShapeDtypeStruct((1,) + a.shape[1:], bf16)] * 2
        + [
            jax.ShapeDtypeStruct((1, LAGS, ch, 2 * BIG), f32),
            jax.ShapeDtypeStruct((1, ch, 2 * BLK), f32),
        ],
        scratch_shapes=[
            pltpu.VMEM((size, BIG), bf16),
            pltpu.VMEM((size, 2 * BIG), f32),
            pltpu.VMEM((size, 2 * BIG), f32),
            pltpu.VMEM((size, 2 * BIG), bf16),
            pltpu.VMEM((size, BIG), f32),
        ],
        compiler_params=params(60),
        cost_estimate=cost(ch * 80e6, ch * nb * BLK * 16),
    )(tab, seq, a, gm, kh, wave, back, gg, y, dg, da)


def stack_blocks(refs, many):
    return jnp.concatenate(
        [
            jnp.concatenate([ref[k, b] for b in range(many)], axis=1)
            for ref in refs
            for k in range(ref.shape[0])
        ],
        axis=0,
    )


def mul_body(count, more, many, start_ref, w_ref, *refs):
    out = nn(w_ref[...], stack_blocks(refs[:count], many))
    o_ref = refs[-1]
    for h in range(many):
        part = out[:, h * BLK : (h + 1) * BLK]
        if more:
            part = part + refs[count][h].astype(f32)
        o_ref[h] = part.astype(o_ref.dtype)


def mul_rows(w, arrays, start, many, dtype=bf16, extra=None):
    width, deep = w.shape
    ch = arrays[0].shape[2]
    count = len(arrays)
    step = 4
    out = pl.BlockSpec((step, width, BLK), lambda i, at: (i, 0, 0))
    return pl.pallas_call(
        partial(mul_body, count, extra is not None, step),
        grid_spec=pltpu.PrefetchScalarGridSpec(
            num_scalar_prefetch=1,
            grid=(many // step,),
            in_specs=[pl.BlockSpec((width, deep), lambda i, at: (0, 0))]
            + [pl.BlockSpec((x.shape[0], step, ch, BLK), lambda i, at: (0, at[0] + i, 0, 0)) for x in arrays]
            + ([] if extra is None else [out]),
            out_specs=out,
        ),
        out_shape=jax.ShapeDtypeStruct((many, width, BLK), dtype),
        compiler_params=params(40),
        cost_estimate=cost(2 * many * BLK * width * deep, 2 * many * BLK * (2 * width + deep)),
    )(start // step, w, *arrays, *([] if extra is None else [extra]))


def outer_body(ch, many, cuts, parts, at_ref, *refs):
    step = pl.program_id(0)
    xs, gs = refs[:parts], refs[parts : 2 * parts]
    gp_refs, gpg_refs, mix_ref = refs[2 * parts : 2 * parts + 2], refs[2 * parts + 2 : 2 * parts + 4], refs[2 * parts + 4]
    outs = refs[2 * parts + 5 : 2 * parts + 5 + cuts]
    acc_s, x_s, g_s = refs[-3:]

    def fill(at):
        for b in range(many):
            x_s[:, b * BLK : (b + 1) * BLK] = xs[at][b]
            g_s[:, b * BLK : (b + 1) * BLK] = gs[at][b]

    if parts == 1:
        fill(0)
    else:
        for at in range(parts):

            @pl.when(step == at)
            def _(at=at):
                fill(at)

    def part(ref, k):
        return jnp.concatenate([ref[k, b] for b in range(many)], axis=1)

    @pl.when(step == 0)
    def _():
        acc_s[...] = jnp.zeros_like(acc_s)

    split = 4 * ch
    left = jnp.concatenate([part(ref, 0) for ref in (*gp_refs, *gpg_refs)], axis=0)
    acc_s[:, :split] += nt(x_s[...], left)
    acc_s[:, split:] += nt(g_s[...], jnp.concatenate([part(mix_ref, 0), part(mix_ref, 1)], axis=0))

    @pl.when(step == pl.num_programs(0) - 1)
    def _():
        deep = acc_s.shape[0] // cuts
        for cut in range(cuts):
            start = pl.multiple_of(at_ref[pl.num_programs(0) + cut] * deep, 8)
            outs[cut][...] = acc_s[pl.ds(start, deep), :].astype(bf16)


def outer_sums(order, cuts, xs, gs, gp, gpg, mix):
    width = xs[0].shape[1]
    _, nb, ch, _ = mix.shape
    many = 8
    parts = len(xs)
    if parts == 1:
        rows = pl.BlockSpec((many, width, BLK), lambda i, at: (i, 0, 0))
    else:
        rows = pl.BlockSpec((many, width, BLK), lambda i, at: (0, 0, 0), pipeline_mode=pl.Buffered(1))
    chan = pl.BlockSpec((2, many, ch, BLK), lambda i, at: (0, at[i], 0, 0))
    one = pl.BlockSpec((1, many, ch, BLK), lambda i, at: (0, at[i], 0, 0))
    tok = nb * BLK
    return pl.pallas_call(
        partial(outer_body, ch, many, cuts, parts),
        grid_spec=pltpu.PrefetchScalarGridSpec(
            num_scalar_prefetch=1,
            grid=(nb // many,),
            in_specs=[rows] * (2 * parts) + [one] * 4 + [chan],
            out_specs=[pl.BlockSpec((width // cuts, 6 * ch), lambda i, at: (0, 0))] * cuts,
            scratch_shapes=[
                pltpu.VMEM((width, 6 * ch), f32),
                pltpu.VMEM((width, many * BLK), bf16),
                pltpu.VMEM((width, many * BLK), bf16),
            ],
        ),
        out_shape=[jax.ShapeDtypeStruct((width // cuts, 6 * ch), bf16)] * cuts,
        compiler_params=params(60),
        cost_estimate=cost(12 * tok * width * ch, tok * (4 * width + 12 * ch)),
    )(order, *xs, *gs, *gp, *gpg, mix)


def join_body(parts, split, at_ref, *refs):
    head_ref, tail_ref, head_t_ref, tail_t_ref = refs[parts:]
    deep = refs[0].shape[0]
    for at in range(parts):
        rows = pl.ds(pl.multiple_of(at_ref[at] * deep, 16), deep)
        head_ref[rows, :] = refs[at][:, :split]
        tail_ref[rows, :] = refs[at][:, split:]
    head_t_ref[...] = head_ref[...].T
    tail_t_ref[...] = tail_ref[...].T


def join_weights(order, parts, split):
    count = len(parts)
    deep, wide = parts[0].shape
    rows = deep * count
    vmem = pl.BlockSpec(memory_space=pltpu.VMEM)
    return pl.pallas_call(
        partial(join_body, count, split),
        in_specs=[pl.BlockSpec(memory_space=pltpu.SMEM)] + [vmem] * count,
        out_specs=[vmem] * 4,
        out_shape=[
            jax.ShapeDtypeStruct(shape, bf16)
            for shape in ((rows, split), (rows, wide - split), (split, rows), (wide - split, rows))
        ],
        compiler_params=params(48),
        cost_estimate=cost(0, 6 * rows * wide),
    )(order, *parts)


def meet_body(axes, rank_ref, x_ref, chan_ref, norm_ref, got_ref, call_ref, nall_ref, send_s, *sems):
    xs_sem, xr_sem, cs_sem, cr_sem, ns_sem, nr_sem, own_sem = sems
    q, c, h, w = (lax.axis_index(name) for name in axes)
    rows = x_ref.shape[0]
    piece = rows // 8
    flat = ((2 * q + c) * 2 + h) * 2 + w

    def peer(bits):
        return (q ^ (bits // 8), c ^ (bits // 4 % 2), h ^ (bits // 2 % 2), w ^ (bits % 2))

    barrier = pltpu.get_barrier_semaphore()
    for bits in range(1, 32):
        pl.semaphore_signal(barrier, inc=1, device_id=peer(bits), device_id_type=pl.DeviceIdType.MESH)
    pl.semaphore_wait(barrier, 31)

    def remote(src, dst, send, recv, to):
        return pltpu.make_async_remote_copy(
            src_ref=src, dst_ref=dst, send_sem=send, recv_sem=recv, device_id=to, device_id_type=pl.DeviceIdType.MESH
        )

    nall_ref[flat] = norm_ref[...]

    def norm_copy(bits):
        return remote(norm_ref, nall_ref.at[flat], ns_sem.at[bits], nr_sem.at[bits], peer(bits))

    for bits in range(1, 32):
        norm_copy(bits).start()

    place = 2 * (1 - c) + w
    spot_c = 4 * c + 2 * h + w

    def chan_copy(at):
        to = (q ^ at, 1 - q // 2, h, q % 2) if at < 4 else (2 * c + w, 1 - q // 2, 1 - h, q % 2)
        return remote(chan_ref, call_ref.at[spot_c], cs_sem.at[at], cr_sem.at[spot_c], to)

    def own_chan():
        return pltpu.make_async_copy(chan_ref, call_ref.at[spot_c], own_sem.at[1])

    def chan_came(at):
        return remote(chan_ref, call_ref.at[at], cs_sem.at[0], cr_sem.at[at], peer(1))

    far_spot = 4 * (q // 2) + 2 * (1 - h) + q % 2

    def chan_pass(bits):
        return remote(
            call_ref.at[far_spot], call_ref.at[far_spot], cs_sem.at[4 + bits], cr_sem.at[far_spot], (q ^ bits, c, h, w)
        )

    for at in (4, 1, 2, 3, 0):
        if at:
            chan_copy(at).start()
        else:

            @pl.when(place == q)
            def _():
                own_chan().start()

            @pl.when(place != q)
            def _():
                chan_copy(0).start()

    pieces = [(kq, kh) for kh in (1, 0) for kq in (1, 2, 3, 0)]
    spot = lax.broadcasted_iota(jnp.int32, (piece, rows), 0)

    def row_copy(kq, kh):
        at = 2 * kq + kh
        return remote(
            send_s.at[at], got_ref.at[2 * q + c], xs_sem.at[at], xr_sem.at[2 * kq + c], (q ^ kq, 1 - h, h ^ kh, w)
        )

    def own_copy():
        return pltpu.make_async_copy(send_s.at[0], got_ref.at[2 * q + c], own_sem.at[0])

    for kq, kh in pieces:
        chunk = 2 * (q ^ kq) + (h ^ kh)
        pick = jnp.where(spot + chunk * piece == rank_ref[...], 1.0, 0.0).astype(bf16)
        send_s[2 * kq + kh] = nn(pick, x_ref[...]).astype(bf16)
        if (kq, kh) == (0, 0):

            @pl.when(c != h)
            def _():
                own_copy().start()

            @pl.when(c == h)
            def _():
                row_copy(0, 0).start()

        else:
            row_copy(kq, kh).start()

    for bits in range(1, 32):
        norm_copy(bits).wait()
    for at in range(8):

        @pl.when((c != h) & (at == c))
        def _():
            own_copy().wait()

        @pl.when(jnp.logical_not((c != h) & (at == c)))
        def _(at=at):
            remote(send_s.at[at], got_ref.at[at], xs_sem.at[at], xr_sem.at[at], peer(1)).wait_recv()

    chan_came(far_spot).wait_recv()
    for bits in range(1, 4):
        chan_pass(bits).start()
    for at in range(8):

        @pl.when((place == q) & (at == spot_c))
        def _():
            own_chan().wait()

        @pl.when(jnp.logical_not((place == q) & (at == spot_c)) & (at != far_spot))
        def _(at=at):
            chan_came(at).wait_recv()

    for bits in range(1, 4):
        chan_pass(bits).wait_send()
    for kq, kh in pieces:
        if (kq, kh) == (0, 0):

            @pl.when(c == h)
            def _():
                row_copy(0, 0).wait_send()

        else:
            row_copy(kq, kh).wait_send()
    for at in range(1, 5):
        chan_copy(at).wait_send()

    @pl.when(place != q)
    def _():
        chan_copy(0).wait_send()


def meet(axes, rank, x, chan, norm):
    rows, width = x.shape
    vmem = pl.BlockSpec(memory_space=pltpu.VMEM)
    sem = pltpu.SemaphoreType.DMA
    return pl.pallas_call(
        partial(meet_body, axes),
        in_specs=[vmem] * 4,
        out_specs=[vmem] * 3,
        out_shape=[
            jax.ShapeDtypeStruct((8, rows // 8, width), bf16),
            jax.ShapeDtypeStruct((8,) + chan.shape, f32),
            jax.ShapeDtypeStruct((32,) + norm.shape, f32),
        ],
        scratch_shapes=[pltpu.VMEM((8, rows // 8, width), bf16)]
        + [sem((8,)), sem((8,)), sem((8,)), sem((8,)), sem((32,)), sem((32,)), sem((2,))],
        compiler_params=pltpu.CompilerParams(collective_id=1, has_side_effects=True, vmem_limit_bytes=60 * MIB),
        cost_estimate=cost(2 * rows * rows * width, 100 * rows * width),
    )(rank.reshape(1, rows), x, chan, norm)


def sequence_tables(lens, nb):
    nseq = lens.shape[0]
    blocks = (lens + BLK - 1) // BLK
    start = jnp.cumsum(blocks) - blocks
    bigs = (blocks + 1) // 2
    first_big = jnp.cumsum(bigs) - bigs
    h = jnp.arange((nb + nseq) // 2, dtype=jnp.int32)
    owner = (h[:, None] >= first_big[None, :]).astype(jnp.int32).sum(axis=1) - 1
    mine = owner[:, None] == jnp.arange(nseq, dtype=jnp.int32)[None, :]

    def at_owner(values):
        return jnp.sum(jnp.where(mine, values[None, :], 0), axis=1)

    rel = h - at_owner(first_big)
    first = jnp.minimum(at_owner(start) + 2 * rel, nb - 1)
    whole = (2 * rel + 1 < at_owner(blocks)).astype(jnp.int32)
    tab = jnp.stack([first, whole]).astype(jnp.int32)
    seq = jnp.stack(
        [jnp.append(first_big, jnp.sum(blocks)), jnp.append(bigs, jnp.sum(bigs))]
    ).astype(jnp.int32)
    return tab, seq


def live_rows(lens, rows):
    slot = (lens + BLK - 1) // BLK * BLK
    begin = jnp.cumsum(slot) - slot
    pos = jnp.arange(rows, dtype=jnp.int32)
    inside = (pos[:, None] >= begin[None, :]) & (pos[:, None] < (begin + lens)[None, :])
    return jnp.sum(inside.astype(f32), axis=1)


def after(values):
    return lax.optimization_barrier(values)


def rank_of(keys):
    return jnp.sum((keys[None, :] < keys[:, None]).astype(jnp.int32), axis=1)


class Line:
    def __init__(self, n_dp, n_t):
        self.n_dp, self.n_t = n_dp, n_t
        self.axes = {"dp": n_dp, "tensor": n_t}
        self.both = ("dp", "tensor")
        self.cuts = 1

    def place_of_group(self):
        return lax.axis_index("tensor")

    def gather_first(self, x):
        return [lax.all_gather(x, "tensor", axis=0, tiled=True)]

    def gathered(self, x, early):
        return []

    def gather_last(self, x, got):
        return [(got[0], jnp.zeros((1,), jnp.int32))]

    def scatter_first(self, w, arrays, many):
        return [mul_rows(w, arrays, jnp.zeros((1,), jnp.int32), many * self.n_t)]

    def scatter_send(self, parts):
        return [lax.psum_scatter(parts[0], "tensor", scatter_dimension=0, tiled=True)]

    def scatter_own(self, w, arrays, many):
        return []

    def regroup(self, x):
        return x

    def ungroup(self, x):
        return x

    def spread(self, x):
        return lax.all_to_all(x, "dp", split_axis=0, concat_axis=0, tiled=True)

    def order(self, pieces):
        return jnp.append(jnp.arange(pieces * self.n_t, dtype=jnp.int32), 0)

    def enter(self, rank, x, chan, norm):
        (sent,) = permute_to(rank, [x])
        return (self.spread(sent),) + self.gather_channels(chan, norm)

    def weights_first(self, pack):
        return [pack]

    def weights_send(self, packs):
        return [lax.all_gather(packs[0], "dp", axis=0, tiled=True)]

    def gather_channels(self, chan, norm):
        perm = [(f, (f % self.n_dp) * self.n_t + f // self.n_dp) for f in range(self.n_dp * self.n_t)]
        chan = lax.ppermute(chan, self.both, perm)
        norm = lax.all_gather(norm, self.both, axis=1, tiled=True)
        return lax.all_gather(chan[None], "dp", axis=0, tiled=True), norm

    def cut_order(self):
        return jnp.zeros((1,), jnp.int32)

    def grads_send(self, gw):
        return [lax.psum_scatter(gw[0], "dp", scatter_dimension=0, tiled=True)]

    def grads_last(self, parts):
        return parts[0], lambda part: part.astype(f32)

    def scatter_small(self, sums, norm):
        sums = lax.psum_scatter(sums, "dp", scatter_dimension=0, tiled=True)
        norm = lax.psum_scatter(norm, self.both, scatter_dimension=1, tiled=True)
        perm = [((f % self.n_dp) * self.n_t + f // self.n_dp, f) for f in range(self.n_dp * self.n_t)]
        return (sums, norm), lambda part: (lax.ppermute(part[0], self.both, perm), part[1])


class Pairs:
    def __init__(self, n_dp, n_t):
        self.quads = n_dp // 2
        self.axes = {"q": self.quads, "c": 2, "h": 2, "w": 2}
        self.both = ("q", "c", "h", "w")
        self.cuts = self.quads
        self.other = [(0, 1), (1, 0)]
        self.there = [(2 * c + h, 2 * (1 - h) + c) for c in range(2) for h in range(2)]
        self.back = [(b, a) for a, b in self.there]
        self.turned = [(2 * c + h, 2 * (1 - h) + 1 - c) for c in range(2) for h in range(2)]

    def flip(self, x, axis, bit=1):
        return lax.ppermute(x, axis, [(i, i ^ bit) for i in range(self.axes[axis])])

    def place_of_group(self):
        return 2 * (1 - lax.axis_index("c")) + lax.axis_index("w")

    def regroup(self, x):
        return lax.ppermute(x, ("c", "h"), self.there)

    def ungroup(self, x):
        return lax.ppermute(x, ("c", "h"), self.back)

    def spread(self, x):
        return lax.all_to_all(x, ("q", "c"), split_axis=0, concat_axis=0, tiled=True)

    def places(self):
        c, w = lax.axis_index("c"), lax.axis_index("w")
        return [2 * (1 - c) + w, 2 * c + w, 2 * (1 - c) + 1 - w, 2 * c + 1 - w]

    def starts(self, many):
        return [(place * many).astype(jnp.int32).reshape(1) for place in self.places()]

    def gather_first(self, x):
        return [self.flip(x, "c"), self.flip(x, "w")]

    def gathered(self, x, early):
        return list(zip([x] + early, self.starts(x.shape[0])))

    def gather_last(self, x, got):
        beside, near = got
        return list(zip([x, beside, near, self.flip(near, "c")], self.starts(x.shape[0])))

    def scatter_first(self, w, arrays, many):
        _, beside, near, far = self.starts(many)
        first = mul_rows(w, arrays, far, many)
        give = self.flip(first, "c")
        beside, first = after((beside, first))
        second = mul_rows(w, arrays, beside, many)
        second, give = after((second, give))
        return [second, mul_rows(w, arrays, near, many, extra=give)]

    def scatter_send(self, parts):
        return [self.flip(parts[0], "c"), self.flip(parts[1], "w")]

    def scatter_own(self, w, arrays, many):
        return [mul_rows(w, arrays, self.starts(many)[0], many, dtype=f32)]

    def order(self, pieces):
        place = jnp.stack(self.places())[:, None] * pieces + jnp.arange(pieces)[None, :]
        return jnp.concatenate([place.reshape(-1).astype(jnp.int32), self.cut_order()])

    def steps(self):
        bit = self.quads // 2
        while bit:
            yield "q", bit
            bit //= 2
        yield "h", 1

    def spot(self):
        return 2 * lax.axis_index("q") + lax.axis_index("h")

    def enter(self, rank, x, chan, norm):
        small = norm.shape[1]
        norm = jnp.pad(norm, ((0, 5), (0, BLK - small)))
        got, chan, norm = meet(self.both, rank, x, chan, norm)
        norm = norm[:, :3, :small].transpose(1, 0, 2).reshape(3, -1)
        return got.reshape(x.shape), chan, norm

    def weights_first(self, pack):
        return [self.regroup(pack), lax.ppermute(pack, ("c", "h"), self.turned)]

    def weights_send(self, packs):
        h = lax.axis_index("h")
        first, second = packs
        pair = jnp.concatenate([jnp.where(h == 0, first, second), jnp.where(h == 0, second, first)], axis=0)
        return [pair] + [self.flip(pair, "q", bit) for bit in range(1, self.quads)]

    def grads_send(self, gw):
        return [gw[0]] + [self.flip(gw[bit], "q", bit) for bit in range(1, self.quads)]

    def grads_last(self, parts):
        total = parts[0].astype(f32)
        for part in parts[1:]:
            total = total + part.astype(f32)
        total = total.astype(bf16)
        half = total.shape[0] // 2
        h = lax.axis_index("h")
        first = jnp.where(h == 0, total[:half], total[half:])
        second = jnp.where(h == 0, total[half:], total[:half])

        def finish(parts):
            return self.ungroup(parts[0]).astype(f32) + lax.ppermute(parts[1], ("c", "h"), self.turned).astype(f32)

        return (first, second), finish

    def cut_order(self):
        return (lax.axis_index("q") ^ jnp.arange(self.quads)).astype(jnp.int32)

    def scatter_small(self, sums, norm):
        count = 2 * self.quads
        rows, wide = sums.shape[0] // count, sums.shape[1]
        norm = norm.reshape(3, 4 * count, -1).transpose(1, 0, 2)
        small = norm.shape[2]
        norm = jnp.pad(norm, ((0, 0), (0, 5), (0, BLK - small)))
        norm = lax.all_to_all(norm, self.both, split_axis=0, concat_axis=0, tiled=True)
        flat = jnp.pad(sums, ((0, 0), (0, -wide % 8))).reshape(count, -1, BLK)
        near = jnp.arange(self.quads) ^ lax.axis_index("q")
        h = lax.axis_index("h")
        keep, give = jnp.take(flat, 2 * near + h, axis=0), jnp.take(flat, 2 * near + 1 - h, axis=0)

        def finish(parts):
            keep, give, norm = parts
            part = keep + self.flip(give, "h")
            total = None
            for apart in range(self.quads):
                perm = []
                for source in range(4 * count):
                    q, c, h, w = source // 8, source // 4 % 2, source // 2 % 2, source % 2
                    perm.append((source, count * (2 * (1 - c) + w) + 2 * (q ^ apart) + h))
                got = lax.ppermute(part[apart], self.both, perm)
                total = got if total is None else total + got
            return total.reshape(rows, -1)[:, :wide], jnp.sum(norm, axis=0)[:3, :small]

        return (keep, give, norm), finish


def local(
    net, wave, tokens, cotangent, source, target, lengths, ln_gain, ln_bias, w_fwd, b_fwd, w_bwd, b_bwd,
    w_gate, b_gate, w_out, b_out, log_dt, log_rate, ssm_b, ssm_c, ssm_d,
):
    rows, width = tokens.shape
    many = rows // BLK
    n_t = net.n_t
    group = rows * n_t
    nb = group // BLK
    ch = w_fwd.shape[1]
    back = (wave.T / BIG).astype(bf16)
    wave = wave.astype(bf16)

    def lanes(column):
        return jnp.broadcast_to(column[..., None], column.shape + (BLK,))

    def decays(log_dt, log_rate, ssm_b):
        rate = jnp.exp(log_rate)
        ld = -jnp.exp(log_dt)[..., None] * rate
        return rate, ld, (1.0 - jnp.exp(ld)) / rate * ssm_b

    rank = rank_of(target)
    sender = source // group
    place = rank_of(sender * rows + jnp.arange(rows, dtype=jnp.int32))
    pack = jnp.concatenate(
        [w_fwd, w_bwd, w_gate.reshape(-1, 2 * ch), w_out.transpose(2, 0, 1).reshape(-1, 2 * ch)], axis=1
    )
    table = net.regroup(jnp.concatenate([place, lengths[0]]))
    rate, ld, drive = decays(log_dt, log_rate, ssm_b)
    own = b_fwd.shape[0]
    small = jnp.concatenate([ssm_d, b_fwd[None], b_bwd[None], b_gate])
    chan = jnp.concatenate(
        [
            (ld * log2e).reshape(own, 2 * STATE),
            (ssm_c * drive).reshape(own, 2 * STATE),
            jnp.pad(small, ((0, -(2 * own + 6) % 8 + 0), (0, 2 * STATE - own))),
        ]
    )
    norm = jnp.stack([ln_gain, ln_bias, b_out])
    (sent_g,) = permute_to(rank, [cotangent])
    sent_g, tokens = after((sent_g, tokens))
    got_g = net.spread(sent_g)
    got_x, chan_all, norm_all = net.enter(rank, tokens, chan, norm)
    got_x, got_g, chan_all, norm_all, pack, table = after((got_x, got_g, chan_all, norm_all, pack, table))
    packs = net.weights_first(pack)

    place, lens = table[:rows], table[rows:]
    gain = lanes(norm_all[0])
    shift = lanes(norm_all[1])
    small = chan_all[:, 2 * own : 2 * own + 6, :own].transpose(1, 0, 2).reshape(6, ch)

    def pairs(at):
        both = chan_all[:, at : at + own].reshape(-1, 2, own // 2, 2 * STATE)
        return both.transpose(1, 0, 2, 3).reshape(2, ch // 2, 2 * STATE)

    ld_pairs = pairs(0)
    w_pairs = pairs(own)
    skip = lanes(small[0:2])
    live = live_rows(lens, group)
    live_own = lax.dynamic_slice_in_dim(live, net.place_of_group() * rows, rows, 0).reshape(many, 1, BLK)
    live = live.reshape(nb // 2, 1, BIG)
    tab, seq = sequence_tables(lens, nb)

    xt, xd = deal_x(place, got_x, gain, shift)
    x_got = net.gather_first(xt)
    _, ld_pairs, w_pairs, skip, packs = after((xt, ld_pairs, w_pairs, skip, packs))
    w_parts = net.weights_send(packs)
    kh = spectra(ld_pairs, w_pairs, skip, wave)
    bias_in = lanes(small[2:6].reshape(-1))
    bias_out = lanes(norm_all[2])
    made = (bias_in, bias_out, tab, seq, live, live_own, net.cut_order(), net.order(many // 8))
    w_parts, x_got, kh, got_g, made = after((w_parts, x_got, kh, got_g, made))
    bias_in, bias_out, tab, seq, live, live_own, cut_order, order = made
    got_g = net.regroup(got_g)
    w_in, w_back, w_in_t, w_back_t = join_weights(cut_order, w_parts, 4 * ch)
    xs = net.gather_last(xt, x_got)
    kept = None
    for part, start in xs:
        kept = project(part, start, nb, live, w_in_t, bias_in, kept)
    kept, got_g = after((kept, got_g))
    a, da, gg, dg = kept
    gt, gd, g_bias_out = deal_g(place, got_g, live_own)
    gt, a = after((gt, a))
    g_got = net.gather_first(gt)
    y, mix = ssm_scan(tab, seq, a, kh, wave, back, gg)
    g_got, y, mix = after((g_got, y, mix))
    gs = net.gather_last(gt, g_got)
    branch = net.scatter_first(w_back, [mix], many)
    gm = gate_grad(gs, nb, w_back_t)
    branch, gm = after((branch, gm))

    branch = net.scatter_send(branch)
    branch = net.scatter_own(w_back, [mix], many) + branch
    first = ssm_back(0, tab, seq, a, gm, kh, wave, back, gg, y, dg, da)
    branch, first, a = after((branch, first, a))
    sent_out = layer_rows(place, branch, xd, live_own, bias_out)
    sent_out, a = after((sent_out, a))
    sent_out = net.ungroup(sent_out)
    second = ssm_back(1, tab, seq, a, gm, kh, wave, back, gg, y, dg, da)
    sent_out, first, second = after((sent_out, first, second))
    gpg, gp, gh, bsum = zip(first, second)
    sent_out = net.spread(sent_out)
    back_list = [gp[0], gp[1], gpg[0], gpg[1]]
    g_normed = net.scatter_first(w_in, back_list, many)
    g_normed, back_list, mix = after((g_normed, back_list, mix))
    gp, gpg = back_list[:2], back_list[2:]
    g_normed = net.scatter_send(g_normed)
    g_normed = net.scatter_own(w_in, back_list, many) + g_normed
    gw = outer_sums(order, net.cuts, [part for part, _ in xs], [part for part, _ in gs], gp, gpg, mix)
    g_normed, gw, gh, sent_out = after((g_normed, gw, gh, sent_out))
    sent_in, norm_sums = input_rows(place, g_normed, xd, gd, gain)
    sent_in, gh, gw, norm_sums, sent_out, bsum = after((sent_in, gh, gw, norm_sums, sent_out, bsum))
    sent_in = net.ungroup(sent_in)
    gw = net.grads_send(gw)
    s0, s1, g0 = [jnp.concatenate(part) for part in zip(*[moments(k, ld_pairs, gh[k], back) for k in range(2)])]
    layer_out = permute_from(rank, sent_out)

    s0 = s0.reshape(2, ch, STATE)
    s1 = s1.reshape(2, ch, STATE)
    bsum = jnp.concatenate(bsum)
    gb_gate = jnp.sum(bsum[:, :, :BLK], axis=2)
    gb_in = jnp.sum(bsum[:, :, BLK:], axis=2)
    sums = jnp.concatenate(
        [s0[0], s0[1], s1[0], s1[1], jnp.concatenate([g0[:, :, 0], gb_gate, gb_in], axis=0).T], axis=1
    )
    norm_sums = jnp.sum(jnp.concatenate([norm_sums, g_bias_out[None]], axis=0), axis=2)
    part, finish = net.scatter_small(sums, norm_sums)
    gw, gw_finish = net.grads_last(gw)
    sent_in, gw, part, layer_out = after((sent_in, gw, part, layer_out))
    in_grad = permute_from(rank, net.spread(sent_in))
    gw = gw_finish(gw)
    sums, norm_sums = finish(part)
    s0 = jnp.stack([sums[:, :STATE], sums[:, STATE : 2 * STATE]])
    s1 = jnp.stack([sums[:, 2 * STATE : 3 * STATE], sums[:, 3 * STATE : 4 * STATE]])
    tail = sums[:, 4 * STATE :].T
    step = jnp.exp(log_dt)[..., None]
    g_c = s0 * drive
    g_drive = s0 * ssm_c
    g_b = g_drive * (1.0 - jnp.exp(ld)) / rate
    g_ld = s1 * ssm_c * drive - g_drive * ssm_b / rate * jnp.exp(ld)
    g_rate = -g_drive * drive / rate - g_ld * step
    g_dt = jnp.sum(g_ld * ld, axis=2)
    return (
        layer_out,
        in_grad,
        norm_sums[0],
        norm_sums[1],
        gw[:, :ch],
        tail[4],
        gw[:, ch : 2 * ch],
        tail[5],
        gw[:, 2 * ch : 4 * ch].reshape(-1, 2, ch),
        tail[2:4],
        gw[:, 4 * ch :].T.reshape(2, ch, -1),
        norm_sums[2],
        g_dt,
        g_rate * rate,
        g_b,
        g_c,
        tail[0:2],
    )


def solution(mesh):
    n_dp, n_t = mesh.shape["dp"], mesh.shape["tensor"]
    if n_t == 4 and n_dp == 8:
        net = Pairs(n_dp, n_t)
        dp, tensor = ("q", "c"), ("h", "w")
    else:
        net = Line(n_dp, n_t)
        dp, tensor = ("dp",), ("tensor",)
    net.n_t = n_t
    mesh = jax.sharding.Mesh(mesh.devices.reshape(tuple(net.axes.values())), tuple(net.axes))
    both = P(dp + tensor)
    rows = P(dp + tensor, None)
    pair = P(None, dp + tensor)
    state = P(None, dp + tensor, None)
    proj = P(dp, tensor)
    gate = P(dp, None, tensor)
    out = P(None, tensor, dp)
    wave = wave_table()

    def run(*args):
        return local(net, jnp.asarray(wave), *args)

    return jax.shard_map(
        run,
        mesh=mesh,
        in_specs=(
            rows, rows, both, both, P(dp, None), both, both, proj, both, proj, both, gate, pair, out, both,
            pair, state, state, state, pair,
        ),
        out_specs=(
            rows, rows, both, both, proj, both, proj, both, gate, pair, out, both, pair, state, state, state, pair,
        ),
        check_vma=False,
    )
```

```python
from functools import partial

import jax
import jax.numpy as jnp
import numpy as np
from jax import lax
from jax.experimental import pallas as pl
from jax.experimental.pallas import tpu as pltpu
from jax.sharding import PartitionSpec as P

BLK = 128
BIG = 256
MOST = 2048
LAGS = MOST // BIG
STATE = 64
epsilon = 1e-05
log2e = 1.4426950408889634
f32 = jnp.float32
bf16 = jnp.bfloat16
MIB = 2**20


def nn(a, b):
    return lax.dot_general(a, b, (((1,), (0,)), ((), ())), preferred_element_type=f32)


def nt(a, b):
    return lax.dot_general(a, b, (((1,), (1,)), ((), ())), preferred_element_type=f32)


def params(limit):
    return pltpu.CompilerParams(vmem_limit_bytes=60 * MIB)


def cost(flops, moved, trans=0):
    scale = 0.05
    return pl.CostEstimate(
        flops=int(scale * flops), bytes_accessed=int(scale * moved), transcendentals=int(scale * trans)
    )


def halves(x):
    high = x.astype(bf16)
    return high, (x - high.astype(f32)).astype(bf16)


def wave_table():
    pos = np.arange(BIG)[:, None]
    freq = np.arange(BIG)[None, :]
    angle = 2 * np.pi * ((2 * freq + 1) * pos % (4 * BIG)) / (4 * BIG)
    return np.concatenate([np.cos(angle), np.sin(angle)], 1).astype(np.float32)


def chunk_of(channels, most):
    best = 16
    for size in range(16, most + 1, 16):
        if channels % size == 0:
            best = size
    return best


def permute_row_body(count, rank_ref, *refs):
    rows = rank_ref.shape[1]
    spot = lax.broadcasted_iota(jnp.int32, (rows, rows), 0)
    pick = jnp.where(spot == rank_ref[...], 1.0, 0.0).astype(bf16)
    for at in range(count):
        refs[count + at][...] = nn(pick, refs[at][...]).astype(bf16)


def permute_to(rank, arrays):
    rows, width = arrays[0].shape
    count = len(arrays)
    return pl.pallas_call(
        partial(permute_row_body, count),
        out_shape=[jax.ShapeDtypeStruct((rows, width), bf16)] * count,
        compiler_params=params(48),
        cost_estimate=cost(2 * count * rows * rows * width, 4 * count * rows * width),
    )(rank.reshape(1, rows), *arrays)


def permute_col_body(rank_ref, x_ref, o_ref):
    rows = x_ref.shape[0]
    spot = lax.broadcasted_iota(jnp.int32, (rows, rows), 1)
    pick = jnp.where(spot == rank_ref[...], 1.0, 0.0).astype(bf16)
    o_ref[...] = nn(pick, x_ref[...]).astype(bf16)


def permute_from(rank, x):
    rows, width = x.shape
    return pl.pallas_call(
        permute_col_body,
        out_shape=jax.ShapeDtypeStruct((rows, width), bf16),
        compiler_params=params(48),
        cost_estimate=cost(2 * rows * rows * width, 4 * rows * width),
    )(rank.reshape(rows, 1), x)


def pick_rows(place_ref, x_ref):
    spot = lax.broadcasted_iota(jnp.int32, (BLK, x_ref.shape[0]), 1)
    pick = jnp.where(spot == place_ref[...], 1.0, 0.0).astype(bf16)
    return nn(pick, x_ref[...]).T


def deal_x_body(place_ref, x_ref, gain_ref, shift_ref, xt_ref, xd_ref):
    x = pick_rows(place_ref, x_ref)
    xd_ref[0] = x.astype(bf16)
    centred = x - jnp.mean(x, axis=0, keepdims=True)
    inv_std = lax.rsqrt(jnp.mean(centred * centred, axis=0, keepdims=True) + epsilon)
    xt_ref[0] = (centred * inv_std * gain_ref[...] + shift_ref[...]).astype(bf16)


def deal_g_body(place_ref, g_ref, live_ref, gt_ref, gd_ref, bo_ref):
    g = pick_rows(place_ref, g_ref)
    gd_ref[0] = g.astype(bf16)
    g = g * live_ref[0]
    gt_ref[0] = g.astype(bf16)

    @pl.when(pl.program_id(0) == 0)
    def _():
        bo_ref[...] = jnp.zeros_like(bo_ref)

    bo_ref[...] += g


def deal_specs(rows, width):
    place = pl.BlockSpec((BLK, 1), lambda i: (i, 0))
    whole = pl.BlockSpec((rows, width), lambda i: (0, 0))
    wide = pl.BlockSpec((width, BLK), lambda i: (0, 0))
    out = pl.BlockSpec((1, width, BLK), lambda i: (i, 0, 0))
    return place, whole, wide, out


def deal_x(place, x, gain, shift):
    rows, width = x.shape
    blocks = rows // BLK
    spot, whole, wide, out = deal_specs(rows, width)
    return pl.pallas_call(
        deal_x_body,
        grid=(blocks,),
        in_specs=[spot, whole, wide, wide],
        out_specs=[out, out],
        out_shape=[jax.ShapeDtypeStruct((blocks, width, BLK), bf16)] * 2,
        compiler_params=params(40),
        cost_estimate=cost(2 * rows * rows * width, 6 * rows * width),
    )(place.reshape(rows, 1), x, gain, shift)


def deal_g(place, g, live):
    rows, width = g.shape
    blocks = rows // BLK
    spot, whole, wide, out = deal_specs(rows, width)
    return pl.pallas_call(
        deal_g_body,
        grid=(blocks,),
        in_specs=[spot, whole, pl.BlockSpec((1, 1, BLK), lambda i: (i, 0, 0))],
        out_specs=[out, out, wide],
        out_shape=[jax.ShapeDtypeStruct((blocks, width, BLK), bf16)] * 2
        + [jax.ShapeDtypeStruct((width, BLK), f32)],
        compiler_params=params(40),
        cost_estimate=cost(2 * rows * rows * width, 6 * rows * width),
    )(place.reshape(rows, 1), g, live)


def send_back(place_ref, out_s, o_ref):
    rows = out_s.shape[0]
    spot = lax.broadcasted_iota(jnp.int32, (rows, rows), 0)
    pick = jnp.where(spot == place_ref[...], 1.0, 0.0).astype(bf16)
    o_ref[...] = nn(pick, out_s[...]).astype(bf16)


def total(refs, at):
    value = refs[0][at].astype(f32)
    for ref in refs[1:]:
        value = value + ref[at].astype(f32)
    return value


def layer_body(place_ref, xd_ref, live_ref, bias_ref, *refs):
    o_ref, out_s = refs[-2:]
    for at in range(xd_ref.shape[0]):
        y = xd_ref[at].astype(f32) + live_ref[at] * (total(refs[:-2], at) + bias_ref[...])
        out_s[at * BLK : (at + 1) * BLK, :] = y.T.astype(bf16)
    send_back(place_ref, out_s, o_ref)


def layer_rows(place, parts, xd, live, bias):
    blocks, width, _ = xd.shape
    rows = blocks * BLK
    return pl.pallas_call(
        layer_body,
        out_shape=jax.ShapeDtypeStruct((rows, width), bf16),
        scratch_shapes=[pltpu.VMEM((rows, width), bf16)],
        compiler_params=params(48),
        cost_estimate=cost(2 * rows * rows * width, 6 * rows * width),
    )(place.reshape(1, rows), xd, live, bias, *parts)


def input_body(place_ref, xd_ref, gd_ref, gain_ref, *refs):
    o_ref, sums_ref, out_s = refs[-3:]
    g_gain = jnp.zeros(gain_ref.shape, f32)
    g_shift = jnp.zeros(gain_ref.shape, f32)
    for at in range(xd_ref.shape[0]):
        x = xd_ref[at].astype(f32)
        centred = x - jnp.mean(x, axis=0, keepdims=True)
        inv_std = lax.rsqrt(jnp.mean(centred * centred, axis=0, keepdims=True) + epsilon)
        x_hat = centred * inv_std
        g = total(refs[:-3], at)
        g_gain = g_gain + g * x_hat
        g_shift = g_shift + g
        hat = g * gain_ref[...]
        back = inv_std * (
            hat
            - jnp.mean(hat, axis=0, keepdims=True)
            - x_hat * jnp.mean(hat * x_hat, axis=0, keepdims=True)
        )
        out_s[at * BLK : (at + 1) * BLK, :] = (gd_ref[at].astype(f32) + back).T.astype(bf16)
    sums_ref[0] = g_gain
    sums_ref[1] = g_shift
    send_back(place_ref, out_s, o_ref)


def input_rows(place, parts, xd, gd, gain):
    blocks, width, _ = xd.shape
    rows = blocks * BLK
    return pl.pallas_call(
        input_body,
        out_shape=[
            jax.ShapeDtypeStruct((rows, width), bf16),
            jax.ShapeDtypeStruct((2, width, BLK), f32),
        ],
        scratch_shapes=[pltpu.VMEM((rows, width), bf16)],
        compiler_params=params(48),
        cost_estimate=cost(2 * rows * rows * width, 8 * rows * width),
    )(place.reshape(1, rows), xd, gd, gain, *parts)


def project_body(ch, many, start_ref, x_ref, live_ref, wt_ref, bias_ref, *refs):
    a_ref, da_ref, gg_ref, dg_ref = refs[-4:]
    x = jnp.concatenate([x_ref[0], x_ref[1]], axis=1)
    live = live_ref[0]
    root = 0.7978845608028654
    step = 64 if ch % 128 else 128

    def act(pre):
        square = pre * pre
        rise = 0.5 + 0.5 * jnp.tanh(pre * (root + (0.044715 * root) * square))
        value = pre * rise
        slope = rise + rise * (pre - value) * (2.0 * root + (6.0 * 0.044715 * root) * square)
        return value, slope

    def put(ref, k, at, value):
        value = value.astype(bf16)
        ref[k, 0, at, :] = value[:, :BLK]
        ref[k, 1, at, :] = value[:, BLK:]

    for k in range(2):
        for first, value_ref, slope_ref in ((k * ch, a_ref, da_ref), ((2 + k) * ch, gg_ref, dg_ref)):
            for at in range(0, ch, step):
                rows = pl.ds(first + at, step)
                bias = bias_ref[rows, :]
                pre = nn(wt_ref[rows, :], x) + jnp.concatenate([bias, bias], axis=1)
                value, slope = act(pre)
                if value_ref is a_ref:
                    value, slope = live * value, live * slope
                put(value_ref, k, pl.ds(at, step), value)
                put(slope_ref, k, pl.ds(at, step), slope)


def chained(body, grid, in_specs, out_specs, shapes, scratch, limit, estimate, start, operands, kept):
    kept = [] if kept is None else list(kept)
    specs = list(in_specs) + [pl.BlockSpec(memory_space=pl.ANY)] * len(kept)
    first = 1 + len(operands)
    return pl.pallas_call(
        body,
        grid_spec=pltpu.PrefetchScalarGridSpec(
            num_scalar_prefetch=1, grid=grid, in_specs=specs, out_specs=out_specs, scratch_shapes=scratch
        ),
        out_shape=shapes,
        input_output_aliases={first + at: at for at in range(len(kept))},
        compiler_params=params(limit),
        cost_estimate=estimate,
    )(start, *operands, *kept)


def project(xt, start, nb, live, wt, bias, kept):
    many, width, _ = xt.shape
    ch = wt.shape[0] // 4
    out = pl.BlockSpec((2, 2, ch, BLK), lambda i, at: (0, at[0] + i, 0, 0))
    tok = many * BLK
    return chained(
        partial(project_body, ch, many),
        (many // 2,),
        [
            pl.BlockSpec((2, width, BLK), lambda i, at: (i, 0, 0)),
            pl.BlockSpec((1, 1, BIG), lambda i, at: (at[0] + i, 0, 0)),
            pl.BlockSpec((4 * ch, width), lambda i, at: (0, 0)),
            pl.BlockSpec((4 * ch, BLK), lambda i, at: (0, 0)),
        ],
        [out] * 4,
        [jax.ShapeDtypeStruct((2, nb, ch, BLK), bf16)] * 4,
        [],
        48,
        cost(8 * tok * width * ch, 2 * tok * width + 16 * tok * ch, 4 * tok * ch),
        start // 2,
        [xt, live, wt, bias],
        kept,
    )


def gate_grad_body(ch, parts, at_ref, *refs):
    wt_ref, o_ref, g_s = refs[parts:]
    steps = pl.num_programs(0) // parts
    many = refs[0].shape[0]

    for part in range(parts):

        @pl.when(pl.program_id(0) // steps == part)
        def _(part=part):
            for h in range(many):
                g_s[:, h * BLK : (h + 1) * BLK] = refs[part][h]

    for k in range(2):
        gm = nn(wt_ref[k * ch : (k + 1) * ch, :], g_s[...]).astype(bf16)
        for h in range(many):
            o_ref[k, h] = gm[:, h * BLK : (h + 1) * BLK]


def gate_grad(gs, nb, wt):
    parts = len(gs)
    rows_in, width, _ = gs[0][0].shape
    many = 4
    steps = rows_in // many
    ch = wt.shape[0] // 2
    tok = nb * BLK

    def rows(part):
        return pl.BlockSpec((many, width, BLK), lambda i, at: (jnp.clip(i - part * steps, 0, steps - 1), 0, 0))

    order = jnp.concatenate([start // many for _, start in gs]).astype(jnp.int32)
    return pl.pallas_call(
        partial(gate_grad_body, ch, parts),
        grid_spec=pltpu.PrefetchScalarGridSpec(
            num_scalar_prefetch=1,
            grid=(parts * steps,),
            in_specs=[rows(part) for part in range(parts)] + [pl.BlockSpec((2 * ch, width), lambda i, at: (0, 0))],
            out_specs=pl.BlockSpec((2, many, ch, BLK), lambda i, at: (0, at[i // steps] + i % steps, 0, 0)),
            scratch_shapes=[pltpu.VMEM((width, many * BLK), bf16)],
        ),
        out_shape=jax.ShapeDtypeStruct((2, nb, ch, BLK), bf16),
        compiler_params=params(40),
        cost_estimate=cost(4 * tok * width * ch, 2 * tok * width + 4 * tok * ch),
    )(order, *[part for part, _ in gs], wt)


def spectra_body(cc, ld_ref, w_ref, d_ref, wave_ref, kh_ref, k_s):
    t = lax.broadcasted_iota(jnp.int32, (BLK, BLK), 0).astype(f32)
    block = lax.broadcasted_iota(jnp.int32, (2 * LAGS, BLK), 0).astype(f32) * float(BLK)
    low = lax.broadcasted_iota(jnp.int32, (2 * LAGS, BLK), 1) < STATE
    count = 2 * LAGS

    def one(p, carry):
        ld = ld_ref[0, pl.ds(p, 1), :]
        decay = jnp.exp2(t * ld)
        scale = w_ref[0, pl.ds(p, 1), :] * jnp.exp2(block * ld)
        lhs = jnp.concatenate([jnp.where(low, scale, 0.0), jnp.where(low, 0.0, scale)], axis=0)
        lhs_high, lhs_low = halves(lhs)
        k = nt(jnp.concatenate([lhs_high, lhs_low], axis=0), decay.astype(bf16))
        k = k[0 : 2 * count] + k[2 * count : 4 * count]
        k_s[pl.ds(2 * p, count, stride=cc), :] = k[0:count]
        k_s[pl.ds(2 * p + 1, count, stride=cc), :] = k[count : 2 * count]
        return carry

    lax.fori_loop(0, cc // 2, one, 0, unroll=16)
    sign = jnp.where(lax.broadcasted_iota(jnp.int32, (cc, BIG), 1) % 2 == 0, 1.0, -1.0)
    before = None
    for big in range(LAGS):
        rows = jnp.concatenate(
            [k_s[pl.ds(2 * big * cc, cc), :], k_s[pl.ds((2 * big + 1) * cc, cc), :]], axis=1
        )
        high, rest = halves(rows)
        x = nn(high, wave_ref[...]) + nn(rest, wave_ref[...])
        xc, xs = x[:, :BIG], x[:, BIG:]
        if big == 0:
            kh_ref[0, 0, :, :BIG] = xc + d_ref[0][:, 0:1]
            kh_ref[0, 0, :, BIG:] = xs
        else:
            kh_ref[0, big, :, :BIG] = xc + sign * before[1]
            kh_ref[0, big, :, BIG:] = xs - sign * before[0]
        before = (xc, xs)


def spectra(ld, w, d, wave):
    ch = 2 * ld.shape[1]
    cc = chunk_of(ch, 128)
    return pl.pallas_call(
        partial(spectra_body, cc),
        grid=(2, ch // cc),
        in_specs=[pl.BlockSpec((1, cc // 2, BLK), lambda k, i: (k, i, 0))] * 2
        + [
            pl.BlockSpec((1, cc, BLK), lambda k, i: (k, i, 0)),
            pl.BlockSpec((BIG, 2 * BIG), lambda k, i: (0, 0)),
        ],
        out_specs=pl.BlockSpec((1, LAGS, cc, 2 * BIG), lambda k, i: (k, 0, i, 0)),
        out_shape=jax.ShapeDtypeStruct((2, LAGS, ch, 2 * BIG), f32),
        scratch_shapes=[pltpu.VMEM((2 * LAGS * cc, BLK), f32)],
        compiler_params=params(40),
        cost_estimate=cost(2 * ch * 40e6, 2 * ch * LAGS * 2 * BIG * 4),
    )(ld, w, d, wave)


def moments_body(cc, ld_ref, gh_ref, back_ref, s0_ref, s1_ref, g0_ref, g_s):
    sign = jnp.where(lax.broadcasted_iota(jnp.int32, (cc, BIG), 1) % 2 == 0, 1.0, -1.0)
    count = 2 * LAGS
    for big in range(LAGS):
        c = gh_ref[0, big, :, :BIG]
        s = gh_ref[0, big, :, BIG:]
        if big < LAGS - 1:
            c, s = c - sign * gh_ref[0, big + 1, :, BIG:], s + sign * gh_ref[0, big + 1, :, :BIG]
        high, rest = halves(jnp.concatenate([c, s], axis=1))
        g = nn(high, back_ref[...]) + nn(rest, back_ref[...])
        g_s[pl.ds(2 * big * cc, cc), :] = g[:, :BLK]
        g_s[pl.ds((2 * big + 1) * cc, cc), :] = g[:, BLK:]
        if big == 0:
            g0_ref[0] = g[:, :BLK]
    t = lax.broadcasted_iota(jnp.int32, (BLK, BLK), 0).astype(f32)
    lane = lax.broadcasted_iota(jnp.int32, (count, BLK), 1)
    lag = lane.astype(f32)
    block = lax.broadcasted_iota(jnp.int32, (count, BLK), 0).astype(f32) * float(BLK)
    low = lane < STATE

    def one(p, carry):
        ld = ld_ref[0, pl.ds(p, 1), :]
        decay = jnp.exp2(t * ld).astype(bf16)
        far = jnp.exp2(block * ld)
        ga = g_s[pl.ds(2 * p, count, stride=cc), :]
        gb = g_s[pl.ds(2 * p + 1, count, stride=cc), :]
        high, rest = halves(jnp.concatenate([ga, gb, ga * lag, gb * lag], axis=0))
        m = nn(jnp.concatenate([high, rest], axis=0), decay)
        m = m[0 : 4 * count] + m[4 * count : 8 * count]
        m0 = jnp.where(low, m[0:count], m[count : 2 * count])
        m1 = jnp.where(low, m[2 * count : 3 * count], m[3 * count : 4 * count]) + block * m0
        s0_ref[0, pl.ds(p, 1), :] = jnp.sum(far * m0, axis=0, keepdims=True)
        s1_ref[0, pl.ds(p, 1), :] = jnp.sum(far * m1, axis=0, keepdims=True)
        return carry

    lax.fori_loop(0, cc // 2, one, 0, unroll=16)


def moments(k, ld, gh, back):
    ch = gh.shape[2]
    cc = chunk_of(ch, 128)
    row = pl.BlockSpec((1, cc // 2, BLK), lambda i: (0, i, 0))
    return pl.pallas_call(
        partial(moments_body, cc),
        grid=(ch // cc,),
        in_specs=[
            pl.BlockSpec((1, cc // 2, BLK), lambda i: (k, i, 0)),
            pl.BlockSpec((1, LAGS, cc, 2 * BIG), lambda i: (0, 0, i, 0)),
            pl.BlockSpec((2 * BIG, BIG), lambda i: (0, 0)),
        ],
        out_specs=[row, row, pl.BlockSpec((1, cc, BLK), lambda i: (0, i, 0))],
        out_shape=[jax.ShapeDtypeStruct((1, ch // 2, BLK), f32)] * 2
        + [jax.ShapeDtypeStruct((1, ch, BLK), f32)],
        scratch_shapes=[pltpu.VMEM((2 * LAGS * cc, BLK), f32)],
        compiler_params=params(40),
        cost_estimate=cost(ch * 40e6, ch * LAGS * 2 * BIG * 4),
    )(ld, gh, back)


def load_pieces(nb, pieces, cc, tab_ref, block, in_s, wave_ref, dst):
    for h in range(pieces):
        first = tab_ref[0, h]
        whole = tab_ref[1, h].astype(f32)
        in_s[pl.ds(h * cc, cc), 0:BLK] = block(first).astype(bf16)
        in_s[pl.ds(h * cc, cc), BLK:BIG] = (block(jnp.minimum(first + 1, nb - 1)) * whole).astype(bf16)
    for h in range(pieces):
        at = pl.ds(h * cc, cc)
        dst[at, :] = nn(in_s[at, :], wave_ref[...])


def over_pieces(nseq, cc, rg, seq_ref, piece):
    def group(r, carry):
        off = pl.multiple_of(r * rg, rg)
        for s in range(nseq):
            base = seq_ref[0, s]
            count = seq_ref[1, s]

            def outer(i, carry):
                piece(i, count, base, off)
                return carry

            lax.fori_loop(0, count, outer, 0)
        return carry

    lax.fori_loop(0, cc // rg, group, 0)


def scan_body(
    nb, nseq, cc, rg, tab_ref, seq_ref, a_ref, kh_ref, wave_ref, back_ref, gg_ref, y_ref, mix_ref, in_s, ah_s, yh_s, y_s
):
    pieces = (nb + nseq) // 2
    load_pieces(nb, pieces, cc, tab_ref, lambda b: a_ref[0, b].astype(f32), in_s, wave_ref, ah_s)
    zero = jnp.zeros((rg, BIG), f32)

    def products(flip):
        def piece(i, count, base, off):
            def inner(j, acc):
                yc, ys = acc
                other = (base + i + j) if flip else (base + i - j)
                m = pl.ds(pl.multiple_of(other * cc + off, rg), rg)
                rows = pl.ds(off, rg)
                ac = ah_s[m, :BIG]
                as_ = ah_s[m, BIG:]
                kc = kh_ref[0, j, rows, :BIG]
                ks = kh_ref[0, j, rows, BIG:]
                if flip:
                    return (yc + kc * ac + ks * as_, ys + kc * as_ - ks * ac)
                return (yc + kc * ac - ks * as_, ys + kc * as_ + ks * ac)

            yc, ys = lax.fori_loop(0, (count - i) if flip else (i + 1), inner, (zero, zero))
            at = pl.ds(pl.multiple_of((base + i) * cc + off, rg), rg)
            yh_s[at, :BIG] = yc.astype(bf16)
            yh_s[at, BIG:] = ys.astype(bf16)

        over_pieces(nseq, cc, rg, seq_ref, piece)

    @pl.when(pl.program_id(0) == 0)
    def _():
        products(False)

    @pl.when(pl.program_id(0) == 1)
    def _():
        products(True)

    for h in range(pieces):
        at = pl.ds(h * cc, cc)
        y_s[at, :] = nn(yh_s[at, :], back_ref[...])

    def one(b, y):
        y_ref[0, b] = y.astype(bf16)
        mix_ref[0, b] = (y * gg_ref[0, b].astype(f32)).astype(bf16)

    def last(h, carry):
        b = tab_ref[0, h]
        at = pl.ds(pl.multiple_of(h * cc, cc), cc)
        one(b, y_s[at, 0:BLK])

        @pl.when(tab_ref[1, h] == 1)
        def _():
            one(b + 1, y_s[at, BLK:])

        return carry

    lax.fori_loop(0, seq_ref[1, nseq], last, 0)
    nothing = jnp.zeros((cc, BLK), bf16)

    def fill(b, carry):
        y_ref[0, b] = nothing
        mix_ref[0, b] = nothing
        return carry

    lax.fori_loop(seq_ref[0, nseq], nb, fill, 0)


def back_body(
    nb, nseq, cc, rg, flip, tab_ref, seq_ref, a_ref, gm_ref, kh_ref, wave_ref, back_ref, gg_ref, y_ref, dg_ref, da_ref,
    gpg_ref, gp_ref, gh_ref, bs_ref, in_s, ah_s, gh_s, xh_s, x_s,
):
    pieces = (nb + nseq) // 2
    load_pieces(nb, pieces, cc, tab_ref, lambda b: a_ref[0, b].astype(f32), in_s, wave_ref, ah_s)
    load_pieces(
        nb, pieces, cc, tab_ref, lambda b: gm_ref[0, b].astype(f32) * gg_ref[0, b].astype(f32), in_s, wave_ref, gh_s
    )
    gh_ref[...] = jnp.zeros_like(gh_ref)
    zero = jnp.zeros((rg, BIG), f32)

    def piece(i, count, base, off):
        at = pl.ds(pl.multiple_of((base + i) * cc + off, rg), rg)
        ac = ah_s[at, :BIG]
        as_ = ah_s[at, BIG:]

        def inner(j, acc):
            xc, xs = acc
            other = (base + i - j) if flip else (base + i + j)
            m = pl.ds(pl.multiple_of(other * cc + off, rg), rg)
            rows = pl.ds(off, rg)
            gc = gh_s[m, :BIG]
            gs = gh_s[m, BIG:]
            kc = kh_ref[0, j, rows, :BIG]
            ks = kh_ref[0, j, rows, BIG:]
            gh_ref[0, j, rows, :BIG] += ac * gc + as_ * gs
            if flip:
                gh_ref[0, j, rows, BIG:] += gc * as_ - gs * ac
                return (xc + kc * gc - ks * gs, xs + kc * gs + ks * gc)
            gh_ref[0, j, rows, BIG:] += ac * gs - as_ * gc
            return (xc + kc * gc + ks * gs, xs + kc * gs - ks * gc)

        xc, xs = lax.fori_loop(0, (i + 1) if flip else (count - i), inner, (zero, zero))
        xh_s[at, :BIG] = xc.astype(bf16)
        xh_s[at, BIG:] = xs.astype(bf16)

    over_pieces(nseq, cc, rg, seq_ref, piece)

    for h in range(pieces):
        at = pl.ds(h * cc, cc)
        x_s[at, :] = nn(xh_s[at, :], back_ref[...])

    none = jnp.zeros((cc, BLK), f32)

    def one(b, gx, carry):
        s0, s1 = carry
        gpg = (y_ref[0, b].astype(f32) * gm_ref[0, b].astype(f32) * dg_ref[0, b].astype(f32)).astype(bf16)
        gpg_ref[0, b] = gpg
        gp = (gx * da_ref[0, b].astype(f32)).astype(bf16)
        gp_ref[0, b] = gp
        return (s0 + gpg.astype(f32), s1 + gp.astype(f32))

    def last(h, carry):
        b = tab_ref[0, h]
        at = pl.ds(pl.multiple_of(h * cc, cc), cc)
        carry = one(b, x_s[at, 0:BLK], carry)

        def more(kept):
            return one(b + 1, x_s[at, BLK:], kept)

        return lax.cond(tab_ref[1, h] == 1, more, lambda kept: kept, carry)

    s0, s1 = lax.fori_loop(0, seq_ref[1, nseq], last, (none, none))
    bs_ref[0, :, 0:BLK] = s0
    bs_ref[0, :, BLK:] = s1
    nothing = jnp.zeros((cc, BLK), bf16)

    def fill(b, carry):
        gpg_ref[0, b] = nothing
        gp_ref[0, b] = nothing
        return carry

    lax.fori_loop(seq_ref[0, nseq], nb, fill, 0)


def ssm_specs(shape, seq):
    _, nb, ch, _ = shape
    nseq = seq.shape[1] - 1
    pieces = (nb + nseq) // 2
    cc = chunk_of(ch, 128 if nb <= 32 else 64)
    big = pl.BlockSpec((1, nb, cc, BLK), lambda k, i: (k, 0, i, 0))
    spec = pl.BlockSpec((1, LAGS, cc, 2 * BIG), lambda k, i: (k, 0, i, 0))
    smem = pl.BlockSpec(memory_space=pltpu.SMEM)
    head = [smem, smem]
    tables = [pl.BlockSpec((BIG, 2 * BIG), lambda k, i: (0, 0)), pl.BlockSpec((2 * BIG, BIG), lambda k, i: (0, 0))]
    return nb, nseq, ch, cc, pieces * cc, big, spec, head, tables


def ssm_scan(tab, seq, a, kh, wave, back, gg):
    nb, nseq, ch, cc, size, big, spec, head, tables = ssm_specs(a.shape, seq)
    return pl.pallas_call(
        partial(scan_body, nb, nseq, cc, 32),
        grid=(2, ch // cc),
        in_specs=head + [big, spec] + tables + [big],
        out_specs=[big, big],
        out_shape=[jax.ShapeDtypeStruct(a.shape, bf16)] * 2,
        scratch_shapes=[
            pltpu.VMEM((size, BIG), bf16),
            pltpu.VMEM((size, 2 * BIG), f32),
            pltpu.VMEM((size, 2 * BIG), bf16),
            pltpu.VMEM((size, BIG), f32),
        ],
        compiler_params=params(56),
        cost_estimate=cost(2 * ch * 50e6, 2 * ch * nb * BLK * 8),
    )(tab, seq, a, kh, wave, back, gg)


def ssm_back(k, tab, seq, a, gm, kh, wave, back, gg, y, dg, da):
    nb, nseq, ch, cc, size, _, _, head, tables = ssm_specs(a.shape, seq)
    big = pl.BlockSpec((1, nb, cc, BLK), lambda i: (k, 0, i, 0))
    spec = pl.BlockSpec((1, LAGS, cc, 2 * BIG), lambda i: (k, 0, i, 0))
    out = pl.BlockSpec((1, nb, cc, BLK), lambda i: (0, 0, i, 0))
    out_spec = pl.BlockSpec((1, LAGS, cc, 2 * BIG), lambda i: (0, 0, i, 0))
    tables = [
        pl.BlockSpec((BIG, 2 * BIG), lambda i: (0, 0)),
        pl.BlockSpec((2 * BIG, BIG), lambda i: (0, 0)),
    ]
    return pl.pallas_call(
        partial(back_body, nb, nseq, cc, 64, k == 1),
        grid=(ch // cc,),
        in_specs=head + [big, big, spec] + tables + [big] * 4,
        out_specs=[out, out, out_spec, pl.BlockSpec((1, cc, 2 * BLK), lambda i: (0, i, 0))],
        out_shape=[jax.ShapeDtypeStruct((1,) + a.shape[1:], bf16)] * 2
        + [
            jax.ShapeDtypeStruct((1, LAGS, ch, 2 * BIG), f32),
            jax.ShapeDtypeStruct((1, ch, 2 * BLK), f32),
        ],
        scratch_shapes=[
            pltpu.VMEM((size, BIG), bf16),
            pltpu.VMEM((size, 2 * BIG), f32),
            pltpu.VMEM((size, 2 * BIG), f32),
            pltpu.VMEM((size, 2 * BIG), bf16),
            pltpu.VMEM((size, BIG), f32),
        ],
        compiler_params=params(60),
        cost_estimate=cost(ch * 80e6, ch * nb * BLK * 16),
    )(tab, seq, a, gm, kh, wave, back, gg, y, dg, da)


def stack_blocks(refs, many):
    return jnp.concatenate(
        [
            jnp.concatenate([ref[k, b] for b in range(many)], axis=1)
            for ref in refs
            for k in range(ref.shape[0])
        ],
        axis=0,
    )


def mul_body(count, more, many, start_ref, w_ref, *refs):
    out = nn(w_ref[...], stack_blocks(refs[:count], many))
    o_ref = refs[-1]
    for h in range(many):
        part = out[:, h * BLK : (h + 1) * BLK]
        if more:
            part = part + refs[count][h].astype(f32)
        o_ref[h] = part.astype(o_ref.dtype)


def mul_rows(w, arrays, start, many, dtype=bf16, extra=None):
    width, deep = w.shape
    ch = arrays[0].shape[2]
    count = len(arrays)
    step = 4
    out = pl.BlockSpec((step, width, BLK), lambda i, at: (i, 0, 0))
    return pl.pallas_call(
        partial(mul_body, count, extra is not None, step),
        grid_spec=pltpu.PrefetchScalarGridSpec(
            num_scalar_prefetch=1,
            grid=(many // step,),
            in_specs=[pl.BlockSpec((width, deep), lambda i, at: (0, 0))]
            + [pl.BlockSpec((x.shape[0], step, ch, BLK), lambda i, at: (0, at[0] + i, 0, 0)) for x in arrays]
            + ([] if extra is None else [out]),
            out_specs=out,
        ),
        out_shape=jax.ShapeDtypeStruct((many, width, BLK), dtype),
        compiler_params=params(40),
        cost_estimate=cost(2 * many * BLK * width * deep, 2 * many * BLK * (2 * width + deep)),
    )(start // step, w, *arrays, *([] if extra is None else [extra]))


def outer_body(ch, many, cuts, parts, at_ref, *refs):
    step = pl.program_id(0)
    xs, gs = refs[:parts], refs[parts : 2 * parts]
    gp_refs, gpg_refs, mix_ref = refs[2 * parts : 2 * parts + 2], refs[2 * parts + 2 : 2 * parts + 4], refs[2 * parts + 4]
    outs = refs[2 * parts + 5 : 2 * parts + 5 + cuts]
    acc_s, x_s, g_s = refs[-3:]

    def fill(at):
        for b in range(many):
            x_s[:, b * BLK : (b + 1) * BLK] = xs[at][b]
            g_s[:, b * BLK : (b + 1) * BLK] = gs[at][b]

    if parts == 1:
        fill(0)
    else:
        for at in range(parts):

            @pl.when(step == at)
            def _(at=at):
                fill(at)

    def part(ref, k):
        return jnp.concatenate([ref[k, b] for b in range(many)], axis=1)

    @pl.when(step == 0)
    def _():
        acc_s[...] = jnp.zeros_like(acc_s)

    split = 4 * ch
    left = jnp.concatenate([part(ref, 0) for ref in (*gp_refs, *gpg_refs)], axis=0)
    acc_s[:, :split] += nt(x_s[...], left)
    acc_s[:, split:] += nt(g_s[...], jnp.concatenate([part(mix_ref, 0), part(mix_ref, 1)], axis=0))

    @pl.when(step == pl.num_programs(0) - 1)
    def _():
        deep = acc_s.shape[0] // cuts
        for cut in range(cuts):
            start = pl.multiple_of(at_ref[pl.num_programs(0) + cut] * deep, 8)
            outs[cut][...] = acc_s[pl.ds(start, deep), :].astype(bf16)


def outer_sums(order, cuts, xs, gs, gp, gpg, mix):
    width = xs[0].shape[1]
    _, nb, ch, _ = mix.shape
    many = 8
    parts = len(xs)
    if parts == 1:
        rows = pl.BlockSpec((many, width, BLK), lambda i, at: (i, 0, 0))
    else:
        rows = pl.BlockSpec((many, width, BLK), lambda i, at: (0, 0, 0), pipeline_mode=pl.Buffered(1))
    chan = pl.BlockSpec((2, many, ch, BLK), lambda i, at: (0, at[i], 0, 0))
    one = pl.BlockSpec((1, many, ch, BLK), lambda i, at: (0, at[i], 0, 0))
    tok = nb * BLK
    return pl.pallas_call(
        partial(outer_body, ch, many, cuts, parts),
        grid_spec=pltpu.PrefetchScalarGridSpec(
            num_scalar_prefetch=1,
            grid=(nb // many,),
            in_specs=[rows] * (2 * parts) + [one] * 4 + [chan],
            out_specs=[pl.BlockSpec((width // cuts, 6 * ch), lambda i, at: (0, 0))] * cuts,
            scratch_shapes=[
                pltpu.VMEM((width, 6 * ch), f32),
                pltpu.VMEM((width, many * BLK), bf16),
                pltpu.VMEM((width, many * BLK), bf16),
            ],
        ),
        out_shape=[jax.ShapeDtypeStruct((width // cuts, 6 * ch), bf16)] * cuts,
        compiler_params=params(60),
        cost_estimate=cost(12 * tok * width * ch, tok * (4 * width + 12 * ch)),
    )(order, *xs, *gs, *gp, *gpg, mix)


def join_body(parts, split, at_ref, *refs):
    head_ref, tail_ref, head_t_ref, tail_t_ref = refs[parts:]
    deep = refs[0].shape[0]
    for at in range(parts):
        rows = pl.ds(pl.multiple_of(at_ref[at] * deep, 16), deep)
        head_ref[rows, :] = refs[at][:, :split]
        tail_ref[rows, :] = refs[at][:, split:]
    head_t_ref[...] = head_ref[...].T
    tail_t_ref[...] = tail_ref[...].T


def join_weights(order, parts, split):
    count = len(parts)
    deep, wide = parts[0].shape
    rows = deep * count
    vmem = pl.BlockSpec(memory_space=pltpu.VMEM)
    return pl.pallas_call(
        partial(join_body, count, split),
        in_specs=[pl.BlockSpec(memory_space=pltpu.SMEM)] + [vmem] * count,
        out_specs=[vmem] * 4,
        out_shape=[
            jax.ShapeDtypeStruct(shape, bf16)
            for shape in ((rows, split), (rows, wide - split), (split, rows), (wide - split, rows))
        ],
        compiler_params=params(48),
        cost_estimate=cost(0, 6 * rows * wide),
    )(order, *parts)


def meet_body(axes, rank_ref, x_ref, chan_ref, norm_ref, got_ref, call_ref, nall_ref, send_s, *sems):
    xs_sem, xr_sem, cs_sem, cr_sem, ns_sem, nr_sem, own_sem = sems
    q, c, h, w = (lax.axis_index(name) for name in axes)
    rows = x_ref.shape[0]
    piece = rows // 8
    flat = ((2 * q + c) * 2 + h) * 2 + w

    def peer(bits):
        return (q ^ (bits // 8), c ^ (bits // 4 % 2), h ^ (bits // 2 % 2), w ^ (bits % 2))

    barrier = pltpu.get_barrier_semaphore()
    for bits in range(1, 32):
        pl.semaphore_signal(barrier, inc=1, device_id=peer(bits), device_id_type=pl.DeviceIdType.MESH)
    pl.semaphore_wait(barrier, 31)

    def remote(src, dst, send, recv, to):
        return pltpu.make_async_remote_copy(
            src_ref=src, dst_ref=dst, send_sem=send, recv_sem=recv, device_id=to, device_id_type=pl.DeviceIdType.MESH
        )

    nall_ref[flat] = norm_ref[...]

    def norm_copy(bits):
        return remote(norm_ref, nall_ref.at[flat], ns_sem.at[bits], nr_sem.at[bits], peer(bits))

    for bits in range(1, 32):
        norm_copy(bits).start()

    place = 2 * (1 - c) + w
    spot_c = 4 * c + 2 * h + w

    def chan_copy(at):
        to = (q ^ at, 1 - q // 2, h, q % 2) if at < 4 else (2 * c + w, 1 - q // 2, 1 - h, q % 2)
        return remote(chan_ref, call_ref.at[spot_c], cs_sem.at[at], cr_sem.at[spot_c], to)

    def own_chan():
        return pltpu.make_async_copy(chan_ref, call_ref.at[spot_c], own_sem.at[1])

    def chan_came(at):
        return remote(chan_ref, call_ref.at[at], cs_sem.at[0], cr_sem.at[at], peer(1))

    far_spot = 4 * (q // 2) + 2 * (1 - h) + q % 2

    def chan_pass(bits):
        return remote(
            call_ref.at[far_spot], call_ref.at[far_spot], cs_sem.at[4 + bits], cr_sem.at[far_spot], (q ^ bits, c, h, w)
        )

    for at in (4, 1, 2, 3, 0):
        if at:
            chan_copy(at).start()
        else:

            @pl.when(place == q)
            def _():
                own_chan().start()

            @pl.when(place != q)
            def _():
                chan_copy(0).start()

    pieces = [(kq, kh) for kh in (1, 0) for kq in (1, 2, 3, 0)]
    spot = lax.broadcasted_iota(jnp.int32, (piece, rows), 0)

    def row_copy(kq, kh):
        at = 2 * kq + kh
        return remote(
            send_s.at[at], got_ref.at[2 * q + c], xs_sem.at[at], xr_sem.at[2 * kq + c], (q ^ kq, 1 - h, h ^ kh, w)
        )

    def own_copy():
        return pltpu.make_async_copy(send_s.at[0], got_ref.at[2 * q + c], own_sem.at[0])

    for kq, kh in pieces:
        chunk = 2 * (q ^ kq) + (h ^ kh)
        pick = jnp.where(spot + chunk * piece == rank_ref[...], 1.0, 0.0).astype(bf16)
        send_s[2 * kq + kh] = nn(pick, x_ref[...]).astype(bf16)
        if (kq, kh) == (0, 0):

            @pl.when(c != h)
            def _():
                own_copy().start()

            @pl.when(c == h)
            def _():
                row_copy(0, 0).start()

        else:
            row_copy(kq, kh).start()

    for bits in range(1, 32):
        norm_copy(bits).wait()
    for at in range(8):

        @pl.when((c != h) & (at == c))
        def _():
            own_copy().wait()

        @pl.when(jnp.logical_not((c != h) & (at == c)))
        def _(at=at):
            remote(send_s.at[at], got_ref.at[at], xs_sem.at[at], xr_sem.at[at], peer(1)).wait_recv()

    chan_came(far_spot).wait_recv()
    for bits in range(1, 4):
        chan_pass(bits).start()
    for at in range(8):

        @pl.when((place == q) & (at == spot_c))
        def _():
            own_chan().wait()

        @pl.when(jnp.logical_not((place == q) & (at == spot_c)) & (at != far_spot))
        def _(at=at):
            chan_came(at).wait_recv()

    for bits in range(1, 4):
        chan_pass(bits).wait_send()
    for kq, kh in pieces:
        if (kq, kh) == (0, 0):

            @pl.when(c == h)
            def _():
                row_copy(0, 0).wait_send()

        else:
            row_copy(kq, kh).wait_send()
    for at in range(1, 5):
        chan_copy(at).wait_send()

    @pl.when(place != q)
    def _():
        chan_copy(0).wait_send()


def meet(axes, rank, x, chan, norm):
    rows, width = x.shape
    vmem = pl.BlockSpec(memory_space=pltpu.VMEM)
    sem = pltpu.SemaphoreType.DMA
    return pl.pallas_call(
        partial(meet_body, axes),
        in_specs=[vmem] * 4,
        out_specs=[vmem] * 3,
        out_shape=[
            jax.ShapeDtypeStruct((8, rows // 8, width), bf16),
            jax.ShapeDtypeStruct((8,) + chan.shape, f32),
            jax.ShapeDtypeStruct((32,) + norm.shape, f32),
        ],
        scratch_shapes=[pltpu.VMEM((8, rows // 8, width), bf16)]
        + [sem((8,)), sem((8,)), sem((8,)), sem((8,)), sem((32,)), sem((32,)), sem((2,))],
        compiler_params=pltpu.CompilerParams(collective_id=1, has_side_effects=True, vmem_limit_bytes=60 * MIB),
        cost_estimate=cost(2 * rows * rows * width, 100 * rows * width),
    )(rank.reshape(1, rows), x, chan, norm)


def sequence_tables(lens, nb):
    nseq = lens.shape[0]
    blocks = (lens + BLK - 1) // BLK
    start = jnp.cumsum(blocks) - blocks
    bigs = (blocks + 1) // 2
    first_big = jnp.cumsum(bigs) - bigs
    h = jnp.arange((nb + nseq) // 2, dtype=jnp.int32)
    owner = (h[:, None] >= first_big[None, :]).astype(jnp.int32).sum(axis=1) - 1
    mine = owner[:, None] == jnp.arange(nseq, dtype=jnp.int32)[None, :]

    def at_owner(values):
        return jnp.sum(jnp.where(mine, values[None, :], 0), axis=1)

    rel = h - at_owner(first_big)
    first = jnp.minimum(at_owner(start) + 2 * rel, nb - 1)
    whole = (2 * rel + 1 < at_owner(blocks)).astype(jnp.int32)
    tab = jnp.stack([first, whole]).astype(jnp.int32)
    seq = jnp.stack(
        [jnp.append(first_big, jnp.sum(blocks)), jnp.append(bigs, jnp.sum(bigs))]
    ).astype(jnp.int32)
    return tab, seq


def live_rows(lens, rows):
    slot = (lens + BLK - 1) // BLK * BLK
    begin = jnp.cumsum(slot) - slot
    pos = jnp.arange(rows, dtype=jnp.int32)
    inside = (pos[:, None] >= begin[None, :]) & (pos[:, None] < (begin + lens)[None, :])
    return jnp.sum(inside.astype(f32), axis=1)


def after(values):
    return lax.optimization_barrier(values)


def rank_of(keys):
    return jnp.sum((keys[None, :] < keys[:, None]).astype(jnp.int32), axis=1)


class Line:
    def __init__(self, n_dp, n_t):
        self.n_dp, self.n_t = n_dp, n_t
        self.axes = {"dp": n_dp, "tensor": n_t}
        self.both = ("dp", "tensor")
        self.cuts = 1

    def place_of_group(self):
        return lax.axis_index("tensor")

    def gather_first(self, x):
        return [lax.all_gather(x, "tensor", axis=0, tiled=True)]

    def gathered(self, x, early):
        return []

    def gather_last(self, x, got):
        return [(got[0], jnp.zeros((1,), jnp.int32))]

    def scatter_first(self, w, arrays, many):
        return [mul_rows(w, arrays, jnp.zeros((1,), jnp.int32), many * self.n_t)]

    def scatter_send(self, parts):
        return [lax.psum_scatter(parts[0], "tensor", scatter_dimension=0, tiled=True)]

    def scatter_own(self, w, arrays, many):
        return []

    def regroup(self, x):
        return x

    def ungroup(self, x):
        return x

    def spread(self, x):
        return lax.all_to_all(x, "dp", split_axis=0, concat_axis=0, tiled=True)

    def order(self, pieces):
        return jnp.append(jnp.arange(pieces * self.n_t, dtype=jnp.int32), 0)

    def enter(self, rank, x, chan, norm):
        (sent,) = permute_to(rank, [x])
        return (self.spread(sent),) + self.gather_channels(chan, norm)

    def weights_first(self, pack):
        return [pack]

    def weights_send(self, packs):
        return [lax.all_gather(packs[0], "dp", axis=0, tiled=True)]

    def gather_channels(self, chan, norm):
        perm = [(f, (f % self.n_dp) * self.n_t + f // self.n_dp) for f in range(self.n_dp * self.n_t)]
        chan = lax.ppermute(chan, self.both, perm)
        norm = lax.all_gather(norm, self.both, axis=1, tiled=True)
        return lax.all_gather(chan[None], "dp", axis=0, tiled=True), norm

    def cut_order(self):
        return jnp.zeros((1,), jnp.int32)

    def grads_send(self, gw):
        return [lax.psum_scatter(gw[0], "dp", scatter_dimension=0, tiled=True)]

    def grads_last(self, parts):
        return parts[0], lambda part: part.astype(f32)

    def scatter_small(self, sums, norm):
        sums = lax.psum_scatter(sums, "dp", scatter_dimension=0, tiled=True)
        norm = lax.psum_scatter(norm, self.both, scatter_dimension=1, tiled=True)
        perm = [((f % self.n_dp) * self.n_t + f // self.n_dp, f) for f in range(self.n_dp * self.n_t)]
        return (sums, norm), lambda part: (lax.ppermute(part[0], self.both, perm), part[1])


class Pairs:
    def __init__(self, n_dp, n_t):
        self.quads = n_dp // 2
        self.axes = {"q": self.quads, "c": 2, "h": 2, "w": 2}
        self.both = ("q", "c", "h", "w")
        self.cuts = self.quads
        self.other = [(0, 1), (1, 0)]
        self.there = [(2 * c + h, 2 * (1 - h) + c) for c in range(2) for h in range(2)]
        self.back = [(b, a) for a, b in self.there]
        self.turned = [(2 * c + h, 2 * (1 - h) + 1 - c) for c in range(2) for h in range(2)]

    def flip(self, x, axis, bit=1):
        return lax.ppermute(x, axis, [(i, i ^ bit) for i in range(self.axes[axis])])

    def place_of_group(self):
        return 2 * (1 - lax.axis_index("c")) + lax.axis_index("w")

    def regroup(self, x):
        return lax.ppermute(x, ("c", "h"), self.there)

    def ungroup(self, x):
        return lax.ppermute(x, ("c", "h"), self.back)

    def spread(self, x):
        return lax.all_to_all(x, ("q", "c"), split_axis=0, concat_axis=0, tiled=True)

    def places(self):
        c, w = lax.axis_index("c"), lax.axis_index("w")
        return [2 * (1 - c) + w, 2 * c + w, 2 * (1 - c) + 1 - w, 2 * c + 1 - w]

    def starts(self, many):
        return [(place * many).astype(jnp.int32).reshape(1) for place in self.places()]

    def gather_first(self, x):
        return [self.flip(x, "c"), self.flip(x, "w")]

    def gathered(self, x, early):
        return list(zip([x] + early, self.starts(x.shape[0])))

    def gather_last(self, x, got):
        beside, near = got
        return list(zip([x, beside, near, self.flip(near, "c")], self.starts(x.shape[0])))

    def scatter_first(self, w, arrays, many):
        _, beside, near, far = self.starts(many)
        first = mul_rows(w, arrays, far, many)
        give = self.flip(first, "c")
        beside, first = after((beside, first))
        second = mul_rows(w, arrays, beside, many)
        second, give = after((second, give))
        return [second, mul_rows(w, arrays, near, many, extra=give)]

    def scatter_send(self, parts):
        return [self.flip(parts[0], "c"), self.flip(parts[1], "w")]

    def scatter_own(self, w, arrays, many):
        return [mul_rows(w, arrays, self.starts(many)[0], many, dtype=f32)]

    def order(self, pieces):
        place = jnp.stack(self.places())[:, None] * pieces + jnp.arange(pieces)[None, :]
        return jnp.concatenate([place.reshape(-1).astype(jnp.int32), self.cut_order()])

    def steps(self):
        bit = self.quads // 2
        while bit:
            yield "q", bit
            bit //= 2
        yield "h", 1

    def spot(self):
        return 2 * lax.axis_index("q") + lax.axis_index("h")

    def enter(self, rank, x, chan, norm):
        small = norm.shape[1]
        norm = jnp.pad(norm, ((0, 5), (0, BLK - small)))
        got, chan, norm = meet(self.both, rank, x, chan, norm)
        norm = norm[:, :3, :small].transpose(1, 0, 2).reshape(3, -1)
        return got.reshape(x.shape), chan, norm

    def weights_first(self, pack):
        return [self.regroup(pack), lax.ppermute(pack, ("c", "h"), self.turned)]

    def weights_send(self, packs):
        h = lax.axis_index("h")
        first, second = packs
        pair = jnp.concatenate([jnp.where(h == 0, first, second), jnp.where(h == 0, second, first)], axis=0)
        return [pair] + [self.flip(pair, "q", bit) for bit in range(1, self.quads)]

    def grads_send(self, gw):
        return [gw[0]] + [self.flip(gw[bit], "q", bit) for bit in range(1, self.quads)]

    def grads_last(self, parts):
        total = parts[0].astype(f32)
        for part in parts[1:]:
            total = total + part.astype(f32)
        total = total.astype(bf16)
        half = total.shape[0] // 2
        h = lax.axis_index("h")
        first = jnp.where(h == 0, total[:half], total[half:])
        second = jnp.where(h == 0, total[half:], total[:half])

        def finish(parts):
            return self.ungroup(parts[0]).astype(f32) + lax.ppermute(parts[1], ("c", "h"), self.turned).astype(f32)

        return (first, second), finish

    def cut_order(self):
        return (lax.axis_index("q") ^ jnp.arange(self.quads)).astype(jnp.int32)

    def scatter_small(self, sums, norm):
        count = 2 * self.quads
        rows, wide = sums.shape[0] // count, sums.shape[1]
        norm = norm.reshape(3, 4 * count, -1).transpose(1, 0, 2)
        small = norm.shape[2]
        norm = jnp.pad(norm, ((0, 0), (0, 5), (0, BLK - small)))
        norm = lax.all_to_all(norm, self.both, split_axis=0, concat_axis=0, tiled=True)
        flat = jnp.pad(sums, ((0, 0), (0, -wide % 8))).reshape(count, -1, BLK)
        near = jnp.arange(self.quads) ^ lax.axis_index("q")
        h = lax.axis_index("h")
        keep, give = jnp.take(flat, 2 * near + h, axis=0), jnp.take(flat, 2 * near + 1 - h, axis=0)

        def finish(parts):
            keep, give, norm = parts
            part = keep + self.flip(give, "h")
            total = None
            for apart in range(self.quads):
                perm = []
                for source in range(4 * count):
                    q, c, h, w = source // 8, source // 4 % 2, source // 2 % 2, source % 2
                    perm.append((source, count * (2 * (1 - c) + w) + 2 * (q ^ apart) + h))
                got = lax.ppermute(part[apart], self.both, perm)
                total = got if total is None else total + got
            return total.reshape(rows, -1)[:, :wide], jnp.sum(norm, axis=0)[:3, :small]

        return (keep, give, norm), finish


def local(
    net, wave, tokens, cotangent, source, target, lengths, ln_gain, ln_bias, w_fwd, b_fwd, w_bwd, b_bwd,
    w_gate, b_gate, w_out, b_out, log_dt, log_rate, ssm_b, ssm_c, ssm_d,
):
    rows, width = tokens.shape
    many = rows // BLK
    n_t = net.n_t
    group = rows * n_t
    nb = group // BLK
    ch = w_fwd.shape[1]
    back = (wave.T / BIG).astype(bf16)
    wave = wave.astype(bf16)

    def lanes(column):
        return jnp.broadcast_to(column[..., None], column.shape + (BLK,))

    def decays(log_dt, log_rate, ssm_b):
        rate = jnp.exp(log_rate)
        ld = -jnp.exp(log_dt)[..., None] * rate
        return rate, ld, (1.0 - jnp.exp(ld)) / rate * ssm_b

    rank = rank_of(target)
    sender = source // group
    place = rank_of(sender * rows + jnp.arange(rows, dtype=jnp.int32))
    pack = jnp.concatenate(
        [w_fwd, w_bwd, w_gate.reshape(-1, 2 * ch), w_out.transpose(2, 0, 1).reshape(-1, 2 * ch)], axis=1
    )
    table = net.regroup(jnp.concatenate([place, lengths[0]]))
    rate, ld, drive = decays(log_dt, log_rate, ssm_b)
    own = b_fwd.shape[0]
    small = jnp.concatenate([ssm_d, b_fwd[None], b_bwd[None], b_gate])
    chan = jnp.concatenate(
        [
            (ld * log2e).reshape(own, 2 * STATE),
            (ssm_c * drive).reshape(own, 2 * STATE),
            jnp.pad(small, ((0, -(2 * own + 6) % 8 + 0), (0, 2 * STATE - own))),
        ]
    )
    norm = jnp.stack([ln_gain, ln_bias, b_out])
    (sent_g,) = permute_to(rank, [cotangent])
    sent_g, tokens = after((sent_g, tokens))
    got_g = net.spread(sent_g)
    got_x, chan_all, norm_all = net.enter(rank, tokens, chan, norm)
    got_x, got_g, chan_all, norm_all, pack, table = after((got_x, got_g, chan_all, norm_all, pack, table))
    packs = net.weights_first(pack)

    place, lens = table[:rows], table[rows:]
    gain = lanes(norm_all[0])
    shift = lanes(norm_all[1])
    small = chan_all[:, 2 * own : 2 * own + 6, :own].transpose(1, 0, 2).reshape(6, ch)

    def pairs(at):
        both = chan_all[:, at : at + own].reshape(-1, 2, own // 2, 2 * STATE)
        return both.transpose(1, 0, 2, 3).reshape(2, ch // 2, 2 * STATE)

    ld_pairs = pairs(0)
    w_pairs = pairs(own)
    skip = lanes(small[0:2])

    xt, xd = deal_x(place, got_x, gain, shift)
    x_got = net.gather_first(xt)
    _, ld_pairs, w_pairs, skip, packs = after((xt, ld_pairs, w_pairs, skip, packs))
    w_parts = net.weights_send(packs)
    kh = spectra(ld_pairs, w_pairs, skip, wave)
    kh, lens, small, norm_all = after((kh, lens, small, norm_all))
    live = live_rows(lens, group)
    live_own = lax.dynamic_slice_in_dim(live, net.place_of_group() * rows, rows, 0).reshape(many, 1, BLK)
    live = live.reshape(nb // 2, 1, BIG)
    tab, seq = sequence_tables(lens, nb)
    bias_in = lanes(small[2:6].reshape(-1))
    bias_out = lanes(norm_all[2])
    made = (bias_in, bias_out, tab, seq, live, live_own, net.cut_order(), net.order(many // 8))
    w_parts, x_got, kh, got_g, made = after((w_parts, x_got, kh, got_g, made))
    bias_in, bias_out, tab, seq, live, live_own, cut_order, order = made
    got_g = net.regroup(got_g)
    w_in, w_back, w_in_t, w_back_t = join_weights(cut_order, w_parts, 4 * ch)
    xs = net.gather_last(xt, x_got)
    kept = None
    for part, start in xs:
        kept = project(part, start, nb, live, w_in_t, bias_in, kept)
    kept, got_g = after((kept, got_g))
    a, da, gg, dg = kept
    gt, gd, g_bias_out = deal_g(place, got_g, live_own)
    gt, a = after((gt, a))
    g_got = net.gather_first(gt)
    y, mix = ssm_scan(tab, seq, a, kh, wave, back, gg)
    g_got, y, mix = after((g_got, y, mix))
    gs = net.gather_last(gt, g_got)
    branch = net.scatter_first(w_back, [mix], many)
    gm = gate_grad(gs, nb, w_back_t)
    branch, gm = after((branch, gm))

    branch = net.scatter_send(branch)
    branch = net.scatter_own(w_back, [mix], many) + branch
    first = ssm_back(0, tab, seq, a, gm, kh, wave, back, gg, y, dg, da)
    branch, first, a = after((branch, first, a))
    sent_out = layer_rows(place, branch, xd, live_own, bias_out)
    sent_out, a = after((sent_out, a))
    sent_out = net.ungroup(sent_out)
    second = ssm_back(1, tab, seq, a, gm, kh, wave, back, gg, y, dg, da)
    sent_out, first, second = after((sent_out, first, second))
    gpg, gp, gh, bsum = zip(first, second)
    sent_out = net.spread(sent_out)
    back_list = [gp[0], gp[1], gpg[0], gpg[1]]
    g_normed = net.scatter_first(w_in, back_list, many)
    g_normed, back_list, mix = after((g_normed, back_list, mix))
    gp, gpg = back_list[:2], back_list[2:]
    g_normed = net.scatter_send(g_normed)
    g_normed = net.scatter_own(w_in, back_list, many) + g_normed
    gw = outer_sums(order, net.cuts, [part for part, _ in xs], [part for part, _ in gs], gp, gpg, mix)
    g_normed, gw, gh, sent_out = after((g_normed, gw, gh, sent_out))
    sent_in, norm_sums = input_rows(place, g_normed, xd, gd, gain)
    sent_in, gh, gw, norm_sums, sent_out, bsum = after((sent_in, gh, gw, norm_sums, sent_out, bsum))
    sent_in = net.ungroup(sent_in)
    gw = net.grads_send(gw)
    s0, s1, g0 = [jnp.concatenate(part) for part in zip(*[moments(k, ld_pairs, gh[k], back) for k in range(2)])]
    layer_out = permute_from(rank, sent_out)

    s0 = s0.reshape(2, ch, STATE)
    s1 = s1.reshape(2, ch, STATE)
    bsum = jnp.concatenate(bsum)
    gb_gate = jnp.sum(bsum[:, :, :BLK], axis=2)
    gb_in = jnp.sum(bsum[:, :, BLK:], axis=2)
    sums = jnp.concatenate(
        [s0[0], s0[1], s1[0], s1[1], jnp.concatenate([g0[:, :, 0], gb_gate, gb_in], axis=0).T], axis=1
    )
    norm_sums = jnp.sum(jnp.concatenate([norm_sums, g_bias_out[None]], axis=0), axis=2)
    part, finish = net.scatter_small(sums, norm_sums)
    gw, gw_finish = net.grads_last(gw)
    sent_in, gw, part, layer_out = after((sent_in, gw, part, layer_out))
    in_grad = permute_from(rank, net.spread(sent_in))
    gw = gw_finish(gw)
    sums, norm_sums = finish(part)
    s0 = jnp.stack([sums[:, :STATE], sums[:, STATE : 2 * STATE]])
    s1 = jnp.stack([sums[:, 2 * STATE : 3 * STATE], sums[:, 3 * STATE : 4 * STATE]])
    tail = sums[:, 4 * STATE :].T
    step = jnp.exp(log_dt)[..., None]
    g_c = s0 * drive
    g_drive = s0 * ssm_c
    g_b = g_drive * (1.0 - jnp.exp(ld)) / rate
    g_ld = s1 * ssm_c * drive - g_drive * ssm_b / rate * jnp.exp(ld)
    g_rate = -g_drive * drive / rate - g_ld * step
    g_dt = jnp.sum(g_ld * ld, axis=2)
    return (
        layer_out,
        in_grad,
        norm_sums[0],
        norm_sums[1],
        gw[:, :ch],
        tail[4],
        gw[:, ch : 2 * ch],
        tail[5],
        gw[:, 2 * ch : 4 * ch].reshape(-1, 2, ch),
        tail[2:4],
        gw[:, 4 * ch :].T.reshape(2, ch, -1),
        norm_sums[2],
        g_dt,
        g_rate * rate,
        g_b,
        g_c,
        tail[0:2],
    )


def solution(mesh):
    n_dp, n_t = mesh.shape["dp"], mesh.shape["tensor"]
    if n_t == 4 and n_dp == 8:
        net = Pairs(n_dp, n_t)
        dp, tensor = ("q", "c"), ("h", "w")
    else:
        net = Line(n_dp, n_t)
        dp, tensor = ("dp",), ("tensor",)
    net.n_t = n_t
    mesh = jax.sharding.Mesh(mesh.devices.reshape(tuple(net.axes.values())), tuple(net.axes))
    both = P(dp + tensor)
    rows = P(dp + tensor, None)
    pair = P(None, dp + tensor)
    state = P(None, dp + tensor, None)
    proj = P(dp, tensor)
    gate = P(dp, None, tensor)
    out = P(None, tensor, dp)
    wave = wave_table()

    def run(*args):
        return local(net, jnp.asarray(wave), *args)

    return jax.shard_map(
        run,
        mesh=mesh,
        in_specs=(
            rows, rows, both, both, P(dp, None), both, both, proj, both, proj, both, gate, pair, out, both,
            pair, state, state, state, pair,
        ),
        out_specs=(
            rows, rows, both, both, proj, both, proj, both, gate, pair, out, both, pair, state, state, state, pair,
        ),
        check_vma=False,
    )
```

```python
from functools import partial

import jax
import jax.numpy as jnp
import numpy as np
from jax import lax
from jax.experimental import pallas as pl
from jax.experimental.pallas import tpu as pltpu
from jax.sharding import PartitionSpec as P

BLK = 128
BIG = 256
MOST = 2048
LAGS = MOST // BIG
STATE = 64
epsilon = 1e-05
log2e = 1.4426950408889634
f32 = jnp.float32
bf16 = jnp.bfloat16
MIB = 2**20


def nn(a, b):
    return lax.dot_general(a, b, (((1,), (0,)), ((), ())), preferred_element_type=f32)


def nt(a, b):
    return lax.dot_general(a, b, (((1,), (1,)), ((), ())), preferred_element_type=f32)


def params(limit):
    return pltpu.CompilerParams(vmem_limit_bytes=60 * MIB)


def cost(flops, moved, trans=0):
    scale = 0.05
    return pl.CostEstimate(
        flops=int(scale * flops), bytes_accessed=int(scale * moved), transcendentals=int(scale * trans)
    )


def halves(x):
    high = x.astype(bf16)
    return high, (x - high.astype(f32)).astype(bf16)


def wave_table():
    pos = np.arange(BIG)[:, None]
    freq = np.arange(BIG)[None, :]
    angle = 2 * np.pi * ((2 * freq + 1) * pos % (4 * BIG)) / (4 * BIG)
    return np.concatenate([np.cos(angle), np.sin(angle)], 1).astype(np.float32)


def chunk_of(channels, most):
    best = 16
    for size in range(16, most + 1, 16):
        if channels % size == 0:
            best = size
    return best


def permute_row_body(count, rank_ref, *refs):
    rows = rank_ref.shape[1]
    spot = lax.broadcasted_iota(jnp.int32, (rows, rows), 0)
    pick = jnp.where(spot == rank_ref[...], 1.0, 0.0).astype(bf16)
    for at in range(count):
        refs[count + at][...] = nn(pick, refs[at][...]).astype(bf16)


def permute_to(rank, arrays):
    rows, width = arrays[0].shape
    count = len(arrays)
    return pl.pallas_call(
        partial(permute_row_body, count),
        out_shape=[jax.ShapeDtypeStruct((rows, width), bf16)] * count,
        compiler_params=params(48),
        cost_estimate=cost(2 * count * rows * rows * width, 4 * count * rows * width),
    )(rank.reshape(1, rows), *arrays)


def permute_col_body(rank_ref, x_ref, o_ref):
    rows = x_ref.shape[0]
    spot = lax.broadcasted_iota(jnp.int32, (rows, rows), 1)
    pick = jnp.where(spot == rank_ref[...], 1.0, 0.0).astype(bf16)
    o_ref[...] = nn(pick, x_ref[...]).astype(bf16)


def permute_from(rank, x):
    rows, width = x.shape
    return pl.pallas_call(
        permute_col_body,
        out_shape=jax.ShapeDtypeStruct((rows, width), bf16),
        compiler_params=params(48),
        cost_estimate=cost(2 * rows * rows * width, 4 * rows * width),
    )(rank.reshape(rows, 1), x)


def pick_rows(place_ref, x_ref):
    spot = lax.broadcasted_iota(jnp.int32, (BLK, x_ref.shape[0]), 1)
    pick = jnp.where(spot == place_ref[...], 1.0, 0.0).astype(bf16)
    return nn(pick, x_ref[...]).T


def deal_x_body(place_ref, x_ref, gain_ref, shift_ref, xt_ref, xd_ref):
    x = pick_rows(place_ref, x_ref)
    xd_ref[0] = x.astype(bf16)
    centred = x - jnp.mean(x, axis=0, keepdims=True)
    inv_std = lax.rsqrt(jnp.mean(centred * centred, axis=0, keepdims=True) + epsilon)
    xt_ref[0] = (centred * inv_std * gain_ref[...] + shift_ref[...]).astype(bf16)


def deal_g_body(place_ref, g_ref, live_ref, gt_ref, gd_ref, bo_ref):
    g = pick_rows(place_ref, g_ref)
    gd_ref[0] = g.astype(bf16)
    g = g * live_ref[0]
    gt_ref[0] = g.astype(bf16)

    @pl.when(pl.program_id(0) == 0)
    def _():
        bo_ref[...] = jnp.zeros_like(bo_ref)

    bo_ref[...] += g


def deal_specs(rows, width):
    place = pl.BlockSpec((BLK, 1), lambda i: (i, 0))
    whole = pl.BlockSpec((rows, width), lambda i: (0, 0))
    wide = pl.BlockSpec((width, BLK), lambda i: (0, 0))
    out = pl.BlockSpec((1, width, BLK), lambda i: (i, 0, 0))
    return place, whole, wide, out


def deal_x(place, x, gain, shift):
    rows, width = x.shape
    blocks = rows // BLK
    spot, whole, wide, out = deal_specs(rows, width)
    return pl.pallas_call(
        deal_x_body,
        grid=(blocks,),
        in_specs=[spot, whole, wide, wide],
        out_specs=[out, out],
        out_shape=[jax.ShapeDtypeStruct((blocks, width, BLK), bf16)] * 2,
        compiler_params=params(40),
        cost_estimate=cost(2 * rows * rows * width, 6 * rows * width),
    )(place.reshape(rows, 1), x, gain, shift)


def deal_g(place, g, live):
    rows, width = g.shape
    blocks = rows // BLK
    spot, whole, wide, out = deal_specs(rows, width)
    return pl.pallas_call(
        deal_g_body,
        grid=(blocks,),
        in_specs=[spot, whole, pl.BlockSpec((1, 1, BLK), lambda i: (i, 0, 0))],
        out_specs=[out, out, wide],
        out_shape=[jax.ShapeDtypeStruct((blocks, width, BLK), bf16)] * 2
        + [jax.ShapeDtypeStruct((width, BLK), f32)],
        compiler_params=params(40),
        cost_estimate=cost(2 * rows * rows * width, 6 * rows * width),
    )(place.reshape(rows, 1), g, live)


def send_back(place_ref, out_s, o_ref):
    rows = out_s.shape[0]
    spot = lax.broadcasted_iota(jnp.int32, (rows, rows), 0)
    pick = jnp.where(spot == place_ref[...], 1.0, 0.0).astype(bf16)
    o_ref[...] = nn(pick, out_s[...]).astype(bf16)


def total(refs, at):
    value = refs[0][at].astype(f32)
    for ref in refs[1:]:
        value = value + ref[at].astype(f32)
    return value


def layer_body(place_ref, xd_ref, live_ref, bias_ref, *refs):
    o_ref, out_s = refs[-2:]
    for at in range(xd_ref.shape[0]):
        y = xd_ref[at].astype(f32) + live_ref[at] * (total(refs[:-2], at) + bias_ref[...])
        out_s[at * BLK : (at + 1) * BLK, :] = y.T.astype(bf16)
    send_back(place_ref, out_s, o_ref)


def layer_rows(place, parts, xd, live, bias):
    blocks, width, _ = xd.shape
    rows = blocks * BLK
    return pl.pallas_call(
        layer_body,
        out_shape=jax.ShapeDtypeStruct((rows, width), bf16),
        scratch_shapes=[pltpu.VMEM((rows, width), bf16)],
        compiler_params=params(48),
        cost_estimate=cost(2 * rows * rows * width, 6 * rows * width),
    )(place.reshape(1, rows), xd, live, bias, *parts)


def input_body(place_ref, xd_ref, gd_ref, gain_ref, *refs):
    o_ref, sums_ref, out_s = refs[-3:]
    g_gain = jnp.zeros(gain_ref.shape, f32)
    g_shift = jnp.zeros(gain_ref.shape, f32)
    for at in range(xd_ref.shape[0]):
        x = xd_ref[at].astype(f32)
        centred = x - jnp.mean(x, axis=0, keepdims=True)
        inv_std = lax.rsqrt(jnp.mean(centred * centred, axis=0, keepdims=True) + epsilon)
        x_hat = centred * inv_std
        g = total(refs[:-3], at)
        g_gain = g_gain + g * x_hat
        g_shift = g_shift + g
        hat = g * gain_ref[...]
        back = inv_std * (
            hat
            - jnp.mean(hat, axis=0, keepdims=True)
            - x_hat * jnp.mean(hat * x_hat, axis=0, keepdims=True)
        )
        out_s[at * BLK : (at + 1) * BLK, :] = (gd_ref[at].astype(f32) + back).T.astype(bf16)
    sums_ref[0] = g_gain
    sums_ref[1] = g_shift
    send_back(place_ref, out_s, o_ref)


def input_rows(place, parts, xd, gd, gain):
    blocks, width, _ = xd.shape
    rows = blocks * BLK
    return pl.pallas_call(
        input_body,
        out_shape=[
            jax.ShapeDtypeStruct((rows, width), bf16),
            jax.ShapeDtypeStruct((2, width, BLK), f32),
        ],
        scratch_shapes=[pltpu.VMEM((rows, width), bf16)],
        compiler_params=params(48),
        cost_estimate=cost(2 * rows * rows * width, 8 * rows * width),
    )(place.reshape(1, rows), xd, gd, gain, *parts)


def project_body(ch, many, start_ref, x_ref, live_ref, wt_ref, bias_ref, *refs):
    a_ref, da_ref, gg_ref, dg_ref = refs[-4:]
    x = jnp.concatenate([x_ref[0], x_ref[1]], axis=1)
    live = live_ref[0]
    root = 0.7978845608028654
    step = 64 if ch % 128 else 128

    def act(pre):
        square = pre * pre
        rise = 0.5 + 0.5 * jnp.tanh(pre * (root + (0.044715 * root) * square))
        value = pre * rise
        slope = rise + rise * (pre - value) * (2.0 * root + (6.0 * 0.044715 * root) * square)
        return value, slope

    def put(ref, k, at, value):
        value = value.astype(bf16)
        ref[k, 0, at, :] = value[:, :BLK]
        ref[k, 1, at, :] = value[:, BLK:]

    for k in range(2):
        for first, value_ref, slope_ref in ((k * ch, a_ref, da_ref), ((2 + k) * ch, gg_ref, dg_ref)):
            for at in range(0, ch, step):
                rows = pl.ds(first + at, step)
                bias = bias_ref[rows, :]
                pre = nn(wt_ref[rows, :], x) + jnp.concatenate([bias, bias], axis=1)
                value, slope = act(pre)
                if value_ref is a_ref:
                    value, slope = live * value, live * slope
                put(value_ref, k, pl.ds(at, step), value)
                put(slope_ref, k, pl.ds(at, step), slope)


def chained(body, grid, in_specs, out_specs, shapes, scratch, limit, estimate, start, operands, kept):
    kept = [] if kept is None else list(kept)
    specs = list(in_specs) + [pl.BlockSpec(memory_space=pl.ANY)] * len(kept)
    first = 1 + len(operands)
    return pl.pallas_call(
        body,
        grid_spec=pltpu.PrefetchScalarGridSpec(
            num_scalar_prefetch=1, grid=grid, in_specs=specs, out_specs=out_specs, scratch_shapes=scratch
        ),
        out_shape=shapes,
        input_output_aliases={first + at: at for at in range(len(kept))},
        compiler_params=params(limit),
        cost_estimate=estimate,
    )(start, *operands, *kept)


def project(xt, start, nb, live, wt, bias, kept):
    many, width, _ = xt.shape
    ch = wt.shape[0] // 4
    out = pl.BlockSpec((2, 2, ch, BLK), lambda i, at: (0, at[0] + i, 0, 0))
    tok = many * BLK
    return chained(
        partial(project_body, ch, many),
        (many // 2,),
        [
            pl.BlockSpec((2, width, BLK), lambda i, at: (i, 0, 0)),
            pl.BlockSpec((1, 1, BIG), lambda i, at: (at[0] + i, 0, 0)),
            pl.BlockSpec((4 * ch, width), lambda i, at: (0, 0)),
            pl.BlockSpec((4 * ch, BLK), lambda i, at: (0, 0)),
        ],
        [out] * 4,
        [jax.ShapeDtypeStruct((2, nb, ch, BLK), bf16)] * 4,
        [],
        48,
        cost(8 * tok * width * ch, 2 * tok * width + 16 * tok * ch, 4 * tok * ch),
        start // 2,
        [xt, live, wt, bias],
        kept,
    )


def gate_grad_body(ch, parts, at_ref, *refs):
    wt_ref, o_ref, g_s = refs[parts:]
    steps = pl.num_programs(0) // parts
    many = refs[0].shape[0]

    for part in range(parts):

        @pl.when(pl.program_id(0) // steps == part)
        def _(part=part):
            for h in range(many):
                g_s[:, h * BLK : (h + 1) * BLK] = refs[part][h]

    for k in range(2):
        gm = nn(wt_ref[k * ch : (k + 1) * ch, :], g_s[...]).astype(bf16)
        for h in range(many):
            o_ref[k, h] = gm[:, h * BLK : (h + 1) * BLK]


def gate_grad(gs, nb, wt):
    parts = len(gs)
    rows_in, width, _ = gs[0][0].shape
    many = 4
    steps = rows_in // many
    ch = wt.shape[0] // 2
    tok = nb * BLK

    def rows(part):
        return pl.BlockSpec((many, width, BLK), lambda i, at: (jnp.clip(i - part * steps, 0, steps - 1), 0, 0))

    order = jnp.concatenate([start // many for _, start in gs]).astype(jnp.int32)
    return pl.pallas_call(
        partial(gate_grad_body, ch, parts),
        grid_spec=pltpu.PrefetchScalarGridSpec(
            num_scalar_prefetch=1,
            grid=(parts * steps,),
            in_specs=[rows(part) for part in range(parts)] + [pl.BlockSpec((2 * ch, width), lambda i, at: (0, 0))],
            out_specs=pl.BlockSpec((2, many, ch, BLK), lambda i, at: (0, at[i // steps] + i % steps, 0, 0)),
            scratch_shapes=[pltpu.VMEM((width, many * BLK), bf16)],
        ),
        out_shape=jax.ShapeDtypeStruct((2, nb, ch, BLK), bf16),
        compiler_params=params(40),
        cost_estimate=cost(4 * tok * width * ch, 2 * tok * width + 4 * tok * ch),
    )(order, *[part for part, _ in gs], wt)


def spectra_body(cc, ld_ref, w_ref, d_ref, wave_ref, kh_ref, k_s):
    t = lax.broadcasted_iota(jnp.int32, (BLK, BLK), 0).astype(f32)
    block = lax.broadcasted_iota(jnp.int32, (2 * LAGS, BLK), 0).astype(f32) * float(BLK)
    low = lax.broadcasted_iota(jnp.int32, (2 * LAGS, BLK), 1) < STATE
    count = 2 * LAGS

    def one(p, carry):
        ld = ld_ref[0, pl.ds(p, 1), :]
        decay = jnp.exp2(t * ld)
        scale = w_ref[0, pl.ds(p, 1), :] * jnp.exp2(block * ld)
        lhs = jnp.concatenate([jnp.where(low, scale, 0.0), jnp.where(low, 0.0, scale)], axis=0)
        lhs_high, lhs_low = halves(lhs)
        k = nt(jnp.concatenate([lhs_high, lhs_low], axis=0), decay.astype(bf16))
        k = k[0 : 2 * count] + k[2 * count : 4 * count]
        k_s[pl.ds(2 * p, count, stride=cc), :] = k[0:count]
        k_s[pl.ds(2 * p + 1, count, stride=cc), :] = k[count : 2 * count]
        return carry

    lax.fori_loop(0, cc // 2, one, 0, unroll=16)
    sign = jnp.where(lax.broadcasted_iota(jnp.int32, (cc, BIG), 1) % 2 == 0, 1.0, -1.0)
    before = None
    for big in range(LAGS):
        rows = jnp.concatenate(
            [k_s[pl.ds(2 * big * cc, cc), :], k_s[pl.ds((2 * big + 1) * cc, cc), :]], axis=1
        )
        high, rest = halves(rows)
        x = nn(high, wave_ref[...]) + nn(rest, wave_ref[...])
        xc, xs = x[:, :BIG], x[:, BIG:]
        if big == 0:
            kh_ref[0, 0, :, :BIG] = xc + d_ref[0][:, 0:1]
            kh_ref[0, 0, :, BIG:] = xs
        else:
            kh_ref[0, big, :, :BIG] = xc + sign * before[1]
            kh_ref[0, big, :, BIG:] = xs - sign * before[0]
        before = (xc, xs)


def spectra(ld, w, d, wave):
    ch = 2 * ld.shape[1]
    cc = chunk_of(ch, 128)
    return pl.pallas_call(
        partial(spectra_body, cc),
        grid=(2, ch // cc),
        in_specs=[pl.BlockSpec((1, cc // 2, BLK), lambda k, i: (k, i, 0))] * 2
        + [
            pl.BlockSpec((1, cc, BLK), lambda k, i: (k, i, 0)),
            pl.BlockSpec((BIG, 2 * BIG), lambda k, i: (0, 0)),
        ],
        out_specs=pl.BlockSpec((1, LAGS, cc, 2 * BIG), lambda k, i: (k, 0, i, 0)),
        out_shape=jax.ShapeDtypeStruct((2, LAGS, ch, 2 * BIG), f32),
        scratch_shapes=[pltpu.VMEM((2 * LAGS * cc, BLK), f32)],
        compiler_params=params(40),
        cost_estimate=cost(2 * ch * 40e6, 2 * ch * LAGS * 2 * BIG * 4),
    )(ld, w, d, wave)


def moments_body(cc, ld_ref, gh_ref, back_ref, s0_ref, s1_ref, g0_ref, g_s):
    sign = jnp.where(lax.broadcasted_iota(jnp.int32, (cc, BIG), 1) % 2 == 0, 1.0, -1.0)
    count = 2 * LAGS
    for big in range(LAGS):
        c = gh_ref[0, big, :, :BIG]
        s = gh_ref[0, big, :, BIG:]
        if big < LAGS - 1:
            c, s = c - sign * gh_ref[0, big + 1, :, BIG:], s + sign * gh_ref[0, big + 1, :, :BIG]
        high, rest = halves(jnp.concatenate([c, s], axis=1))
        g = nn(high, back_ref[...]) + nn(rest, back_ref[...])
        g_s[pl.ds(2 * big * cc, cc), :] = g[:, :BLK]
        g_s[pl.ds((2 * big + 1) * cc, cc), :] = g[:, BLK:]
        if big == 0:
            g0_ref[0] = g[:, :BLK]
    t = lax.broadcasted_iota(jnp.int32, (BLK, BLK), 0).astype(f32)
    lane = lax.broadcasted_iota(jnp.int32, (count, BLK), 1)
    lag = lane.astype(f32)
    block = lax.broadcasted_iota(jnp.int32, (count, BLK), 0).astype(f32) * float(BLK)
    low = lane < STATE

    def one(p, carry):
        ld = ld_ref[0, pl.ds(p, 1), :]
        decay = jnp.exp2(t * ld).astype(bf16)
        far = jnp.exp2(block * ld)
        ga = g_s[pl.ds(2 * p, count, stride=cc), :]
        gb = g_s[pl.ds(2 * p + 1, count, stride=cc), :]
        high, rest = halves(jnp.concatenate([ga, gb, ga * lag, gb * lag], axis=0))
        m = nn(jnp.concatenate([high, rest], axis=0), decay)
        m = m[0 : 4 * count] + m[4 * count : 8 * count]
        m0 = jnp.where(low, m[0:count], m[count : 2 * count])
        m1 = jnp.where(low, m[2 * count : 3 * count], m[3 * count : 4 * count]) + block * m0
        s0_ref[0, pl.ds(p, 1), :] = jnp.sum(far * m0, axis=0, keepdims=True)
        s1_ref[0, pl.ds(p, 1), :] = jnp.sum(far * m1, axis=0, keepdims=True)
        return carry

    lax.fori_loop(0, cc // 2, one, 0, unroll=16)


def moments(k, ld, gh, back):
    ch = gh.shape[2]
    cc = chunk_of(ch, 128)
    row = pl.BlockSpec((1, cc // 2, BLK), lambda i: (0, i, 0))
    return pl.pallas_call(
        partial(moments_body, cc),
        grid=(ch // cc,),
        in_specs=[
            pl.BlockSpec((1, cc // 2, BLK), lambda i: (k, i, 0)),
            pl.BlockSpec((1, LAGS, cc, 2 * BIG), lambda i: (0, 0, i, 0)),
            pl.BlockSpec((2 * BIG, BIG), lambda i: (0, 0)),
        ],
        out_specs=[row, row, pl.BlockSpec((1, cc, BLK), lambda i: (0, i, 0))],
        out_shape=[jax.ShapeDtypeStruct((1, ch // 2, BLK), f32)] * 2
        + [jax.ShapeDtypeStruct((1, ch, BLK), f32)],
        scratch_shapes=[pltpu.VMEM((2 * LAGS * cc, BLK), f32)],
        compiler_params=params(40),
        cost_estimate=cost(ch * 40e6, ch * LAGS * 2 * BIG * 4),
    )(ld, gh, back)


def load_pieces(nb, pieces, cc, tab_ref, block, in_s, wave_ref, dst):
    for h in range(pieces):
        first = tab_ref[0, h]
        whole = tab_ref[1, h].astype(f32)
        in_s[pl.ds(h * cc, cc), 0:BLK] = block(first).astype(bf16)
        in_s[pl.ds(h * cc, cc), BLK:BIG] = (block(jnp.minimum(first + 1, nb - 1)) * whole).astype(bf16)
    for h in range(pieces):
        at = pl.ds(h * cc, cc)
        dst[at, :] = nn(in_s[at, :], wave_ref[...])


def over_pairs(nseq, cc, rg, seq_ref, pair):
    def group(r, carry):
        off = pl.multiple_of(r * rg, rg)
        for s in range(nseq):
            base = seq_ref[0, s]
            count = seq_ref[1, s]

            def outer(i, carry):
                pair(i, count, base, off)
                return carry

            lax.fori_loop(0, (count + 1) // 2, outer, 0)
        return carry

    lax.fori_loop(0, cc // rg, group, 0)


def times(k, u):
    return (k[0] * u[0] - k[1] * u[1], k[0] * u[1] + k[1] * u[0])


def times_conj(k, u):
    return (k[0] * u[0] + k[1] * u[1], k[0] * u[1] - k[1] * u[0])


def plus(*terms):
    return (sum(term[0] for term in terms[1:]) + terms[0][0], sum(term[1] for term in terms[1:]) + terms[0][1])


def both(ref, at):
    return (ref[at, :BIG], ref[at, BIG:])


def over_pieces(nseq, cc, rg, seq_ref, piece):
    def group(r, carry):
        off = pl.multiple_of(r * rg, rg)
        for s in range(nseq):
            base = seq_ref[0, s]
            count = seq_ref[1, s]

            def outer(i, carry):
                piece(i, count, base, off)
                return carry

            lax.fori_loop(0, count, outer, 0)
        return carry

    lax.fori_loop(0, cc // rg, group, 0)


def scan_body(
    nb, nseq, cc, rg, tab_ref, seq_ref, a_ref, kh_ref, wave_ref, back_ref, gg_ref, y_ref, mix_ref, in_s, ah_s, yh_s, y_s
):
    pieces = (nb + nseq) // 2
    load_pieces(nb, pieces, cc, tab_ref, lambda b: a_ref[0, b].astype(f32), in_s, wave_ref, ah_s)
    ah_s[pl.ds(pieces * cc, cc), :] = jnp.zeros((cc, 2 * BIG), f32)

    def products(flip):
        def pair(i, count, base, off):
            rows = pl.ds(off, rg)

            def at(place):
                return pl.ds(pl.multiple_of((base + place) * cc + off, rg), rg)

            def lag(j):
                return (kh_ref[0, j, rows, :BIG], kh_ref[0, j, rows, BIG:])

            def two(m):
                u0 = both(ah_s, at(2 * m))
                u1 = both(ah_s, at(2 * m + 1))
                if flip:
                    real = (2 * m + 1 < count).astype(f32)
                    u1 = (u1[0] * real, u1[1] * real)
                return u0, u1

            u0, u1 = two(i)
            k0, k1 = lag(0), lag(1)
            if flip:
                y0 = plus(times_conj(k0, u0), times_conj(k1, u1))
                y1 = times_conj(k0, u1)
            else:
                y0 = times(k0, u0)
                y1 = plus(times(k1, u0), times(k0, u1))

            def inner(d, acc):
                y0, y1 = acc
                u0, u1 = two((i + d) if flip else (i - d))
                k0, k1, k2 = lag(2 * d - 1), lag(2 * d), lag(2 * d + 1)
                if flip:
                    y0 = plus(y0, times_conj(k1, u0), times_conj(k2, u1))
                    y1 = plus(y1, times_conj(k0, u0), times_conj(k1, u1))
                else:
                    y0 = plus(y0, times(k1, u0), times(k0, u1))
                    y1 = plus(y1, times(k2, u0), times(k1, u1))
                return y0, y1

            y0, y1 = lax.fori_loop(1, ((count + 1) // 2 - i) if flip else (i + 1), inner, (y0, y1))
            for place, y in ((2 * i, y0), (2 * i + 1, y1)):
                yh_s[at(place), :BIG] = y[0].astype(bf16)
                yh_s[at(place), BIG:] = y[1].astype(bf16)

        over_pairs(nseq, cc, rg, seq_ref, pair)

    @pl.when(pl.program_id(0) == 0)
    def _():
        products(False)

    @pl.when(pl.program_id(0) == 1)
    def _():
        products(True)

    for h in range(pieces):
        at = pl.ds(h * cc, cc)
        y_s[at, :] = nn(yh_s[at, :], back_ref[...])

    def one(b, y):
        y_ref[0, b] = y.astype(bf16)
        mix_ref[0, b] = (y * gg_ref[0, b].astype(f32)).astype(bf16)

    def last(h, carry):
        b = tab_ref[0, h]
        at = pl.ds(pl.multiple_of(h * cc, cc), cc)
        one(b, y_s[at, 0:BLK])

        @pl.when(tab_ref[1, h] == 1)
        def _():
            one(b + 1, y_s[at, BLK:])

        return carry

    lax.fori_loop(0, seq_ref[1, nseq], last, 0)
    nothing = jnp.zeros((cc, BLK), bf16)

    def fill(b, carry):
        y_ref[0, b] = nothing
        mix_ref[0, b] = nothing
        return carry

    lax.fori_loop(seq_ref[0, nseq], nb, fill, 0)


def back_body(
    nb, nseq, cc, rg, flip, tab_ref, seq_ref, a_ref, gm_ref, kh_ref, wave_ref, back_ref, gg_ref, y_ref, dg_ref, da_ref,
    gpg_ref, gp_ref, gh_ref, bs_ref, in_s, ah_s, gh_s, xh_s, x_s,
):
    pieces = (nb + nseq) // 2
    load_pieces(nb, pieces, cc, tab_ref, lambda b: a_ref[0, b].astype(f32), in_s, wave_ref, ah_s)
    load_pieces(
        nb, pieces, cc, tab_ref, lambda b: gm_ref[0, b].astype(f32) * gg_ref[0, b].astype(f32), in_s, wave_ref, gh_s
    )
    gh_ref[...] = jnp.zeros_like(gh_ref)
    zero = jnp.zeros((rg, BIG), f32)

    def piece(i, count, base, off):
        at = pl.ds(pl.multiple_of((base + i) * cc + off, rg), rg)
        ac = ah_s[at, :BIG]
        as_ = ah_s[at, BIG:]

        def inner(j, acc):
            xc, xs = acc
            other = (base + i - j) if flip else (base + i + j)
            m = pl.ds(pl.multiple_of(other * cc + off, rg), rg)
            rows = pl.ds(off, rg)
            gc = gh_s[m, :BIG]
            gs = gh_s[m, BIG:]
            kc = kh_ref[0, j, rows, :BIG]
            ks = kh_ref[0, j, rows, BIG:]
            gh_ref[0, j, rows, :BIG] += ac * gc + as_ * gs
            if flip:
                gh_ref[0, j, rows, BIG:] += gc * as_ - gs * ac
                return (xc + kc * gc - ks * gs, xs + kc * gs + ks * gc)
            gh_ref[0, j, rows, BIG:] += ac * gs - as_ * gc
            return (xc + kc * gc + ks * gs, xs + kc * gs - ks * gc)

        xc, xs = lax.fori_loop(0, (i + 1) if flip else (count - i), inner, (zero, zero))
        xh_s[at, :BIG] = xc.astype(bf16)
        xh_s[at, BIG:] = xs.astype(bf16)

    over_pieces(nseq, cc, rg, seq_ref, piece)

    for h in range(pieces):
        at = pl.ds(h * cc, cc)
        x_s[at, :] = nn(xh_s[at, :], back_ref[...])

    none = jnp.zeros((cc, BLK), f32)

    def one(b, gx, carry):
        s0, s1 = carry
        gpg = (y_ref[0, b].astype(f32) * gm_ref[0, b].astype(f32) * dg_ref[0, b].astype(f32)).astype(bf16)
        gpg_ref[0, b] = gpg
        gp = (gx * da_ref[0, b].astype(f32)).astype(bf16)
        gp_ref[0, b] = gp
        return (s0 + gpg.astype(f32), s1 + gp.astype(f32))

    def last(h, carry):
        b = tab_ref[0, h]
        at = pl.ds(pl.multiple_of(h * cc, cc), cc)
        carry = one(b, x_s[at, 0:BLK], carry)

        def more(kept):
            return one(b + 1, x_s[at, BLK:], kept)

        return lax.cond(tab_ref[1, h] == 1, more, lambda kept: kept, carry)

    s0, s1 = lax.fori_loop(0, seq_ref[1, nseq], last, (none, none))
    bs_ref[0, :, 0:BLK] = s0
    bs_ref[0, :, BLK:] = s1
    nothing = jnp.zeros((cc, BLK), bf16)

    def fill(b, carry):
        gpg_ref[0, b] = nothing
        gp_ref[0, b] = nothing
        return carry

    lax.fori_loop(seq_ref[0, nseq], nb, fill, 0)


def ssm_specs(shape, seq):
    _, nb, ch, _ = shape
    nseq = seq.shape[1] - 1
    pieces = (nb + nseq) // 2
    cc = chunk_of(ch, 128 if nb <= 32 else 64)
    big = pl.BlockSpec((1, nb, cc, BLK), lambda k, i: (k, 0, i, 0))
    spec = pl.BlockSpec((1, LAGS, cc, 2 * BIG), lambda k, i: (k, 0, i, 0))
    smem = pl.BlockSpec(memory_space=pltpu.SMEM)
    head = [smem, smem]
    tables = [pl.BlockSpec((BIG, 2 * BIG), lambda k, i: (0, 0)), pl.BlockSpec((2 * BIG, BIG), lambda k, i: (0, 0))]
    return nb, nseq, ch, cc, pieces * cc, big, spec, head, tables


def ssm_scan(tab, seq, a, kh, wave, back, gg):
    nb, nseq, ch, cc, size, big, spec, head, tables = ssm_specs(a.shape, seq)
    return pl.pallas_call(
        partial(scan_body, nb, nseq, cc, 32),
        grid=(2, ch // cc),
        in_specs=head + [big, spec] + tables + [big],
        out_specs=[big, big],
        out_shape=[jax.ShapeDtypeStruct(a.shape, bf16)] * 2,
        scratch_shapes=[
            pltpu.VMEM((size, BIG), bf16),
            pltpu.VMEM((size + cc, 2 * BIG), f32),
            pltpu.VMEM((size + cc, 2 * BIG), bf16),
            pltpu.VMEM((size, BIG), f32),
        ],
        compiler_params=params(56),
        cost_estimate=cost(2 * ch * 50e6, 2 * ch * nb * BLK * 8),
    )(tab, seq, a, kh, wave, back, gg)


def ssm_back(k, tab, seq, a, gm, kh, wave, back, gg, y, dg, da):
    nb, nseq, ch, cc, size, _, _, head, tables = ssm_specs(a.shape, seq)
    big = pl.BlockSpec((1, nb, cc, BLK), lambda i: (k, 0, i, 0))
    spec = pl.BlockSpec((1, LAGS, cc, 2 * BIG), lambda i: (k, 0, i, 0))
    out = pl.BlockSpec((1, nb, cc, BLK), lambda i: (0, 0, i, 0))
    out_spec = pl.BlockSpec((1, LAGS, cc, 2 * BIG), lambda i: (0, 0, i, 0))
    tables = [
        pl.BlockSpec((BIG, 2 * BIG), lambda i: (0, 0)),
        pl.BlockSpec((2 * BIG, BIG), lambda i: (0, 0)),
    ]
    return pl.pallas_call(
        partial(back_body, nb, nseq, cc, 64, k == 1),
        grid=(ch // cc,),
        in_specs=head + [big, big, spec] + tables + [big] * 4,
        out_specs=[out, out, out_spec, pl.BlockSpec((1, cc, 2 * BLK), lambda i: (0, i, 0))],
        out_shape=[jax.ShapeDtypeStruct((1,) + a.shape[1:], bf16)] * 2
        + [
            jax.ShapeDtypeStruct((1, LAGS, ch, 2 * BIG), f32),
            jax.ShapeDtypeStruct((1, ch, 2 * BLK), f32),
        ],
        scratch_shapes=[
            pltpu.VMEM((size, BIG), bf16),
            pltpu.VMEM((size, 2 * BIG), f32),
            pltpu.VMEM((size, 2 * BIG), f32),
            pltpu.VMEM((size, 2 * BIG), bf16),
            pltpu.VMEM((size, BIG), f32),
        ],
        compiler_params=params(60),
        cost_estimate=cost(ch * 80e6, ch * nb * BLK * 16),
    )(tab, seq, a, gm, kh, wave, back, gg, y, dg, da)


def stack_blocks(refs, many):
    return jnp.concatenate(
        [
            jnp.concatenate([ref[k, b] for b in range(many)], axis=1)
            for ref in refs
            for k in range(ref.shape[0])
        ],
        axis=0,
    )


def mul_body(count, more, many, start_ref, w_ref, *refs):
    out = nn(w_ref[...], stack_blocks(refs[:count], many))
    o_ref = refs[-1]
    for h in range(many):
        part = out[:, h * BLK : (h + 1) * BLK]
        if more:
            part = part + refs[count][h].astype(f32)
        o_ref[h] = part.astype(o_ref.dtype)


def mul_rows(w, arrays, start, many, dtype=bf16, extra=None):
    width, deep = w.shape
    ch = arrays[0].shape[2]
    count = len(arrays)
    step = 4
    out = pl.BlockSpec((step, width, BLK), lambda i, at: (i, 0, 0))
    return pl.pallas_call(
        partial(mul_body, count, extra is not None, step),
        grid_spec=pltpu.PrefetchScalarGridSpec(
            num_scalar_prefetch=1,
            grid=(many // step,),
            in_specs=[pl.BlockSpec((width, deep), lambda i, at: (0, 0))]
            + [pl.BlockSpec((x.shape[0], step, ch, BLK), lambda i, at: (0, at[0] + i, 0, 0)) for x in arrays]
            + ([] if extra is None else [out]),
            out_specs=out,
        ),
        out_shape=jax.ShapeDtypeStruct((many, width, BLK), dtype),
        compiler_params=params(40),
        cost_estimate=cost(2 * many * BLK * width * deep, 2 * many * BLK * (2 * width + deep)),
    )(start // step, w, *arrays, *([] if extra is None else [extra]))


def outer_body(ch, many, cuts, parts, at_ref, *refs):
    step = pl.program_id(0)
    xs, gs = refs[:parts], refs[parts : 2 * parts]
    gp_refs, gpg_refs, mix_ref = refs[2 * parts : 2 * parts + 2], refs[2 * parts + 2 : 2 * parts + 4], refs[2 * parts + 4]
    outs = refs[2 * parts + 5 : 2 * parts + 5 + cuts]
    acc_s, x_s, g_s = refs[-3:]

    def fill(at):
        for b in range(many):
            x_s[:, b * BLK : (b + 1) * BLK] = xs[at][b]
            g_s[:, b * BLK : (b + 1) * BLK] = gs[at][b]

    if parts == 1:
        fill(0)
    else:
        for at in range(parts):

            @pl.when(step == at)
            def _(at=at):
                fill(at)

    def part(ref, k):
        return jnp.concatenate([ref[k, b] for b in range(many)], axis=1)

    @pl.when(step == 0)
    def _():
        acc_s[...] = jnp.zeros_like(acc_s)

    split = 4 * ch
    left = jnp.concatenate([part(ref, 0) for ref in (*gp_refs, *gpg_refs)], axis=0)
    acc_s[:, :split] += nt(x_s[...], left)
    acc_s[:, split:] += nt(g_s[...], jnp.concatenate([part(mix_ref, 0), part(mix_ref, 1)], axis=0))

    @pl.when(step == pl.num_programs(0) - 1)
    def _():
        deep = acc_s.shape[0] // cuts
        for cut in range(cuts):
            start = pl.multiple_of(at_ref[pl.num_programs(0) + cut] * deep, 8)
            outs[cut][...] = acc_s[pl.ds(start, deep), :].astype(bf16)


def outer_sums(order, cuts, xs, gs, gp, gpg, mix):
    width = xs[0].shape[1]
    _, nb, ch, _ = mix.shape
    many = 8
    parts = len(xs)
    if parts == 1:
        rows = pl.BlockSpec((many, width, BLK), lambda i, at: (i, 0, 0))
    else:
        rows = pl.BlockSpec((many, width, BLK), lambda i, at: (0, 0, 0), pipeline_mode=pl.Buffered(1))
    chan = pl.BlockSpec((2, many, ch, BLK), lambda i, at: (0, at[i], 0, 0))
    one = pl.BlockSpec((1, many, ch, BLK), lambda i, at: (0, at[i], 0, 0))
    tok = nb * BLK
    return pl.pallas_call(
        partial(outer_body, ch, many, cuts, parts),
        grid_spec=pltpu.PrefetchScalarGridSpec(
            num_scalar_prefetch=1,
            grid=(nb // many,),
            in_specs=[rows] * (2 * parts) + [one] * 4 + [chan],
            out_specs=[pl.BlockSpec((width // cuts, 6 * ch), lambda i, at: (0, 0))] * cuts,
            scratch_shapes=[
                pltpu.VMEM((width, 6 * ch), f32),
                pltpu.VMEM((width, many * BLK), bf16),
                pltpu.VMEM((width, many * BLK), bf16),
            ],
        ),
        out_shape=[jax.ShapeDtypeStruct((width // cuts, 6 * ch), bf16)] * cuts,
        compiler_params=params(60),
        cost_estimate=cost(12 * tok * width * ch, tok * (4 * width + 12 * ch)),
    )(order, *xs, *gs, *gp, *gpg, mix)


def join_body(parts, split, at_ref, *refs):
    head_ref, tail_ref, head_t_ref, tail_t_ref = refs[parts:]
    deep = refs[0].shape[0]
    for at in range(parts):
        rows = pl.ds(pl.multiple_of(at_ref[at] * deep, 16), deep)
        head_ref[rows, :] = refs[at][:, :split]
        tail_ref[rows, :] = refs[at][:, split:]
    head_t_ref[...] = head_ref[...].T
    tail_t_ref[...] = tail_ref[...].T


def join_weights(order, parts, split):
    count = len(parts)
    deep, wide = parts[0].shape
    rows = deep * count
    vmem = pl.BlockSpec(memory_space=pltpu.VMEM)
    return pl.pallas_call(
        partial(join_body, count, split),
        in_specs=[pl.BlockSpec(memory_space=pltpu.SMEM)] + [vmem] * count,
        out_specs=[vmem] * 4,
        out_shape=[
            jax.ShapeDtypeStruct(shape, bf16)
            for shape in ((rows, split), (rows, wide - split), (split, rows), (wide - split, rows))
        ],
        compiler_params=params(48),
        cost_estimate=cost(0, 6 * rows * wide),
    )(order, *parts)


def meet_body(axes, rank_ref, x_ref, chan_ref, norm_ref, got_ref, call_ref, nall_ref, send_s, *sems):
    xs_sem, xr_sem, cs_sem, cr_sem, ns_sem, nr_sem, own_sem = sems
    q, c, h, w = (lax.axis_index(name) for name in axes)
    rows = x_ref.shape[0]
    piece = rows // 8
    flat = ((2 * q + c) * 2 + h) * 2 + w

    def peer(bits):
        return (q ^ (bits // 8), c ^ (bits // 4 % 2), h ^ (bits // 2 % 2), w ^ (bits % 2))

    barrier = pltpu.get_barrier_semaphore()
    for bits in range(1, 32):
        pl.semaphore_signal(barrier, inc=1, device_id=peer(bits), device_id_type=pl.DeviceIdType.MESH)
    pl.semaphore_wait(barrier, 31)

    def remote(src, dst, send, recv, to):
        return pltpu.make_async_remote_copy(
            src_ref=src, dst_ref=dst, send_sem=send, recv_sem=recv, device_id=to, device_id_type=pl.DeviceIdType.MESH
        )

    nall_ref[flat] = norm_ref[...]

    def norm_copy(bits):
        return remote(norm_ref, nall_ref.at[flat], ns_sem.at[bits], nr_sem.at[bits], peer(bits))

    for bits in range(1, 32):
        norm_copy(bits).start()

    place = 2 * (1 - c) + w
    spot_c = 4 * c + 2 * h + w

    def chan_copy(at):
        to = (q ^ at, 1 - q // 2, h, q % 2) if at < 4 else (2 * c + w, 1 - q // 2, 1 - h, q % 2)
        return remote(chan_ref, call_ref.at[spot_c], cs_sem.at[at], cr_sem.at[spot_c], to)

    def own_chan():
        return pltpu.make_async_copy(chan_ref, call_ref.at[spot_c], own_sem.at[1])

    def chan_came(at):
        return remote(chan_ref, call_ref.at[at], cs_sem.at[0], cr_sem.at[at], peer(1))

    far_spot = 4 * (q // 2) + 2 * (1 - h) + q % 2

    def chan_pass(bits):
        return remote(
            call_ref.at[far_spot], call_ref.at[far_spot], cs_sem.at[4 + bits], cr_sem.at[far_spot], (q ^ bits, c, h, w)
        )

    for at in (4, 1, 2, 3, 0):
        if at:
            chan_copy(at).start()
        else:

            @pl.when(place == q)
            def _():
                own_chan().start()

            @pl.when(place != q)
            def _():
                chan_copy(0).start()

    pieces = [(kq, kh) for kh in (1, 0) for kq in (1, 2, 3, 0)]
    spot = lax.broadcasted_iota(jnp.int32, (piece, rows), 0)

    def row_copy(kq, kh):
        at = 2 * kq + kh
        return remote(
            send_s.at[at], got_ref.at[2 * q + c], xs_sem.at[at], xr_sem.at[2 * kq + c], (q ^ kq, 1 - h, h ^ kh, w)
        )

    def own_copy():
        return pltpu.make_async_copy(send_s.at[0], got_ref.at[2 * q + c], own_sem.at[0])

    for kq, kh in pieces:
        chunk = 2 * (q ^ kq) + (h ^ kh)
        pick = jnp.where(spot + chunk * piece == rank_ref[...], 1.0, 0.0).astype(bf16)
        send_s[2 * kq + kh] = nn(pick, x_ref[...]).astype(bf16)
        if (kq, kh) == (0, 0):

            @pl.when(c != h)
            def _():
                own_copy().start()

            @pl.when(c == h)
            def _():
                row_copy(0, 0).start()

        else:
            row_copy(kq, kh).start()

    for bits in range(1, 32):
        norm_copy(bits).wait()
    for at in range(8):

        @pl.when((c != h) & (at == c))
        def _():
            own_copy().wait()

        @pl.when(jnp.logical_not((c != h) & (at == c)))
        def _(at=at):
            remote(send_s.at[at], got_ref.at[at], xs_sem.at[at], xr_sem.at[at], peer(1)).wait_recv()

    chan_came(far_spot).wait_recv()
    for bits in range(1, 4):
        chan_pass(bits).start()
    for at in range(8):

        @pl.when((place == q) & (at == spot_c))
        def _():
            own_chan().wait()

        @pl.when(jnp.logical_not((place == q) & (at == spot_c)) & (at != far_spot))
        def _(at=at):
            chan_came(at).wait_recv()

    for bits in range(1, 4):
        chan_pass(bits).wait_send()
    for kq, kh in pieces:
        if (kq, kh) == (0, 0):

            @pl.when(c == h)
            def _():
                row_copy(0, 0).wait_send()

        else:
            row_copy(kq, kh).wait_send()
    for at in range(1, 5):
        chan_copy(at).wait_send()

    @pl.when(place != q)
    def _():
        chan_copy(0).wait_send()


def meet(axes, rank, x, chan, norm):
    rows, width = x.shape
    vmem = pl.BlockSpec(memory_space=pltpu.VMEM)
    sem = pltpu.SemaphoreType.DMA
    return pl.pallas_call(
        partial(meet_body, axes),
        in_specs=[vmem] * 4,
        out_specs=[vmem] * 3,
        out_shape=[
            jax.ShapeDtypeStruct((8, rows // 8, width), bf16),
            jax.ShapeDtypeStruct((8,) + chan.shape, f32),
            jax.ShapeDtypeStruct((32,) + norm.shape, f32),
        ],
        scratch_shapes=[pltpu.VMEM((8, rows // 8, width), bf16)]
        + [sem((8,)), sem((8,)), sem((8,)), sem((8,)), sem((32,)), sem((32,)), sem((2,))],
        compiler_params=pltpu.CompilerParams(collective_id=1, has_side_effects=True, vmem_limit_bytes=60 * MIB),
        cost_estimate=cost(2 * rows * rows * width, 100 * rows * width),
    )(rank.reshape(1, rows), x, chan, norm)


def sequence_tables(lens, nb):
    nseq = lens.shape[0]
    blocks = (lens + BLK - 1) // BLK
    start = jnp.cumsum(blocks) - blocks
    bigs = (blocks + 1) // 2
    first_big = jnp.cumsum(bigs) - bigs
    h = jnp.arange((nb + nseq) // 2, dtype=jnp.int32)
    owner = (h[:, None] >= first_big[None, :]).astype(jnp.int32).sum(axis=1) - 1
    mine = owner[:, None] == jnp.arange(nseq, dtype=jnp.int32)[None, :]

    def at_owner(values):
        return jnp.sum(jnp.where(mine, values[None, :], 0), axis=1)

    rel = h - at_owner(first_big)
    first = jnp.minimum(at_owner(start) + 2 * rel, nb - 1)
    whole = (2 * rel + 1 < at_owner(blocks)).astype(jnp.int32)
    tab = jnp.stack([first, whole]).astype(jnp.int32)
    seq = jnp.stack(
        [jnp.append(first_big, jnp.sum(blocks)), jnp.append(bigs, jnp.sum(bigs))]
    ).astype(jnp.int32)
    return tab, seq


def live_rows(lens, rows):
    slot = (lens + BLK - 1) // BLK * BLK
    begin = jnp.cumsum(slot) - slot
    pos = jnp.arange(rows, dtype=jnp.int32)
    inside = (pos[:, None] >= begin[None, :]) & (pos[:, None] < (begin + lens)[None, :])
    return jnp.sum(inside.astype(f32), axis=1)


def after(values):
    return lax.optimization_barrier(values)


def rank_of(keys):
    return jnp.sum((keys[None, :] < keys[:, None]).astype(jnp.int32), axis=1)


class Line:
    def __init__(self, n_dp, n_t):
        self.n_dp, self.n_t = n_dp, n_t
        self.axes = {"dp": n_dp, "tensor": n_t}
        self.both = ("dp", "tensor")
        self.cuts = 1

    def place_of_group(self):
        return lax.axis_index("tensor")

    def gather_first(self, x):
        return [lax.all_gather(x, "tensor", axis=0, tiled=True)]

    def gathered(self, x, early):
        return []

    def gather_last(self, x, got):
        return [(got[0], jnp.zeros((1,), jnp.int32))]

    def scatter_first(self, w, arrays, many):
        return [mul_rows(w, arrays, jnp.zeros((1,), jnp.int32), many * self.n_t)]

    def scatter_send(self, parts):
        return [lax.psum_scatter(parts[0], "tensor", scatter_dimension=0, tiled=True)]

    def scatter_own(self, w, arrays, many):
        return []

    def regroup(self, x):
        return x

    def ungroup(self, x):
        return x

    def spread(self, x):
        return lax.all_to_all(x, "dp", split_axis=0, concat_axis=0, tiled=True)

    def order(self, pieces):
        return jnp.append(jnp.arange(pieces * self.n_t, dtype=jnp.int32), 0)

    def enter(self, rank, x, chan, norm):
        (sent,) = permute_to(rank, [x])
        return (self.spread(sent),) + self.gather_channels(chan, norm)

    def weights_first(self, pack):
        return [pack]

    def weights_send(self, packs):
        return [lax.all_gather(packs[0], "dp", axis=0, tiled=True)]

    def gather_channels(self, chan, norm):
        perm = [(f, (f % self.n_dp) * self.n_t + f // self.n_dp) for f in range(self.n_dp * self.n_t)]
        chan = lax.ppermute(chan, self.both, perm)
        norm = lax.all_gather(norm, self.both, axis=1, tiled=True)
        return lax.all_gather(chan[None], "dp", axis=0, tiled=True), norm

    def cut_order(self):
        return jnp.zeros((1,), jnp.int32)

    def grads_send(self, gw):
        return [lax.psum_scatter(gw[0], "dp", scatter_dimension=0, tiled=True)]

    def grads_last(self, parts):
        return parts[0], lambda part: part.astype(f32)

    def scatter_small(self, sums, norm):
        sums = lax.psum_scatter(sums, "dp", scatter_dimension=0, tiled=True)
        norm = lax.psum_scatter(norm, self.both, scatter_dimension=1, tiled=True)
        perm = [((f % self.n_dp) * self.n_t + f // self.n_dp, f) for f in range(self.n_dp * self.n_t)]
        return (sums, norm), lambda part: (lax.ppermute(part[0], self.both, perm), part[1])


class Pairs:
    def __init__(self, n_dp, n_t):
        self.quads = n_dp // 2
        self.axes = {"q": self.quads, "c": 2, "h": 2, "w": 2}
        self.both = ("q", "c", "h", "w")
        self.cuts = self.quads
        self.other = [(0, 1), (1, 0)]
        self.there = [(2 * c + h, 2 * (1 - h) + c) for c in range(2) for h in range(2)]
        self.back = [(b, a) for a, b in self.there]
        self.turned = [(2 * c + h, 2 * (1 - h) + 1 - c) for c in range(2) for h in range(2)]

    def flip(self, x, axis, bit=1):
        return lax.ppermute(x, axis, [(i, i ^ bit) for i in range(self.axes[axis])])

    def place_of_group(self):
        return 2 * (1 - lax.axis_index("c")) + lax.axis_index("w")

    def regroup(self, x):
        return lax.ppermute(x, ("c", "h"), self.there)

    def ungroup(self, x):
        return lax.ppermute(x, ("c", "h"), self.back)

    def spread(self, x):
        return lax.all_to_all(x, ("q", "c"), split_axis=0, concat_axis=0, tiled=True)

    def places(self):
        c, w = lax.axis_index("c"), lax.axis_index("w")
        return [2 * (1 - c) + w, 2 * c + w, 2 * (1 - c) + 1 - w, 2 * c + 1 - w]

    def starts(self, many):
        return [(place * many).astype(jnp.int32).reshape(1) for place in self.places()]

    def gather_first(self, x):
        return [self.flip(x, "c"), self.flip(x, "w")]

    def gathered(self, x, early):
        return list(zip([x] + early, self.starts(x.shape[0])))

    def gather_last(self, x, got):
        beside, near = got
        return list(zip([x, beside, near, self.flip(near, "c")], self.starts(x.shape[0])))

    def scatter_first(self, w, arrays, many):
        _, beside, near, far = self.starts(many)
        first = mul_rows(w, arrays, far, many)
        give = self.flip(first, "c")
        beside, first = after((beside, first))
        second = mul_rows(w, arrays, beside, many)
        second, give = after((second, give))
        return [second, mul_rows(w, arrays, near, many, extra=give)]

    def scatter_send(self, parts):
        return [self.flip(parts[0], "c"), self.flip(parts[1], "w")]

    def scatter_own(self, w, arrays, many):
        return [mul_rows(w, arrays, self.starts(many)[0], many, dtype=f32)]

    def order(self, pieces):
        place = jnp.stack(self.places())[:, None] * pieces + jnp.arange(pieces)[None, :]
        return jnp.concatenate([place.reshape(-1).astype(jnp.int32), self.cut_order()])

    def steps(self):
        bit = self.quads // 2
        while bit:
            yield "q", bit
            bit //= 2
        yield "h", 1

    def spot(self):
        return 2 * lax.axis_index("q") + lax.axis_index("h")

    def enter(self, rank, x, chan, norm):
        small = norm.shape[1]
        norm = jnp.pad(norm, ((0, 5), (0, BLK - small)))
        got, chan, norm = meet(self.both, rank, x, chan, norm)
        norm = norm[:, :3, :small].transpose(1, 0, 2).reshape(3, -1)
        return got.reshape(x.shape), chan, norm

    def weights_first(self, pack):
        return [self.regroup(pack), lax.ppermute(pack, ("c", "h"), self.turned)]

    def weights_send(self, packs):
        h = lax.axis_index("h")
        first, second = packs
        pair = jnp.concatenate([jnp.where(h == 0, first, second), jnp.where(h == 0, second, first)], axis=0)
        return [pair] + [self.flip(pair, "q", bit) for bit in range(1, self.quads)]

    def grads_send(self, gw):
        return [gw[0]] + [self.flip(gw[bit], "q", bit) for bit in range(1, self.quads)]

    def grads_last(self, parts):
        total = parts[0].astype(f32)
        for part in parts[1:]:
            total = total + part.astype(f32)
        total = total.astype(bf16)
        half = total.shape[0] // 2
        h = lax.axis_index("h")
        first = jnp.where(h == 0, total[:half], total[half:])
        second = jnp.where(h == 0, total[half:], total[:half])

        def finish(parts):
            return self.ungroup(parts[0]).astype(f32) + lax.ppermute(parts[1], ("c", "h"), self.turned).astype(f32)

        return (first, second), finish

    def cut_order(self):
        return (lax.axis_index("q") ^ jnp.arange(self.quads)).astype(jnp.int32)

    def scatter_small(self, sums, norm):
        count = 2 * self.quads
        rows, wide = sums.shape[0] // count, sums.shape[1]
        norm = norm.reshape(3, 4 * count, -1).transpose(1, 0, 2)
        small = norm.shape[2]
        norm = jnp.pad(norm, ((0, 0), (0, 5), (0, BLK - small)))
        norm = lax.all_to_all(norm, self.both, split_axis=0, concat_axis=0, tiled=True)
        flat = jnp.pad(sums, ((0, 0), (0, -wide % 8))).reshape(count, -1, BLK)
        near = jnp.arange(self.quads) ^ lax.axis_index("q")
        h = lax.axis_index("h")
        keep, give = jnp.take(flat, 2 * near + h, axis=0), jnp.take(flat, 2 * near + 1 - h, axis=0)

        def finish(parts):
            keep, give, norm = parts
            part = keep + self.flip(give, "h")
            total = None
            for apart in range(self.quads):
                perm = []
                for source in range(4 * count):
                    q, c, h, w = source // 8, source // 4 % 2, source // 2 % 2, source % 2
                    perm.append((source, count * (2 * (1 - c) + w) + 2 * (q ^ apart) + h))
                got = lax.ppermute(part[apart], self.both, perm)
                total = got if total is None else total + got
            return total.reshape(rows, -1)[:, :wide], jnp.sum(norm, axis=0)[:3, :small]

        return (keep, give, norm), finish


def local(
    net, wave, tokens, cotangent, source, target, lengths, ln_gain, ln_bias, w_fwd, b_fwd, w_bwd, b_bwd,
    w_gate, b_gate, w_out, b_out, log_dt, log_rate, ssm_b, ssm_c, ssm_d,
):
    rows, width = tokens.shape
    many = rows // BLK
    n_t = net.n_t
    group = rows * n_t
    nb = group // BLK
    ch = w_fwd.shape[1]
    back = (wave.T / BIG).astype(bf16)
    wave = wave.astype(bf16)

    def lanes(column):
        return jnp.broadcast_to(column[..., None], column.shape + (BLK,))

    def decays(log_dt, log_rate, ssm_b):
        rate = jnp.exp(log_rate)
        ld = -jnp.exp(log_dt)[..., None] * rate
        return rate, ld, (1.0 - jnp.exp(ld)) / rate * ssm_b

    rank = rank_of(target)
    sender = source // group
    place = rank_of(sender * rows + jnp.arange(rows, dtype=jnp.int32))
    pack = jnp.concatenate(
        [w_fwd, w_bwd, w_gate.reshape(-1, 2 * ch), w_out.transpose(2, 0, 1).reshape(-1, 2 * ch)], axis=1
    )
    table = net.regroup(jnp.concatenate([place, lengths[0]]))
    rate, ld, drive = decays(log_dt, log_rate, ssm_b)
    own = b_fwd.shape[0]
    small = jnp.concatenate([ssm_d, b_fwd[None], b_bwd[None], b_gate])
    chan = jnp.concatenate(
        [
            (ld * log2e).reshape(own, 2 * STATE),
            (ssm_c * drive).reshape(own, 2 * STATE),
            jnp.pad(small, ((0, -(2 * own + 6) % 8 + 0), (0, 2 * STATE - own))),
        ]
    )
    norm = jnp.stack([ln_gain, ln_bias, b_out])
    (sent_g,) = permute_to(rank, [cotangent])
    sent_g, tokens = after((sent_g, tokens))
    got_g = net.spread(sent_g)
    got_x, chan_all, norm_all = net.enter(rank, tokens, chan, norm)
    got_x, got_g, chan_all, norm_all, pack, table = after((got_x, got_g, chan_all, norm_all, pack, table))
    packs = net.weights_first(pack)

    place, lens = table[:rows], table[rows:]
    gain = lanes(norm_all[0])
    shift = lanes(norm_all[1])
    small = chan_all[:, 2 * own : 2 * own + 6, :own].transpose(1, 0, 2).reshape(6, ch)

    def pairs(at):
        both = chan_all[:, at : at + own].reshape(-1, 2, own // 2, 2 * STATE)
        return both.transpose(1, 0, 2, 3).reshape(2, ch // 2, 2 * STATE)

    ld_pairs = pairs(0)
    w_pairs = pairs(own)
    skip = lanes(small[0:2])

    xt, xd = deal_x(place, got_x, gain, shift)
    x_got = net.gather_first(xt)
    _, ld_pairs, w_pairs, skip, packs = after((xt, ld_pairs, w_pairs, skip, packs))
    w_parts = net.weights_send(packs)
    kh = spectra(ld_pairs, w_pairs, skip, wave)
    kh, lens, small, norm_all = after((kh, lens, small, norm_all))
    live = live_rows(lens, group)
    live_own = lax.dynamic_slice_in_dim(live, net.place_of_group() * rows, rows, 0).reshape(many, 1, BLK)
    live = live.reshape(nb // 2, 1, BIG)
    tab, seq = sequence_tables(lens, nb)
    bias_in = lanes(small[2:6].reshape(-1))
    bias_out = lanes(norm_all[2])
    made = (bias_in, bias_out, tab, seq, live, live_own, net.cut_order(), net.order(many // 8))
    w_parts, x_got, kh, got_g, made = after((w_parts, x_got, kh, got_g, made))
    bias_in, bias_out, tab, seq, live, live_own, cut_order, order = made
    got_g = net.regroup(got_g)
    w_in, w_back, w_in_t, w_back_t = join_weights(cut_order, w_parts, 4 * ch)
    xs = net.gather_last(xt, x_got)
    kept = None
    for part, start in xs:
        kept = project(part, start, nb, live, w_in_t, bias_in, kept)
    kept, got_g = after((kept, got_g))
    a, da, gg, dg = kept
    gt, gd, g_bias_out = deal_g(place, got_g, live_own)
    gt, a = after((gt, a))
    g_got = net.gather_first(gt)
    y, mix = ssm_scan(tab, seq, a, kh, wave, back, gg)
    g_got, y, mix = after((g_got, y, mix))
    gs = net.gather_last(gt, g_got)
    branch = net.scatter_first(w_back, [mix], many)
    gm = gate_grad(gs, nb, w_back_t)
    branch, gm = after((branch, gm))

    branch = net.scatter_send(branch)
    branch = net.scatter_own(w_back, [mix], many) + branch
    first = ssm_back(0, tab, seq, a, gm, kh, wave, back, gg, y, dg, da)
    branch, first, a = after((branch, first, a))
    sent_out = layer_rows(place, branch, xd, live_own, bias_out)
    sent_out, a = after((sent_out, a))
    sent_out = net.ungroup(sent_out)
    second = ssm_back(1, tab, seq, a, gm, kh, wave, back, gg, y, dg, da)
    sent_out, first, second = after((sent_out, first, second))
    gpg, gp, gh, bsum = zip(first, second)
    sent_out = net.spread(sent_out)
    back_list = [gp[0], gp[1], gpg[0], gpg[1]]
    g_normed = net.scatter_first(w_in, back_list, many)
    g_normed, back_list, mix = after((g_normed, back_list, mix))
    gp, gpg = back_list[:2], back_list[2:]
    g_normed = net.scatter_send(g_normed)
    g_normed = net.scatter_own(w_in, back_list, many) + g_normed
    gw = outer_sums(order, net.cuts, [part for part, _ in xs], [part for part, _ in gs], gp, gpg, mix)
    g_normed, gw, gh, sent_out = after((g_normed, gw, gh, sent_out))
    sent_in, norm_sums = input_rows(place, g_normed, xd, gd, gain)
    sent_in, gh, gw, norm_sums, sent_out, bsum = after((sent_in, gh, gw, norm_sums, sent_out, bsum))
    sent_in = net.ungroup(sent_in)
    gw = net.grads_send(gw)
    s0, s1, g0 = [jnp.concatenate(part) for part in zip(*[moments(k, ld_pairs, gh[k], back) for k in range(2)])]
    layer_out = permute_from(rank, sent_out)

    s0 = s0.reshape(2, ch, STATE)
    s1 = s1.reshape(2, ch, STATE)
    bsum = jnp.concatenate(bsum)
    gb_gate = jnp.sum(bsum[:, :, :BLK], axis=2)
    gb_in = jnp.sum(bsum[:, :, BLK:], axis=2)
    sums = jnp.concatenate(
        [s0[0], s0[1], s1[0], s1[1], jnp.concatenate([g0[:, :, 0], gb_gate, gb_in], axis=0).T], axis=1
    )
    norm_sums = jnp.sum(jnp.concatenate([norm_sums, g_bias_out[None]], axis=0), axis=2)
    part, finish = net.scatter_small(sums, norm_sums)
    gw, gw_finish = net.grads_last(gw)
    sent_in, gw, part, layer_out = after((sent_in, gw, part, layer_out))
    in_grad = permute_from(rank, net.spread(sent_in))
    gw = gw_finish(gw)
    sums, norm_sums = finish(part)
    s0 = jnp.stack([sums[:, :STATE], sums[:, STATE : 2 * STATE]])
    s1 = jnp.stack([sums[:, 2 * STATE : 3 * STATE], sums[:, 3 * STATE : 4 * STATE]])
    tail = sums[:, 4 * STATE :].T
    step = jnp.exp(log_dt)[..., None]
    g_c = s0 * drive
    g_drive = s0 * ssm_c
    g_b = g_drive * (1.0 - jnp.exp(ld)) / rate
    g_ld = s1 * ssm_c * drive - g_drive * ssm_b / rate * jnp.exp(ld)
    g_rate = -g_drive * drive / rate - g_ld * step
    g_dt = jnp.sum(g_ld * ld, axis=2)
    return (
        layer_out,
        in_grad,
        norm_sums[0],
        norm_sums[1],
        gw[:, :ch],
        tail[4],
        gw[:, ch : 2 * ch],
        tail[5],
        gw[:, 2 * ch : 4 * ch].reshape(-1, 2, ch),
        tail[2:4],
        gw[:, 4 * ch :].T.reshape(2, ch, -1),
        norm_sums[2],
        g_dt,
        g_rate * rate,
        g_b,
        g_c,
        tail[0:2],
    )


def solution(mesh):
    n_dp, n_t = mesh.shape["dp"], mesh.shape["tensor"]
    if n_t == 4 and n_dp == 8:
        net = Pairs(n_dp, n_t)
        dp, tensor = ("q", "c"), ("h", "w")
    else:
        net = Line(n_dp, n_t)
        dp, tensor = ("dp",), ("tensor",)
    net.n_t = n_t
    mesh = jax.sharding.Mesh(mesh.devices.reshape(tuple(net.axes.values())), tuple(net.axes))
    both = P(dp + tensor)
    rows = P(dp + tensor, None)
    pair = P(None, dp + tensor)
    state = P(None, dp + tensor, None)
    proj = P(dp, tensor)
    gate = P(dp, None, tensor)
    out = P(None, tensor, dp)
    wave = wave_table()

    def run(*args):
        return local(net, jnp.asarray(wave), *args)

    return jax.shard_map(
        run,
        mesh=mesh,
        in_specs=(
            rows, rows, both, both, P(dp, None), both, both, proj, both, proj, both, gate, pair, out, both,
            pair, state, state, state, pair,
        ),
        out_specs=(
            rows, rows, both, both, proj, both, proj, both, gate, pair, out, both, pair, state, state, state, pair,
        ),
        check_vma=False,
    )
```
